32 devices in a mesh: grp: 4 (over y, x), dp: 8 (over z, core).
Axes of the slice: x: 2, y: 2, z: 4, core: 2. Of those that a mesh axis runs over, the one named last changes fastest.
Arguments:
- pixels: bfloat16 [4, 64, 256, 1024], P('grp', 'dp'), may hold values from -6 to 6
- keep_index: int32 [4, 64, 64], P('grp', 'dp'), may hold values from 0 to 255, as said below
- band_group: int32 [4, 64, 256], P('grp', 'dp'), may hold values from 0 to 3, as said below
- gsd_index: int32 [4, 64, 256], P('grp', 'dp'), may hold values from 0 to 511
- gsd_table: float32 [4, 512, 1536], P('grp'), may hold values from -4 to 4
- group_items: int32 [4], P('grp'), may hold values from 32 to 64, as said below
- step_count: int32 [1], replicated, may hold values from 2 to 20
- enc_cols: float32 [1024, 8192], P('dp'), may hold values from -0.1875 to 0.1875
- enc_rows: float32 [8192, 1024], P('dp'), may hold values from -0.09375 to 0.09375
- dec_cols: float32 [512, 4096], P('dp'), may hold values from -0.25 to 0.25
- dec_rows: float32 [4096, 512], P('dp'), may hold values from -0.1875 to 0.1875
- enc_gains: float32 [6, 1024], replicated
- dec_gains: float32 [7, 512], replicated
- moment_ecols: float32 [1024, 8192], P('dp'), may hold values from -1.5258789e-05 to 1.5258789e-05
- moment_erows: float32 [8192, 1024], P('dp'), may hold values from -1.5258789e-05 to 1.5258789e-05
- moment_dcols: float32 [512, 4096], P('dp'), may hold values from -1.5258789e-05 to 1.5258789e-05
- moment_drows: float32 [4096, 512], P('dp'), may hold values from -1.5258789e-05 to 1.5258789e-05
- moment_egains: float32 [6, 1024], replicated, may hold values from -3.0517578e-05 to 3.0517578e-05
- moment_dgains: float32 [7, 512], replicated, may hold values from -3.0517578e-05 to 3.0517578e-05
- square_ecols: float32 [1024, 8192], P('dp'), may hold values from 1.1915401e-12 to 4.7661606e-12
- square_erows: float32 [8192, 1024], P('dp'), may hold values from 1.1915401e-12 to 4.7661606e-12
- square_dcols: float32 [512, 4096], P('dp'), may hold values from 1.1915401e-12 to 4.7661606e-12
- square_drows: float32 [4096, 512], P('dp'), may hold values from 1.1915401e-12 to 4.7661606e-12
- square_egains: float32 [6, 1024], replicated, may hold values from 2.3830803e-12 to 9.532321e-12
- square_dgains: float32 [7, 512], replicated, may hold values from 2.3830803e-12 to 9.532321e-12
Outputs:
- clipped_ecols: float32 [1024, 8192], P('dp')
- squares_ecols: float32 [1024, 8192], P('dp')
- updated_ecols: float32 [1024, 8192], P('dp')
- clipped_erows: float32 [8192, 1024], P('dp')
- squares_erows: float32 [8192, 1024], P('dp')
- updated_erows: float32 [8192, 1024], P('dp')
- clipped_dcols: float32 [512, 4096], P('dp')
- squares_dcols: float32 [512, 4096], P('dp')
- updated_dcols: float32 [512, 4096], P('dp')
- clipped_drows: float32 [4096, 512], P('dp')
- squares_drows: float32 [4096, 512], P('dp')
- updated_drows: float32 [4096, 512], P('dp')
- clipped_egains: float32 [6, 1024], replicated
- squares_egains: float32 [6, 1024], replicated
- updated_egains: float32 [6, 1024], replicated
- clipped_dgains: float32 [7, 512], replicated
- squares_dgains: float32 [7, 512], replicated
- updated_dgains: float32 [7, 512], replicated
- loss: float32 [], replicated
- grad_norm: float32 [], replicated
The draws below stay inside these ranges and needn't reach their ends.
Inputs may be any that keep to these rules, and one draw needn't show every extreme that they name: `keep_index`: each item's 64 entries are distinct patch positions. `band_group`: in groups of odd index every entry is 3. `group_items`: one group uses all 64 slots and another group 64 // 2.
All inputs are finite; a program needn't handle non-finite values.
Results may differ from the reference program's by a relative error of at most 0.017.
Values may be sent and summed in bfloat16 or wider, within the bound.
A program may use at most 384 MiB of HBM per device.

```python
import math
import jax
import jax.numpy as jnp
from jax import lax

D = 1024
HEADS = 16
FF = 4096
DD = 512
DHEADS = 16
DFF = 2048
PIX = 1024
NBG = 4
L = 256
NPOS = 512
ITEMS_DEV = 8
K = 64
GROUPS = 4
ITEMS_GRP = 64
DE = 1536
PARAMS = 20981248
N_DP = 8


def draw_keep_index(key, part):
    keys = jax.random.split(key, GROUPS * ITEMS_GRP)
    orders = jax.vmap(lambda item_key: jax.random.permutation(item_key, L)[:K])(keys)
    return orders.reshape(GROUPS, ITEMS_GRP, K).astype(jnp.int32)


def draw_band_group(key, part):
    labels = jax.random.randint(key, (GROUPS, ITEMS_GRP, L), 0, NBG)
    odd_group = (jnp.arange(GROUPS) % 2 == 1)[:, None, None]
    return jnp.where(odd_group, NBG - 1, labels).astype(jnp.int32)


def draw_group_items(key, part):
    first_key, second_key = jax.random.split(key)
    low_end = ITEMS_GRP // 2
    counts = jax.random.randint(first_key, (GROUPS,), low_end, ITEMS_GRP + 1)
    order = jax.random.permutation(second_key, GROUPS)
    counts = counts.at[order[0]].set(ITEMS_GRP).at[order[1]].set(low_end)
    return counts.astype(jnp.int32)


def vector_rows(key, count_rows, width, with_token):
    noise = jax.random.normal(key, (count_rows, width), jnp.float32)
    index = jnp.arange(count_rows)[:, None]
    values = jnp.where(index % 2 == 0, 1.0 + 0.2 * noise, 0.3 * noise)
    if with_token:
        values = jnp.where(index == count_rows - 1, noise, values)
    return values


def draw_enc_gains(key, part):
    return vector_rows(key, 6, D, False)


def draw_dec_gains(key, part):
    return vector_rows(key, 7, DD, True)


def touch_ends(drawn, key, low, top_value):
    longest = drawn.shape.index(max(drawn.shape))
    spots = []
    for shift in (0, 1):
        where = [jax.random.randint(jax.random.fold_in(key, axis), (), 0, length) for axis, length in enumerate(drawn.shape)]
        where[longest] = (where[longest] + shift) % drawn.shape[longest]
        spots.append(tuple(where))
    return drawn.at[spots[0]].set(low).at[spots[1]].set(top_value)


def steps_of(rng, extent, cuts, least, top_value):
    level, own = 1.0, jax.random.fold_in(rng, 6)
    for axis_at, blocks in cuts:
        draws = jnp.exp(jax.random.uniform(jax.random.fold_in(own, axis_at), (blocks,), jnp.float32, least / len(cuts), top_value / len(cuts)))
        level = level * jnp.repeat(draws, extent[axis_at] // blocks).reshape([-1 if axis == axis_at else 1 for axis in range(len(extent))])
    return level


def scatter_about(rng, shape, scale, limit, shards=(), kind=jnp.bfloat16):
    result = scale * jax.random.normal(rng, shape, jnp.float32)
    if shards:
        result = result * steps_of(rng, shape, shards, -0.22, 0.18)
    return jnp.clip(result, -limit, limit).astype(kind)


def setup_inputs(seed: int = 0) -> dict:
    arg_keys = jax.random.split(jax.random.key(seed), 26)
    return {
        "pixels": scatter_about(arg_keys[0], (GROUPS, ITEMS_GRP, L, PIX), 1.0, 6.0, ((0, 4), (1, 8))),
        "keep_index": draw_keep_index(jax.random.fold_in(arg_keys[25], 71), 0),
        "band_group": draw_band_group(jax.random.fold_in(arg_keys[25], 71), 0),
        "gsd_index": touch_ends(jax.random.randint(arg_keys[3], (GROUPS, ITEMS_GRP, L), 0, NPOS), jax.random.fold_in(arg_keys[3], 1), 0, NPOS - 1).astype(jnp.int32),
        "gsd_table": scatter_about(arg_keys[4], (GROUPS, NPOS, DE), 0.5, 4.0, ((0, 4),), jnp.float32),
        "group_items": draw_group_items(jax.random.fold_in(arg_keys[25], 71), 0),
        "step_count": jax.random.randint(arg_keys[6], (1,), 2, 21).astype(jnp.int32),
        "enc_cols": scatter_about(arg_keys[7], (D, 4 * D + FF), D ** -0.5, 0.1875, ((0, 8),), jnp.float32),
        "enc_rows": scatter_about(arg_keys[8], (FF + NBG * PIX, D), FF ** -0.5, 0.09375, ((0, 8),), jnp.float32),
        "dec_cols": scatter_about(arg_keys[9], (DD, 4 * DD + DFF), DD ** -0.5, 0.25, ((0, 8),), jnp.float32),
        "dec_rows": scatter_about(arg_keys[10], (DFF + D + PIX, DD), D ** -0.5, 0.1875, ((0, 8),), jnp.float32),
        "enc_gains": draw_enc_gains(jax.random.fold_in(arg_keys[25], 71), 0),
        "dec_gains": draw_dec_gains(jax.random.fold_in(arg_keys[25], 71), 0),
        "moment_ecols": scatter_about(arg_keys[13], (D, 4 * D + FF), (0.005 * PARAMS ** -0.5), 1.52587890625e-05, ((0, 8),), jnp.float32),
        "moment_erows": scatter_about(arg_keys[14], (FF + NBG * PIX, D), (0.005 * PARAMS ** -0.5), 1.52587890625e-05, ((0, 8),), jnp.float32),
        "moment_dcols": scatter_about(arg_keys[15], (DD, 4 * DD + DFF), (0.005 * PARAMS ** -0.5), 1.52587890625e-05, ((0, 8),), jnp.float32),
        "moment_drows": scatter_about(arg_keys[16], (DFF + D + PIX, DD), (0.005 * PARAMS ** -0.5), 1.52587890625e-05, ((0, 8),), jnp.float32),
        "moment_egains": scatter_about(arg_keys[17], (6, D), (0.01 * PARAMS ** -0.5), 3.0517578125e-05, (), jnp.float32),
        "moment_dgains": scatter_about(arg_keys[18], (7, DD), (0.01 * PARAMS ** -0.5), 3.0517578125e-05, (), jnp.float32),
        "square_ecols": jnp.clip(jnp.exp(math.log(4.766160556501919e-12) - 1.3862944 * jax.random.uniform(arg_keys[19], (D, 4 * D + FF), jnp.float32) ** steps_of(arg_keys[19], (D, 4 * D + FF), ((0, 8),), -0.2, 0.2)), 1.1915401391254798e-12, 4.766160556501919e-12),
        "square_erows": jnp.clip(jnp.exp(math.log(4.766160556501919e-12) - 1.3862944 * jax.random.uniform(arg_keys[20], (FF + NBG * PIX, D), jnp.float32) ** steps_of(arg_keys[20], (FF + NBG * PIX, D), ((0, 8),), -0.2, 0.2)), 1.1915401391254798e-12, 4.766160556501919e-12),
        "square_dcols": jnp.clip(jnp.exp(math.log(4.766160556501919e-12) - 1.3862944 * jax.random.uniform(arg_keys[21], (DD, 4 * DD + DFF), jnp.float32) ** steps_of(arg_keys[21], (DD, 4 * DD + DFF), ((0, 8),), -0.2, 0.2)), 1.1915401391254798e-12, 4.766160556501919e-12),
        "square_drows": jnp.clip(jnp.exp(math.log(4.766160556501919e-12) - 1.3862944 * jax.random.uniform(arg_keys[22], (DFF + D + PIX, DD), jnp.float32) ** steps_of(arg_keys[22], (DFF + D + PIX, DD), ((0, 8),), -0.2, 0.2)), 1.1915401391254798e-12, 4.766160556501919e-12),
        "square_egains": jnp.clip(jnp.exp(jax.random.uniform(arg_keys[23], (6, D), jnp.float32, math.log(2.3830802782509597e-12), math.log(9.532321113003839e-12))), 2.3830802782509597e-12, 9.532321113003839e-12),
        "square_dgains": jnp.clip(jnp.exp(jax.random.uniform(arg_keys[24], (7, DD), jnp.float32, math.log(2.3830802782509597e-12), math.log(9.532321113003839e-12))), 2.3830802782509597e-12, 9.532321113003839e-12),
    }


@jax.custom_vjp
def low(v):
    return lax.optimization_barrier(v.astype(jnp.bfloat16)).astype(jnp.float32)

@jax.custom_vjp
def low_back(v):
    return v

def low_keep(v):
    return (low(v), None)

def low_pass(kept, grad):
    return (grad,)

def back_keep(v):
    return (v, None)

def back_low(kept, grad):
    return (low(grad),)
low.defvjp(low_keep, low_pass)
low_back.defvjp(back_keep, back_low)
norm_eps = 1e-06
clip_level = 0.005
learn_rate = 0.02
gain_rate = 0.25
weight_decay = 0.05
adam_eps = 1e-08
beta_first = 0.5
beta_second = 0.5
highest = lax.Precision.HIGHEST

def project(inputs, matrix):
    return jnp.einsum('...n,nm->...m', inputs, matrix, precision=highest)

def layer_norm(values, gain, shift):
    centred = values - lax.optimization_barrier(jnp.mean(values, -1, keepdims=True))
    return centred * lax.rsqrt(lax.optimization_barrier(jnp.mean(centred * centred, -1, keepdims=True)) + norm_eps) * gain + shift

def block(inputs, columns, down_rows, gains, heads):
    batch, tokens, width = inputs.shape
    size_head = width // heads
    first_in = low(layer_norm(inputs, gains[0], gains[1]))
    packed = low(low_back(project(first_in, columns[:, :3 * width])))
    shape = (batch, tokens, heads, size_head)
    queries = packed[..., :width].reshape(shape)
    key_part = packed[..., width:2 * width].reshape(shape)
    val_part = packed[..., 2 * width:].reshape(shape)
    scores = low_back(jnp.einsum('bqhe,bkhe->bhqk', queries, key_part, precision=highest) * size_head ** (-0.5))
    attn_prob = low(jnp.exp(scores - jax.nn.logsumexp(scores, -1, keepdims=True)))
    mixed = low_back(jnp.einsum('bhqk,bkhe->bqhe', attn_prob, val_part, precision=highest).reshape(inputs.shape))
    middle = inputs + low_back(project(low(mixed), columns[:, 3 * width:4 * width]))
    second_in = low(layer_norm(middle, gains[2], gains[3]))
    hidden = low_back(project(second_in, columns[:, 4 * width:]))
    activated = low(jax.nn.gelu(hidden, approximate=False))
    return middle + low_back(project(activated, down_rows))

def items_loss(weights, pixel_rows, keep_rows, band_rows, index_rows, table, valid, masked):
    enc_cols, enc_rows, dec_cols, dec_rows, enc_gains, dec_gains = weights
    batch = pixel_rows.shape[0]
    pixel_float = pixel_rows.astype(jnp.float32)
    kept_pixels = jnp.take_along_axis(pixel_float, keep_rows[..., None], 1)
    kept_bands = jnp.take_along_axis(band_rows, keep_rows, 1)
    onehot = (kept_bands[..., None] == jnp.arange(NBG, dtype=jnp.int32)).astype(jnp.float32)
    spread = low((onehot[..., None] * kept_pixels[:, :, None, :]).reshape(batch, K, NBG * PIX))
    embedded = low_back(project(spread, enc_rows[FF:]))
    position = jnp.take(table, index_rows, axis=0)
    enc_input = embedded + jnp.take_along_axis(position[..., :D], keep_rows[..., None], 1)
    enc_out = block(enc_input, enc_cols, enc_rows[:FF], enc_gains, HEADS)
    enc_low = low(layer_norm(enc_out, enc_gains[4], enc_gains[5]))
    latent = low_back(project(enc_low, dec_rows[DFF:DFF + D]))
    item_rows = jnp.arange(batch)[:, None]
    hidden_mask = jnp.ones((batch, L), jnp.float32).at[item_rows, keep_rows].set(0.0)
    dec_input = hidden_mask[..., None] * dec_gains[6] + position[..., D:]
    dec_input = dec_input.at[item_rows, keep_rows].add(latent)
    dec_out = block(dec_input, dec_cols, dec_rows[:DFF], dec_gains, DHEADS)
    dec_low = low(layer_norm(dec_out, dec_gains[4], dec_gains[5]))
    predicted = low_back(jnp.einsum('blj,pj->blp', dec_low, dec_rows[DFF + D:], precision=highest))
    centred = pixel_float - lax.optimization_barrier(jnp.mean(pixel_float, -1, keepdims=True))
    target = centred * lax.rsqrt(lax.optimization_barrier(jnp.mean(centred * centred, -1, keepdims=True)) + norm_eps)
    per_patch = lax.optimization_barrier(jnp.mean((predicted - target) ** 2, -1))
    return jnp.sum(per_patch * hidden_mask * valid[:, None]) / masked

def adam_step(master, moment, square, grad, factor, fix_one, fix_two, decay, rate):
    clipped = grad * factor
    moment_new = beta_first * moment + (1.0 - beta_first) * clipped
    square_new = beta_second * square + (1.0 - beta_second) * clipped * clipped
    direction = moment_new / fix_one / (jnp.sqrt(square_new / fix_two) + adam_eps) + decay * master
    return (clipped, square_new, master - rate * direction)

def reference(pixels, keep_index, band_group, gsd_index, gsd_table, group_items, step_count, enc_cols, enc_rows, dec_cols, dec_rows, enc_gains, dec_gains, moment_ecols, moment_erows, moment_dcols, moment_drows, moment_egains, moment_dgains, square_ecols, square_erows, square_dcols, square_drows, square_egains, square_dgains):
    masked = jnp.sum(group_items).astype(jnp.float32) * (L - K)
    blocks = GROUPS * N_DP

    def regroup(array):
        return array.reshape((blocks, ITEMS_DEV) + array.shape[2:])
    numbers = jnp.arange(blocks, dtype=jnp.int32)
    data = (regroup(pixels), regroup(keep_index), regroup(band_group), regroup(gsd_index), numbers)

    def total(params):
        weights = tuple((low(param) for param in params[:4])) + tuple(params[4:])

        def one_block(carry, block_in):
            pixel_rows, keep_rows, band_rows, index_rows, number = block_in
            group = number // N_DP
            table = lax.dynamic_index_in_dim(gsd_table, group, 0, keepdims=False)
            count = lax.dynamic_index_in_dim(group_items, group, 0, keepdims=False)
            items = number % N_DP * ITEMS_DEV + jnp.arange(ITEMS_DEV, dtype=jnp.int32)
            valid = (items < count).astype(jnp.float32)
            part_loss = jax.checkpoint(items_loss)(weights, pixel_rows, keep_rows, band_rows, index_rows, table, valid, masked)
            return (carry + part_loss, None)
        summed, unused = lax.scan(one_block, jnp.zeros((), jnp.float32), data)
        return summed
    params = (enc_cols, enc_rows, dec_cols, dec_rows, enc_gains, dec_gains)
    loss, pull = jax.vjp(total, params)
    grads = pull(jnp.ones((), jnp.float32))[0]
    grad_norm = jnp.sqrt(sum((jnp.sum(grad * grad) for grad in grads)))
    factor = clip_level / jnp.maximum(grad_norm, clip_level)
    count_steps = step_count[0].astype(jnp.float32)
    fix_one = 1.0 - beta_first ** count_steps
    fix_two = 1.0 - beta_second ** count_steps
    clipped_ecols, squares_ecols, updated_ecols = adam_step(enc_cols, moment_ecols, square_ecols, grads[0], factor, fix_one, fix_two, weight_decay, learn_rate)
    clipped_erows, squares_erows, updated_erows = adam_step(enc_rows, moment_erows, square_erows, grads[1], factor, fix_one, fix_two, weight_decay, learn_rate)
    clipped_dcols, squares_dcols, updated_dcols = adam_step(dec_cols, moment_dcols, square_dcols, grads[2], factor, fix_one, fix_two, weight_decay, learn_rate)
    clipped_drows, squares_drows, updated_drows = adam_step(dec_rows, moment_drows, square_drows, grads[3], factor, fix_one, fix_two, weight_decay, learn_rate)
    clipped_egains, squares_egains, updated_egains = adam_step(enc_gains, moment_egains, square_egains, grads[4], factor, fix_one, fix_two, 0.0, gain_rate)
    clipped_dgains, squares_dgains, updated_dgains = adam_step(dec_gains, moment_dgains, square_dgains, grads[5], factor, fix_one, fix_two, 0.0, gain_rate)
    return (clipped_ecols, squares_ecols, updated_ecols, clipped_erows, squares_erows, updated_erows, clipped_dcols, squares_dcols, updated_dcols, clipped_drows, squares_drows, updated_drows, clipped_egains, squares_egains, updated_egains, clipped_dgains, squares_dgains, updated_dgains, loss, grad_norm)
```

```python
import functools

import jax
import jax.numpy as jnp
from jax import lax
from jax.experimental import pallas as pl
from jax.experimental.pallas import tpu as pltpu
from jax.sharding import PartitionSpec as P

D = 1024
HEADS = 16
FF = 4096
DHEADS = 16
DFF = 2048
PIX = 1024
NBG = 4
L = 256
K = 64


norm_eps = 1e-06
clip_level = 0.005
learn_rate = 0.02
gain_rate = 0.25
weight_decay = 0.05
adam_eps = 1e-08
beta_first = 0.5
beta_second = 0.5


def to_low(value):
    return value.astype(jnp.bfloat16)


def project(inputs, matrix):
    return jnp.einsum("...n,nm->...m", inputs, matrix, preferred_element_type=jnp.float32)


def project_back(grads, matrix):
    return jnp.einsum("...m,nm->...n", grads, matrix, preferred_element_type=jnp.float32)


def weight_grad(inputs, grads):
    flat_in = inputs.reshape(-1, inputs.shape[-1])
    flat_grad = grads.reshape(-1, grads.shape[-1])
    return lax.dot_general(
        flat_in, flat_grad, (((0,), (0,)), ((), ())), preferred_element_type=jnp.float32
    )


def norm_forward(values, gain, shift):
    centred = values - jnp.mean(values, -1, keepdims=True)
    scaled = lax.rsqrt(jnp.mean(centred * centred, -1, keepdims=True) + norm_eps)
    normed = centred * scaled
    return (normed * gain + shift, normed, scaled)


def norm_backward(grads, normed, scaled, gain):
    inner = grads * gain
    back = scaled * (
        inner
        - jnp.mean(inner, -1, keepdims=True)
        - normed * jnp.mean(inner * normed, -1, keepdims=True)
    )
    flat_grad = grads.reshape(-1, grads.shape[-1])
    flat_norm = normed.reshape(-1, normed.shape[-1])
    return (back, jnp.sum(flat_grad * flat_norm, 0), jnp.sum(flat_grad, 0))


def gelu_parts(hidden):
    cumul = 0.5 * (1.0 + jax.scipy.special.erf(hidden * 0.7071067811865476))
    return (hidden * cumul, cumul + hidden * jnp.exp(-0.5 * hidden * hidden) * 0.3989422804014327)


def split_heads(packed, width, heads):
    shape = (packed.shape[0], packed.shape[1], heads, width // heads)
    return (
        packed[..., :width].reshape(shape),
        packed[..., width : 2 * width].reshape(shape),
        packed[..., 2 * width :].reshape(shape),
    )


def head_scores(queries, key_part, scale):
    return (
        jnp.einsum("bqhe,bkhe->bhqk", queries, key_part, preferred_element_type=jnp.float32) * scale
    )


def block_forward(inputs, columns, down_rows, gains, heads):
    width = inputs.shape[-1]
    scale = (width // heads) ** (-0.5)
    normed_one, hat_one, scale_one = norm_forward(inputs, gains[0], gains[1])
    first_in = to_low(normed_one)
    packed = to_low(project(first_in, columns[:, : 3 * width]))
    queries, key_part, val_part = split_heads(packed, width, heads)
    scores = head_scores(queries, key_part, scale)
    log_total = jax.nn.logsumexp(scores, -1, keepdims=True)
    attn_prob = to_low(jnp.exp(scores - log_total))
    mixed = jnp.einsum("bhqk,bkhe->bqhe", attn_prob, val_part, preferred_element_type=jnp.float32)
    mixed = to_low(mixed.reshape(inputs.shape))
    middle = inputs + project(mixed, columns[:, 3 * width : 4 * width])
    normed_two, hat_two, scale_two = norm_forward(middle, gains[2], gains[3])
    second_in = to_low(normed_two)
    hidden = project(second_in, columns[:, 4 * width :])
    activated = to_low(gelu_parts(hidden)[0])
    output = middle + project(activated, down_rows)
    saved = (
        hat_one,
        scale_one,
        first_in,
        packed,
        log_total,
        mixed,
        hat_two,
        scale_two,
        second_in,
        hidden,
        activated,
    )
    return (output, saved)


def block_backward(grad_out, columns, down_rows, gains, heads, saved):
    (
        hat_one,
        scale_one,
        first_in,
        packed,
        log_total,
        mixed,
        hat_two,
        scale_two,
        second_in,
        hidden,
        activated,
    ) = saved
    width = grad_out.shape[-1]
    scale = (width // heads) ** (-0.5)
    grad_low = to_low(grad_out)
    grad_down = weight_grad(activated, grad_low)
    grad_hidden = to_low(project_back(grad_low, down_rows) * gelu_parts(hidden)[1])
    grad_up = weight_grad(second_in, grad_hidden)
    back_two, gain_two, shift_two = norm_backward(
        project_back(grad_hidden, columns[:, 4 * width :]), hat_two, scale_two, gains[2]
    )
    grad_middle = grad_out + back_two
    middle_low = to_low(grad_middle)
    grad_proj = weight_grad(mixed, middle_low)
    head_shape = packed.shape[:2] + (heads, width // heads)
    grad_mixed = to_low(
        project_back(middle_low, columns[:, 3 * width : 4 * width]).reshape(head_shape)
    )
    queries, key_part, val_part = split_heads(packed, width, heads)
    attn_prob = jnp.exp(head_scores(queries, key_part, scale) - log_total)
    grad_prob = jnp.einsum(
        "bqhe,bkhe->bhqk", grad_mixed, val_part, preferred_element_type=jnp.float32
    )
    grad_val = jnp.einsum(
        "bhqk,bqhe->bkhe", to_low(attn_prob), grad_mixed, preferred_element_type=jnp.float32
    )
    grad_score = to_low(attn_prob * (grad_prob - jnp.sum(grad_prob * attn_prob, -1, keepdims=True)))
    grad_query = (
        jnp.einsum("bhqk,bkhe->bqhe", grad_score, key_part, preferred_element_type=jnp.float32)
        * scale
    )
    grad_key = (
        jnp.einsum("bhqk,bqhe->bkhe", grad_score, queries, preferred_element_type=jnp.float32)
        * scale
    )
    flat_shape = packed.shape[:2] + (width,)
    grad_packed = to_low(
        jnp.concatenate(
            [
                grad_query.reshape(flat_shape),
                grad_key.reshape(flat_shape),
                grad_val.reshape(flat_shape),
            ],
            -1,
        )
    )
    grad_qkv = weight_grad(first_in, grad_packed)
    back_one, gain_one, shift_one = norm_backward(
        project_back(grad_packed, columns[:, : 3 * width]), hat_one, scale_one, gains[0]
    )
    grad_in = grad_middle + back_one
    grad_cols = (grad_qkv, grad_proj, grad_up)
    grad_gains = jnp.stack([gain_one, shift_one, gain_two, shift_two])
    return (grad_in, grad_cols, grad_down, grad_gains)


def dot_nn(a, b):
    return lax.dot_general(a, b, (((1,), (0,)), ((), ())), preferred_element_type=jnp.float32)


def dot_nt(a, b):
    return lax.dot_general(a, b, (((1,), (1,)), ((), ())), preferred_element_type=jnp.float32)


def dot_tn(a, b):
    return lax.dot_general(a, b, (((0,), (0,)), ((), ())), preferred_element_type=jnp.float32)


def unit_rows(values):
    centred = values - jnp.mean(values, -1, keepdims=True)
    scaled = lax.rsqrt(jnp.mean(centred * centred, -1, keepdims=True) + norm_eps)
    return centred * scaled, scaled


def unit_back(grads, hat, scaled, gain):
    inner = grads * gain
    return scaled * (
        inner
        - jnp.mean(inner, -1, keepdims=True)
        - hat * jnp.mean(inner * hat, -1, keepdims=True)
    )


def decoder_kernel(
    items, heads, scal_ref, z_ref, pos_ref, pix_ref, cols_ref, down_ref, head_ref, gains_ref,
    dz_ref, gcols_out, gdown_out, ghead_out, ggains_ref, loss_ref,
    x_s, h1_s, qkv_s, p_s, o_s, x1_s, h2_s, a_s, gp_s, x2_s, hd_s, dx_s, dy_s, acc_s, dqkv_s,
    gcols, gdown, ghead,
):
    low = jnp.bfloat16
    step = pl.program_id(0)
    width = x_s.shape[1]
    tokens = pos_ref.shape[1]
    hide = tokens - K
    rows = items * tokens
    tile = 512
    grp_heads = 4
    lanes = 128
    ee = width // heads
    scale = ee ** (-0.5)
    expo = scale * 1.4426950408889634

    @pl.when(step == 0)
    def _():
        gcols[...] = jnp.zeros_like(gcols)
        gdown[...] = jnp.zeros_like(gdown)
        ghead[...] = jnp.zeros_like(ghead)
        ggains_ref[...] = jnp.zeros_like(ggains_ref)
        loss_ref[...] = jnp.zeros_like(loss_ref)

    def gain(i):
        return gains_ref[i : i + 1, :]

    for i in range(items):
        base = i * tokens
        x_s[base : base + K, :] = pos_ref[i, :K, :] + z_ref[i]
        x_s[base + K : base + tokens, :] = pos_ref[i, K:, :] + gain(6)
    hat, _ = unit_rows(x_s[...])
    h1_s[...] = (hat * gain(0) + gain(1)).astype(low)

    @pl.loop(0, 3)
    def _(t):
        at = pl.ds(pl.multiple_of(t * width, width), width)
        qkv_s[:, at] = dot_nn(h1_s[...], cols_ref[:, at]).astype(low)

    lane = lax.broadcasted_iota(jnp.int32, (1, lanes), 1) // ee
    groups = width // lanes

    def masked(value, h):
        return jnp.where(lane == h, value, jnp.zeros_like(value))

    @pl.loop(0, items * groups)
    def _(n):
        item = n // groups
        g = n % groups
        rs = pl.ds(pl.multiple_of(item * tokens, tokens), tokens)
        q = qkv_s[rs, pl.ds(pl.multiple_of(g * lanes, lanes), lanes)]
        k = qkv_s[rs, pl.ds(pl.multiple_of(width + g * lanes, lanes), lanes)]
        v = qkv_s[rs, pl.ds(pl.multiple_of(2 * width + g * lanes, lanes), lanes)]
        out = jnp.zeros((tokens, lanes), jnp.float32)
        for h in range(grp_heads):
            s = dot_nt(masked(q, h), k)
            top = jnp.max(s, -1, keepdims=True)
            e = jnp.exp2((s - top) * expo)
            p = (e * (1.0 / jnp.sum(e, -1, keepdims=True))).astype(low)
            p_s[n * grp_heads + h] = p
            out = out + dot_nn(p, masked(v, h))
        o_s[rs, pl.ds(pl.multiple_of(g * lanes, lanes), lanes)] = out.astype(low)

    x1_s[...] = x_s[...] + dot_nn(o_s[...], cols_ref[:, 3 * width : 4 * width])
    hat, _ = unit_rows(x1_s[...])
    h2_s[...] = (hat * gain(2) + gain(3)).astype(low)
    x2_s[...] = x1_s[...]

    @pl.loop(0, down_ref.shape[0] // tile)
    def _(t):
        at = pl.ds(pl.multiple_of(t * tile, tile), tile)
        up = pl.ds(pl.multiple_of(4 * width + t * tile, tile), tile)
        u = dot_nn(h2_s[...], cols_ref[:, up])
        cumul = 0.5 * (1.0 + lax.erf(u * 0.7071067811865476))
        act = (u * cumul).astype(low)
        a_s[:, at] = act
        gp_s[:, at] = (cumul + u * jnp.exp(-0.5 * u * u) * 0.3989422804014327).astype(gp_s.dtype)
        x2_s[...] += dot_nn(act, down_ref[at, :])

    hat, _ = unit_rows(x2_s[...])
    hd_s[...] = (hat * gain(4) + gain(5)).astype(low)

    pixel_count = head_ref.shape[0]
    for i in range(items):
        base = i * tokens
        weight = scal_ref[0, step * items + i]
        coef = scal_ref[1, step * items + i]
        pixel = pix_ref[i].astype(jnp.float32)
        target, _ = unit_rows(pixel)
        hd = hd_s[base + K : base + tokens, :]
        back = jnp.zeros((hide, width), jnp.float32)
        for t in range(pixel_count // tile):
            at = slice(t * tile, (t + 1) * tile)
            err = dot_nt(hd, head_ref[at, :]) - target[:, at]
            loss_ref[...] += weight * jnp.sum(err * err, keepdims=True).reshape(1, 1)
            dpred = (err * coef).astype(low)
            ghead[at, :] += dot_tn(dpred, hd)
            back = back + dot_nn(dpred, head_ref[at, :])
        hat, scaled = unit_rows(x2_s[base + K : base + tokens, :])
        ggains_ref[4:5, :] += jnp.sum(back * hat, 0, keepdims=True)
        ggains_ref[5:6, :] += jnp.sum(back, 0, keepdims=True)
        dx = unit_back(back, hat, scaled, gain(4))
        dx_s[base : base + K, :] = jnp.zeros((K, width), jnp.float32)
        dx_s[base + K : base + tokens, :] = dx
        dy_s[base : base + K, :] = jnp.zeros((K, width), low)
        dy_s[base + K : base + tokens, :] = dx.astype(low)

    acc_s[...] = jnp.zeros_like(acc_s)

    @pl.loop(0, down_ref.shape[0] // tile)
    def _(t):
        at = pl.ds(pl.multiple_of(t * tile, tile), tile)
        up = pl.ds(pl.multiple_of(4 * width + t * tile, tile), tile)
        gdown[at, :] += dot_tn(a_s[:, at], dy_s[...])
        du = (dot_nt(dy_s[...], down_ref[at, :]) * gp_s[:, at].astype(jnp.float32)).astype(low)
        gcols[:, up] += dot_tn(h2_s[...], du)
        acc_s[...] += dot_nt(du, cols_ref[:, up])

    hat, scaled = unit_rows(x1_s[...])
    grads = acc_s[...]
    ggains_ref[2:3, :] += jnp.sum(grads * hat, 0, keepdims=True)
    ggains_ref[3:4, :] += jnp.sum(grads, 0, keepdims=True)
    dx_s[...] += unit_back(grads, hat, scaled, gain(2))
    dy_s[...] = dx_s[...].astype(low)
    gcols[:, 3 * width : 4 * width] += dot_tn(o_s[...], dy_s[...])
    o_s[...] = dot_nt(dy_s[...], cols_ref[:, 3 * width : 4 * width]).astype(low)

    @pl.loop(0, items * groups)
    def _(n):
        item = n // groups
        g = n % groups
        rs = pl.ds(pl.multiple_of(item * tokens, tokens), tokens)
        qa = pl.ds(pl.multiple_of(g * lanes, lanes), lanes)
        ka = pl.ds(pl.multiple_of(width + g * lanes, lanes), lanes)
        va = pl.ds(pl.multiple_of(2 * width + g * lanes, lanes), lanes)
        q = qkv_s[rs, qa]
        k = qkv_s[rs, ka]
        v = qkv_s[rs, va]
        do = o_s[rs, qa]
        dq = jnp.zeros((tokens, lanes), jnp.float32)
        dk = jnp.zeros((tokens, lanes), jnp.float32)
        dv = jnp.zeros((tokens, lanes), jnp.float32)
        for h in range(grp_heads):
            p = p_s[n * grp_heads + h]
            dom = masked(do, h)
            dp = dot_nt(dom, v)
            pf = p.astype(jnp.float32)
            ds = (pf * (dp - jnp.sum(dp * pf, -1, keepdims=True))).astype(low)
            dv = dv + dot_tn(p, dom)
            dq = dq + dot_nn(ds, masked(k, h))
            dk = dk + dot_tn(ds, masked(q, h))
        dqkv_s[rs, qa] = (dq * scale).astype(low)
        dqkv_s[rs, ka] = (dk * scale).astype(low)
        dqkv_s[rs, va] = dv.astype(low)

    acc_s[...] = jnp.zeros_like(acc_s)

    @pl.loop(0, 3)
    def _(t):
        at = pl.ds(pl.multiple_of(t * width, width), width)
        gcols[:, at] += dot_tn(h1_s[...], dqkv_s[:, at])
        acc_s[...] += dot_nt(dqkv_s[:, at], cols_ref[:, at])

    hat, scaled = unit_rows(x_s[...])
    grads = acc_s[...]
    ggains_ref[0:1, :] += jnp.sum(grads * hat, 0, keepdims=True)
    ggains_ref[1:2, :] += jnp.sum(grads, 0, keepdims=True)
    dx_s[...] += unit_back(grads, hat, scaled, gain(0))
    for i in range(items):
        base = i * tokens
        dz_ref[i] = dx_s[base : base + K, :].astype(low)
        ggains_ref[6:7, :] += jnp.sum(dx_s[base + K : base + tokens, :], 0, keepdims=True)

    @pl.when(step == pl.num_programs(0) - 1)
    def _():
        gcols_out[...] = gcols[...].astype(low)
        gdown_out[...] = gdown[...].astype(low)
        ghead_out[...] = ghead[...].astype(low)


def decoder_call(scal, latent, position, pixel_rows, cols, down, head, gains, heads):
    batch, tokens, width = position.shape
    pixel_count = head.shape[0]
    items = 2
    rows = items * tokens
    hide = tokens - K
    low = jnp.bfloat16
    full = pl.Buffered(1)

    def whole(array):
        return pl.BlockSpec(array.shape, lambda s: (0,) * array.ndim, pipeline_mode=full)

    def by_item(shape):
        return pl.BlockSpec((items,) + shape, lambda s: (s, 0, 0))

    outs = (
        jax.ShapeDtypeStruct((batch, K, width), low),
        jax.ShapeDtypeStruct(cols.shape, low),
        jax.ShapeDtypeStruct(down.shape, low),
        jax.ShapeDtypeStruct(head.shape, low),
        jax.ShapeDtypeStruct((8, width), jnp.float32),
        jax.ShapeDtypeStruct((1, 1), jnp.float32),
    )
    vmem = pltpu.VMEM
    f32 = jnp.float32
    return pl.pallas_call(
        functools.partial(decoder_kernel, items, heads),
        grid=(batch // items,),
        in_specs=[
            pl.BlockSpec(memory_space=pltpu.SMEM),
            by_item((K, width)),
            by_item((tokens, width)),
            by_item((hide, pixel_count)),
            whole(cols),
            whole(down),
            whole(head),
            whole(gains),
        ],
        out_specs=(by_item((K, width)),) + tuple(whole(out) for out in outs[1:]),
        out_shape=outs,
        scratch_shapes=[
            vmem((rows, width), f32),
            vmem((rows, width), low),
            vmem((rows, 3 * width), low),
            vmem((items * heads, tokens, tokens), low),
            vmem((rows, width), low),
            vmem((rows, width), f32),
            vmem((rows, width), low),
            vmem((rows, down.shape[0]), low),
            vmem((rows, down.shape[0]), f32),
            vmem((rows, width), f32),
            vmem((rows, width), low),
            vmem((rows, width), f32),
            vmem((rows, width), low),
            vmem((rows, width), f32),
            vmem((rows, 3 * width), low),
            vmem(cols.shape, f32),
            vmem(down.shape, f32),
            vmem(head.shape, f32),
        ],
        compiler_params=pltpu.CompilerParams(
            dimension_semantics=("arbitrary",), vmem_limit_bytes=60 * 1024 * 1024
        ),
        cost_estimate=pl.CostEstimate(
            flops=70_000_000_000, bytes_accessed=40_000_000, transcendentals=20_000_000
        ),
    )(scal, latent, position, pixel_rows, cols, down, head, gains)


MESH_ID = pl.DeviceIdType.MESH


def place():
    g = lax.axis_index("grp")
    d = lax.axis_index("dp")
    z, c = d // 2, d % 2
    xn = g + 1 - 2 * (g % 2)
    yn = (g + 2) % 4
    return g, z, c, xn, yn


def pieces(shape, parts):
    rows, columns = shape
    if rows // parts >= 32:
        n = rows // parts
        cut = [(slice(i * n, (i + 1) * n), slice(0, columns)) for i in range(parts)]
    else:
        n = columns // parts
        cut = [(slice(0, rows), slice(i * n, (i + 1) * n)) for i in range(parts)]
    return cut


def halves(cut):
    rows, columns = cut
    mid = (columns.start + columns.stop) // 2
    return (rows, slice(columns.start, mid)), (rows, slice(mid, columns.stop))


def greet(peers):
    barrier = pltpu.get_barrier_semaphore()
    for peer in peers:
        pl.semaphore_signal(barrier, inc=1, device_id=peer, device_id_type=MESH_ID)
    pl.semaphore_wait(barrier, len(peers))


def gather_kernel(count, chunks, ahead, *refs):
    ins, outs = refs[:count], refs[count : 2 * count]
    zs, zr, xs, xr, ys, yr, fs, fr, gs, gr, cs, os, cr, ls = refs[2 * count :]
    g, z, c, xn, yn = place()
    dg = (xn + 2) % 4
    here = 2 * z + c
    sib = (g, 2 * z + 1 - c)
    zpeer = [(g, 2 * ((z + j) % 4) + c) for j in (1, 2, 3)]
    zfrom = [(z + 4 - j) % 4 for j in (1, 2, 3)]
    greet([sib, (xn, here), (yn, here)] + zpeer)

    def send(src, dst, send_sem, recv_sem, peer):
        return pltpu.make_async_remote_copy(
            src_ref=src, dst_ref=dst, send_sem=send_sem, recv_sem=recv_sem,
            device_id=peer, device_id_type=MESH_ID,
        )

    def block(array, z_at, q, cut, core=None):
        return outs[array].at[z_at, c if core is None else core, q, cut[0], cut[1]]

    work = []
    for array in range(count):
        for cut in pieces(ins[array].shape[1:], chunks[array]):
            work.append((array, cut))
    steps = len(work)
    sent = []

    def go(copy):
        copy.start()
        sent.append(copy)

    def zcopy(k, j):
        array, cut = work[k]
        return send(
            ins[array].at[g, cut[0], cut[1]], block(array, z, g, cut), zs.at[k, j], zr.at[k, j], zpeer[j]
        )

    def relay(k, j, q, cut, ssem, rsem, peer):
        at = block(work[k][0], zfrom[j], q, cut)
        return send(at, at, ssem, rsem, peer)

    local = []
    for array in range(count):
        copy = pltpu.make_async_copy(ins[array], outs[array].at[z, c], ls.at[array])
        copy.start()
        local.append(copy)
    for k in range(min(ahead, steps)):
        for j in range(3):
            go(zcopy(k, j))
    for array in range(count):
        go(send(ins[array], outs[array].at[z, c], os.at[array], cr.at[array], sib))

    for t in range(steps + 2):
        if t < steps:
            array, cut = work[t]
            for j in range(3):
                zcopy(t, j).wait_recv()
                go(relay(t, j, g, cut, xs.at[t, j], xr.at[t, j], (xn, here)))
                go(relay(t, j, g, cut, ys.at[t, j], yr.at[t, j], (yn, here)))
                go(relay(t, j, g, cut, cs.at[t, j, 0], cr.at[array], sib))
            if t + ahead < steps:
                for j in range(3):
                    go(zcopy(t + ahead, j))
        if 1 <= t <= steps:
            k = t - 1
            array, cut = work[k]
            left, right = halves(cut)
            for j in range(3):
                relay(k, j, xn, cut, xs.at[k, j], xr.at[k, j], (xn, here)).wait_recv()
                go(relay(k, j, xn, left, fs.at[k, j], fr.at[k, j], (yn, here)))
                go(relay(k, j, xn, cut, cs.at[k, j, 1], cr.at[array], sib))
                relay(k, j, yn, cut, ys.at[k, j], yr.at[k, j], (yn, here)).wait_recv()
                go(relay(k, j, yn, right, gs.at[k, j], gr.at[k, j], (xn, here)))
                go(relay(k, j, yn, cut, cs.at[k, j, 2], cr.at[array], sib))
        if 2 <= t:
            k = t - 2
            array, cut = work[k]
            left, right = halves(cut)
            for j in range(3):
                relay(k, j, dg, left, fs.at[k, j], fr.at[k, j], (yn, here)).wait_recv()
                relay(k, j, dg, right, gs.at[k, j], gr.at[k, j], (xn, here)).wait_recv()
                go(relay(k, j, dg, cut, cs.at[k, j, 3], cr.at[array], sib))
    for copy in sent:
        copy.wait_send()
    for array in range(count):
        whole = outs[array].at[:, 1 - c]
        send(whole, whole, os.at[array], cr.at[array], sib).wait_recv()
        local[array].wait()


def gather_call(shards, chunks, ahead=2, collective_id=0):
    count = len(shards)
    steps = sum(chunks)
    views = [s.reshape(4, s.shape[0] // 4, s.shape[1]) for s in shards]
    dma = pltpu.SemaphoreType.DMA
    hbm = pl.BlockSpec(memory_space=pl.ANY)
    outs = pl.pallas_call(
        functools.partial(gather_kernel, count, chunks, ahead),
        out_shape=tuple(jax.ShapeDtypeStruct((4, 2) + v.shape, v.dtype) for v in views),
        in_specs=[hbm] * count,
        out_specs=tuple([hbm] * count),
        scratch_shapes=[dma((steps, 3))] * 10
        + [dma((steps, 3, 4)), dma((count,)), dma((count,)), dma((count,))],
        compiler_params=pltpu.CompilerParams(collective_id=collective_id, has_side_effects=True),
    )(*views)
    return [o.reshape(-1, o.shape[-1]) for o in outs]


def reduce_kernel(n_in, n_out, work, ahead, *refs):
    ins = refs[:n_in]
    small_ref = refs[n_in]
    outs = refs[n_in + 1 : n_in + 1 + n_out]
    small_out = refs[n_in + 1 + n_out]
    (s, own, xa, yb, xb, ya, zb, fin, sm,
     cs, cr, os, x1s, x1r, x2s, x2r, z_s, z_r, ags, agr, ls, sms, smr) = refs[n_in + n_out + 2 :]
    g, z, c, xn, yn = place()
    dg = (xn + 2) % 4
    here = 2 * z + c
    sib = (g, 2 * z + 1 - c)
    right, up = (xn, here), (yn, here)
    zto = [(z + j) % 4 for j in (1, 2, 3)]
    zpeer = [(g, 2 * t + c) for t in zto]
    greet([sib, right, up] + zpeer)
    steps = len(work)
    rows, columns = s.shape[3:]
    half = columns // 2
    left_half, right_half = pl.ds(0, half), pl.ds(half, half)
    sent = []
    f32 = jnp.float32

    def send(src, dst, send_sem, recv_sem, peer):
        return pltpu.make_async_remote_copy(
            src_ref=src, dst_ref=dst, send_sem=send_sem, recv_sem=recv_sem,
            device_id=peer, device_id_type=MESH_ID,
        )

    def go(copy):
        copy.start()
        sent.append(copy)

    def c_copies(k):
        return [
            send(
                ins[array].at[:, 1 - c, :, cut[0], cut[1]], s.at[k, pl.ds(z0, nz)],
                cs.at[k, i], cr.at[k, i], sib,
            )
            for i, (array, z0, nz, cut) in enumerate(work[k][0])
        ]

    def own_copies(k):
        slot = k % own.shape[0]
        return [
            pltpu.make_async_copy(
                ins[array].at[:, c, :, cut[0], cut[1]], own.at[slot, pl.ds(z0, nz)], os.at[slot, i]
            )
            for i, (array, z0, nz, cut) in enumerate(work[k][0])
        ]

    def begin(k):
        for copy in c_copies(k):
            go(copy)
        for copy in own_copies(k):
            copy.start()

    def x1_copies(k):
        return [
            send(s.at[k, :, xn, :, left_half], xa.at[k, 0], x1s.at[k, 0], x1r.at[k, 0], right),
            send(s.at[k, :, dg, :, left_half], xa.at[k, 1], x1s.at[k, 1], x1r.at[k, 1], right),
            send(s.at[k, :, yn, :, right_half], yb.at[k, 0], x1s.at[k, 2], x1r.at[k, 2], up),
            send(s.at[k, :, dg, :, right_half], yb.at[k, 1], x1s.at[k, 3], x1r.at[k, 3], up),
        ]

    def x2_copies(k):
        return [
            send(s.at[k, :, yn, :, left_half], ya.at[k], x2s.at[k, 0], x2r.at[k, 0], up),
            send(s.at[k, :, xn, :, right_half], xb.at[k], x2s.at[k, 1], x2r.at[k, 1], right),
        ]

    def z_copies(k):
        return [
            send(s.at[k, zto[j], g], zb.at[k, j], z_s.at[k, j], z_r.at[k, j], zpeer[j]) for j in range(3)
        ]

    def out_at(k, q, part=None):
        _, index, cut = work[k]
        if part is not None:
            cut = halves(cut)[part]
        return outs[index].at[q, cut[0], cut[1]]

    def ag_copies(k):
        return [
            send(fin.at[k], out_at(k, g), ags.at[k, 0], agr.at[k, 0], right),
            send(fin.at[k], out_at(k, g), ags.at[k, 1], agr.at[k, 1], up),
        ]

    def fwd_copies(k, of_x, of_y):
        return [
            send(out_at(k, of_x, 0), out_at(k, of_x, 0), ags.at[k, 2], agr.at[k, 2], up),
            send(out_at(k, of_y, 1), out_at(k, of_y, 1), ags.at[k, 3], agr.at[k, 3], right),
        ]

    def small_copy(i, j, slot, peer):
        return send(sm.at[slot], sm.at[4 + i], sms.at[j], smr.at[j], peer)

    def stage1(k):
        slot = k % own.shape[0]
        for copy in c_copies(k):
            copy.wait_recv()
        for copy in own_copies(k):
            copy.wait()

        @pl.loop(0, 4)
        def _(i):
            for q in range(4):
                s[k, i, q] = (s[k, i, q].astype(f32) + own[slot, i, q].astype(f32)).astype(s.dtype)

        for copy in x1_copies(k):
            go(copy)

    def add_half(k, q, part, other):
        @pl.loop(0, 4)
        def _(i):
            s[k, i, q, :, part] = (
                s[k, i, q, :, part].astype(f32) + other[i].astype(f32)
            ).astype(s.dtype)

    def stage2(k):
        for copy in x1_copies(k):
            copy.wait_recv()
        add_half(k, yn, left_half, xa.at[k, 1])
        add_half(k, xn, right_half, yb.at[k, 1])
        for copy in x2_copies(k):
            go(copy)
        add_half(k, g, left_half, xa.at[k, 0])
        add_half(k, g, right_half, yb.at[k, 0])

    def stage3(k):
        for copy in x2_copies(k):
            copy.wait_recv()
        add_half(k, g, left_half, ya.at[k])
        add_half(k, g, right_half, xb.at[k])
        for copy in z_copies(k):
            go(copy)

    def stage4(k):
        for copy in z_copies(k):
            copy.wait_recv()
        total = s[k, z, g].astype(f32)
        for j in range(3):
            total = total + zb[k, j].astype(f32)
        fin[k] = total.astype(fin.dtype)
        for copy in ag_copies(k):
            go(copy)
        pltpu.make_async_copy(fin.at[k], out_at(k, g), ls.at[k]).start()

    def stage5(k):
        for copy in ag_copies(k):
            copy.wait_recv()
        for copy in fwd_copies(k, xn, yn):
            go(copy)

    def stage6(k):
        for copy in fwd_copies(k, dg, dg):
            copy.wait_recv()

    stages = [stage1, stage2, stage3, stage4, stage5, stage6]
    sm[0] = small_ref[...]
    go(small_copy(0, 0, 0, sib))
    for k in range(min(ahead, steps)):
        begin(k)
    for t in range(steps + len(stages) - 1):
        for i, stage in enumerate(stages):
            k = t - i
            if 0 <= k < steps:
                stage(k)
                if i == 0 and k + ahead < steps:
                    begin(k + ahead)
        if t == 0:
            small_copy(0, 0, 0, sib).wait_recv()
            sm[1] = sm[0] + sm[4]
            go(small_copy(1, 1, 1, right))
        if t == 1:
            small_copy(1, 1, 1, right).wait_recv()
            sm[2] = sm[1] + sm[5]
            go(small_copy(2, 2, 2, up))
        if t == 2:
            small_copy(2, 2, 2, up).wait_recv()
            sm[3] = sm[2] + sm[6]
            for j in range(3):
                go(small_copy(3 + j, 3 + j, 3, zpeer[j]))
        if t == 3:
            for j in range(3):
                small_copy(3 + j, 3 + j, 3, zpeer[j]).wait_recv()
            total = None
            for t_z in range(4):
                term = jnp.where(z == t_z, sm[3], jnp.zeros_like(sm[3]))
                for j in range(3):
                    came = (z + 3 - j) % 4
                    term = term + jnp.where(came == t_z, sm[7 + j], jnp.zeros_like(sm[3]))
                total = term if total is None else total + term
            small_out[...] = total
    for copy in sent:
        copy.wait_send()
    for k in range(steps):
        pltpu.make_async_copy(fin.at[k], out_at(k, g), ls.at[k]).wait()


def reduce_call(grads, small, work, block, out_shapes, ahead=2, collective_id=1):
    steps = len(work)
    rows, columns = block
    half = columns // 2
    low = jnp.bfloat16
    dma = pltpu.SemaphoreType.DMA
    hbm = pl.BlockSpec(memory_space=pl.ANY)
    vm = pl.BlockSpec(memory_space=pltpu.VMEM)
    vmem = pltpu.VMEM
    return pl.pallas_call(
        functools.partial(reduce_kernel, len(grads), len(out_shapes), work, ahead),
        out_shape=tuple(jax.ShapeDtypeStruct(shape, low) for shape in out_shapes)
        + (jax.ShapeDtypeStruct(small.shape, jnp.float32),),
        in_specs=[hbm] * len(grads) + [vm],
        out_specs=tuple([hbm] * len(out_shapes) + [vm]),
        scratch_shapes=[
            vmem((steps, 4, 4, rows, columns), low),
            vmem((ahead + 1, 4, 4, rows, columns), low),
            vmem((steps, 2, 4, rows, half), low),
            vmem((steps, 2, 4, rows, half), low),
            vmem((steps, 4, rows, half), low),
            vmem((steps, 4, rows, half), low),
            vmem((steps, 3, rows, columns), low),
            vmem((steps, rows, columns), low),
            vmem((10,) + small.shape, jnp.float32),
            dma((steps, 2)), dma((steps, 2)), dma((ahead + 1, 2)),
            dma((steps, 4)), dma((steps, 4)),
            dma((steps, 2)), dma((steps, 2)),
            dma((steps, 3)), dma((steps, 3)),
            dma((steps, 4)), dma((steps, 4)),
            dma((steps,)), dma((6,)), dma((6,)),
        ],
        compiler_params=pltpu.CompilerParams(
            collective_id=collective_id, has_side_effects=True, vmem_limit_bytes=60 * 1024 * 1024
        ),
    )(*grads, small)


def reduce_encoder(edown, embed, qkv, proj, up, small, ahead=2, collective_id=1):
    width = edown.shape[1]
    rows = qkv.shape[0] // 32
    tall = edown.shape[0] // 16

    def cut_rows(k):
        return (slice(k * rows, (k + 1) * rows), slice(0, width))

    def cut_columns(k):
        return (slice(0, rows), slice(k * width, (k + 1) * width))

    work = []
    for k in range(tall // rows):
        work.append((((0, 0, 2, cut_rows(k)), (1, 2, 2, cut_rows(k))), 0, cut_rows(k)))
    grads = [edown.reshape(2, 2, 4, tall, width), embed.reshape(2, 2, 4, tall, width)]
    at = 0
    for index, part in enumerate((qkv, proj, up)):
        grads.append(part.reshape(4, 2, 4, rows, part.shape[1]))
        for k in range(part.shape[1] // width):
            work.append((((2 + index, 0, 4, cut_columns(k)),), 1, cut_columns(at)))
            at += 1
    shapes = ((4, tall, width), (4, rows, at * width))
    erows, ecols, total = reduce_call(
        grads, small, tuple(work), (rows, width), shapes, ahead, collective_id
    )
    return ecols.reshape(4 * rows, -1), erows.reshape(4 * tall, width), total


def adam_step(master, moment, square, grad, factor, fix_one, fix_two, decay, rate):
    clipped = grad * factor
    moment_new = beta_first * moment + (1.0 - beta_first) * clipped
    square_new = beta_second * square + (1.0 - beta_second) * clipped * clipped
    direction = moment_new / fix_one / (jnp.sqrt(square_new / fix_two) + adam_eps) + decay * master
    return (clipped, square_new, master - rate * direction)


def body(
    pixels,
    keep_index,
    band_group,
    gsd_index,
    gsd_table,
    group_items,
    step_count,
    enc_cols,
    enc_rows,
    dec_cols,
    dec_rows,
    enc_gains,
    dec_gains,
    moment_ecols,
    moment_erows,
    moment_dcols,
    moment_drows,
    moment_egains,
    moment_dgains,
    square_ecols,
    square_erows,
    square_dcols,
    square_drows,
    square_egains,
    square_dgains,
):
    n_grp = lax.axis_size("grp")
    grp_at = lax.axis_index("grp")

    def gather_rows(master):
        rows = master.shape[0]
        if rows % (16 * n_grp):
            return lax.all_gather(to_low(master), "dp", axis=0, tiled=True)
        part = rows // n_grp
        mine = lax.dynamic_slice_in_dim(master, grp_at * part, part, 0)
        return lax.all_gather(to_low(mine), ("dp", "grp"), axis=0, tiled=True)

    total_count = lax.psum(jnp.sum(group_items.astype(jnp.float32)), "grp")
    masked = total_count * (L - K)
    direct = (n_grp, lax.axis_size("dp")) == (4, 8)
    if direct:
        whole_rows, whole_cols = gather_call([to_low(enc_rows), to_low(enc_cols)], (4, 4), 2, 0)
    else:
        whole_rows, whole_cols = gather_rows(enc_rows), gather_rows(enc_cols)
    copies = (whole_cols, whole_rows, gather_rows(dec_cols), gather_rows(dec_rows))
    enc_copy = copies[0]
    enc_down = copies[1][:FF]
    embed_w = copies[1][FF:]
    dec_copy = copies[2]
    dec_down = copies[3][:DFF]
    dec_embed = copies[3][DFF : DFF + D]
    head_rows = copies[3][DFF + D :]
    keep_rows = keep_index[0]
    batch = keep_rows.shape[0]
    places = jnp.arange(L, dtype=jnp.int32)
    keep_hot = keep_rows[..., None] == places
    shown = jnp.any(keep_hot, 1)
    earlier = (places[:, None] <= places[None, :]).astype(jnp.bfloat16)
    rank = jnp.dot(
        1.0 - shown.astype(jnp.bfloat16), earlier, preferred_element_type=jnp.float32
    ).astype(jnp.int32)
    hide_hot = (rank[:, None, :] - 1 == jnp.arange(L - K, dtype=jnp.int32)[:, None]) & ~shown[:, None]
    order_hot = jnp.concatenate([keep_hot, hide_hot], 1)
    order_low = order_hot.astype(jnp.bfloat16)
    pixel_rows = jnp.einsum("bsl,blp->bsp", order_low, pixels[0])
    order_gsd = jnp.sum(jnp.where(order_hot, gsd_index[0][:, None, :], 0), -1)
    kept_bands = jnp.sum(jnp.where(keep_hot, band_group[0][:, None, :], 0), -1)
    kept_pixels = pixel_rows[:, :K]
    onehot = (kept_bands[..., None] == jnp.arange(NBG, dtype=jnp.int32)).astype(jnp.bfloat16)
    spread = (onehot[..., None] * kept_pixels[:, :, None, :]).reshape(batch, K, NBG * PIX)
    gsd_hot = (
        order_gsd[..., None] == jnp.arange(gsd_table.shape[1], dtype=jnp.int32)
    ).astype(jnp.bfloat16)
    table_high = to_low(gsd_table[0])
    table_low = to_low(gsd_table[0] - table_high.astype(jnp.float32))
    enc_input = (
        project(spread, embed_w)
        + project(gsd_hot[:, :K], table_high[:, :D])
        + project(gsd_hot[:, :K], table_low[:, :D])
    )
    enc_out, enc_saved = block_forward(enc_input, enc_copy, enc_down, enc_gains, HEADS)
    enc_final, enc_hat, enc_scale = norm_forward(enc_out, enc_gains[4], enc_gains[5])
    enc_low = to_low(enc_final)
    latent = project(enc_low, dec_embed)
    dec_position = project(gsd_hot, table_high[:, D:]) + project(gsd_hot, table_low[:, D:])
    first_item = lax.axis_index("dp") * batch
    valid = (first_item + jnp.arange(batch, dtype=jnp.int32) < group_items[0]).astype(jnp.float32)
    scal = jnp.stack([valid / PIX, valid * (2.0 / PIX) / masked])
    grad_latent, grad_dcols, grad_ddown, grad_head, dec_sums, loss_local = decoder_call(
        scal,
        latent,
        dec_position,
        pixel_rows[:, K:],
        dec_copy,
        dec_down,
        head_rows,
        dec_gains,
        DHEADS,
    )
    loss_local = loss_local[0, 0]
    grad_dembed = weight_grad(enc_low, grad_latent)
    back_enc, gain_ef, shift_ef = norm_backward(
        project_back(grad_latent, dec_embed), enc_hat, enc_scale, enc_gains[4]
    )
    grad_enc_in, grad_ecols, grad_edown, enc_block_gains = block_backward(
        back_enc, enc_copy, enc_down, enc_gains, HEADS, enc_saved
    )
    grad_embed = weight_grad(spread, to_low(grad_enc_in))

    def reduce_rows(pieces, axis):
        whole = jnp.concatenate([to_low(piece) for piece in pieces], axis)
        return lax.psum_scatter(whole, "dp", scatter_dimension=0, tiled=True)

    dec_shards = (
        reduce_rows((grad_dcols,), 1),
        reduce_rows((grad_ddown, grad_dembed, grad_head), 0),
    )
    dec_shards = tuple(lax.psum(piece, "grp") for piece in dec_shards)
    grad_egains = jnp.concatenate([enc_block_gains, jnp.stack([gain_ef, shift_ef])], 0)
    grad_dgains = dec_sums[:7]
    if direct:
        flat = jnp.concatenate([grad_egains.reshape(-1), grad_dgains.reshape(-1), loss_local[None]])
        count_e, count_d = grad_egains.size, grad_dgains.size
        small = jnp.pad(flat, (0, 16 * D - flat.shape[0])).reshape(16, D)
        ecols_shard, erows_shard, small = reduce_encoder(
            to_low(grad_edown), to_low(grad_embed), *[to_low(piece) for piece in grad_ecols], small
        )
        flat = small.reshape(-1)
        enc_sum = flat[:count_e].reshape(grad_egains.shape)
        dec_sum = flat[count_e : count_e + count_d].reshape(grad_dgains.shape)
        loss_sum = flat[count_e + count_d]
    else:
        enc_sum, dec_sum, loss_sum = lax.psum((grad_egains, grad_dgains, loss_local), ("grp", "dp"))
        ecols_shard = lax.psum(reduce_rows(grad_ecols, 1), "grp")
        erows_shard = lax.psum(reduce_rows((grad_edown, grad_embed), 0), "grp")
    shards = tuple(piece.astype(jnp.float32) for piece in (ecols_shard, erows_shard) + dec_shards)
    shard_squares = lax.psum(sum((jnp.sum(piece * piece) for piece in shards)), "dp")
    loss = loss_sum / masked
    grad_norm = jnp.sqrt(shard_squares + jnp.sum(enc_sum * enc_sum) + jnp.sum(dec_sum * dec_sum))
    factor = clip_level / jnp.maximum(grad_norm, clip_level)
    count_steps = step_count[0].astype(jnp.float32)
    fix_one = 1.0 - beta_first**count_steps
    fix_two = 1.0 - beta_second**count_steps
    clipped_ecols, squares_ecols, updated_ecols = adam_step(
        enc_cols,
        moment_ecols,
        square_ecols,
        shards[0],
        factor,
        fix_one,
        fix_two,
        weight_decay,
        learn_rate,
    )
    clipped_erows, squares_erows, updated_erows = adam_step(
        enc_rows,
        moment_erows,
        square_erows,
        shards[1],
        factor,
        fix_one,
        fix_two,
        weight_decay,
        learn_rate,
    )
    clipped_dcols, squares_dcols, updated_dcols = adam_step(
        dec_cols,
        moment_dcols,
        square_dcols,
        shards[2],
        factor,
        fix_one,
        fix_two,
        weight_decay,
        learn_rate,
    )
    clipped_drows, squares_drows, updated_drows = adam_step(
        dec_rows,
        moment_drows,
        square_drows,
        shards[3],
        factor,
        fix_one,
        fix_two,
        weight_decay,
        learn_rate,
    )
    clipped_egains, squares_egains, updated_egains = adam_step(
        enc_gains, moment_egains, square_egains, enc_sum, factor, fix_one, fix_two, 0.0, gain_rate
    )
    clipped_dgains, squares_dgains, updated_dgains = adam_step(
        dec_gains, moment_dgains, square_dgains, dec_sum, factor, fix_one, fix_two, 0.0, gain_rate
    )
    return (
        clipped_ecols,
        squares_ecols,
        updated_ecols,
        clipped_erows,
        squares_erows,
        updated_erows,
        clipped_dcols,
        squares_dcols,
        updated_dcols,
        clipped_drows,
        squares_drows,
        updated_drows,
        clipped_egains,
        squares_egains,
        updated_egains,
        clipped_dgains,
        squares_dgains,
        updated_dgains,
        loss,
        grad_norm,
    )


def solution(mesh):
    return jax.shard_map(
        body,
        mesh=mesh,
        in_specs=(
            P("grp", "dp", None, None),
            P("grp", "dp", None),
            P("grp", "dp", None),
            P("grp", "dp", None),
            P("grp", None, None),
            P("grp"),
            P(),
            P("dp", None),
            P("dp", None),
            P("dp", None),
            P("dp", None),
            P(),
            P(),
            P("dp", None),
            P("dp", None),
            P("dp", None),
            P("dp", None),
            P(),
            P(),
            P("dp", None),
            P("dp", None),
            P("dp", None),
            P("dp", None),
            P(),
            P(),
        ),
        out_specs=(
            P("dp", None),
            P("dp", None),
            P("dp", None),
            P("dp", None),
            P("dp", None),
            P("dp", None),
            P("dp", None),
            P("dp", None),
            P("dp", None),
            P("dp", None),
            P("dp", None),
            P("dp", None),
            P(),
            P(),
            P(),
            P(),
            P(),
            P(),
            P(),
            P(),
        ),
        check_vma=False,
    )
```

```python
import functools

import jax
import jax.numpy as jnp
from jax import lax
from jax.experimental import pallas as pl
from jax.experimental.pallas import tpu as pltpu
from jax.sharding import PartitionSpec as P

D = 1024
HEADS = 16
FF = 4096
DHEADS = 16
DFF = 2048
PIX = 1024
NBG = 4
L = 256
K = 64


norm_eps = 1e-06
clip_level = 0.005
learn_rate = 0.02
gain_rate = 0.25
weight_decay = 0.05
adam_eps = 1e-08
beta_first = 0.5
beta_second = 0.5


def to_low(value):
    return value.astype(jnp.bfloat16)


def project(inputs, matrix):
    return jnp.einsum("...n,nm->...m", inputs, matrix, preferred_element_type=jnp.float32)


def dot_nn(a, b):
    return lax.dot_general(a, b, (((1,), (0,)), ((), ())), preferred_element_type=jnp.float32)


def dot_nt(a, b):
    return lax.dot_general(a, b, (((1,), (1,)), ((), ())), preferred_element_type=jnp.float32)


def dot_tn(a, b):
    return lax.dot_general(a, b, (((0,), (0,)), ((), ())), preferred_element_type=jnp.float32)


def unit_rows(values):
    centred = values - jnp.mean(values, -1, keepdims=True)
    scaled = lax.rsqrt(jnp.mean(centred * centred, -1, keepdims=True) + norm_eps)
    return centred * scaled, scaled


def unit_back(grads, hat, scaled, gain):
    inner = grads * gain
    return scaled * (
        inner
        - jnp.mean(inner, -1, keepdims=True)
        - hat * jnp.mean(inner * hat, -1, keepdims=True)
    )

LANES = 128


def stack_rows(value, ee):
    head = lax.broadcasted_iota(jnp.int32, value.shape, 1) // ee
    return jnp.concatenate(
        [jnp.where(head == h, value, jnp.zeros_like(value)) for h in range(LANES // ee)], 0
    )


def stack_lanes(value, ee):
    head = lax.broadcasted_iota(jnp.int32, value.shape, 0) // ee
    return jnp.concatenate(
        [jnp.where(head == h, value, jnp.zeros_like(value)) for h in range(LANES // ee)], 1
    )


def attend(n, groups, tokens, width, ee, expo, same, qkv_s, s_s, p_s, inv_s, oo_s, o_s):
    item = n // groups
    g = n % groups
    rs = pl.ds(pl.multiple_of(item * tokens, tokens), tokens)
    qa = pl.ds(pl.multiple_of(g * LANES, LANES), LANES)
    q = qkv_s[rs, qa]
    k = qkv_s[rs, pl.ds(pl.multiple_of(width + g * LANES, LANES), LANES)]
    v = qkv_s[rs, pl.ds(pl.multiple_of(2 * width + g * LANES, LANES), LANES)]
    s_s[...] = dot_nt(stack_rows(q, ee), k)
    for h in range(LANES // ee):
        at = slice(h * tokens, (h + 1) * tokens)
        s = s_s[at, :]
        if same is not None:
            s = jnp.where(same, s, -1e30)
        top = jnp.max(s, -1, keepdims=True)
        p_s[n, :, at] = jnp.exp2((s - top) * expo).astype(p_s.dtype)
    ones = jnp.ones_like(v)
    both = jnp.concatenate([stack_rows(v, ee), stack_rows(ones, ee)], 1)
    out = dot_nn(p_s[n], both)
    inv = 1.0 / out[:, LANES:]
    out = out[:, :LANES] * inv
    inv_s[n] = inv
    oo_s[n] = out
    o_s[rs, qa] = out.astype(o_s.dtype)


def attend_back(n, groups, tokens, width, ee, scale, qkv_s, s_s, ds_s, p_s, inv_s, oo_s, do_s, dqkv_s):
    low = dqkv_s.dtype
    item = n // groups
    g = n % groups
    rs = pl.ds(pl.multiple_of(item * tokens, tokens), tokens)
    qa = pl.ds(pl.multiple_of(g * LANES, LANES), LANES)
    ka = pl.ds(pl.multiple_of(width + g * LANES, LANES), LANES)
    va = pl.ds(pl.multiple_of(2 * width + g * LANES, LANES), LANES)
    heads = range(LANES // ee)
    do = do_s[rs, qa].astype(jnp.float32) * inv_s[n]
    rest = (-do * oo_s[n]).astype(low)
    do_t = do.T.astype(low)
    do = do.astype(low)
    v = qkv_s[rs, va]
    s_s[...] = dot_nt(
        jnp.concatenate([stack_rows(do, ee), stack_rows(rest, ee)], 1),
        jnp.concatenate([v, jnp.ones_like(v)], 1),
    )
    for h in heads:
        at = slice(h * tokens, (h + 1) * tokens)
        ds_s[:, at] = (p_s[n, :, at].astype(jnp.float32) * s_s[at, :]).astype(low)
    e_rows = jnp.concatenate([p_s[n, :, h * tokens : (h + 1) * tokens] for h in heads], 0)
    ds_rows = jnp.concatenate([ds_s[:, h * tokens : (h + 1) * tokens] for h in heads], 0)
    dv_t = dot_nn(stack_lanes(do_t, ee), e_rows)
    dk_t = dot_nn(stack_lanes(qkv_s[rs, qa].T, ee), ds_rows)
    dq = dot_nn(ds_s[...], stack_rows(qkv_s[rs, ka], ee))
    dqkv_s[rs, qa] = (dq * scale).astype(low)
    dqkv_s[rs, ka] = (dk_t.T * scale).astype(low)
    dqkv_s[rs, va] = dv_t.T.astype(low)


def one_hot(index, count):
    places = lax.broadcasted_iota(jnp.int32, (index.shape[0], count), 1)
    return jnp.where(places.astype(jnp.float32) == index.astype(jnp.float32), 1.0, 0.0)


def split_table(table_ref, high_s, low_s):
    high = table_ref[...].astype(high_s.dtype)
    high_s[...] = high
    low_s[...] = (table_ref[...] - high.astype(jnp.float32)).astype(low_s.dtype)


def look_up(hot, index_row, high_s, low_s):
    index = jnp.sum(hot * index_row, -1, keepdims=True)
    rows = one_hot(index, high_s.shape[0]).astype(high_s.dtype)
    return dot_nn(rows, high_s[...]) + dot_nn(rows, low_s[...])


def decoder_kernel(
    items, heads, scal_ref, z_ref, keep_ref, gsd_ref, table_ref, pix_ref, cols_ref, down_ref, head_ref, gains_ref,
    dz_ref, gcols_out, gdown_out, ghead_out, ggains_ref, loss_ref,
    x_s, h1_s, qkv_s, p_s, o_s, x1_s, h2_s, a_s, gp_s, x2_s, hd_s, dx_s, dy_s, acc_s, dqkv_s, inv_s, oo_s, s_s, ds_s,
    high_s, low_s, pixel_s, gcols, gdown, ghead,
):
    low = jnp.bfloat16
    step = pl.program_id(0)
    width = x_s.shape[1]
    tokens = pix_ref.shape[1]
    hide = tokens - K
    rows = items * tokens
    tile = 512
    ee = width // heads
    scale = ee ** (-0.5)
    expo = scale * 1.4426950408889634

    @pl.when(step == 0)
    def _():
        gcols[...] = jnp.zeros_like(gcols)
        gdown[...] = jnp.zeros_like(gdown)
        ghead[...] = jnp.zeros_like(ghead)
        ggains_ref[...] = jnp.zeros_like(ggains_ref)
        loss_ref[...] = jnp.zeros_like(loss_ref)
        split_table(table_ref, high_s, low_s)

    def gain(i):
        return gains_ref[i : i + 1, :]

    f32 = jnp.float32
    before = lax.broadcasted_iota(jnp.int32, (tokens, tokens), 0) <= lax.broadcasted_iota(
        jnp.int32, (tokens, tokens), 1
    )
    before = before.astype(f32).astype(low)
    for i in range(items):
        base = i * tokens
        keep_hot = one_hot(keep_ref[i], tokens)
        shown = jnp.max(keep_hot, 0, keepdims=True)
        rank = dot_nn(jnp.broadcast_to(1.0 - shown, (8, tokens)).astype(low), before)[:1]
        slot = lax.broadcasted_iota(jnp.int32, (hide, tokens), 0).astype(f32) + 1.0
        hide_hot = jnp.where(slot == rank, 1.0 - shown, 0.0)
        position = look_up(jnp.concatenate([keep_hot, hide_hot], 0), gsd_ref[i], high_s, low_s)
        x_s[base : base + K, :] = position[:K] + z_ref[i]
        x_s[base + K : base + tokens, :] = position[K:] + gain(6)
        pixel_s[i] = dot_nn(hide_hot.astype(low), pix_ref[i]).astype(low)
    hat, _ = unit_rows(x_s[...])
    h1_s[...] = (hat * gain(0) + gain(1)).astype(low)

    @pl.loop(0, 3)
    def _(t):
        at = pl.ds(pl.multiple_of(t * width, width), width)
        qkv_s[:, at] = dot_nn(h1_s[...], cols_ref[:, at]).astype(low)

    groups = width // LANES

    @pl.loop(0, items * groups)
    def _(n):
        attend(n, groups, tokens, width, ee, expo, None, qkv_s, s_s, p_s, inv_s, oo_s, o_s)

    x1_s[...] = x_s[...] + dot_nn(o_s[...], cols_ref[:, 3 * width : 4 * width])
    hat, _ = unit_rows(x1_s[...])
    h2_s[...] = (hat * gain(2) + gain(3)).astype(low)
    x2_s[...] = x1_s[...]

    @pl.loop(0, down_ref.shape[0] // tile)
    def _(t):
        at = pl.ds(pl.multiple_of(t * tile, tile), tile)
        up = pl.ds(pl.multiple_of(4 * width + t * tile, tile), tile)
        u = dot_nn(h2_s[...], cols_ref[:, up])
        cumul = 0.5 * (1.0 + lax.erf(u * 0.7071067811865476))
        act = (u * cumul).astype(low)
        a_s[:, at] = act
        gp_s[:, at] = (cumul + u * jnp.exp(-0.5 * u * u) * 0.3989422804014327).astype(gp_s.dtype)
        x2_s[...] += dot_nn(act, down_ref[at, :])

    hat, _ = unit_rows(x2_s[...])
    hd_s[...] = (hat * gain(4) + gain(5)).astype(low)

    pixel_count = head_ref.shape[0]
    for i in range(items):
        base = i * tokens
        weight = scal_ref[0, step * items + i]
        coef = scal_ref[1, step * items + i]
        target, _ = unit_rows(pixel_s[i].astype(f32))
        hd = hd_s[base + K : base + tokens, :]
        back = jnp.zeros((hide, width), jnp.float32)
        for t in range(pixel_count // tile):
            at = slice(t * tile, (t + 1) * tile)
            err = dot_nt(hd, head_ref[at, :]) - target[:, at]
            loss_ref[...] += weight * jnp.sum(err * err, keepdims=True).reshape(1, 1)
            dpred = (err * coef).astype(low)
            ghead[at, :] += dot_tn(dpred, hd)
            back = back + dot_nn(dpred, head_ref[at, :])
        hat, scaled = unit_rows(x2_s[base + K : base + tokens, :])
        ggains_ref[4:5, :] += jnp.sum(back * hat, 0, keepdims=True)
        ggains_ref[5:6, :] += jnp.sum(back, 0, keepdims=True)
        dx = unit_back(back, hat, scaled, gain(4))
        dx_s[base : base + K, :] = jnp.zeros((K, width), jnp.float32)
        dx_s[base + K : base + tokens, :] = dx
        dy_s[base : base + K, :] = jnp.zeros((K, width), low)
        dy_s[base + K : base + tokens, :] = dx.astype(low)

    acc_s[...] = jnp.zeros_like(acc_s)

    @pl.loop(0, down_ref.shape[0] // tile)
    def _(t):
        at = pl.ds(pl.multiple_of(t * tile, tile), tile)
        up = pl.ds(pl.multiple_of(4 * width + t * tile, tile), tile)
        gdown[at, :] += dot_tn(a_s[:, at], dy_s[...])
        du = (dot_nt(dy_s[...], down_ref[at, :]) * gp_s[:, at].astype(jnp.float32)).astype(low)
        gcols[:, up] += dot_tn(h2_s[...], du)
        acc_s[...] += dot_nt(du, cols_ref[:, up])

    hat, scaled = unit_rows(x1_s[...])
    grads = acc_s[...]
    ggains_ref[2:3, :] += jnp.sum(grads * hat, 0, keepdims=True)
    ggains_ref[3:4, :] += jnp.sum(grads, 0, keepdims=True)
    dx_s[...] += unit_back(grads, hat, scaled, gain(2))
    dy_s[...] = dx_s[...].astype(low)
    gcols[:, 3 * width : 4 * width] += dot_tn(o_s[...], dy_s[...])
    o_s[...] = dot_nt(dy_s[...], cols_ref[:, 3 * width : 4 * width]).astype(low)

    @pl.loop(0, items * groups)
    def _(n):
        attend_back(n, groups, tokens, width, ee, scale, qkv_s, s_s, ds_s, p_s, inv_s, oo_s, o_s, dqkv_s)

    acc_s[...] = jnp.zeros_like(acc_s)

    @pl.loop(0, 3)
    def _(t):
        at = pl.ds(pl.multiple_of(t * width, width), width)
        gcols[:, at] += dot_tn(h1_s[...], dqkv_s[:, at])
        acc_s[...] += dot_nt(dqkv_s[:, at], cols_ref[:, at])

    hat, scaled = unit_rows(x_s[...])
    grads = acc_s[...]
    ggains_ref[0:1, :] += jnp.sum(grads * hat, 0, keepdims=True)
    ggains_ref[1:2, :] += jnp.sum(grads, 0, keepdims=True)
    dx_s[...] += unit_back(grads, hat, scaled, gain(0))
    for i in range(items):
        base = i * tokens
        dz_ref[i] = dx_s[base : base + K, :].astype(low)
        ggains_ref[6:7, :] += jnp.sum(dx_s[base + K : base + tokens, :], 0, keepdims=True)

    @pl.when(step == pl.num_programs(0) - 1)
    def _():
        gcols_out[...] = gcols[...].astype(low)
        gdown_out[...] = gdown[...].astype(low)
        ghead_out[...] = ghead[...].astype(low)


def decoder_call(scal, latent, keep, gsd, table, pixels, cols, down, head, gains, heads):
    batch, tokens, pixel_count = pixels.shape
    width = cols.shape[0]
    items = 2
    rows = items * tokens
    hide = tokens - K
    low = jnp.bfloat16
    full = pl.Buffered(1)

    def whole(array):
        return pl.BlockSpec(array.shape, lambda s: (0,) * array.ndim, pipeline_mode=full)

    def by_item(shape):
        return pl.BlockSpec((items,) + shape, lambda s: (s, 0, 0))

    outs = (
        jax.ShapeDtypeStruct((batch, K, width), low),
        jax.ShapeDtypeStruct(cols.shape, low),
        jax.ShapeDtypeStruct(down.shape, low),
        jax.ShapeDtypeStruct(head.shape, low),
        jax.ShapeDtypeStruct((8, width), jnp.float32),
        jax.ShapeDtypeStruct((1, 1), jnp.float32),
    )
    vmem = pltpu.VMEM
    f32 = jnp.float32
    return pl.pallas_call(
        functools.partial(decoder_kernel, items, heads),
        grid=(batch // items,),
        in_specs=[
            pl.BlockSpec(memory_space=pltpu.SMEM),
            by_item((K, width)),
            by_item((K, 1)),
            by_item((1, tokens)),
            pl.BlockSpec((table.shape[0], width), lambda s: (0, table.shape[1] // width - 1), pipeline_mode=full),
            by_item((tokens, pixel_count)),
            whole(cols),
            whole(down),
            whole(head),
            whole(gains),
        ],
        out_specs=(by_item((K, width)),) + tuple(whole(out) for out in outs[1:]),
        out_shape=outs,
        scratch_shapes=[
            vmem((rows, width), f32),
            vmem((rows, width), low),
            vmem((rows, 3 * width), low),
            vmem((items * width // 128, tokens, 4 * tokens), low),
            vmem((rows, width), low),
            vmem((rows, width), f32),
            vmem((rows, width), low),
            vmem((rows, down.shape[0]), low),
            vmem((rows, down.shape[0]), low),
            vmem((rows, width), f32),
            vmem((rows, width), low),
            vmem((rows, width), f32),
            vmem((rows, width), low),
            vmem((rows, width), f32),
            vmem((rows, 3 * width), low),
            vmem((items * width // 128, tokens, 128), f32),
            vmem((items * width // 128, tokens, 128), f32),
            vmem((4 * tokens, tokens), f32),
            vmem((tokens, 4 * tokens), low),
            vmem((table.shape[0], width), low),
            vmem((table.shape[0], width), low),
            vmem((items, hide, pixel_count), low),
            vmem(cols.shape, f32),
            vmem(down.shape, f32),
            vmem(head.shape, f32),
        ],
        compiler_params=pltpu.CompilerParams(
            dimension_semantics=("arbitrary",), vmem_limit_bytes=62 * 1024 * 1024
        ),
        cost_estimate=pl.CostEstimate(
            flops=70_000_000_000, bytes_accessed=40_000_000, transcendentals=20_000_000
        ),
    )(scal, latent, keep, gsd, table, pixels, cols, down, head, gains)


RUN = 256


def same_item():
    row = lax.broadcasted_iota(jnp.int32, (RUN, RUN), 0) // K
    column = lax.broadcasted_iota(jnp.int32, (RUN, RUN), 1) // K
    return row == column


def encoder_kernel(
    heads, pixels_ref, keep_ref, bands_ref, gsd_ref, table_ref, rows_ref, cols_ref, de_ref, gains_ref,
    z_ref, pix_ref, band_ref, x_ref, qkv_ref, p_ref, inv_ref, oo_ref, x1_ref, a_ref, gp_ref, x2_ref,
    h_s, s_s, o_s, high_s, low_s,
):
    low = jnp.bfloat16
    step = pl.program_id(0)
    width = x_ref.shape[1]
    ee = width // heads
    groups = width // LANES
    expo = ee ** (-0.5) * 1.4426950408889634

    def gain(i):
        return gains_ref[i : i + 1, :]

    @pl.when(step == 0)
    def _():
        split_table(table_ref, high_s, low_s)

        @pl.loop(0, pixels_ref.shape[0])
        def _(i):
            at = pl.ds(pl.multiple_of(i * K, K), K)
            hot = one_hot(keep_ref[i], pixels_ref.shape[1])
            pix_ref[at, :] = dot_nn(hot.astype(low), pixels_ref[i]).astype(low)
            band_ref[at, :] = jnp.sum(hot * bands_ref[i], -1, keepdims=True).astype(jnp.int32)
            x_ref[at, :] = look_up(hot, gsd_ref[i], high_s, low_s)

    @pl.when(step < 4)
    def _():
        pixel = pix_ref[...]
        x_ref[...] += dot_nn(jnp.where(band_ref[...] == step, pixel, jnp.zeros_like(pixel)), rows_ref[...])

    @pl.when(step == 4)
    def _():
        hat, _ = unit_rows(x_ref[...])
        h_s[...] = (hat * gain(0) + gain(1)).astype(low)

    @pl.when((step >= 4) & (step < 7))
    def _():
        at = pl.ds(pl.multiple_of((step - 4) * width, width), width)
        qkv_ref[:, at] = dot_nn(h_s[...], cols_ref[...]).astype(low)

    @pl.when(step == 7)
    def _():
        same = same_item()

        @pl.loop(0, x_ref.shape[0] // RUN * groups)
        def _(n):
            attend(n, groups, RUN, width, ee, expo, same, qkv_ref, s_s, p_ref, inv_ref, oo_ref, o_s)

        x1_ref[...] = x_ref[...] + dot_nn(o_s[...], cols_ref[...])
        hat, _ = unit_rows(x1_ref[...])
        h_s[...] = (hat * gain(2) + gain(3)).astype(low)
        x2_ref[...] = x1_ref[...]

    @pl.when(step >= 8)
    def _():
        @pl.loop(0, 2)
        def _(t):
            half = width // 2
            at = pl.ds(pl.multiple_of(t * half, half), half)
            u = dot_nn(h_s[...], cols_ref[:, at])
            cumul = 0.5 * (1.0 + lax.erf(u * 0.7071067811865476))
            a_ref[:, at] = (u * cumul).astype(low)
            gp_ref[:, at] = (cumul + u * jnp.exp(-0.5 * u * u) * 0.3989422804014327).astype(low)

        x2_ref[...] += dot_nn(a_ref[...], rows_ref[...])

    @pl.when(step == 11)
    def _():
        hat, _ = unit_rows(x2_ref[...])
        h_s[...] = (hat * gain(4) + gain(5)).astype(low)
        z_ref[...] = dot_nn(h_s[...], de_ref[...])


def encoder_call(pixels, keep, bands, gsd, table, rows, cols, de, gains, heads):
    width = cols.shape[0]
    tokens = keep.shape[0] * K
    low, f32 = jnp.bfloat16, jnp.float32
    runs = tokens // RUN * (width // LANES)
    wide = LANES // (width // heads) * RUN
    one = pl.Buffered(1)

    def whole(shape):
        return pl.BlockSpec(shape, lambda s: (0,) * len(shape), pipeline_mode=one)

    def row_block(s):
        return (jnp.where(s < 4, s + 4, jnp.where(s < 8, 0, s - 8)), 0)

    def column_block(s):
        return (0, jnp.where(s < 4, 0, s - 4))

    def hidden_block(s):
        return (0, jnp.where(s < 8, 0, s - 8))

    def hold(shape, dtype=f32):
        return jax.ShapeDtypeStruct(shape, dtype), whole(shape)

    ff = (tokens, 4 * width)
    outs = [
        hold((tokens, de.shape[1])),
        hold((tokens, pixels.shape[2]), low),
        hold((tokens, 1), jnp.int32),
        hold((tokens, width)),
        hold((tokens, 3 * width), low),
        hold((runs, RUN, wide), low),
        hold((runs, RUN, LANES)),
        hold((runs, RUN, LANES)),
        hold((tokens, width)),
        (jax.ShapeDtypeStruct(ff, low), pl.BlockSpec((tokens, width), hidden_block)),
        (jax.ShapeDtypeStruct(ff, low), pl.BlockSpec((tokens, width), hidden_block)),
        hold((tokens, width)),
    ]
    return pl.pallas_call(
        functools.partial(encoder_kernel, heads),
        grid=(12,),
        in_specs=[
            whole(pixels.shape),
            whole(keep.shape),
            whole(bands.shape),
            whole(gsd.shape),
            pl.BlockSpec((table.shape[0], width), lambda s: (0, 0), pipeline_mode=one),
            pl.BlockSpec((width, width), row_block),
            pl.BlockSpec((width, width), column_block),
            whole(de.shape),
            whole(gains.shape),
        ],
        out_specs=tuple(o[1] for o in outs),
        out_shape=tuple(o[0] for o in outs),
        scratch_shapes=[
            pltpu.VMEM((tokens, width), low),
            pltpu.VMEM((wide, RUN), f32),
            pltpu.VMEM((tokens, width), low),
            pltpu.VMEM((table.shape[0], width), low),
            pltpu.VMEM((table.shape[0], width), low),
        ],
        compiler_params=pltpu.CompilerParams(
            dimension_semantics=("arbitrary",), vmem_limit_bytes=60 * 1024 * 1024
        ),
        cost_estimate=pl.CostEstimate(
            flops=20_000_000_000, bytes_accessed=70_000_000, transcendentals=8_000_000
        ),
    )(pixels, keep, bands, gsd, table, rows, cols, de, gains)


def encoder_back_kernel(
    heads, dz_ref, pix_ref, band_ref, x_ref, qkv_ref, p_ref, inv_ref, oo_ref, x1_ref, a_ref, gp_ref, x2_ref,
    rows_ref, cols_ref, de_ref, gains_ref,
    grows_ref, gcols_ref, gde_ref, ggains_ref,
    h_s, dx_s, dy_s, acc_s, do_s, dqkv_s, s_s, ds_s,
):
    low, f32 = jnp.bfloat16, jnp.float32
    step = pl.program_id(0)
    width = x_ref.shape[1]
    ee = width // heads
    groups = width // LANES
    runs = x_ref.shape[0] // RUN

    def gain(i):
        return gains_ref[i : i + 1, :]

    def back(x, grads, at):
        hat, scaled = unit_rows(x)
        ggains_ref[at : at + 1, :] = jnp.sum(grads * hat, 0, keepdims=True)
        ggains_ref[at + 1 : at + 2, :] = jnp.sum(grads, 0, keepdims=True)
        return unit_back(grads, hat, scaled, gain(at))

    def normed(x, at):
        hat, _ = unit_rows(x)
        h_s[...] = (hat * gain(at) + gain(at + 1)).astype(low)

    @pl.when(step == 0)
    def _():
        ggains_ref[...] = jnp.zeros_like(ggains_ref)
        normed(x2_ref[...], 4)
        gde_ref[...] = dot_tn(h_s[...], dz_ref[...]).astype(low)
        dx_s[...] = back(x2_ref[...], dot_nt(dz_ref[...], de_ref[...]), 4)
        dy_s[...] = dx_s[...].astype(low)
        normed(x1_ref[...], 2)
        acc_s[...] = jnp.zeros_like(acc_s)

    @pl.when(step < 4)
    def _():
        grows_ref[...] = dot_tn(a_ref[...], dy_s[...]).astype(low)
        du = (dot_nt(dy_s[...], rows_ref[...]) * gp_ref[...].astype(f32)).astype(low)
        do_s[...] = du
        gcols_ref[...] = dot_tn(h_s[...], du).astype(low)
        acc_s[...] += dot_nt(do_s[...], cols_ref[...])

    @pl.when(step == 4)
    def _():
        dx_s[...] += back(x1_ref[...], acc_s[...], 2)
        dy_s[...] = dx_s[...].astype(low)
        for run in range(runs):
            for g in range(groups):
                h_s[run * RUN : (run + 1) * RUN, g * LANES : (g + 1) * LANES] = oo_ref[
                    run * groups + g
                ].astype(low)
        gcols_ref[...] = dot_tn(h_s[...], dy_s[...]).astype(low)
        do_s[...] = dot_nt(dy_s[...], cols_ref[...]).astype(low)

        @pl.loop(0, runs * groups)
        def _(n):
            attend_back(
                n, groups, RUN, width, ee, ee ** (-0.5), qkv_ref, s_s, ds_s, p_ref, inv_ref, oo_ref, do_s,
                dqkv_s,
            )

        normed(x_ref[...], 0)
        acc_s[...] = jnp.zeros_like(acc_s)

    @pl.when((step >= 5) & (step < 8))
    def _():
        at = pl.ds(pl.multiple_of((step - 5) * width, width), width)
        gcols_ref[...] = dot_tn(h_s[...], dqkv_s[:, at]).astype(low)
        acc_s[...] += dot_nt(dqkv_s[:, at], cols_ref[...])

    @pl.when(step == 8)
    def _():
        dx_s[...] += back(x_ref[...], acc_s[...], 0)
        dy_s[...] = dx_s[...].astype(low)

    @pl.when(step >= 8)
    def _():
        pixel = pix_ref[...]
        h_s[...] = jnp.where(band_ref[...] == step - 8, pixel, jnp.zeros_like(pixel))
        grows_ref[...] = dot_tn(h_s[...], dy_s[...]).astype(low)


def encoder_back_call(dz, pixel, band, saved, rows, cols, de, gains, heads):
    x, qkv, p, inv, oo, x1, a, gp, x2 = saved
    tokens, width = x.shape
    low, f32 = jnp.bfloat16, jnp.float32
    wide = p.shape[2]
    one = pl.Buffered(1)

    def whole(array):
        return pl.BlockSpec(array.shape, lambda s: (0,) * len(array.shape), pipeline_mode=one)

    def row_block(s):
        return (jnp.minimum(s, 3), 0)

    def column_block(s):
        return (0, jnp.where(s < 4, s + 4, jnp.where(s == 4, 3, jnp.minimum(s - 5, 2))))

    def hidden_block(s):
        return (0, jnp.minimum(s, 3))

    def grow_block(s):
        return (jnp.where(s < 4, s, jnp.where(s < 8, 3, s - 4)), 0)

    hidden = pl.BlockSpec((tokens, width), hidden_block)
    square = (width, width)
    outs = (
        jax.ShapeDtypeStruct(rows.shape, low),
        jax.ShapeDtypeStruct(cols.shape, low),
        jax.ShapeDtypeStruct(de.shape, low),
        jax.ShapeDtypeStruct((8, width), f32),
    )
    vmem = pltpu.VMEM
    return pl.pallas_call(
        functools.partial(encoder_back_kernel, heads),
        grid=(12,),
        in_specs=[
            whole(dz), whole(pixel), whole(band), whole(x), whole(qkv), whole(p), whole(inv), whole(oo),
            whole(x1), hidden, hidden, whole(x2),
            pl.BlockSpec(square, row_block), pl.BlockSpec(square, column_block),
            whole(de), whole(gains),
        ],
        out_specs=(
            pl.BlockSpec(square, grow_block),
            pl.BlockSpec(square, column_block),
            whole(outs[2]),
            whole(outs[3]),
        ),
        out_shape=outs,
        scratch_shapes=[
            vmem((tokens, width), low),
            vmem((tokens, width), f32),
            vmem((tokens, width), low),
            vmem((tokens, width), f32),
            vmem((tokens, width), low),
            vmem((tokens, 3 * width), low),
            vmem((wide, RUN), f32),
            vmem((RUN, wide), low),
        ],
        compiler_params=pltpu.CompilerParams(
            dimension_semantics=("arbitrary",), vmem_limit_bytes=60 * 1024 * 1024
        ),
        cost_estimate=pl.CostEstimate(
            flops=40_000_000_000, bytes_accessed=110_000_000, transcendentals=1_000_000
        ),
    )(dz, pixel, band, x, qkv, p, inv, oo, x1, a, gp, x2, rows, cols, de, gains)


MESH_ID = pl.DeviceIdType.MESH


def place():
    g = lax.axis_index("grp")
    d = lax.axis_index("dp")
    z, c = d // 2, d % 2
    xn = g + 1 - 2 * (g % 2)
    yn = (g + 2) % 4
    return g, z, c, xn, yn


def pieces(shape, parts):
    rows, columns = shape
    if rows // parts >= 32:
        n = rows // parts
        cut = [(slice(i * n, (i + 1) * n), slice(0, columns)) for i in range(parts)]
    else:
        n = columns // parts
        cut = [(slice(0, rows), slice(i * n, (i + 1) * n)) for i in range(parts)]
    return cut


def halves(cut):
    rows, columns = cut
    mid = (columns.start + columns.stop) // 2
    return (rows, slice(columns.start, mid)), (rows, slice(mid, columns.stop))


def greet(peers):
    barrier = pltpu.get_barrier_semaphore()
    for peer in peers:
        pl.semaphore_signal(barrier, inc=1, device_id=peer, device_id_type=MESH_ID)
    pl.semaphore_wait(barrier, len(peers))


def gather_kernel(count, chunks, ahead, *refs):
    ins, items_ref = refs[:count], refs[count]
    outs, items_out = refs[count + 1 : 2 * count + 1], refs[2 * count + 1]
    (zs, zr, xs, xr, ys, yr, fs, fr, gs, gr, cs, os, cr, ls, it, its, itr) = refs[2 * count + 2 :]
    g, z, c, xn, yn = place()
    dg = (xn + 2) % 4
    here = 2 * z + c
    sib = (g, 2 * z + 1 - c)
    zpeer = [(g, 2 * ((z + j) % 4) + c) for j in (1, 2, 3)]
    zfrom = [(z + 4 - j) % 4 for j in (1, 2, 3)]
    greet([sib, (xn, here), (yn, here)] + zpeer)

    def send(src, dst, send_sem, recv_sem, peer):
        return pltpu.make_async_remote_copy(
            src_ref=src, dst_ref=dst, send_sem=send_sem, recv_sem=recv_sem,
            device_id=peer, device_id_type=MESH_ID,
        )

    def block(array, z_at, q, cut, core=None):
        return outs[array].at[z_at, c if core is None else core, q, cut[0], cut[1]]

    work = []
    for array in range(count):
        for cut in pieces(ins[array].shape[1:], chunks[array]):
            work.append((array, cut))
    steps = len(work)
    sent = []

    def go(copy):
        copy.start()
        sent.append(copy)

    def items_copy(i, peer):
        return send(it.at[2 * i], it.at[2 * i + 1], its.at[i], itr.at[i], peer)

    def zcopy(k, j):
        array, cut = work[k]
        return send(
            ins[array].at[g, cut[0], cut[1]], block(array, z, g, cut), zs.at[k, j], zr.at[k, j], zpeer[j]
        )

    def relay(k, j, q, cut, ssem, rsem, peer):
        at = block(work[k][0], zfrom[j], q, cut)
        return send(at, at, ssem, rsem, peer)

    it[0] = items_ref[...]
    go(items_copy(0, (xn, here)))
    local = []
    for array in range(count):
        copy = pltpu.make_async_copy(ins[array], outs[array].at[z, c], ls.at[array])
        copy.start()
        local.append(copy)
    for k in range(min(ahead, steps)):
        for j in range(3):
            go(zcopy(k, j))
    for array in range(count):
        go(send(ins[array], outs[array].at[z, c], os.at[array], cr.at[array], sib))

    for t in range(steps + 2):
        if t < steps:
            array, cut = work[t]
            for j in range(3):
                zcopy(t, j).wait_recv()
                go(relay(t, j, g, cut, xs.at[t, j], xr.at[t, j], (xn, here)))
                go(relay(t, j, g, cut, ys.at[t, j], yr.at[t, j], (yn, here)))
                go(relay(t, j, g, cut, cs.at[t, j, 0], cr.at[array], sib))
            if t + ahead < steps:
                for j in range(3):
                    go(zcopy(t + ahead, j))
        if t == 0:
            items_copy(0, (xn, here)).wait_recv()
            it[2] = it[0] + it[1]
            go(items_copy(1, (yn, here)))
        if t == 1:
            items_copy(1, (yn, here)).wait_recv()
            items_out[...] = it[2] + it[3]
        if 1 <= t <= steps:
            k = t - 1
            array, cut = work[k]
            left, right = halves(cut)
            for j in range(3):
                relay(k, j, xn, cut, xs.at[k, j], xr.at[k, j], (xn, here)).wait_recv()
                go(relay(k, j, xn, left, fs.at[k, j], fr.at[k, j], (yn, here)))
                go(relay(k, j, xn, cut, cs.at[k, j, 1], cr.at[array], sib))
                relay(k, j, yn, cut, ys.at[k, j], yr.at[k, j], (yn, here)).wait_recv()
                go(relay(k, j, yn, right, gs.at[k, j], gr.at[k, j], (xn, here)))
                go(relay(k, j, yn, cut, cs.at[k, j, 2], cr.at[array], sib))
        if 2 <= t:
            k = t - 2
            array, cut = work[k]
            left, right = halves(cut)
            for j in range(3):
                relay(k, j, dg, left, fs.at[k, j], fr.at[k, j], (yn, here)).wait_recv()
                relay(k, j, dg, right, gs.at[k, j], gr.at[k, j], (xn, here)).wait_recv()
                go(relay(k, j, dg, cut, cs.at[k, j, 3], cr.at[array], sib))
    for copy in sent:
        copy.wait_send()
    for array in range(count):
        whole = outs[array].at[:, 1 - c]
        send(whole, whole, os.at[array], cr.at[array], sib).wait_recv()
        local[array].wait()


def gather_call(shards, items, chunks, ahead=2, collective_id=0):
    count = len(shards)
    steps = sum(chunks)
    views = [s.reshape(4, s.shape[0] // 4, s.shape[1]) for s in shards]
    dma = pltpu.SemaphoreType.DMA
    hbm = pl.BlockSpec(memory_space=pl.ANY)
    vm = pl.BlockSpec(memory_space=pltpu.VMEM)
    *outs, total = pl.pallas_call(
        functools.partial(gather_kernel, count, chunks, ahead),
        out_shape=tuple(jax.ShapeDtypeStruct((4, 2) + v.shape, v.dtype) for v in views)
        + (jax.ShapeDtypeStruct((8, 128), jnp.float32),),
        in_specs=[hbm] * count + [vm],
        out_specs=tuple([hbm] * count + [vm]),
        scratch_shapes=[dma((steps, 3))] * 10
        + [dma((steps, 3, 4)), dma((count,)), dma((count,)), dma((count,))]
        + [pltpu.VMEM((4, 8, 128), jnp.float32), dma((2,)), dma((2,))],
        compiler_params=pltpu.CompilerParams(collective_id=collective_id, has_side_effects=True),
    )(*views, jnp.broadcast_to(items, (8, 128)))
    return [o.reshape(-1, o.shape[-1]) for o in outs], total[0, 0]


def reduce_kernel(n_in, n_out, kinds, work, ahead, offsets, z_offsets, newest_last, *refs):
    ins = refs[:n_in]
    small_ref = refs[n_in]
    outs = refs[n_in + 1 : n_in + 1 + n_out]
    small_out, ss_out = refs[n_in + 1 + n_out : n_in + 3 + n_out]
    rest = refs[n_in + 3 + n_out :]
    bufs = [rest[9 * i : 9 * i + 9] for i in range(len(kinds))]
    (sm, ss, ssx, cs, cr, os, x1s, x1r, x2s, x2r, z_s, z_r, ags, agr, ls, sms, smr, sss, ssr) = rest[
        9 * len(kinds) :
    ]
    g, z, c, xn, yn = place()
    dg = (xn + 2) % 4
    here = 2 * z + c
    sib = (g, 2 * z + 1 - c)
    right, up = (xn, here), (yn, here)
    zto = [(z + j) % 4 for j in (1, 2, 3)]
    zpeer = [(g, 2 * t + c) for t in zto]
    greet([sib, right, up] + zpeer)
    steps = len(work)
    sent = []
    f32 = jnp.float32
    slots = ahead + 1

    def send(src, dst, send_sem, recv_sem, peer):
        return pltpu.make_async_remote_copy(
            src_ref=src, dst_ref=dst, send_sem=send_sem, recv_sem=recv_sem,
            device_id=peer, device_id_type=MESH_ID,
        )

    def go(copies):
        for copy in copies:
            copy.start()
            sent.append(copy)

    def got(copies):
        for copy in copies:
            copy.wait_recv()

    def buffers(k):
        kind, at = work[k][:2]
        return bufs[kind], at, kinds[kind][1] // 2

    def c_copies(k):
        (s, *_), at, _ = buffers(k)
        return [
            send(
                ins[array].at[:, 1 - c, :, cut[0], cut[1]], s.at[at, pl.ds(z0, nz)],
                cs.at[k, i], cr.at[k, i], sib,
            )
            for i, (array, z0, nz, cut) in enumerate(work[k][3])
        ]

    def own_copies(k):
        (_, own, *_), at, _ = buffers(k)
        return [
            pltpu.make_async_copy(
                ins[array].at[:, c, :, cut[0], cut[1]], own.at[at % slots, pl.ds(z0, nz)], os.at[k, i]
            )
            for i, (array, z0, nz, cut) in enumerate(work[k][3])
        ]

    def begin(k):
        go(c_copies(k))
        for copy in own_copies(k):
            copy.start()

    def planes(k):
        if work[k][2]:
            return pl.ds(z, 1), pl.ds(0, 1), 1
        return pl.ds(0, 4), pl.ds(0, 4), 4

    def x1_copies(k):
        (s, _, xa, yb, *_), at, half = buffers(k)
        src, dst, _ = planes(k)
        left, right_half = pl.ds(0, half), pl.ds(half, half)
        return [
            send(s.at[at, src, xn, :, left], xa.at[at, 0, dst], x1s.at[k, 0], x1r.at[k, 0], right),
            send(s.at[at, src, dg, :, left], xa.at[at, 1, dst], x1s.at[k, 1], x1r.at[k, 1], right),
            send(s.at[at, src, yn, :, right_half], yb.at[at, 0, dst], x1s.at[k, 2], x1r.at[k, 2], up),
            send(s.at[at, src, dg, :, right_half], yb.at[at, 1, dst], x1s.at[k, 3], x1r.at[k, 3], up),
        ]

    def x2_copies(k):
        (s, _, _, _, xb, ya, *_), at, half = buffers(k)
        src, dst, _ = planes(k)
        left, right_half = pl.ds(0, half), pl.ds(half, half)
        return [
            send(s.at[at, src, yn, :, left], ya.at[at, dst], x2s.at[k, 0], x2r.at[k, 0], up),
            send(s.at[at, src, xn, :, right_half], xb.at[at, dst], x2s.at[k, 1], x2r.at[k, 1], right),
        ]

    def z_copies(k):
        (s, _, _, _, _, _, zb, *_), at, _ = buffers(k)
        if work[k][2]:
            zt = bufs[work[k][0]][8]
            return [
                send(s.at[at, zto[j]], zt.at[work[k][2] - 1, j], z_s.at[k, j], z_r.at[k, j], zpeer[j])
                for j in range(3)
            ]
        return [
            send(s.at[at, zto[j], g], zb.at[at, j], z_s.at[k, j], z_r.at[k, j], zpeer[j])
            for j in range(3)
        ]

    def out_at(k, q, part=None):
        index, cut = work[k][4:]
        if part is not None:
            cut = halves(cut)[part]
        return outs[index].at[q, cut[0], cut[1]]

    def ag_copies(k):
        (*_, fin, _), at, _ = buffers(k)
        return [
            send(fin.at[at], out_at(k, g), ags.at[k, 0], agr.at[k, 0], right),
            send(fin.at[at], out_at(k, g), ags.at[k, 1], agr.at[k, 1], up),
        ]

    def keep_copy(k):
        (*_, fin, _), at, _ = buffers(k)
        return pltpu.make_async_copy(fin.at[at], out_at(k, g), ls.at[k])

    def fwd_copies(k, of_x, of_y):
        return [
            send(out_at(k, of_x, 0), out_at(k, of_x, 0), ags.at[k, 2], agr.at[k, 2], up),
            send(out_at(k, of_y, 1), out_at(k, of_y, 1), ags.at[k, 3], agr.at[k, 3], right),
        ]

    def add_half(k, q, left, other):
        (s, *_), at, half = buffers(k)
        part = pl.ds(0 if left else half, half)
        if work[k][2]:
            s[at, z, q, :, part] = (s[at, z, q, :, part].astype(f32) + other[0].astype(f32)).astype(s.dtype)
            return

        @pl.loop(0, 4)
        def _(i):
            s[at, i, q, :, part] = (s[at, i, q, :, part].astype(f32) + other[i].astype(f32)).astype(s.dtype)

    def pair(k):
        (s, own, *_), at, _ = buffers(k)
        got(c_copies(k))
        for copy in own_copies(k):
            copy.wait()

        @pl.loop(0, 4)
        def _(i):
            for q in range(4):
                s[at, i, q] = (s[at, i, q].astype(f32) + own[at % slots, i, q].astype(f32)).astype(s.dtype)

    def first_half(k):
        (_, _, xa, yb, *_), at, _ = buffers(k)
        got(x1_copies(k))
        add_half(k, yn, True, xa.at[at, 1])
        add_half(k, xn, False, yb.at[at, 1])
        go(x2_copies(k))
        add_half(k, g, True, xa.at[at, 0])
        add_half(k, g, False, yb.at[at, 0])

    def second_half(k):
        (_, _, _, _, xb, ya, *_), at, _ = buffers(k)
        got(x2_copies(k))
        add_half(k, g, True, ya.at[at])
        add_half(k, g, False, xb.at[at])

    def finish(k, total):
        (*_, fin, _), at, _ = buffers(k)
        fin[at] = total.astype(fin.dtype)
        go(ag_copies(k))
        keep_copy(k).start()
        square = fin[at].astype(f32)
        square = square * square
        for i in range(square.shape[1] // ss.shape[1]):
            ss[...] += jnp.sum(
                square[:, i * ss.shape[1] : (i + 1) * ss.shape[1]], 0, keepdims=True
            )

    def collect(k):
        got(ag_copies(k))
        go(fwd_copies(k, xn, yn))

    def close(k):
        got(fwd_copies(k, dg, dg))

    def p1(k):
        pair(k)
        go(x1_copies(k))

    def p3(k):
        second_half(k)
        go(z_copies(k))

    def p4(k):
        (s, _, _, _, _, _, zb, *_), at, _ = buffers(k)
        got(z_copies(k))
        total = s[at, z, g].astype(f32)
        for j in range(3):
            total = total + zb[at, j].astype(f32)
        finish(k, total)

    def z1(k):
        pair(k)
        go(z_copies(k))

    def z2(k):
        (s, *_), at, _ = buffers(k)
        zt = bufs[work[k][0]][8]
        i = work[k][2] - 1
        got(z_copies(k))
        for q in range(4):
            total = s[at, z, q].astype(f32)
            for j in range(3):
                total = total + zt[i, j, q].astype(f32)
            s[at, z, q] = total.astype(s.dtype)
        go(x1_copies(k))

    def z4(k):
        (s, *_), at, _ = buffers(k)
        second_half(k)
        finish(k, s[at, z, g].astype(f32))

    plane_stages = [p1, first_half, p3, p4, collect, close]
    z_stages = [z1, z2, first_half, z4, collect, close]

    def share_rounds(value, sem_s, sem_r, store):
        def copy(i, slot, peer):
            return send(value.at[slot], value.at[4 + i], sem_s.at[i], sem_r.at[i], peer)

        def round_pair(i, peer, following):
            got([copy(i, i, peer)])
            value[i + 1] = value[i] + value[4 + i]
            go(following())

        def last():
            return [copy(3 + j, 3, zpeer[j]) for j in range(3)]

        def end():
            got(last())
            total = None
            for at in range(4):
                term = jnp.where(z == at, value[3], jnp.zeros_like(value[3]))
                for j in range(3):
                    term = term + jnp.where((z + 3 - j) % 4 == at, value[7 + j], jnp.zeros_like(value[3]))
                total = term if total is None else total + term
            store[...] = total

        return [
            lambda: go([copy(0, 0, sib)]),
            lambda: round_pair(0, sib, lambda: [copy(1, 1, right)]),
            lambda: round_pair(1, right, lambda: [copy(2, 2, up)]),
            lambda: round_pair(2, up, last),
            end,
        ]

    sm[0] = small_ref[...]
    ss[...] = jnp.zeros_like(ss)
    small_rounds = share_rounds(sm, sms, smr, small_out)
    small_rounds[0]()
    for k in range(min(ahead, steps)):
        begin(k)
    square_rounds = share_rounds(ssx, sss, ssr, ss_out)
    def at_time(k, i):
        return k + (z_offsets if work[k][2] else offsets)[i]

    last = max(at_time(k, 5) for k in range(steps))
    squared = max(at_time(k, 3) for k in range(steps))
    for t in range(last + 1):
        for k in range(steps) if newest_last else reversed(range(steps)):
            for i in range(6):
                if at_time(k, i) == t:
                    (z_stages if work[k][2] else plane_stages)[i](k)
                    if i == 0 and k + ahead < steps:
                        begin(k + ahead)
        if t < 4:
            small_rounds[t + 1]()
        if t == squared:
            ssx[0] = jnp.broadcast_to(jnp.sum(ss[...], keepdims=True).reshape(1, 1), ssx.shape[1:])
            square_rounds[0]()
        if squared < t < last and t - squared < 3:
            square_rounds[t - squared]()
        if t == last:
            for following in square_rounds[min(3, last - squared) :]:
                following()
    for copy in sent:
        copy.wait_send()
    for k in range(steps):
        keep_copy(k).wait()


def reduce_call(grads, small, kinds, work, out_shapes, ahead, offsets, z_offsets, newest_last, collective_id):
    steps = len(work)
    low, f32 = jnp.bfloat16, jnp.float32
    dma = pltpu.SemaphoreType.DMA
    hbm = pl.BlockSpec(memory_space=pl.ANY)
    vm = pl.BlockSpec(memory_space=pltpu.VMEM)
    vmem = pltpu.VMEM
    scratch = []
    for kind, (rows, columns, count) in enumerate(kinds):
        half = columns // 2
        z_first = max([1] + [w[2] for w in work if w[0] == kind])
        scratch += [
            vmem((count, 4, 4, rows, columns), low),
            vmem((min(count, ahead + 1), 4, 4, rows, columns), low),
            vmem((count, 2, 4, rows, half), low),
            vmem((count, 2, 4, rows, half), low),
            vmem((count, 4, rows, half), low),
            vmem((count, 4, rows, half), low),
            vmem((count, 3, rows, columns), low),
            vmem((count, rows, columns), low),
            vmem((z_first, 3, 4, rows, columns), low),
        ]
    return pl.pallas_call(
        functools.partial(reduce_kernel, len(grads), len(out_shapes), kinds, work, ahead, offsets, z_offsets, newest_last),
        out_shape=tuple(jax.ShapeDtypeStruct(shape, low) for shape in out_shapes)
        + (jax.ShapeDtypeStruct(small.shape, f32), jax.ShapeDtypeStruct((8, 128), f32)),
        in_specs=[hbm] * len(grads) + [vm],
        out_specs=tuple([hbm] * len(out_shapes) + [vm, vm]),
        scratch_shapes=scratch
        + [
            vmem((10,) + small.shape, f32),
            vmem((1, 512), f32),
            vmem((10, 8, 128), f32),
            dma((steps, 3)), dma((steps, 3)), dma((steps, 3)),
            dma((steps, 4)), dma((steps, 4)),
            dma((steps, 2)), dma((steps, 2)),
            dma((steps, 3)), dma((steps, 3)),
            dma((steps, 4)), dma((steps, 4)),
            dma((steps,)), dma((6,)), dma((6,)), dma((6,)), dma((6,)),
        ],
        compiler_params=pltpu.CompilerParams(
            collective_id=collective_id, has_side_effects=True, vmem_limit_bytes=62 * 1024 * 1024
        ),
    )(*grads, small)


def reduce_gradients(
    erows, ecols, dcols, drows, small, z_first=3, ahead=2, offsets=(0, 2, 4, 6, 8, 9),
    z_offsets=(0, 4, 6, 8, 10, 11), newest_last=False, collective_id=1,
):
    grads, shapes = [], []

    def add(array, z_count):
        grads.append(array.reshape(z_count, 2, 4, array.shape[0] // (8 * z_count), array.shape[1]))
        return len(grads) - 1

    chunks = [[], [], []]
    wide = 1024
    tall = erows.shape[0] // 32
    index = add(erows, 4)
    shapes.append((4, tall, wide))
    for k in range(tall // 32):
        cut = (slice(k * 32, (k + 1) * 32), slice(0, wide))
        chunks[0].append((0, ((index, 0, 4, cut),), 0, cut))
    index = add(ecols, 4)
    shapes.append((4, 32, ecols.shape[1]))
    for k in range(ecols.shape[1] // wide):
        cut = (slice(0, 32), slice(k * wide, (k + 1) * wide))
        chunks[0].append((0, ((index, 0, 4, cut),), 1, cut))
    index = add(dcols, 4)
    shapes.append((4, 16, dcols.shape[1]))
    for k in range(dcols.shape[1] // 2048):
        cut = (slice(0, 16), slice(k * 2048, (k + 1) * 2048))
        chunks[1].append((1, ((index, 0, 4, cut),), 2, cut))
    rows = sum(part.shape[0] for part in drows)
    z_rows = rows // 4
    parts = []
    at = 0
    for part in drows:
        count = part.shape[0] // z_rows
        parts.append((add(part, count), at, count))
        at += count
    tall = rows // 32
    shapes.append((4, tall, 512))
    for k in range(tall // 64):
        cut = (slice(k * 64, (k + 1) * 64), slice(0, 512))
        chunks[2].append((2, tuple((i, z0, nz, cut) for i, z0, nz in parts), 3, cut))
    numbered = [[(c[0], i) + c[1:] for i, c in enumerate(group)] for group in chunks]
    order = numbered[1] + numbered[2] + numbered[0]
    total = len(order)
    marks = {}
    if z_first:
        spots = [i for i in range(total) if order[i][0] == 0]
        every = max(1, len(spots) // z_first)
        for n in range(z_first):
            marks[spots[n * every]] = n + 1
    work = tuple(c[:2] + (marks.get(i, 0),) + c[2:] for i, c in enumerate(order))
    kinds = ((32, wide, len(chunks[0])), (16, 2048, len(chunks[1])), (64, 512, len(chunks[2])))
    out = reduce_call(tuple(grads), small, kinds, work, tuple(shapes), ahead, offsets, z_offsets, newest_last, collective_id)
    erows, ecols, dcols, drows = [o.reshape(-1, o.shape[-1]) for o in out[:4]]
    return ecols, erows, dcols, drows, out[4], out[5]


def adam_step(master, moment, square, grad, factor, fix_one, fix_two, decay, rate):
    clipped = grad * factor
    moment_new = beta_first * moment + (1.0 - beta_first) * clipped
    square_new = beta_second * square + (1.0 - beta_second) * clipped * clipped
    direction = moment_new / fix_one / (jnp.sqrt(square_new / fix_two) + adam_eps) + decay * master
    return (clipped, square_new, master - rate * direction)


def body(
    pixels,
    keep_index,
    band_group,
    gsd_index,
    gsd_table,
    group_items,
    step_count,
    enc_cols,
    enc_rows,
    dec_cols,
    dec_rows,
    enc_gains,
    dec_gains,
    moment_ecols,
    moment_erows,
    moment_dcols,
    moment_drows,
    moment_egains,
    moment_dgains,
    square_ecols,
    square_erows,
    square_dcols,
    square_drows,
    square_egains,
    square_dgains,
):
    n_grp = lax.axis_size("grp")
    grp_at = lax.axis_index("grp")

    def gather_rows(master):
        rows = master.shape[0]
        if rows % (16 * n_grp):
            return lax.all_gather(to_low(master), "dp", axis=0, tiled=True)
        part = rows // n_grp
        mine = lax.dynamic_slice_in_dim(master, grp_at * part, part, 0)
        return lax.all_gather(to_low(mine), ("dp", "grp"), axis=0, tiled=True)

    direct = (n_grp, lax.axis_size("dp")) == (4, 8)
    own_count = jnp.sum(group_items.astype(jnp.float32))
    if direct:
        (whole_rows, whole_cols), total_count = gather_call(
            [to_low(enc_rows), to_low(enc_cols)], own_count, (4, 4), 2, 0
        )
    else:
        total_count = lax.psum(own_count, "grp")
        whole_rows, whole_cols = gather_rows(enc_rows), gather_rows(enc_cols)
    masked = total_count * (L - K)
    copies = (whole_cols, whole_rows, gather_rows(dec_cols), gather_rows(dec_rows))
    dec_copy = copies[2]
    dec_down = copies[3][:DFF]
    dec_embed = copies[3][DFF : DFF + D]
    head_rows = copies[3][DFF + D :]
    keep_rows = keep_index[0]
    batch = keep_rows.shape[0]
    keep_column = keep_rows[..., None]
    band_row = band_group[0][:, None, :].astype(jnp.float32)
    gsd_row = gsd_index[0][:, None, :].astype(jnp.float32)
    latent, kept_pixels, kept_bands, *saved = encoder_call(
        pixels[0],
        keep_column,
        band_row,
        gsd_row,
        gsd_table[0],
        whole_rows,
        whole_cols,
        dec_embed,
        enc_gains,
        HEADS,
    )
    latent = latent.reshape(batch, K, -1)
    first_item = lax.axis_index("dp") * batch
    valid = (first_item + jnp.arange(batch, dtype=jnp.int32) < group_items[0]).astype(jnp.float32)
    scal = jnp.stack([valid / PIX, valid * (2.0 / PIX) / masked])
    grad_latent, grad_dcols, grad_ddown, grad_head, dec_sums, loss_local = decoder_call(
        scal,
        latent,
        keep_column,
        gsd_row,
        gsd_table[0],
        pixels[0],
        dec_copy,
        dec_down,
        head_rows,
        dec_gains,
        DHEADS,
    )
    loss_local = loss_local[0, 0]
    grad_erows, grad_ecols, grad_dembed, enc_sums = encoder_back_call(
        grad_latent.reshape(batch * K, -1),
        kept_pixels,
        kept_bands,
        saved,
        whole_rows,
        whole_cols,
        dec_embed,
        enc_gains,
        HEADS,
    )
    grad_egains = enc_sums[:6]

    def reduce_rows(pieces, axis):
        whole = jnp.concatenate([to_low(piece) for piece in pieces], axis)
        return lax.psum_scatter(whole, "dp", scatter_dimension=0, tiled=True)

    grad_dgains = dec_sums[:7]
    drows = (grad_ddown, grad_dembed, grad_head)
    if direct:
        flat = jnp.concatenate([grad_egains.reshape(-1), grad_dgains.reshape(-1), loss_local[None]])
        count_e, count_d = grad_egains.size, grad_dgains.size
        small = jnp.pad(flat, (0, 16 * D - flat.shape[0])).reshape(16, D)
        *shards, small, squares = reduce_gradients(grad_erows, grad_ecols, grad_dcols, drows, small)
        flat = small.reshape(-1)
        enc_sum = flat[:count_e].reshape(grad_egains.shape)
        dec_sum = flat[count_e : count_e + count_d].reshape(grad_dgains.shape)
        loss_sum = flat[count_e + count_d]
        shard_squares = squares[0, 0]
        shards = tuple(piece.astype(jnp.float32) for piece in shards)
    else:
        enc_sum, dec_sum, loss_sum = lax.psum((grad_egains, grad_dgains, loss_local), ("grp", "dp"))
        shards = tuple(
            lax.psum(reduce_rows(pieces, 0), "grp").astype(jnp.float32)
            for pieces in ((grad_ecols,), (grad_erows,), (grad_dcols,), drows)
        )
        shard_squares = lax.psum(sum((jnp.sum(piece * piece) for piece in shards)), "dp")
    loss = loss_sum / masked
    grad_norm = jnp.sqrt(shard_squares + jnp.sum(enc_sum * enc_sum) + jnp.sum(dec_sum * dec_sum))
    factor = clip_level / jnp.maximum(grad_norm, clip_level)
    count_steps = step_count[0].astype(jnp.float32)
    fix_one = 1.0 - beta_first**count_steps
    fix_two = 1.0 - beta_second**count_steps
    clipped_ecols, squares_ecols, updated_ecols = adam_step(
        enc_cols,
        moment_ecols,
        square_ecols,
        shards[0],
        factor,
        fix_one,
        fix_two,
        weight_decay,
        learn_rate,
    )
    clipped_erows, squares_erows, updated_erows = adam_step(
        enc_rows,
        moment_erows,
        square_erows,
        shards[1],
        factor,
        fix_one,
        fix_two,
        weight_decay,
        learn_rate,
    )
    clipped_dcols, squares_dcols, updated_dcols = adam_step(
        dec_cols,
        moment_dcols,
        square_dcols,
        shards[2],
        factor,
        fix_one,
        fix_two,
        weight_decay,
        learn_rate,
    )
    clipped_drows, squares_drows, updated_drows = adam_step(
        dec_rows,
        moment_drows,
        square_drows,
        shards[3],
        factor,
        fix_one,
        fix_two,
        weight_decay,
        learn_rate,
    )
    clipped_egains, squares_egains, updated_egains = adam_step(
        enc_gains, moment_egains, square_egains, enc_sum, factor, fix_one, fix_two, 0.0, gain_rate
    )
    clipped_dgains, squares_dgains, updated_dgains = adam_step(
        dec_gains, moment_dgains, square_dgains, dec_sum, factor, fix_one, fix_two, 0.0, gain_rate
    )
    return (
        clipped_ecols,
        squares_ecols,
        updated_ecols,
        clipped_erows,
        squares_erows,
        updated_erows,
        clipped_dcols,
        squares_dcols,
        updated_dcols,
        clipped_drows,
        squares_drows,
        updated_drows,
        clipped_egains,
        squares_egains,
        updated_egains,
        clipped_dgains,
        squares_dgains,
        updated_dgains,
        loss,
        grad_norm,
    )


def solution(mesh):
    return jax.shard_map(
        body,
        mesh=mesh,
        in_specs=(
            P("grp", "dp", None, None),
            P("grp", "dp", None),
            P("grp", "dp", None),
            P("grp", "dp", None),
            P("grp", None, None),
            P("grp"),
            P(),
            P("dp", None),
            P("dp", None),
            P("dp", None),
            P("dp", None),
            P(),
            P(),
            P("dp", None),
            P("dp", None),
            P("dp", None),
            P("dp", None),
            P(),
            P(),
            P("dp", None),
            P("dp", None),
            P("dp", None),
            P("dp", None),
            P(),
            P(),
        ),
        out_specs=(
            P("dp", None),
            P("dp", None),
            P("dp", None),
            P("dp", None),
            P("dp", None),
            P("dp", None),
            P("dp", None),
            P("dp", None),
            P("dp", None),
            P("dp", None),
            P("dp", None),
            P("dp", None),
            P(),
            P(),
            P(),
            P(),
            P(),
            P(),
            P(),
            P(),
        ),
        check_vma=False,
    )
```

```python
import functools

import jax
import jax.numpy as jnp
from jax import lax
from jax.experimental import pallas as pl
from jax.experimental.pallas import tpu as pltpu
from jax.sharding import PartitionSpec as P

D = 1024
HEADS = 16
FF = 4096
DHEADS = 16
DFF = 2048
PIX = 1024
NBG = 4
L = 256
K = 64


norm_eps = 1e-06
clip_level = 0.005
learn_rate = 0.02
gain_rate = 0.25
weight_decay = 0.05
adam_eps = 1e-08
beta_first = 0.5
beta_second = 0.5


def to_low(value):
    return value.astype(jnp.bfloat16)


def project(inputs, matrix):
    return jnp.einsum("...n,nm->...m", inputs, matrix, preferred_element_type=jnp.float32)


def dot_nn(a, b):
    return lax.dot_general(a, b, (((1,), (0,)), ((), ())), preferred_element_type=jnp.float32)


def dot_nt(a, b):
    return lax.dot_general(a, b, (((1,), (1,)), ((), ())), preferred_element_type=jnp.float32)


def dot_tn(a, b):
    return lax.dot_general(a, b, (((0,), (0,)), ((), ())), preferred_element_type=jnp.float32)


def unit_rows(values):
    centred = values - jnp.mean(values, -1, keepdims=True)
    scaled = lax.rsqrt(jnp.mean(centred * centred, -1, keepdims=True) + norm_eps)
    return centred * scaled, scaled


def unit_back(grads, hat, scaled, gain):
    inner = grads * gain
    return scaled * (
        inner
        - jnp.mean(inner, -1, keepdims=True)
        - hat * jnp.mean(inner * hat, -1, keepdims=True)
    )

LANES = 128


def stack_rows(value, ee):
    head = lax.broadcasted_iota(jnp.int32, value.shape, 1) // ee
    return jnp.concatenate(
        [jnp.where(head == h, value, jnp.zeros_like(value)) for h in range(LANES // ee)], 0
    )


def stack_lanes(value, ee):
    head = lax.broadcasted_iota(jnp.int32, value.shape, 0) // ee
    return jnp.concatenate(
        [jnp.where(head == h, value, jnp.zeros_like(value)) for h in range(LANES // ee)], 1
    )


def attend(n, groups, tokens, width, ee, expo, same, qkv_s, s_s, p_s, inv_s, oo_s, o_s):
    item = n // groups
    g = n % groups
    rs = pl.ds(pl.multiple_of(item * tokens, tokens), tokens)
    qa = pl.ds(pl.multiple_of(g * LANES, LANES), LANES)
    q = qkv_s[rs, qa]
    k = qkv_s[rs, pl.ds(pl.multiple_of(width + g * LANES, LANES), LANES)]
    v = qkv_s[rs, pl.ds(pl.multiple_of(2 * width + g * LANES, LANES), LANES)]
    s_s[...] = dot_nt(stack_rows(q, ee), k)
    for h in range(LANES // ee):
        at = slice(h * tokens, (h + 1) * tokens)
        s = s_s[at, :]
        if same is not None:
            s = jnp.where(same, s, -1e30)
        top = jnp.max(s, -1, keepdims=True)
        p_s[n, :, at] = jnp.exp2((s - top) * expo).astype(p_s.dtype)
    ones = jnp.ones_like(v)
    both = jnp.concatenate([stack_rows(v, ee), stack_rows(ones, ee)], 1)
    out = dot_nn(p_s[n], both)
    inv = 1.0 / out[:, LANES:]
    out = out[:, :LANES] * inv
    inv_s[n] = inv
    oo_s[n] = out
    o_s[rs, qa] = out.astype(o_s.dtype)


def attend_back(n, slot, groups, tokens, width, ee, scale, qkv_s, s_s, ds_s, p_s, inv_s, oo_s, do_s, dqkv_s):
    low = dqkv_s.dtype
    item = n // groups
    g = n % groups
    rs = pl.ds(pl.multiple_of(item * tokens, tokens), tokens)
    qa = pl.ds(pl.multiple_of(g * LANES, LANES), LANES)
    ka = pl.ds(pl.multiple_of(width + g * LANES, LANES), LANES)
    va = pl.ds(pl.multiple_of(2 * width + g * LANES, LANES), LANES)
    heads = range(LANES // ee)
    do = do_s[rs, qa].astype(jnp.float32) * inv_s[slot]
    rest = (-do * oo_s[slot]).astype(low)
    do_t = do.T.astype(low)
    do = do.astype(low)
    v = qkv_s[rs, va]
    s_s[...] = dot_nt(
        jnp.concatenate([stack_rows(do, ee), stack_rows(rest, ee)], 1),
        jnp.concatenate([v, jnp.ones_like(v)], 1),
    )
    for h in heads:
        at = slice(h * tokens, (h + 1) * tokens)
        ds_s[:, at] = (p_s[slot, :, at].astype(jnp.float32) * s_s[at, :]).astype(low)
    e_rows = jnp.concatenate([p_s[slot, :, h * tokens : (h + 1) * tokens] for h in heads], 0)
    ds_rows = jnp.concatenate([ds_s[:, h * tokens : (h + 1) * tokens] for h in heads], 0)
    dv_t = dot_nn(stack_lanes(do_t, ee), e_rows)
    dk_t = dot_nn(stack_lanes(qkv_s[rs, qa].T, ee), ds_rows)
    dq = dot_nn(ds_s[...], stack_rows(qkv_s[rs, ka], ee))
    dqkv_s[rs, qa] = (dq * scale).astype(low)
    dqkv_s[rs, ka] = (dk_t.T * scale).astype(low)
    dqkv_s[rs, va] = dv_t.T.astype(low)


def one_hot(index, count):
    places = lax.broadcasted_iota(jnp.int32, (index.shape[0], count), 1)
    return jnp.where(places.astype(jnp.float32) == index.astype(jnp.float32), 1.0, 0.0)


def split_table(table_ref, high_s, low_s):
    high = table_ref[...].astype(high_s.dtype)
    high_s[...] = high
    low_s[...] = (table_ref[...] - high.astype(jnp.float32)).astype(low_s.dtype)


def look_up(hot, index_row, high_s, low_s):
    index = jnp.sum(hot * index_row, -1, keepdims=True)
    rows = one_hot(index, high_s.shape[0]).astype(high_s.dtype)
    return dot_nn(rows, high_s[...]) + dot_nn(rows, low_s[...])


def decoder_kernel(
    items, heads, scal_ref, z_ref, keep_ref, gsd_ref, table_ref, pix_ref, cols_ref, down_ref, head_ref, gains_ref,
    dz_ref, gcols_out, gdown_out, ghead_out, ggains_ref, loss_ref,
    x_s, h1_s, qkv_s, p_s, o_s, x1_s, h2_s, a_s, gp_s, x2_s, hd_s, dx_s, dy_s, acc_s, dqkv_s, inv_s, oo_s, s_s, ds_s,
    high_s, low_s, pixel_s, gcols, gdown, ghead,
):
    low = jnp.bfloat16
    step = pl.program_id(0)
    width = x_s.shape[1]
    tokens = pix_ref.shape[1]
    hide = tokens - K
    rows = items * tokens
    tile = 512
    ee = width // heads
    scale = ee ** (-0.5)
    expo = scale * 1.4426950408889634

    @pl.when(step == 0)
    def _():
        gcols[...] = jnp.zeros_like(gcols)
        gdown[...] = jnp.zeros_like(gdown)
        ghead[...] = jnp.zeros_like(ghead)
        ggains_ref[...] = jnp.zeros_like(ggains_ref)
        loss_ref[...] = jnp.zeros_like(loss_ref)
        split_table(table_ref, high_s, low_s)

    def gain(i):
        return gains_ref[i : i + 1, :]

    f32 = jnp.float32
    before = lax.broadcasted_iota(jnp.int32, (tokens, tokens), 0) <= lax.broadcasted_iota(
        jnp.int32, (tokens, tokens), 1
    )
    before = before.astype(f32).astype(low)
    for i in range(items):
        base = i * tokens
        keep_hot = one_hot(keep_ref[i], tokens)
        shown = jnp.max(keep_hot, 0, keepdims=True)
        rank = dot_nn(jnp.broadcast_to(1.0 - shown, (8, tokens)).astype(low), before)[:1]
        slot = lax.broadcasted_iota(jnp.int32, (hide, tokens), 0).astype(f32) + 1.0
        hide_hot = jnp.where(slot == rank, 1.0 - shown, 0.0)
        position = look_up(jnp.concatenate([keep_hot, hide_hot], 0), gsd_ref[i], high_s, low_s)
        x_s[base : base + K, :] = position[:K] + z_ref[i]
        x_s[base + K : base + tokens, :] = position[K:] + gain(6)
        pixel_s[i] = dot_nn(hide_hot.astype(low), pix_ref[i]).astype(low)
    hat, _ = unit_rows(x_s[...])
    h1_s[...] = (hat * gain(0) + gain(1)).astype(low)

    @pl.loop(0, 3)
    def _(t):
        at = pl.ds(pl.multiple_of(t * width, width), width)
        qkv_s[:, at] = dot_nn(h1_s[...], cols_ref[:, at]).astype(low)

    groups = width // LANES

    @pl.loop(0, items * groups)
    def _(n):
        attend(n, groups, tokens, width, ee, expo, None, qkv_s, s_s, p_s, inv_s, oo_s, o_s)

    x1_s[...] = x_s[...] + dot_nn(o_s[...], cols_ref[:, 3 * width : 4 * width])
    hat, _ = unit_rows(x1_s[...])
    h2_s[...] = (hat * gain(2) + gain(3)).astype(low)
    x2_s[...] = x1_s[...]

    @pl.loop(0, down_ref.shape[0] // tile)
    def _(t):
        at = pl.ds(pl.multiple_of(t * tile, tile), tile)
        up = pl.ds(pl.multiple_of(4 * width + t * tile, tile), tile)
        u = dot_nn(h2_s[...], cols_ref[:, up])
        cumul = 0.5 * (1.0 + lax.erf(u * 0.7071067811865476))
        act = (u * cumul).astype(low)
        a_s[:, at] = act
        gp_s[:, at] = (cumul + u * jnp.exp(-0.5 * u * u) * 0.3989422804014327).astype(gp_s.dtype)
        x2_s[...] += dot_nn(act, down_ref[at, :])

    hat, _ = unit_rows(x2_s[...])
    hd_s[...] = (hat * gain(4) + gain(5)).astype(low)

    pixel_count = head_ref.shape[0]
    for i in range(items):
        base = i * tokens
        weight = scal_ref[0, step * items + i]
        coef = scal_ref[1, step * items + i]
        target, _ = unit_rows(pixel_s[i].astype(f32))
        hd = hd_s[base + K : base + tokens, :]
        back = jnp.zeros((hide, width), jnp.float32)
        for t in range(pixel_count // tile):
            at = slice(t * tile, (t + 1) * tile)
            err = dot_nt(hd, head_ref[at, :]) - target[:, at]
            loss_ref[...] += weight * jnp.sum(err * err, keepdims=True).reshape(1, 1)
            dpred = (err * coef).astype(low)
            ghead[at, :] += dot_tn(dpred, hd)
            back = back + dot_nn(dpred, head_ref[at, :])
        hat, scaled = unit_rows(x2_s[base + K : base + tokens, :])
        ggains_ref[4:5, :] += jnp.sum(back * hat, 0, keepdims=True)
        ggains_ref[5:6, :] += jnp.sum(back, 0, keepdims=True)
        dx = unit_back(back, hat, scaled, gain(4))
        dx_s[base : base + K, :] = jnp.zeros((K, width), jnp.float32)
        dx_s[base + K : base + tokens, :] = dx
        dy_s[base : base + K, :] = jnp.zeros((K, width), low)
        dy_s[base + K : base + tokens, :] = dx.astype(low)

    acc_s[...] = jnp.zeros_like(acc_s)

    @pl.loop(0, down_ref.shape[0] // tile)
    def _(t):
        at = pl.ds(pl.multiple_of(t * tile, tile), tile)
        up = pl.ds(pl.multiple_of(4 * width + t * tile, tile), tile)
        gdown[at, :] += dot_tn(a_s[:, at], dy_s[...])
        du = (dot_nt(dy_s[...], down_ref[at, :]) * gp_s[:, at].astype(jnp.float32)).astype(low)
        gcols[:, up] += dot_tn(h2_s[...], du)
        acc_s[...] += dot_nt(du, cols_ref[:, up])

    hat, scaled = unit_rows(x1_s[...])
    grads = acc_s[...]
    ggains_ref[2:3, :] += jnp.sum(grads * hat, 0, keepdims=True)
    ggains_ref[3:4, :] += jnp.sum(grads, 0, keepdims=True)
    dx_s[...] += unit_back(grads, hat, scaled, gain(2))
    dy_s[...] = dx_s[...].astype(low)
    gcols[:, 3 * width : 4 * width] += dot_tn(o_s[...], dy_s[...])
    o_s[...] = dot_nt(dy_s[...], cols_ref[:, 3 * width : 4 * width]).astype(low)

    @pl.loop(0, items * groups)
    def _(n):
        attend_back(n, n, groups, tokens, width, ee, scale, qkv_s, s_s, ds_s, p_s, inv_s, oo_s, o_s, dqkv_s)

    acc_s[...] = jnp.zeros_like(acc_s)

    @pl.loop(0, 3)
    def _(t):
        at = pl.ds(pl.multiple_of(t * width, width), width)
        gcols[:, at] += dot_tn(h1_s[...], dqkv_s[:, at])
        acc_s[...] += dot_nt(dqkv_s[:, at], cols_ref[:, at])

    hat, scaled = unit_rows(x_s[...])
    grads = acc_s[...]
    ggains_ref[0:1, :] += jnp.sum(grads * hat, 0, keepdims=True)
    ggains_ref[1:2, :] += jnp.sum(grads, 0, keepdims=True)
    dx_s[...] += unit_back(grads, hat, scaled, gain(0))
    for i in range(items):
        base = i * tokens
        dz_ref[i] = dx_s[base : base + K, :].astype(low)
        ggains_ref[6:7, :] += jnp.sum(dx_s[base + K : base + tokens, :], 0, keepdims=True)

    @pl.when(step == pl.num_programs(0) - 1)
    def _():
        gcols_out[...] = gcols[...].astype(low)
        gdown_out[...] = gdown[...].astype(low)
        ghead_out[...] = ghead[...].astype(low)


def decoder_call(scal, latent, keep, gsd, table, pixels, cols, down, head, gains, heads):
    batch, tokens, pixel_count = pixels.shape
    width = cols.shape[0]
    items = 2
    rows = items * tokens
    hide = tokens - K
    low = jnp.bfloat16
    full = pl.Buffered(1)

    def whole(array):
        return pl.BlockSpec(array.shape, lambda s: (0,) * array.ndim, pipeline_mode=full)

    def by_item(shape):
        return pl.BlockSpec((items,) + shape, lambda s: (s, 0, 0))

    outs = (
        jax.ShapeDtypeStruct((batch, K, width), low),
        jax.ShapeDtypeStruct(cols.shape, low),
        jax.ShapeDtypeStruct(down.shape, low),
        jax.ShapeDtypeStruct(head.shape, low),
        jax.ShapeDtypeStruct((8, width), jnp.float32),
        jax.ShapeDtypeStruct((1, 1), jnp.float32),
    )
    vmem = pltpu.VMEM
    f32 = jnp.float32
    return pl.pallas_call(
        functools.partial(decoder_kernel, items, heads),
        grid=(batch // items,),
        in_specs=[
            pl.BlockSpec(memory_space=pltpu.SMEM),
            by_item((K, width)),
            by_item((K, 1)),
            by_item((1, tokens)),
            pl.BlockSpec((table.shape[0], width), lambda s: (0, table.shape[1] // width - 1), pipeline_mode=full),
            by_item((tokens, pixel_count)),
            whole(cols),
            whole(down),
            whole(head),
            whole(gains),
        ],
        out_specs=(by_item((K, width)),) + tuple(whole(out) for out in outs[1:]),
        out_shape=outs,
        scratch_shapes=[
            vmem((rows, width), f32),
            vmem((rows, width), low),
            vmem((rows, 3 * width), low),
            vmem((items * width // 128, tokens, 4 * tokens), low),
            vmem((rows, width), low),
            vmem((rows, width), f32),
            vmem((rows, width), low),
            vmem((rows, down.shape[0]), low),
            vmem((rows, down.shape[0]), low),
            vmem((rows, width), f32),
            vmem((rows, width), low),
            vmem((rows, width), f32),
            vmem((rows, width), low),
            vmem((rows, width), f32),
            vmem((rows, 3 * width), low),
            vmem((items * width // 128, tokens, 128), f32),
            vmem((items * width // 128, tokens, 128), f32),
            vmem((4 * tokens, tokens), f32),
            vmem((tokens, 4 * tokens), low),
            vmem((table.shape[0], width), low),
            vmem((table.shape[0], width), low),
            vmem((items, hide, pixel_count), low),
            vmem(cols.shape, f32),
            vmem(down.shape, f32),
            vmem(head.shape, f32),
        ],
        compiler_params=pltpu.CompilerParams(
            dimension_semantics=("arbitrary",), vmem_limit_bytes=62 * 1024 * 1024
        ),
        cost_estimate=pl.CostEstimate(
            flops=70_000_000_000, bytes_accessed=40_000_000, transcendentals=20_000_000
        ),
    )(scal, latent, keep, gsd, table, pixels, cols, down, head, gains)


RUN = 256


def same_item():
    row = lax.broadcasted_iota(jnp.int32, (RUN, RUN), 0) // K
    column = lax.broadcasted_iota(jnp.int32, (RUN, RUN), 1) // K
    return row == column


def encoder_kernel(
    heads, pixels_ref, keep_ref, bands_ref, gsd_ref, table_ref, rows_ref, cols_ref, de_ref, gains_ref,
    z_ref, pix_ref, band_ref, x_ref, qkv_ref, p_ref, inv_ref, oo_ref, x1_ref, a_ref, gp_ref, x2_ref, o_s,
    h_s, s_s, high_s, low_s,
):
    low = jnp.bfloat16
    step = pl.program_id(0)
    width = x_ref.shape[1]
    ee = width // heads
    groups = width // LANES
    expo = ee ** (-0.5) * 1.4426950408889634

    def gain(i):
        return gains_ref[i : i + 1, :]

    @pl.when(step == 0)
    def _():
        split_table(table_ref, high_s, low_s)

        @pl.loop(0, pixels_ref.shape[0])
        def _(i):
            at = pl.ds(pl.multiple_of(i * K, K), K)
            hot = one_hot(keep_ref[i], pixels_ref.shape[1])
            pix_ref[at, :] = dot_nn(hot.astype(low), pixels_ref[i]).astype(low)
            band_ref[at, :] = jnp.sum(hot * bands_ref[i], -1, keepdims=True).astype(jnp.int32)
            x_ref[at, :] = look_up(hot, gsd_ref[i], high_s, low_s)

    @pl.when(step < 4)
    def _():
        pixel = pix_ref[...]
        x_ref[...] += dot_nn(jnp.where(band_ref[...] == step, pixel, jnp.zeros_like(pixel)), rows_ref[...])

    @pl.when(step == 4)
    def _():
        hat, _ = unit_rows(x_ref[...])
        h_s[...] = (hat * gain(0) + gain(1)).astype(low)

    @pl.when((step >= 4) & (step < 7))
    def _():
        at = pl.ds(pl.multiple_of((step - 4) * width, width), width)
        qkv_ref[:, at] = dot_nn(h_s[...], cols_ref[...]).astype(low)

    @pl.when(step == 7)
    def _():
        same = same_item()

        @pl.loop(0, x_ref.shape[0] // RUN * groups)
        def _(n):
            attend(n, groups, RUN, width, ee, expo, same, qkv_ref, s_s, p_ref, inv_ref, oo_ref, o_s)

        x1_ref[...] = x_ref[...] + dot_nn(o_s[...], cols_ref[...])
        hat, _ = unit_rows(x1_ref[...])
        h_s[...] = (hat * gain(2) + gain(3)).astype(low)
        x2_ref[...] = x1_ref[...]

    @pl.when(step >= 8)
    def _():
        @pl.loop(0, 2)
        def _(t):
            half = width // 2
            at = pl.ds(pl.multiple_of(t * half, half), half)
            u = dot_nn(h_s[...], cols_ref[:, at])
            cumul = 0.5 * (1.0 + lax.erf(u * 0.7071067811865476))
            a_ref[:, at] = (u * cumul).astype(low)
            gp_ref[:, at] = (cumul + u * jnp.exp(-0.5 * u * u) * 0.3989422804014327).astype(low)

        x2_ref[...] += dot_nn(a_ref[...], rows_ref[...])

    @pl.when(step == 11)
    def _():
        hat, _ = unit_rows(x2_ref[...])
        h_s[...] = (hat * gain(4) + gain(5)).astype(low)
        z_ref[...] = dot_nn(h_s[...], de_ref[...])


def encoder_call(pixels, keep, bands, gsd, table, rows, cols, de, gains, heads):
    width = cols.shape[0]
    tokens = keep.shape[0] * K
    low, f32 = jnp.bfloat16, jnp.float32
    runs = tokens // RUN * (width // LANES)
    wide = LANES // (width // heads) * RUN
    one = pl.Buffered(1)

    def whole(shape):
        return pl.BlockSpec(shape, lambda s: (0,) * len(shape), pipeline_mode=one)

    def row_block(s):
        return (jnp.where(s < 4, s + 4, jnp.where(s < 8, 0, s - 8)), 0)

    def column_block(s):
        return (0, jnp.where(s < 4, 0, s - 4))

    def hidden_block(s):
        return (0, jnp.where(s < 8, 0, s - 8))

    def hold(shape, dtype=f32):
        return jax.ShapeDtypeStruct(shape, dtype), whole(shape)

    ff = (tokens, 4 * width)
    outs = [
        hold((tokens, de.shape[1])),
        hold((tokens, pixels.shape[2]), low),
        hold((tokens, 1), jnp.int32),
        hold((tokens, width)),
        hold((tokens, 3 * width), low),
        hold((runs, RUN, wide), low),
        hold((runs, RUN, LANES)),
        hold((runs, RUN, LANES)),
        hold((tokens, width)),
        (jax.ShapeDtypeStruct(ff, low), pl.BlockSpec((tokens, width), hidden_block)),
        (jax.ShapeDtypeStruct(ff, low), pl.BlockSpec((tokens, width), hidden_block)),
        hold((tokens, width)),
        hold((tokens, width), low),
    ]
    return pl.pallas_call(
        functools.partial(encoder_kernel, heads),
        grid=(12,),
        in_specs=[
            whole(pixels.shape),
            whole(keep.shape),
            whole(bands.shape),
            whole(gsd.shape),
            pl.BlockSpec((table.shape[0], width), lambda s: (0, 0), pipeline_mode=one),
            pl.BlockSpec((width, width), row_block),
            pl.BlockSpec((width, width), column_block),
            whole(de.shape),
            whole(gains.shape),
        ],
        out_specs=tuple(o[1] for o in outs),
        out_shape=tuple(o[0] for o in outs),
        scratch_shapes=[
            pltpu.VMEM((tokens, width), low),
            pltpu.VMEM((wide, RUN), f32),
            pltpu.VMEM((table.shape[0], width), low),
            pltpu.VMEM((table.shape[0], width), low),
        ],
        compiler_params=pltpu.CompilerParams(
            dimension_semantics=("arbitrary",), vmem_limit_bytes=60 * 1024 * 1024
        ),
        cost_estimate=pl.CostEstimate(
            flops=20_000_000_000, bytes_accessed=70_000_000, transcendentals=8_000_000
        ),
    )(pixels, keep, bands, gsd, table, rows, cols, de, gains)


def encoder_back_kernel(
    heads, dz_ref, pix_ref, band_ref, x_ref, qkv_ref, p_ref, inv_ref, oo_ref, x1_ref, a_ref, gp_ref, x2_ref,
    rows_ref, cols_ref, de_ref, gains_ref,
    grows_ref, gcols_ref, gde_ref, ggains_ref,
    h_s, dx_s, dy_s, acc_s, do_s, dqkv_s, s_s, ds_s,
):
    low, f32 = jnp.bfloat16, jnp.float32
    step = pl.program_id(0)
    width = x_ref.shape[1]
    ee = width // heads
    groups = width // LANES
    runs = x_ref.shape[0] // RUN

    def gain(i):
        return gains_ref[i : i + 1, :]

    def back(x, grads, at):
        hat, scaled = unit_rows(x)
        ggains_ref[at : at + 1, :] = jnp.sum(grads * hat, 0, keepdims=True)
        ggains_ref[at + 1 : at + 2, :] = jnp.sum(grads, 0, keepdims=True)
        return unit_back(grads, hat, scaled, gain(at))

    def normed(x, at):
        hat, _ = unit_rows(x)
        h_s[...] = (hat * gain(at) + gain(at + 1)).astype(low)

    @pl.when(step == 0)
    def _():
        ggains_ref[...] = jnp.zeros_like(ggains_ref)
        normed(x2_ref[...], 4)
        gde_ref[...] = dot_tn(h_s[...], dz_ref[...]).astype(low)
        dx_s[...] = back(x2_ref[...], dot_nt(dz_ref[...], de_ref[...]), 4)
        dy_s[...] = dx_s[...].astype(low)
        normed(x1_ref[...], 2)
        acc_s[...] = jnp.zeros_like(acc_s)

    @pl.when(step < 4)
    def _():
        grows_ref[...] = dot_tn(a_ref[...], dy_s[...]).astype(low)
        du = (dot_nt(dy_s[...], rows_ref[...]) * gp_ref[...].astype(f32)).astype(low)
        do_s[...] = du
        gcols_ref[...] = dot_tn(h_s[...], du).astype(low)
        acc_s[...] += dot_nt(do_s[...], cols_ref[...])

    @pl.when(step == 4)
    def _():
        dx_s[...] += back(x1_ref[...], acc_s[...], 2)
        dy_s[...] = dx_s[...].astype(low)
        for run in range(runs):
            for g in range(groups):
                h_s[run * RUN : (run + 1) * RUN, g * LANES : (g + 1) * LANES] = oo_ref[
                    run * groups + g
                ].astype(low)
        gcols_ref[...] = dot_tn(h_s[...], dy_s[...]).astype(low)
        do_s[...] = dot_nt(dy_s[...], cols_ref[...]).astype(low)

        @pl.loop(0, runs * groups)
        def _(n):
            attend_back(
                n, n, groups, RUN, width, ee, ee ** (-0.5), qkv_ref, s_s, ds_s, p_ref, inv_ref, oo_ref, do_s,
                dqkv_s,
            )

        normed(x_ref[...], 0)
        acc_s[...] = jnp.zeros_like(acc_s)

    @pl.when((step >= 5) & (step < 8))
    def _():
        at = pl.ds(pl.multiple_of((step - 5) * width, width), width)
        gcols_ref[...] = dot_tn(h_s[...], dqkv_s[:, at]).astype(low)
        acc_s[...] += dot_nt(dqkv_s[:, at], cols_ref[...])

    @pl.when(step == 8)
    def _():
        dx_s[...] += back(x_ref[...], acc_s[...], 0)
        dy_s[...] = dx_s[...].astype(low)

    @pl.when(step >= 8)
    def _():
        pixel = pix_ref[...]
        h_s[...] = jnp.where(band_ref[...] == step - 8, pixel, jnp.zeros_like(pixel))
        grows_ref[...] = dot_tn(h_s[...], dy_s[...]).astype(low)


def encoder_back_call(dz, pixel, band, saved, rows, cols, de, gains, heads):
    x, qkv, p, inv, oo, x1, a, gp, x2, _ = saved
    tokens, width = x.shape
    low, f32 = jnp.bfloat16, jnp.float32
    wide = p.shape[2]
    one = pl.Buffered(1)

    def whole(array):
        return pl.BlockSpec(array.shape, lambda s: (0,) * len(array.shape), pipeline_mode=one)

    def row_block(s):
        return (jnp.minimum(s, 3), 0)

    def column_block(s):
        return (0, jnp.where(s < 4, s + 4, jnp.where(s == 4, 3, jnp.minimum(s - 5, 2))))

    def hidden_block(s):
        return (0, jnp.minimum(s, 3))

    def grow_block(s):
        return (jnp.where(s < 4, s, jnp.where(s < 8, 3, s - 4)), 0)

    hidden = pl.BlockSpec((tokens, width), hidden_block)
    square = (width, width)
    outs = (
        jax.ShapeDtypeStruct(rows.shape, low),
        jax.ShapeDtypeStruct(cols.shape, low),
        jax.ShapeDtypeStruct(de.shape, low),
        jax.ShapeDtypeStruct((8, width), f32),
    )
    vmem = pltpu.VMEM
    return pl.pallas_call(
        functools.partial(encoder_back_kernel, heads),
        grid=(12,),
        in_specs=[
            whole(dz), whole(pixel), whole(band), whole(x), whole(qkv), whole(p), whole(inv), whole(oo),
            whole(x1), hidden, hidden, whole(x2),
            pl.BlockSpec(square, row_block), pl.BlockSpec(square, column_block),
            whole(de), whole(gains),
        ],
        out_specs=(
            pl.BlockSpec(square, grow_block),
            pl.BlockSpec(square, column_block),
            whole(outs[2]),
            whole(outs[3]),
        ),
        out_shape=outs,
        scratch_shapes=[
            vmem((tokens, width), low),
            vmem((tokens, width), f32),
            vmem((tokens, width), low),
            vmem((tokens, width), f32),
            vmem((tokens, width), low),
            vmem((tokens, 3 * width), low),
            vmem((wide, RUN), f32),
            vmem((RUN, wide), low),
        ],
        compiler_params=pltpu.CompilerParams(
            dimension_semantics=("arbitrary",), vmem_limit_bytes=60 * 1024 * 1024
        ),
        cost_estimate=pl.CostEstimate(
            flops=40_000_000_000, bytes_accessed=110_000_000, transcendentals=1_000_000
        ),
    )(dz, pixel, band, x, qkv, p, inv, oo, x1, a, gp, x2, rows, cols, de, gains)


MESH_ID = pl.DeviceIdType.MESH


def place():
    g = lax.axis_index("grp")
    d = lax.axis_index("dp")
    z, c = d // 2, d % 2
    xn = g + 1 - 2 * (g % 2)
    yn = (g + 2) % 4
    return g, z, c, xn, yn


def pieces(shape, parts):
    rows, columns = shape
    if rows // parts >= 32:
        n = rows // parts
        cut = [(slice(i * n, (i + 1) * n), slice(0, columns)) for i in range(parts)]
    else:
        n = columns // parts
        cut = [(slice(0, rows), slice(i * n, (i + 1) * n)) for i in range(parts)]
    return cut


def halves(cut):
    rows, columns = cut
    mid = (columns.start + columns.stop) // 2
    return (rows, slice(columns.start, mid)), (rows, slice(mid, columns.stop))


def greet(peers):
    barrier = pltpu.get_barrier_semaphore()
    for peer in peers:
        pl.semaphore_signal(barrier, inc=1, device_id=peer, device_id_type=MESH_ID)
    pl.semaphore_wait(barrier, len(peers))


def gather_kernel(count, chunks, ahead, *refs):
    ins, items_ref = refs[:count], refs[count]
    outs, items_out = refs[count + 1 : 2 * count + 1], refs[2 * count + 1]
    (zs, zr, xs, xr, ys, yr, fs, fr, gs, gr, cs, os, cr, ls, it, its, itr) = refs[2 * count + 2 :]
    g, z, c, xn, yn = place()
    dg = (xn + 2) % 4
    here = 2 * z + c
    sib = (g, 2 * z + 1 - c)
    zpeer = [(g, 2 * ((z + j) % 4) + c) for j in (1, 2, 3)]
    zfrom = [(z + 4 - j) % 4 for j in (1, 2, 3)]
    greet([sib, (xn, here), (yn, here)] + zpeer)

    def send(src, dst, send_sem, recv_sem, peer):
        return pltpu.make_async_remote_copy(
            src_ref=src, dst_ref=dst, send_sem=send_sem, recv_sem=recv_sem,
            device_id=peer, device_id_type=MESH_ID,
        )

    def block(array, z_at, q, cut, core=None):
        return outs[array].at[z_at, c if core is None else core, q, cut[0], cut[1]]

    work = []
    for array in range(count):
        for cut in pieces(ins[array].shape[1:], chunks[array]):
            work.append((array, cut))
    steps = len(work)
    sent = []

    def go(copy):
        copy.start()
        sent.append(copy)

    def items_copy(i, peer):
        return send(it.at[2 * i], it.at[2 * i + 1], its.at[i], itr.at[i], peer)

    def zcopy(k, j):
        array, cut = work[k]
        return send(
            ins[array].at[g, cut[0], cut[1]], block(array, z, g, cut), zs.at[k, j], zr.at[k, j], zpeer[j]
        )

    def relay(k, j, q, cut, ssem, rsem, peer):
        at = block(work[k][0], zfrom[j], q, cut)
        return send(at, at, ssem, rsem, peer)

    it[0] = items_ref[...]
    go(items_copy(0, (xn, here)))
    local = []
    for array in range(count):
        copy = pltpu.make_async_copy(ins[array], outs[array].at[z, c], ls.at[array])
        copy.start()
        local.append(copy)
    for k in range(min(ahead, steps)):
        for j in range(3):
            go(zcopy(k, j))
    for array in range(count):
        go(send(ins[array], outs[array].at[z, c], os.at[array], cr.at[array], sib))

    for t in range(steps + 2):
        if t < steps:
            array, cut = work[t]
            for j in range(3):
                zcopy(t, j).wait_recv()
                go(relay(t, j, g, cut, xs.at[t, j], xr.at[t, j], (xn, here)))
                go(relay(t, j, g, cut, ys.at[t, j], yr.at[t, j], (yn, here)))
                go(relay(t, j, g, cut, cs.at[t, j, 0], cr.at[array], sib))
            if t + ahead < steps:
                for j in range(3):
                    go(zcopy(t + ahead, j))
        if t == 0:
            items_copy(0, (xn, here)).wait_recv()
            it[2] = it[0] + it[1]
            go(items_copy(1, (yn, here)))
        if t == 1:
            items_copy(1, (yn, here)).wait_recv()
            items_out[...] = it[2] + it[3]
        if 1 <= t <= steps:
            k = t - 1
            array, cut = work[k]
            left, right = halves(cut)
            for j in range(3):
                relay(k, j, xn, cut, xs.at[k, j], xr.at[k, j], (xn, here)).wait_recv()
                go(relay(k, j, xn, left, fs.at[k, j], fr.at[k, j], (yn, here)))
                go(relay(k, j, xn, cut, cs.at[k, j, 1], cr.at[array], sib))
                relay(k, j, yn, cut, ys.at[k, j], yr.at[k, j], (yn, here)).wait_recv()
                go(relay(k, j, yn, right, gs.at[k, j], gr.at[k, j], (xn, here)))
                go(relay(k, j, yn, cut, cs.at[k, j, 2], cr.at[array], sib))
        if 2 <= t:
            k = t - 2
            array, cut = work[k]
            left, right = halves(cut)
            for j in range(3):
                relay(k, j, dg, left, fs.at[k, j], fr.at[k, j], (yn, here)).wait_recv()
                relay(k, j, dg, right, gs.at[k, j], gr.at[k, j], (xn, here)).wait_recv()
                go(relay(k, j, dg, cut, cs.at[k, j, 3], cr.at[array], sib))
    for copy in sent:
        copy.wait_send()
    for array in range(count):
        whole = outs[array].at[:, 1 - c]
        send(whole, whole, os.at[array], cr.at[array], sib).wait_recv()
        local[array].wait()


def gather_call(shards, items, chunks, ahead=2, collective_id=0):
    count = len(shards)
    steps = sum(chunks)
    views = [s.reshape(4, s.shape[0] // 4, s.shape[1]) for s in shards]
    dma = pltpu.SemaphoreType.DMA
    hbm = pl.BlockSpec(memory_space=pl.ANY)
    vm = pl.BlockSpec(memory_space=pltpu.VMEM)
    *outs, total = pl.pallas_call(
        functools.partial(gather_kernel, count, chunks, ahead),
        out_shape=tuple(jax.ShapeDtypeStruct((4, 2) + v.shape, v.dtype) for v in views)
        + (jax.ShapeDtypeStruct((8, 128), jnp.float32),),
        in_specs=[hbm] * count + [vm],
        out_specs=tuple([hbm] * count + [vm]),
        scratch_shapes=[dma((steps, 3))] * 10
        + [dma((steps, 3, 4)), dma((count,)), dma((count,)), dma((count,))]
        + [pltpu.VMEM((4, 8, 128), jnp.float32), dma((2,)), dma((2,))],
        compiler_params=pltpu.CompilerParams(collective_id=collective_id, has_side_effects=True),
    )(*views, jnp.broadcast_to(items, (8, 128)))
    return [o.reshape(-1, o.shape[-1]) for o in outs], total[0, 0]


def back_reduce_kernel(heads, kinds, work, pieces, refs_in, refs_out, *refs):
    low, f32 = jnp.bfloat16, jnp.float32
    ref = dict(zip(refs_in + refs_out, refs))
    rest = refs[len(refs_in) + len(refs_out) :]
    per = 9
    bufs = [rest[per * i : per * i + per] for i in range(len(kinds))]
    (sm, ss, ssx, dx, acc, xin, h, dy, wide, wt, wu, out_r, out_c, out_e, p_t, inv_t, oo_t, s_s, ds_s, gsum,
     cs, cr, ls, os, x1s, x1r, x2s, x2r, z_s, z_r, ags, agr, ks, sms, smr, sss, ssr, dma, att_sem) = rest[
        per * len(kinds) :
    ]
    g, z, c, xn, yn = place()
    dg = (xn + 2) % 4
    here = 2 * z + c
    sib = (g, 2 * z + 1 - c)
    right, up = (xn, here), (yn, here)
    zto = [(z + j) % 4 for j in (1, 2, 3)]
    zpeer = [(g, 2 * t + c) for t in zto]
    greet([sib, right, up] + zpeer)
    steps = len(work)
    sent = []
    from_slot = [[] for _ in range(steps)]

    def send(src, dst, send_sem, recv_sem, peer):
        return pltpu.make_async_remote_copy(
            src_ref=src, dst_ref=dst, send_sem=send_sem, recv_sem=recv_sem,
            device_id=peer, device_id_type=MESH_ID,
        )

    def guarded(test, action):
        if test is None:
            action()
        else:
            pl.when(test)(action)

    def go(copies, keep=None, tests=None):
        for i, copy in enumerate(copies):
            test = tests[i] if tests else None
            guarded(test, copy.start)
            (sent if keep is None else keep).append((test, copy))

    def left(entries):
        for test, copy in entries:
            guarded(test, copy.wait_send)

    def got(copies):
        for copy in copies:
            copy.wait_recv()

    def mine(k, at=None):
        base = work[k][2]
        at = z if at is None else at
        return None if base is None else ((at >= base) & (at < base + 2))

    def buffers(k):
        kind, at = work[k][:2]
        return bufs[kind], at, at % kinds[kind][4], kinds[kind][2] // 2

    def c_copies(k):
        (_, crecv, *_), at, _, _ = buffers(k)
        return [
            send(
                ref[array].at[:, 1 - c, :, cut[0], cut[1]], crecv.at[at, pl.ds(z0, nz)],
                cs.at[k, i], cr.at[k, i], sib,
            )
            for i, (array, z0, nz, cut) in enumerate(work[k][3])
        ]

    def own_copies(k):
        (s, *_), _, slot, _ = buffers(k)
        return [
            pltpu.make_async_copy(
                ref[array].at[:, c, :, cut[0], cut[1]], s.at[slot, pl.ds(z0, nz)], os.at[k, i]
            )
            for i, (array, z0, nz, cut) in enumerate(work[k][3])
        ]

    def recv_load(k, i):
        (_, crecv, tmp, *_), at, _, _ = buffers(k)
        return pltpu.make_async_copy(crecv.at[at, i], tmp.at[i % 2], ls.at[k, i])

    def x1_copies(k):
        (s, _, _, xa, yb, *_), at, slot, half = buffers(k)
        lo, hi = pl.ds(0, half), pl.ds(half, half)
        return [
            send(s.at[slot, :, xn, :, lo], xa.at[at, 0], x1s.at[k, 0], x1r.at[k, 0], right),
            send(s.at[slot, :, dg, :, lo], xa.at[at, 1], x1s.at[k, 1], x1r.at[k, 1], right),
            send(s.at[slot, :, yn, :, hi], yb.at[at, 0], x1s.at[k, 2], x1r.at[k, 2], up),
            send(s.at[slot, :, dg, :, hi], yb.at[at, 1], x1s.at[k, 3], x1r.at[k, 3], up),
        ]

    def x2_copies(k):
        (s, _, _, _, _, xb, ya, *_), at, slot, half = buffers(k)
        lo, hi = pl.ds(0, half), pl.ds(half, half)
        return [
            send(s.at[slot, :, yn, :, lo], ya.at[at], x2s.at[k, 0], x2r.at[k, 0], up),
            send(s.at[slot, :, xn, :, hi], xb.at[at], x2s.at[k, 1], x2r.at[k, 1], right),
        ]

    def z_copies(k):
        (s, *_, zb, _), at, slot, _ = buffers(k)
        base = work[k][2] or 0
        return [
            send(
                s.at[slot, (zto[j] - base) % kinds[work[k][0]][0], g], zb.at[at, j],
                z_s.at[k, j], z_r.at[k, j], zpeer[j],
            )
            for j in range(3)
        ]

    def out_at(k, q, part=None):
        name, cut = work[k][4:6]
        if part is not None:
            cut = halves(cut)[part]
        return ref[name].at[q, cut[0], cut[1]]

    def ag_copies(k):
        (*_, fin), at, _, _ = buffers(k)
        return [
            send(fin.at[at], out_at(k, g), ags.at[k, 0], agr.at[k, 0], right),
            send(fin.at[at], out_at(k, g), ags.at[k, 1], agr.at[k, 1], up),
        ]

    def keep_copy(k):
        (*_, fin), at, _, _ = buffers(k)
        return pltpu.make_async_copy(fin.at[at], out_at(k, g), ks.at[k])

    def fwd_copies(k, of_x, of_y):
        return [
            send(out_at(k, of_x, 0), out_at(k, of_x, 0), ags.at[k, 2], agr.at[k, 2], up),
            send(out_at(k, of_y, 1), out_at(k, of_y, 1), ags.at[k, 3], agr.at[k, 3], right),
        ]

    def add_half(k, q, first, other):
        (s, *_), _, slot, half = buffers(k)
        part = pl.ds(0 if first else half, half)

        @pl.loop(0, kinds[work[k][0]][0])
        def _(i):
            s[slot, i, q, :, part] = (s[slot, i, q, :, part].astype(f32) + other[i].astype(f32)).astype(low)

    def load(k):
        kind, at = work[k][:2]
        slots = kinds[kind][4]
        if at >= slots:
            before = [j for j in range(steps) if work[j][:2] == (kind, at - slots)][0]
            left(from_slot[before])
            from_slot[before].clear()
        for copy in own_copies(k):
            copy.start()

    def pair(k):
        (s, _, tmp, *_), _, slot, _ = buffers(k)
        count = kinds[work[k][0]][0]
        got(c_copies(k))
        for i in range(2):
            recv_load(k, i).start()
        for copy in own_copies(k):
            copy.wait()
        for i in range(count):
            recv_load(k, i).wait()

            @pl.loop(0, 4)
            def _(q):
                s[slot, i, q] = (s[slot, i, q].astype(f32) + tmp[i % 2, q].astype(f32)).astype(low)

            if i + 2 < count:
                recv_load(k, i + 2).start()
        go(x1_copies(k), from_slot[k])

    def first_half(k):
        (_, _, _, xa, yb, *_), at, _, _ = buffers(k)
        got(x1_copies(k))
        add_half(k, yn, True, xa.at[at, 1])
        add_half(k, xn, False, yb.at[at, 1])
        go(x2_copies(k), from_slot[k])
        add_half(k, g, True, xa.at[at, 0])
        add_half(k, g, False, yb.at[at, 0])

    def second_half(k):
        (_, _, _, _, _, xb, ya, *_), at, _, _ = buffers(k)
        got(x2_copies(k))
        add_half(k, g, True, ya.at[at])
        add_half(k, g, False, xb.at[at])
        go(z_copies(k), from_slot[k], [mine(k, t) for t in zto])

    def finish(k):
        def act():
            (s, *_, zb, fin), at, slot, _ = buffers(k)
            got(z_copies(k))
            base = work[k][2] or 0
            total = s[slot, (z - base) % kinds[work[k][0]][0], g].astype(f32)
            for j in range(3):
                total = total + zb[at, j].astype(f32)
            fin[at] = total.astype(low)
            keep_copy(k).start()
            square = fin[at].astype(f32)
            square = square * square
            for i in range(square.shape[1] // ss.shape[1]):
                ss[...] += jnp.sum(
                    square[:, i * ss.shape[1] : (i + 1) * ss.shape[1]], 0, keepdims=True
                )

        guarded(mine(k), act)
        go(ag_copies(k), None, [mine(k)] * 2)

    def collect(k):
        guarded(mine(k), lambda: got(ag_copies(k)))
        go(fwd_copies(k, xn, yn), None, [mine(k)] * 2)

    def close(k):
        guarded(mine(k), lambda: got(fwd_copies(k, dg, dg)))

    stages = [load, pair, first_half, second_half, finish, collect, close]

    def share_rounds(value, sem_s, sem_r, store):
        def copy(i, slot, peer):
            return send(value.at[slot], value.at[4 + i], sem_s.at[i], sem_r.at[i], peer)

        def round_pair(i, peer, following):
            got([copy(i, i, peer)])
            value[i + 1] = value[i] + value[4 + i]
            go(following())

        def last():
            return [copy(3 + j, 3, zpeer[j]) for j in range(3)]

        def end():
            got(last())
            total = None
            for at in range(4):
                term = jnp.where(z == at, value[3], jnp.zeros_like(value[3]))
                for j in range(3):
                    term = term + jnp.where((z + 3 - j) % 4 == at, value[7 + j], jnp.zeros_like(value[3]))
                total = term if total is None else total + term
            store[...] = total

        return [
            lambda: go([copy(0, 0, sib)]),
            lambda: round_pair(0, sib, lambda: [copy(1, 1, right)]),
            lambda: round_pair(1, right, lambda: [copy(2, 2, up)]),
            lambda: round_pair(2, up, last),
            end,
        ]

    tokens, width = dx.shape
    ee = width // heads
    groups = width // LANES
    runs = tokens // RUN
    gains = ref["gains"]

    moving = {}

    def move(name, src, dst):
        copy = pltpu.make_async_copy(src, dst, dma.at[lanes_of.index(name)])
        copy.start()
        moving[name] = copy

    def done(*names):
        for name in names:
            if name in moving:
                moving.pop(name).wait()

    lanes_of = (
        "a", "gp", "rows", "cols", "x", "dz", "de", "o", "qkv", "pix", "out_r", "out_c", "out_e",
    )

    def tile(i):
        return pl.ds(i * width, width)

    def gain(i):
        return gains[i : i + 1, :]

    def back(grads, at):
        hat, scaled = unit_rows(xin[...])
        gsum[at : at + 1, :] = jnp.sum(grads * hat, 0, keepdims=True)
        gsum[at + 1 : at + 2, :] = jnp.sum(grads, 0, keepdims=True)
        return unit_back(grads, hat, scaled, gain(at))

    def normed(at):
        hat, _ = unit_rows(xin[...])
        h[...] = (hat * gain(at) + gain(at + 1)).astype(low)

    def column_grads(block, source):
        done("out_c")
        for d in range(8):
            value = dot_tn(h[:, d * 128 : (d + 1) * 128], source()).astype(low)
            out_c[d // 2, d % 2] = value.reshape(out_c.shape[2:])
        move("out_c", out_c, ref["g_cols"].at[:, :, :, :, tile(block)])

    def load_hidden(s):
        move("a", ref["a"].at[:, tile(s)], wide.at[:, tile(0)])
        move("gp", ref["gp"].at[:, tile(s)], wide.at[:, tile(1)])
        move("rows", ref["rows"].at[tile(s)], wt)

    def load_columns(block):
        move("cols", ref["cols"].at[:, tile(block)], wu)

    narrow = ref["dz"].shape[1]

    def first_loads():
        move("x", ref["x2"], xin)
        move("dz", ref["dz"], wide.at[:, pl.ds(2 * width, narrow)])
        move("de", ref["de"], wt.at[:, pl.ds(0, narrow)])
        move("a", ref["a"].at[:, tile(0)], wide.at[:, tile(0)])
        move("gp", ref["gp"].at[:, tile(0)], wide.at[:, tile(1)])
        load_columns(4)

    def head_piece(_):
        done("x", "dz", "de")
        dz = wide[:, 2 * width : 2 * width + narrow]
        normed(4)
        for d in range(8):
            out_e[0, d // 4, d % 4] = dot_tn(h[:, d * 128 : (d + 1) * 128], dz).astype(low)
        move("out_e", out_e, ref["g_de"])
        dx[...] = back(dot_nt(dz, wt[:, :narrow]), 4)
        move("rows", ref["rows"].at[tile(0)], wt)
        move("x", ref["x1"], xin)
        dy[...] = dx[...].astype(low)
        done("x")
        normed(2)
        acc[...] = jnp.zeros_like(acc)

    def hidden_piece(s):
        done("a", "gp", "rows", "out_r")
        wide[:, 2 * width :] = (dot_nt(dy[...], wt[...]) * wide[:, width : 2 * width].astype(f32)).astype(low)
        for q in range(4):
            out_r[q] = dot_tn(wide[:, q * 256 : (q + 1) * 256], dy[...]).astype(low)
        move("out_r", out_r, ref["g_down"].at[s // 2, s % 2])
        if s < 3:
            load_hidden(s + 1)
        column_grads(4 + s, lambda: wide[:, 2 * width :])
        done("cols")
        acc[...] += dot_nt(wide[:, 2 * width :], wu[...])
        load_columns(5 + s if s < 3 else 3)
        if s == 3:
            move("o", ref["o"], h)
            move("qkv", ref["qkv"], wide)

    def middle_piece(_):
        dx[...] += back(acc[...], 2)
        dy[...] = dx[...].astype(low)
        move("x", ref["x"], xin)
        done("o")
        column_grads(3, lambda: dy[...])
        done("cols")
        h[...] = dot_nt(dy[...], wu[...]).astype(low)
        load_columns(0)
        done("qkv")

    def attention_loads(n):
        slot = n % 2
        return [
            pltpu.make_async_copy(ref[name].at[n], buf.at[slot], att_sem.at[slot, i])
            for i, (name, buf) in enumerate((("p", p_t), ("inv", inv_t), ("oo", oo_t)))
        ]

    def attention_piece(part):
        count = runs * groups // 4
        first = part * count
        for copy in attention_loads(first):
            copy.start()

        @pl.loop(0, count)
        def _(i):
            n = first + i
            for copy in attention_loads(n):
                copy.wait()

            @pl.when(i + 1 < count)
            def _():
                for copy in attention_loads(n + 1):
                    copy.start()

            attend_back(
                n, n % 2, groups, RUN, width, ee, ee ** (-0.5), wide, s_s, ds_s, p_t, inv_t, oo_t, h, wide
            )

    def input_piece(t):
        if t == 0:
            done("x")
            normed(0)
            acc[...] = jnp.zeros_like(acc)
        column_grads(t, lambda: wide[:, t * width : (t + 1) * width])
        done("cols")
        acc[...] += dot_nt(wide[:, t * width : (t + 1) * width], wu[...])
        if t < 2:
            load_columns(t + 1)
        else:
            move("pix", ref["pix"], h)

    def first_piece(_):
        dx[...] += back(acc[...], 0)
        dy[...] = dx[...].astype(low)
        sm[0] = ref["small"][...]
        sm[0, 0:6, :] = gsum[0:6, :]

    def embed_piece(b):
        done("pix", "out_r")
        for q in range(4):
            part = h[:, q * 256 : (q + 1) * 256]
            part = jnp.where(ref["band"][...] == b, part, jnp.zeros_like(part))
            out_r[q] = dot_tn(part, dy[...]).astype(low)
        move("out_r", out_r, ref["g_emb"].at[b // 2, b % 2])

    action = {
        "head": head_piece, "hidden": hidden_piece, "middle": middle_piece, "attention": attention_piece,
        "input": input_piece, "first": first_piece, "embed": embed_piece,
    }

    ss[...] = jnp.zeros_like(ss)
    gsum[...] = jnp.zeros_like(gsum)
    small_rounds = share_rounds(sm, sms, smr, ref["small_out"])
    square_rounds = share_rounds(ssx, sss, ssr, ref["ss_out"])
    ends = [w[6] + 6 for w in work]
    last = max(ends)
    squared = max(w[6] + 4 for w in work)
    compute_end = max(t for t, _, _ in pieces)
    for t in range(last + 1):
        for i in (1, 6, 5, 4, 3, 2, 0):
            for k in range(steps):
                if work[k][6] + i == t:
                    stages[i](k)
        if t == 0:
            first_loads()
        done("out_r", "out_c", "out_e")
        for k in range(steps):
            if work[k][7] == t:
                go(c_copies(k))
        for at, name, argument in pieces:
            if at == t:
                action[name](argument)
        if compute_end < t <= compute_end + 5:
            small_rounds[t - compute_end - 1]()
        if t == squared:
            ssx[0] = jnp.broadcast_to(jnp.sum(ss[...], keepdims=True).reshape(1, 1), ssx.shape[1:])
            square_rounds[0]()
        if squared < t < last:
            square_rounds[t - squared]()
        if t == last:
            for following in square_rounds[last - squared :]:
                following()
    for k in range(steps):
        left(from_slot[k])
    left(sent)
    for k in range(steps):
        guarded(mine(k), keep_copy(k).wait)


def back_reduce_call(dz, pix, band, saved, rows, cols, de, gains, dcols, ddown, dhead, small, heads):
    x, qkv, p, inv, oo, x1, a, gp, x2, o = saved
    tokens, width = x.shape
    low, f32 = jnp.bfloat16, jnp.float32
    narrow = de.shape[1]
    ins = dict(
        dz=dz, pix=pix, band=band, x=x, x1=x1, x2=x2, qkv=qkv, p=p, inv=inv, oo=oo, o=o, a=a, gp=gp,
        rows=rows, cols=cols, de=de, gains=gains, small=small,
        d_cols=dcols.reshape(4, 2, 4, 16, dcols.shape[1]),
        d_down=ddown.reshape(2, 2, 4, 128, narrow),
        d_head=dhead.reshape(1, 2, 4, 128, narrow),
    )
    outs = dict(
        erows=((4, 256, width), low), ecols=((4, 32, cols.shape[1]), low),
        dcols=((4, 16, dcols.shape[1]), low), drows=((4, 128, narrow), low),
        small_out=(small.shape, f32), ss_out=((8, 128), f32),
        g_down=((2, 2, 4, 256, width), low), g_emb=((2, 2, 4, 256, width), low),
        g_cols=((4, 2, 4, 32, cols.shape[1]), low), g_de=((1, 2, 4, 128, narrow), low),
    )
    kinds = ((4, 32, 1024, 16, 6), (4, 16, 2048, 2, 2), (4, 64, 512, 2, 2))

    def column_chunk(at, block):
        cut = (slice(0, 32), slice(block * 1024, (block + 1) * 1024))
        return (0, at, None, (("g_cols", 0, 4, cut),), "ecols", cut)

    def row_chunk(at, i):
        cut = (slice(i * 32, (i + 1) * 32), slice(0, width))
        return (0, at, None, (("g_down", 0, 2, cut), ("g_emb", 2, 2, cut)), "erows", cut)

    chunks = []
    for i in range(2):
        cut = (slice(0, 16), slice(i * 2048, (i + 1) * 2048))
        chunks.append((1, i, None, (("d_cols", 0, 4, cut),), "dcols", cut))
    for i in range(2):
        cut = (slice(i * 64, (i + 1) * 64), slice(0, narrow))
        sources = (("d_down", 0, 2, cut), ("g_de", 2, 1, cut), ("d_head", 3, 1, cut))
        chunks.append((2, i, None, sources, "drows", cut))
    chunks += [column_chunk(i, 4 + i) for i in range(4)]
    chunks += [column_chunk(4 + i, block) for i, block in enumerate((3, 0, 1, 2))]
    chunks += [row_chunk(8 + i, i) for i in range(8)]
    starts = (0, 1, 3, 4, 5, 6, 7, 8, 9, 11, 12, 13) + tuple(range(14, 22))
    begins = (0, 0, 2, 2, 3, 4, 5, 6, 7, 10, 10, 11) + tuple(range(13, 21))
    work = tuple(chunk + (starts[i], begins[i]) for i, chunk in enumerate(chunks))
    pieces = [(1, "head", 0)] + [(2 + s, "hidden", s) for s in range(4)] + [(6, "middle", 0)]
    pieces += [(7 + i // 2, "attention", i) for i in range(4)]
    pieces += [(9, "input", 0), (9, "input", 1), (10, "input", 2), (10, "first", 0)]
    pieces += [(11 + i // 2, "embed", i) for i in range(4)]
    steps = len(work)
    hbm = pl.BlockSpec(memory_space=pl.ANY)
    vm = pl.BlockSpec(memory_space=pltpu.VMEM)
    vmem, sems = pltpu.VMEM, pltpu.SemaphoreType.DMA
    scratch, landing = [], {}
    for i, (nz, r, col, count, slots) in enumerate(kinds):
        landing[f"land{i}"] = ((count, nz, 4, r, col), low)
        half = col // 2
        scratch += [
            vmem((slots, nz, 4, r, col), low),
            None,
            vmem((2, 4, r, col), low),
            vmem((count, 2, nz, r, half), low),
            vmem((count, 2, nz, r, half), low),
            vmem((count, nz, r, half), low),
            vmem((count, nz, r, half), low),
            vmem((count, 3, r, col), low),
            vmem((count, r, col), low),
        ]
    outs.update(landing)
    in_names, out_names = tuple(ins), tuple(outs)

    def kernel(*refs):
        n = len(in_names) + len(out_names)
        ref = dict(zip(in_names + out_names, refs))
        kept = list(refs[n:])
        for i in range(len(kinds)):
            kept.insert(9 * i + 1, ref[f"land{i}"])
        back_reduce_kernel(heads, kinds, work, pieces, in_names, out_names, *refs[:n], *kept)

    result = pl.pallas_call(
        kernel,
        out_shape=tuple(jax.ShapeDtypeStruct(*outs[name]) for name in out_names),
        in_specs=[vm if name in ("band", "gains", "small") else hbm for name in in_names],
        out_specs=tuple(vm if name in ("small_out", "ss_out") else hbm for name in out_names),
        scratch_shapes=[s for s in scratch if s is not None]
        + [
            vmem((10,) + small.shape, f32),
            vmem((1, 512), f32),
            vmem((10, 8, 128), f32),
            vmem((tokens, width), f32),
            vmem((tokens, width), f32),
            vmem((tokens, width), f32),
            vmem((tokens, width), low),
            vmem((tokens, width), low),
            vmem((tokens, 3 * width), low),
            vmem((width, width), low),
            vmem((width, width), low),
            vmem((4, 256, width), low),
            vmem((4, 2, 4, 32, width), low),
            vmem((1, 2, 4, 128, narrow), low),
            vmem((2,) + p.shape[1:], low),
            vmem((2,) + inv.shape[1:], f32),
            vmem((2,) + oo.shape[1:], f32),
            vmem((p.shape[2], RUN), f32),
            vmem((RUN, p.shape[2]), low),
            vmem((8, width), f32),
            sems((steps, 3)), sems((steps, 3)), sems((steps, 4)), sems((steps, 3)),
            sems((steps, 4)), sems((steps, 4)),
            sems((steps, 2)), sems((steps, 2)),
            sems((steps, 3)), sems((steps, 3)),
            sems((steps, 4)), sems((steps, 4)),
            sems((steps,)), sems((6,)), sems((6,)), sems((6,)), sems((6,)), sems((13,)), sems((2, 3)),
        ],
        compiler_params=pltpu.CompilerParams(
            collective_id=1, has_side_effects=True, vmem_limit_bytes=63 * 1024 * 1024
        ),
    )(*ins.values())
    got = dict(zip(out_names, result))
    shards = [got[name].reshape(-1, got[name].shape[-1]) for name in ("ecols", "erows", "dcols", "drows")]
    return shards, got["small_out"], got["ss_out"]


def adam_step(master, moment, square, grad, factor, fix_one, fix_two, decay, rate):
    clipped = grad * factor
    moment_new = beta_first * moment + (1.0 - beta_first) * clipped
    square_new = beta_second * square + (1.0 - beta_second) * clipped * clipped
    direction = moment_new / fix_one / (jnp.sqrt(square_new / fix_two) + adam_eps) + decay * master
    return (clipped, square_new, master - rate * direction)


def body(
    pixels,
    keep_index,
    band_group,
    gsd_index,
    gsd_table,
    group_items,
    step_count,
    enc_cols,
    enc_rows,
    dec_cols,
    dec_rows,
    enc_gains,
    dec_gains,
    moment_ecols,
    moment_erows,
    moment_dcols,
    moment_drows,
    moment_egains,
    moment_dgains,
    square_ecols,
    square_erows,
    square_dcols,
    square_drows,
    square_egains,
    square_dgains,
):
    n_grp = lax.axis_size("grp")
    grp_at = lax.axis_index("grp")

    def gather_rows(master):
        rows = master.shape[0]
        if rows % (16 * n_grp):
            return lax.all_gather(to_low(master), "dp", axis=0, tiled=True)
        part = rows // n_grp
        mine = lax.dynamic_slice_in_dim(master, grp_at * part, part, 0)
        return lax.all_gather(to_low(mine), ("dp", "grp"), axis=0, tiled=True)

    direct = (n_grp, lax.axis_size("dp")) == (4, 8)
    own_count = jnp.sum(group_items.astype(jnp.float32))
    if direct:
        (whole_rows, whole_cols), total_count = gather_call(
            [to_low(enc_rows), to_low(enc_cols)], own_count, (4, 4), 2, 0
        )
    else:
        total_count = lax.psum(own_count, "grp")
        whole_rows, whole_cols = gather_rows(enc_rows), gather_rows(enc_cols)
    masked = total_count * (L - K)
    copies = (whole_cols, whole_rows, gather_rows(dec_cols), gather_rows(dec_rows))
    dec_copy = copies[2]
    dec_down = copies[3][:DFF]
    dec_embed = copies[3][DFF : DFF + D]
    head_rows = copies[3][DFF + D :]
    keep_rows = keep_index[0]
    batch = keep_rows.shape[0]
    keep_column = keep_rows[..., None]
    band_row = band_group[0][:, None, :].astype(jnp.float32)
    gsd_row = gsd_index[0][:, None, :].astype(jnp.float32)
    latent, kept_pixels, kept_bands, *saved = encoder_call(
        pixels[0],
        keep_column,
        band_row,
        gsd_row,
        gsd_table[0],
        whole_rows,
        whole_cols,
        dec_embed,
        enc_gains,
        HEADS,
    )
    latent = latent.reshape(batch, K, -1)
    first_item = lax.axis_index("dp") * batch
    valid = (first_item + jnp.arange(batch, dtype=jnp.int32) < group_items[0]).astype(jnp.float32)
    scal = jnp.stack([valid / PIX, valid * (2.0 / PIX) / masked])
    grad_latent, grad_dcols, grad_ddown, grad_head, dec_sums, loss_local = decoder_call(
        scal,
        latent,
        keep_column,
        gsd_row,
        gsd_table[0],
        pixels[0],
        dec_copy,
        dec_down,
        head_rows,
        dec_gains,
        DHEADS,
    )
    loss_local = loss_local[0, 0]
    grad_latent = grad_latent.reshape(batch * K, -1)
    grad_dgains = dec_sums[:7]

    def reduce_rows(pieces, axis):
        whole = jnp.concatenate([to_low(piece) for piece in pieces], axis)
        return lax.psum_scatter(whole, "dp", scatter_dimension=0, tiled=True)

    if direct:
        count_e, count_d = enc_gains.size, grad_dgains.size
        flat = jnp.concatenate([grad_dgains.reshape(-1), loss_local[None]])
        small = jnp.pad(flat, (count_e, 16 * D - count_e - flat.shape[0])).reshape(16, D)
        shards, small, squares = back_reduce_call(
            grad_latent,
            kept_pixels,
            kept_bands,
            saved,
            whole_rows,
            whole_cols,
            dec_embed,
            enc_gains,
            grad_dcols,
            grad_ddown,
            grad_head,
            small,
            HEADS,
        )
        flat = small.reshape(-1)
        enc_sum = flat[:count_e].reshape(enc_gains.shape)
        dec_sum = flat[count_e : count_e + count_d].reshape(grad_dgains.shape)
        loss_sum = flat[count_e + count_d]
        shard_squares = squares[0, 0]
        shards = tuple(piece.astype(jnp.float32) for piece in shards)
    else:
        grad_erows, grad_ecols, grad_dembed, enc_sums = encoder_back_call(
            grad_latent,
            kept_pixels,
            kept_bands,
            saved,
            whole_rows,
            whole_cols,
            dec_embed,
            enc_gains,
            HEADS,
        )
        grad_egains = enc_sums[:6]
        drows = (grad_ddown, grad_dembed, grad_head)
        enc_sum, dec_sum, loss_sum = lax.psum((grad_egains, grad_dgains, loss_local), ("grp", "dp"))
        shards = tuple(
            lax.psum(reduce_rows(pieces, 0), "grp").astype(jnp.float32)
            for pieces in ((grad_ecols,), (grad_erows,), (grad_dcols,), drows)
        )
        shard_squares = lax.psum(sum((jnp.sum(piece * piece) for piece in shards)), "dp")
    loss = loss_sum / masked
    grad_norm = jnp.sqrt(shard_squares + jnp.sum(enc_sum * enc_sum) + jnp.sum(dec_sum * dec_sum))
    factor = clip_level / jnp.maximum(grad_norm, clip_level)
    count_steps = step_count[0].astype(jnp.float32)
    fix_one = 1.0 - beta_first**count_steps
    fix_two = 1.0 - beta_second**count_steps
    clipped_ecols, squares_ecols, updated_ecols = adam_step(
        enc_cols,
        moment_ecols,
        square_ecols,
        shards[0],
        factor,
        fix_one,
        fix_two,
        weight_decay,
        learn_rate,
    )
    clipped_erows, squares_erows, updated_erows = adam_step(
        enc_rows,
        moment_erows,
        square_erows,
        shards[1],
        factor,
        fix_one,
        fix_two,
        weight_decay,
        learn_rate,
    )
    clipped_dcols, squares_dcols, updated_dcols = adam_step(
        dec_cols,
        moment_dcols,
        square_dcols,
        shards[2],
        factor,
        fix_one,
        fix_two,
        weight_decay,
        learn_rate,
    )
    clipped_drows, squares_drows, updated_drows = adam_step(
        dec_rows,
        moment_drows,
        square_drows,
        shards[3],
        factor,
        fix_one,
        fix_two,
        weight_decay,
        learn_rate,
    )
    clipped_egains, squares_egains, updated_egains = adam_step(
        enc_gains, moment_egains, square_egains, enc_sum, factor, fix_one, fix_two, 0.0, gain_rate
    )
    clipped_dgains, squares_dgains, updated_dgains = adam_step(
        dec_gains, moment_dgains, square_dgains, dec_sum, factor, fix_one, fix_two, 0.0, gain_rate
    )
    return (
        clipped_ecols,
        squares_ecols,
        updated_ecols,
        clipped_erows,
        squares_erows,
        updated_erows,
        clipped_dcols,
        squares_dcols,
        updated_dcols,
        clipped_drows,
        squares_drows,
        updated_drows,
        clipped_egains,
        squares_egains,
        updated_egains,
        clipped_dgains,
        squares_dgains,
        updated_dgains,
        loss,
        grad_norm,
    )


def solution(mesh):
    return jax.shard_map(
        body,
        mesh=mesh,
        in_specs=(
            P("grp", "dp", None, None),
            P("grp", "dp", None),
            P("grp", "dp", None),
            P("grp", "dp", None),
            P("grp", None, None),
            P("grp"),
            P(),
            P("dp", None),
            P("dp", None),
            P("dp", None),
            P("dp", None),
            P(),
            P(),
            P("dp", None),
            P("dp", None),
            P("dp", None),
            P("dp", None),
            P(),
            P(),
            P("dp", None),
            P("dp", None),
            P("dp", None),
            P("dp", None),
            P(),
            P(),
        ),
        out_specs=(
            P("dp", None),
            P("dp", None),
            P("dp", None),
            P("dp", None),
            P("dp", None),
            P("dp", None),
            P("dp", None),
            P("dp", None),
            P("dp", None),
            P("dp", None),
            P("dp", None),
            P("dp", None),
            P(),
            P(),
            P(),
            P(),
            P(),
            P(),
            P(),
            P(),
        ),
        check_vma=False,
    )
```

```python
import functools

import jax
import jax.numpy as jnp
from jax import lax
from jax.experimental import pallas as pl
from jax.experimental.pallas import tpu as pltpu
from jax.sharding import PartitionSpec as P

D = 1024
HEADS = 16
FF = 4096
DHEADS = 16
DFF = 2048
PIX = 1024
NBG = 4
L = 256
K = 64


norm_eps = 1e-06
clip_level = 0.005
learn_rate = 0.02
gain_rate = 0.25
weight_decay = 0.05
adam_eps = 1e-08
beta_first = 0.5
beta_second = 0.5


def to_low(value):
    return value.astype(jnp.bfloat16)


def project(inputs, matrix):
    return jnp.einsum("...n,nm->...m", inputs, matrix, preferred_element_type=jnp.float32)


def dot_nn(a, b):
    return lax.dot_general(a, b, (((1,), (0,)), ((), ())), preferred_element_type=jnp.float32)


def dot_nt(a, b):
    return lax.dot_general(a, b, (((1,), (1,)), ((), ())), preferred_element_type=jnp.float32)


def dot_tn(a, b):
    return lax.dot_general(a, b, (((0,), (0,)), ((), ())), preferred_element_type=jnp.float32)


def unit_rows(values):
    centred = values - jnp.mean(values, -1, keepdims=True)
    scaled = lax.rsqrt(jnp.mean(centred * centred, -1, keepdims=True) + norm_eps)
    return centred * scaled, scaled


def unit_back(grads, hat, scaled, gain):
    inner = grads * gain
    return scaled * (
        inner
        - jnp.mean(inner, -1, keepdims=True)
        - hat * jnp.mean(inner * hat, -1, keepdims=True)
    )

LANES = 128


def stack_rows(value, ee):
    head = lax.broadcasted_iota(jnp.int32, value.shape, 1) // ee
    return jnp.concatenate(
        [jnp.where(head == h, value, jnp.zeros_like(value)) for h in range(LANES // ee)], 0
    )


def stack_lanes(value, ee):
    head = lax.broadcasted_iota(jnp.int32, value.shape, 0) // ee
    return jnp.concatenate(
        [jnp.where(head == h, value, jnp.zeros_like(value)) for h in range(LANES // ee)], 1
    )


def attend(n, groups, tokens, width, ee, expo, same, qkv_s, s_s, p_s, inv_s, oo_s, o_s):
    item = n // groups
    g = n % groups
    rs = pl.ds(pl.multiple_of(item * tokens, tokens), tokens)
    qa = pl.ds(pl.multiple_of(g * LANES, LANES), LANES)
    q = qkv_s[rs, qa]
    k = qkv_s[rs, pl.ds(pl.multiple_of(width + g * LANES, LANES), LANES)]
    v = qkv_s[rs, pl.ds(pl.multiple_of(2 * width + g * LANES, LANES), LANES)]
    s_s[...] = dot_nt(stack_rows(q, ee), k)
    for h in range(LANES // ee):
        at = slice(h * tokens, (h + 1) * tokens)
        s = s_s[at, :]
        if same is not None:
            s = jnp.where(same, s, -1e30)
        top = jnp.max(s, -1, keepdims=True)
        p_s[n, :, at] = jnp.exp2((s - top) * expo).astype(p_s.dtype)
    ones = jnp.ones_like(v)
    both = jnp.concatenate([stack_rows(v, ee), stack_rows(ones, ee)], 1)
    out = dot_nn(p_s[n], both)
    inv = 1.0 / out[:, LANES:]
    out = out[:, :LANES] * inv
    inv_s[n] = inv
    oo_s[n] = out
    o_s[rs, qa] = out.astype(o_s.dtype)


def attend_back(n, slot, groups, tokens, width, ee, scale, qkv_s, s_s, ds_s, p_s, inv_s, oo_s, do_s, dqkv_s):
    low = dqkv_s.dtype
    item = n // groups
    g = n % groups
    rs = pl.ds(pl.multiple_of(item * tokens, tokens), tokens)
    qa = pl.ds(pl.multiple_of(g * LANES, LANES), LANES)
    ka = pl.ds(pl.multiple_of(width + g * LANES, LANES), LANES)
    va = pl.ds(pl.multiple_of(2 * width + g * LANES, LANES), LANES)
    heads = range(LANES // ee)
    do = do_s[rs, qa].astype(jnp.float32) * inv_s[slot]
    rest = (-do * oo_s[slot]).astype(low)
    do_t = do.T.astype(low)
    do = do.astype(low)
    v = qkv_s[rs, va]
    s_s[...] = dot_nt(
        jnp.concatenate([stack_rows(do, ee), stack_rows(rest, ee)], 1),
        jnp.concatenate([v, jnp.ones_like(v)], 1),
    )
    for h in heads:
        at = slice(h * tokens, (h + 1) * tokens)
        ds_s[:, at] = (p_s[slot, :, at].astype(jnp.float32) * s_s[at, :]).astype(low)
    e_rows = jnp.concatenate([p_s[slot, :, h * tokens : (h + 1) * tokens] for h in heads], 0)
    ds_rows = jnp.concatenate([ds_s[:, h * tokens : (h + 1) * tokens] for h in heads], 0)
    dv_t = dot_nn(stack_lanes(do_t, ee), e_rows)
    dk_t = dot_nn(stack_lanes(qkv_s[rs, qa].T, ee), ds_rows)
    dq = dot_nn(ds_s[...], stack_rows(qkv_s[rs, ka], ee))
    dqkv_s[rs, qa] = (dq * scale).astype(low)
    dqkv_s[rs, ka] = (dk_t.T * scale).astype(low)
    dqkv_s[rs, va] = dv_t.T.astype(low)


def one_hot(index, count):
    places = lax.broadcasted_iota(jnp.int32, (index.shape[0], count), 1)
    return jnp.where(places.astype(jnp.float32) == index.astype(jnp.float32), 1.0, 0.0)


def split_table(table_ref, high_s, low_s):
    high = table_ref[...].astype(high_s.dtype)
    high_s[...] = high
    low_s[...] = (table_ref[...] - high.astype(jnp.float32)).astype(low_s.dtype)


def look_up(hot, index_row, high_s, low_s):
    index = jnp.sum(hot * index_row, -1, keepdims=True)
    rows = one_hot(index, high_s.shape[0]).astype(high_s.dtype)
    return dot_nn(rows, high_s[...]) + dot_nn(rows, low_s[...])


def decoder_kernel(
    items, heads, scal_ref, z_ref, keep_ref, gsd_ref, table_ref, pix_ref, cols_ref, down_ref, head_ref, gains_ref,
    dz_ref, gcols_out, gdown_out, ghead_out, ggains_ref, loss_ref,
    x_s, h1_s, qkv_s, p_s, o_s, x1_s, h2_s, a_s, gp_s, x2_s, hd_s, dx_s, dy_s, acc_s, dqkv_s, inv_s, oo_s, s_s, ds_s,
    high_s, low_s, pixel_s, gcols, gdown, ghead,
):
    low = jnp.bfloat16
    step = pl.program_id(0)
    width = x_s.shape[1]
    tokens = pix_ref.shape[1]
    hide = tokens - K
    rows = items * tokens
    tile = 512
    ee = width // heads
    scale = ee ** (-0.5)
    expo = scale * 1.4426950408889634

    @pl.when(step == 0)
    def _():
        gcols[...] = jnp.zeros_like(gcols)
        gdown[...] = jnp.zeros_like(gdown)
        ghead[...] = jnp.zeros_like(ghead)
        ggains_ref[...] = jnp.zeros_like(ggains_ref)
        loss_ref[...] = jnp.zeros_like(loss_ref)
        split_table(table_ref, high_s, low_s)

    def gain(i):
        return gains_ref[i : i + 1, :]

    f32 = jnp.float32
    before = lax.broadcasted_iota(jnp.int32, (tokens, tokens), 0) <= lax.broadcasted_iota(
        jnp.int32, (tokens, tokens), 1
    )
    before = before.astype(f32).astype(low)
    for i in range(items):
        base = i * tokens
        keep_hot = one_hot(keep_ref[i], tokens)
        shown = jnp.max(keep_hot, 0, keepdims=True)
        rank = dot_nn(jnp.broadcast_to(1.0 - shown, (8, tokens)).astype(low), before)[:1]
        slot = lax.broadcasted_iota(jnp.int32, (hide, tokens), 0).astype(f32) + 1.0
        hide_hot = jnp.where(slot == rank, 1.0 - shown, 0.0)
        position = look_up(jnp.concatenate([keep_hot, hide_hot], 0), gsd_ref[i], high_s, low_s)
        x_s[base : base + K, :] = position[:K] + z_ref[i]
        x_s[base + K : base + tokens, :] = position[K:] + gain(6)
        pixel_s[i] = dot_nn(hide_hot.astype(low), pix_ref[i]).astype(low)
    hat, _ = unit_rows(x_s[...])
    h1_s[...] = (hat * gain(0) + gain(1)).astype(low)

    @pl.loop(0, 3)
    def _(t):
        at = pl.ds(pl.multiple_of(t * width, width), width)
        qkv_s[:, at] = dot_nn(h1_s[...], cols_ref[:, at]).astype(low)

    groups = width // LANES

    @pl.loop(0, items * groups)
    def _(n):
        attend(n, groups, tokens, width, ee, expo, None, qkv_s, s_s, p_s, inv_s, oo_s, o_s)

    x1_s[...] = x_s[...] + dot_nn(o_s[...], cols_ref[:, 3 * width : 4 * width])
    hat, _ = unit_rows(x1_s[...])
    h2_s[...] = (hat * gain(2) + gain(3)).astype(low)
    x2_s[...] = x1_s[...]

    @pl.loop(0, down_ref.shape[0] // tile)
    def _(t):
        at = pl.ds(pl.multiple_of(t * tile, tile), tile)
        up = pl.ds(pl.multiple_of(4 * width + t * tile, tile), tile)
        u = dot_nn(h2_s[...], cols_ref[:, up])
        cumul = 0.5 * (1.0 + lax.erf(u * 0.7071067811865476))
        act = (u * cumul).astype(low)
        a_s[:, at] = act
        gp_s[:, at] = (cumul + u * jnp.exp(-0.5 * u * u) * 0.3989422804014327).astype(gp_s.dtype)
        x2_s[...] += dot_nn(act, down_ref[at, :])

    hat, _ = unit_rows(x2_s[...])
    hd_s[...] = (hat * gain(4) + gain(5)).astype(low)

    pixel_count = head_ref.shape[0]
    for i in range(items):
        base = i * tokens
        weight = scal_ref[0, step * items + i]
        coef = scal_ref[1, step * items + i]
        target, _ = unit_rows(pixel_s[i].astype(f32))
        hd = hd_s[base + K : base + tokens, :]
        back = jnp.zeros((hide, width), jnp.float32)
        for t in range(pixel_count // tile):
            at = slice(t * tile, (t + 1) * tile)
            err = dot_nt(hd, head_ref[at, :]) - target[:, at]
            loss_ref[...] += weight * jnp.sum(err * err, keepdims=True).reshape(1, 1)
            dpred = (err * coef).astype(low)
            ghead[at, :] += dot_tn(dpred, hd)
            back = back + dot_nn(dpred, head_ref[at, :])
        hat, scaled = unit_rows(x2_s[base + K : base + tokens, :])
        ggains_ref[4:5, :] += jnp.sum(back * hat, 0, keepdims=True)
        ggains_ref[5:6, :] += jnp.sum(back, 0, keepdims=True)
        dx = unit_back(back, hat, scaled, gain(4))
        dx_s[base : base + K, :] = jnp.zeros((K, width), jnp.float32)
        dx_s[base + K : base + tokens, :] = dx
        dy_s[base : base + K, :] = jnp.zeros((K, width), low)
        dy_s[base + K : base + tokens, :] = dx.astype(low)

    acc_s[...] = jnp.zeros_like(acc_s)

    @pl.loop(0, down_ref.shape[0] // tile)
    def _(t):
        at = pl.ds(pl.multiple_of(t * tile, tile), tile)
        up = pl.ds(pl.multiple_of(4 * width + t * tile, tile), tile)
        gdown[at, :] += dot_tn(a_s[:, at], dy_s[...])
        du = (dot_nt(dy_s[...], down_ref[at, :]) * gp_s[:, at].astype(jnp.float32)).astype(low)
        gcols[:, up] += dot_tn(h2_s[...], du)
        acc_s[...] += dot_nt(du, cols_ref[:, up])

    hat, scaled = unit_rows(x1_s[...])
    grads = acc_s[...]
    ggains_ref[2:3, :] += jnp.sum(grads * hat, 0, keepdims=True)
    ggains_ref[3:4, :] += jnp.sum(grads, 0, keepdims=True)
    dx_s[...] += unit_back(grads, hat, scaled, gain(2))
    dy_s[...] = dx_s[...].astype(low)
    gcols[:, 3 * width : 4 * width] += dot_tn(o_s[...], dy_s[...])
    o_s[...] = dot_nt(dy_s[...], cols_ref[:, 3 * width : 4 * width]).astype(low)

    @pl.loop(0, items * groups)
    def _(n):
        attend_back(n, n, groups, tokens, width, ee, scale, qkv_s, s_s, ds_s, p_s, inv_s, oo_s, o_s, dqkv_s)

    acc_s[...] = jnp.zeros_like(acc_s)

    @pl.loop(0, 3)
    def _(t):
        at = pl.ds(pl.multiple_of(t * width, width), width)
        gcols[:, at] += dot_tn(h1_s[...], dqkv_s[:, at])
        acc_s[...] += dot_nt(dqkv_s[:, at], cols_ref[:, at])

    hat, scaled = unit_rows(x_s[...])
    grads = acc_s[...]
    ggains_ref[0:1, :] += jnp.sum(grads * hat, 0, keepdims=True)
    ggains_ref[1:2, :] += jnp.sum(grads, 0, keepdims=True)
    dx_s[...] += unit_back(grads, hat, scaled, gain(0))
    for i in range(items):
        base = i * tokens
        dz_ref[i] = dx_s[base : base + K, :].astype(low)
        ggains_ref[6:7, :] += jnp.sum(dx_s[base + K : base + tokens, :], 0, keepdims=True)

    @pl.when(step == pl.num_programs(0) - 1)
    def _():
        gcols_out[...] = gcols[...].astype(low)
        gdown_out[...] = gdown[...].astype(low)
        ghead_out[...] = ghead[...].astype(low)


def decoder_call(scal, latent, keep, gsd, table, pixels, cols, rows, gains, heads):
    batch, tokens, pixel_count = pixels.shape
    width = cols.shape[0]
    down = jax.ShapeDtypeStruct((cols.shape[1] - 4 * width, width), rows.dtype)
    head = jax.ShapeDtypeStruct((pixel_count, width), rows.dtype)
    last = rows.shape[0] // pixel_count - 1
    items = 2
    run = items * tokens
    hide = tokens - K
    low = jnp.bfloat16
    full = pl.Buffered(1)

    def whole(array):
        return pl.BlockSpec(array.shape, lambda s: (0,) * len(array.shape), pipeline_mode=full)

    def by_item(shape):
        return pl.BlockSpec((items,) + shape, lambda s: (s, 0, 0))

    outs = (
        jax.ShapeDtypeStruct((batch, K, width), low),
        jax.ShapeDtypeStruct(cols.shape, low),
        jax.ShapeDtypeStruct(down.shape, low),
        jax.ShapeDtypeStruct(head.shape, low),
        jax.ShapeDtypeStruct((8, width), jnp.float32),
        jax.ShapeDtypeStruct((1, 1), jnp.float32),
    )
    vmem = pltpu.VMEM
    f32 = jnp.float32
    return pl.pallas_call(
        functools.partial(decoder_kernel, items, heads),
        grid=(batch // items,),
        in_specs=[
            pl.BlockSpec(memory_space=pltpu.SMEM),
            by_item((K, width)),
            by_item((K, 1)),
            by_item((1, tokens)),
            pl.BlockSpec((table.shape[0], width), lambda s: (0, table.shape[1] // width - 1), pipeline_mode=full),
            by_item((tokens, pixel_count)),
            whole(cols),
            whole(down),
            pl.BlockSpec(head.shape, lambda s: (last, 0), pipeline_mode=full),
            whole(gains),
        ],
        out_specs=(by_item((K, width)),) + tuple(whole(out) for out in outs[1:]),
        out_shape=outs,
        scratch_shapes=[
            vmem((run, width), f32),
            vmem((run, width), low),
            vmem((run, 3 * width), low),
            vmem((items * width // 128, tokens, 4 * tokens), low),
            vmem((run, width), low),
            vmem((run, width), f32),
            vmem((run, width), low),
            vmem((run, down.shape[0]), low),
            vmem((run, down.shape[0]), low),
            vmem((run, width), f32),
            vmem((run, width), low),
            vmem((run, width), f32),
            vmem((run, width), low),
            vmem((run, width), f32),
            vmem((run, 3 * width), low),
            vmem((items * width // 128, tokens, 128), f32),
            vmem((items * width // 128, tokens, 128), f32),
            vmem((4 * tokens, tokens), f32),
            vmem((tokens, 4 * tokens), low),
            vmem((table.shape[0], width), low),
            vmem((table.shape[0], width), low),
            vmem((items, hide, pixel_count), low),
            vmem(cols.shape, f32),
            vmem(down.shape, f32),
            vmem(head.shape, f32),
        ],
        compiler_params=pltpu.CompilerParams(
            dimension_semantics=("arbitrary",), vmem_limit_bytes=62 * 1024 * 1024
        ),
        cost_estimate=pl.CostEstimate(
            flops=70_000_000_000, bytes_accessed=40_000_000, transcendentals=20_000_000
        ),
    )(scal, latent, keep, gsd, table, pixels, cols, rows, rows, gains)


MESH_ID = pl.DeviceIdType.MESH


def place():
    g = lax.axis_index("grp")
    d = lax.axis_index("dp")
    z, c = d // 2, d % 2
    xn = g + 1 - 2 * (g % 2)
    yn = (g + 2) % 4
    return g, z, c, xn, yn


def pieces(shape, parts):
    rows, columns = shape
    if rows // parts >= 32:
        n = rows // parts
        cut = [(slice(i * n, (i + 1) * n), slice(0, columns)) for i in range(parts)]
    else:
        n = columns // parts
        cut = [(slice(0, rows), slice(i * n, (i + 1) * n)) for i in range(parts)]
    return cut


def halves(cut):
    rows, columns = cut
    mid = (columns.start + columns.stop) // 2
    return (rows, slice(columns.start, mid)), (rows, slice(mid, columns.stop))


def greet(peers):
    barrier = pltpu.get_barrier_semaphore()
    for peer in peers:
        pl.semaphore_signal(barrier, inc=1, device_id=peer, device_id_type=MESH_ID)
    pl.semaphore_wait(barrier, len(peers))


GATHER_SEMS = 14


def gather_events(count, chunks, ahead, ins, outs, sems):
    zs, zr, xs, xr, ys, yr, fs, fr, gs, gr, cs, os, cr, ls = sems
    g, z, c, xn, yn = place()
    dg = (xn + 2) % 4
    here = 2 * z + c
    other = 1 - c
    sib = (g, 2 * z + 1 - c)
    right, up = (xn, here), (yn, here)
    zpeer = [(g, 2 * ((z + j) % 4) + c) for j in (1, 2, 3)]
    zfrom = [(z + 4 - j) % 4 for j in (1, 2, 3)]
    peers = [sib, right, up] + zpeer
    work = []
    for array in range(count):
        for cut in pieces(ins[array].shape[1:], chunks[array]):
            work.append((array, cut))
    steps = len(work)
    sent = []

    def send(src, dst, send_sem, recv_sem, peer):
        return pltpu.make_async_remote_copy(
            src_ref=src, dst_ref=dst, send_sem=send_sem, recv_sem=recv_sem,
            device_id=peer, device_id_type=MESH_ID,
        )

    def go(make):
        make().start()
        sent.append(make)

    def block(array, z_at, q, cut):
        return outs[array].at[z_at, c, q, cut[0], cut[1]]

    def zcopy(k, j):
        array, cut = work[k]
        return send(
            ins[array].at[g, cut[0], cut[1]], block(array, z, g, cut), zs.at[k, j], zr.at[k, j], zpeer[j]
        )

    def relay(k, j, q, cut, ssem, rsem, peer):
        at = block(work[k][0], zfrom[j], q, cut)
        return send(at, at, ssem, rsem, peer)

    def to_x(k, j):
        return relay(k, j, g, work[k][1], xs.at[k, j], xr.at[k, j], right)

    def to_y(k, j):
        return relay(k, j, g, work[k][1], ys.at[k, j], yr.at[k, j], up)

    def to_core(k, j, i, q):
        return relay(k, j, q, work[k][1], cs.at[k, j, i], cr.at[work[k][0]], sib)

    def on_y(k, j, q):
        return relay(k, j, q, halves(work[k][1])[0], fs.at[k, j], fr.at[k, j], up)

    def on_x(k, j, q):
        return relay(k, j, q, halves(work[k][1])[1], gs.at[k, j], gr.at[k, j], right)

    def own(array):
        return pltpu.make_async_copy(ins[array], outs[array].at[z, c], ls.at[array])

    def own_to_core(array):
        return send(ins[array], outs[array].at[z, c], os.at[array], cr.at[array], sib)

    def begin():
        for array in range(count):
            own(array).start()
        for k in range(min(ahead, steps)):
            for j in range(3):
                go(functools.partial(zcopy, k, j))
        for array in range(count):
            go(functools.partial(own_to_core, array))

    def event(t):
        if t < steps:
            for j in range(3):
                zcopy(t, j).wait_recv()
                go(functools.partial(to_x, t, j))
                go(functools.partial(to_y, t, j))
                go(functools.partial(to_core, t, j, 0, g))
            if t + ahead < steps:
                for j in range(3):
                    go(functools.partial(zcopy, t + ahead, j))
        if 1 <= t <= steps:
            k = t - 1
            for j in range(3):
                relay(k, j, xn, work[k][1], xs.at[k, j], xr.at[k, j], right).wait_recv()
                go(functools.partial(on_y, k, j, xn))
                go(functools.partial(to_core, k, j, 1, xn))
                relay(k, j, yn, work[k][1], ys.at[k, j], yr.at[k, j], up).wait_recv()
                go(functools.partial(on_x, k, j, yn))
                go(functools.partial(to_core, k, j, 2, yn))
        if 2 <= t:
            k = t - 2
            for j in range(3):
                on_y(k, j, dg).wait_recv()
                on_x(k, j, dg).wait_recv()
                go(functools.partial(to_core, k, j, 3, dg))

    def finish():
        for make in sent:
            make().wait_send()
        for array in range(count):
            whole = outs[array].at[:, other]
            send(whole, whole, os.at[array], cr.at[array], sib).wait_recv()
            own(array).wait()

    return peers, begin, [functools.partial(event, t) for t in range(steps + 2)], finish


def gather_scratch(count, steps):
    dma = pltpu.SemaphoreType.DMA
    return [dma((steps, 3))] * 10 + [dma((steps, 3, 4)), dma((count,)), dma((count,)), dma((count,))]


def gather_kernel(count, chunks, ahead, *refs):
    ins, items_ref = refs[:count], refs[count]
    outs, items_out = refs[count + 1 : 2 * count + 1], refs[2 * count + 1]
    sems = refs[2 * count + 2 :]
    it, its, itr = sems[GATHER_SEMS:]
    peers, begin, events, finish = gather_events(count, chunks, ahead, ins, outs, sems[:GATHER_SEMS])
    greet(peers)
    _, right, up = peers[:3]

    def items_copy(i, peer):
        return pltpu.make_async_remote_copy(
            src_ref=it.at[2 * i], dst_ref=it.at[2 * i + 1], send_sem=its.at[i], recv_sem=itr.at[i],
            device_id=peer, device_id_type=MESH_ID,
        )

    it[0] = items_ref[...]
    items_copy(0, right).start()
    begin()
    for t, event in enumerate(events):
        event()
        if t == 0:
            items_copy(0, right).wait_recv()
            it[2] = it[0] + it[1]
            items_copy(1, up).start()
        if t == 1:
            items_copy(1, up).wait_recv()
            items_out[...] = it[2] + it[3]
    finish()
    items_copy(0, right).wait_send()
    items_copy(1, up).wait_send()


def gather_call(shards, items, chunks, ahead=2, collective_id=0):
    count = len(shards)
    steps = sum(chunks)
    views = [s.reshape(4, s.shape[0] // 4, s.shape[1]) for s in shards]
    dma = pltpu.SemaphoreType.DMA
    hbm = pl.BlockSpec(memory_space=pl.ANY)
    vm = pl.BlockSpec(memory_space=pltpu.VMEM)
    *outs, total = pl.pallas_call(
        functools.partial(gather_kernel, count, chunks, ahead),
        out_shape=tuple(jax.ShapeDtypeStruct((4, 2) + v.shape, v.dtype) for v in views)
        + (jax.ShapeDtypeStruct((8, 128), jnp.float32),),
        in_specs=[hbm] * count + [vm],
        out_specs=tuple([hbm] * count + [vm]),
        scratch_shapes=gather_scratch(count, steps)
        + [pltpu.VMEM((4, 8, 128), jnp.float32), dma((2,)), dma((2,))],
        compiler_params=pltpu.CompilerParams(collective_id=collective_id, has_side_effects=True),
    )(*views, jnp.broadcast_to(items, (8, 128)))
    return [o.reshape(-1, o.shape[-1]) for o in outs], total[0, 0]


RUN = 256


def same_item():
    row = lax.broadcasted_iota(jnp.int32, (RUN, RUN), 0) // K
    column = lax.broadcasted_iota(jnp.int32, (RUN, RUN), 1) // K
    return row == column


def encoder_kernel(heads, chunks, *refs):
    count = 2 if chunks else 0
    (pixels_ref, keep_ref, bands_ref, gsd_ref, table_ref, rows_ref, cols_ref, de_ref, gains_ref) = refs[:9]
    shards = refs[9 : 9 + count]
    outs = refs[9 + count :]
    z_ref, band_ref, a_ref, gp_ref, x2_ref = outs[:5]
    stored = outs[5:13]
    gathered = outs[13 : 13 + count]
    rest = outs[13 + count :]
    pix_ref, x_ref, qkv_ref, p_ref, inv_ref, oo_ref, x1_ref, o_s = rest[:8]
    h_s, s_s, high_s, low_s, de_s, store_sem, de_sem = rest[8:15]
    low = jnp.bfloat16
    step = pl.program_id(0)
    width = x_ref.shape[1]
    ee = width // heads
    groups = width // LANES
    expo = ee ** (-0.5) * 1.4426950408889634
    if chunks:
        peers, begin, events, finish = gather_events(
            count, chunks, 2, shards, gathered, rest[15 : 15 + GATHER_SEMS]
        )

    def gain(i):
        return gains_ref[i : i + 1, :]

    def store(i):
        return pltpu.make_async_copy(rest[i], stored[i], store_sem.at[i])

    def load_de():
        return pltpu.make_async_copy(gathered[1].at[2] if chunks else de_ref, de_s, de_sem)

    if chunks:

        @pl.when(step == 0)
        def _():
            greet(peers)
            begin()

        for at, event in zip((3, 6, 7, 8, 9, 10), events):
            pl.when(step == at)(event)

    @pl.when(step == 11)
    def _():
        if chunks:
            finish()
        load_de().start()

    @pl.when(step == 0)
    def _():
        split_table(table_ref, high_s, low_s)

        @pl.loop(0, pixels_ref.shape[0])
        def _(i):
            at = pl.ds(pl.multiple_of(i * K, K), K)
            hot = one_hot(keep_ref[i], pixels_ref.shape[1])
            pix_ref[at, :] = dot_nn(hot.astype(low), pixels_ref[i]).astype(low)
            band_ref[at, :] = jnp.sum(hot * bands_ref[i], -1, keepdims=True).astype(jnp.int32)
            x_ref[at, :] = look_up(hot, gsd_ref[i], high_s, low_s)

        store(0).start()

    @pl.when(step < 4)
    def _():
        pixel = pix_ref[...]
        x_ref[...] += dot_nn(jnp.where(band_ref[...] == step, pixel, jnp.zeros_like(pixel)), rows_ref[...])

    @pl.when(step == 4)
    def _():
        store(1).start()
        hat, _ = unit_rows(x_ref[...])
        h_s[...] = (hat * gain(0) + gain(1)).astype(low)

    @pl.when((step >= 4) & (step < 7))
    def _():
        at = pl.ds(pl.multiple_of((step - 4) * width, width), width)
        qkv_ref[:, at] = dot_nn(h_s[...], cols_ref[...]).astype(low)

    @pl.when(step == 7)
    def _():
        store(2).start()
        same = same_item()

        @pl.loop(0, x_ref.shape[0] // RUN * groups)
        def _(n):
            attend(n, groups, RUN, width, ee, expo, same, qkv_ref, s_s, p_ref, inv_ref, oo_ref, o_s)

        for i in (3, 4, 5, 7):
            store(i).start()
        x1_ref[...] = x_ref[...] + dot_nn(o_s[...], cols_ref[...])
        store(6).start()
        hat, _ = unit_rows(x1_ref[...])
        h_s[...] = (hat * gain(2) + gain(3)).astype(low)
        x2_ref[...] = x1_ref[...]

    @pl.when(step >= 8)
    def _():
        @pl.loop(0, 2)
        def _(t):
            half = width // 2
            at = pl.ds(pl.multiple_of(t * half, half), half)
            u = dot_nn(h_s[...], cols_ref[:, at])
            cumul = 0.5 * (1.0 + lax.erf(u * 0.7071067811865476))
            a_ref[:, at] = (u * cumul).astype(low)
            gp_ref[:, at] = (cumul + u * jnp.exp(-0.5 * u * u) * 0.3989422804014327).astype(low)

        x2_ref[...] += dot_nn(a_ref[...], rows_ref[...])

    @pl.when(step == 11)
    def _():
        hat, _ = unit_rows(x2_ref[...])
        h_s[...] = (hat * gain(4) + gain(5)).astype(low)
        load_de().wait()
        z_ref[...] = dot_nn(h_s[...], de_s[...].reshape(width, z_ref.shape[1]))
        for i in range(8):
            store(i).wait()


def encoder_call(pixels, keep, bands, gsd, table, rows, cols, de, gains, heads, shards=()):
    width = cols.shape[0]
    tokens = keep.shape[0] * K
    low, f32 = jnp.bfloat16, jnp.float32
    runs = tokens // RUN * (width // LANES)
    wide = LANES // (width // heads) * RUN
    one = pl.Buffered(1)
    hbm = pl.BlockSpec(memory_space=pl.ANY)
    vmem = pltpu.VMEM
    chunks = (2, 2) if shards else ()
    views = [s.reshape(4, s.shape[0] // 4, s.shape[1]) for s in shards]
    if shards:
        narrow = shards[1].shape[1]
        de, de_shape = jnp.zeros((8, 128), low), (2, 4, 128, narrow)
    else:
        narrow, de_shape = de.shape[1], de.shape

    def whole(shape):
        return pl.BlockSpec(shape, lambda s: (0,) * len(shape), pipeline_mode=one)

    def row_block(s):
        return (jnp.where(s < 4, s + 4, jnp.where(s < 8, 0, s - 8)), 0)

    def column_block(s):
        return (0, jnp.where(s < 4, 0, s - 4))

    def hidden_block(s):
        return (0, jnp.where(s < 8, 0, s - 8))

    hidden = pl.BlockSpec((tokens, width), hidden_block)
    blocks = [
        ((tokens, narrow), f32, whole((tokens, narrow))),
        ((tokens, 1), jnp.int32, whole((tokens, 1))),
        ((tokens, 4 * width), low, hidden),
        ((tokens, 4 * width), low, hidden),
        ((tokens, width), f32, whole((tokens, width))),
    ]
    held = [
        ((tokens, pixels.shape[2]), low),
        ((tokens, width), f32),
        ((tokens, 3 * width), low),
        ((runs, RUN, wide), low),
        ((runs, RUN, LANES), f32),
        ((runs, RUN, LANES), f32),
        ((tokens, width), f32),
        ((tokens, width), low),
    ]
    struct = jax.ShapeDtypeStruct
    out = pl.pallas_call(
        functools.partial(encoder_kernel, heads, chunks),
        grid=(12,),
        in_specs=[
            whole(pixels.shape),
            whole(keep.shape),
            whole(bands.shape),
            whole(gsd.shape),
            pl.BlockSpec((table.shape[0], width), lambda s: (0, 0), pipeline_mode=one),
            pl.BlockSpec((width, width), row_block),
            pl.BlockSpec((width, width), column_block),
            hbm,
            whole(gains.shape),
        ]
        + [hbm] * len(views),
        out_specs=tuple(b[2] for b in blocks) + (hbm,) * (len(held) + len(views)),
        out_shape=tuple(struct(b[0], b[1]) for b in blocks)
        + tuple(struct(*h) for h in held)
        + tuple(struct((4, 2) + v.shape, low) for v in views),
        scratch_shapes=[vmem(*h) for h in held]
        + [
            vmem((tokens, width), low),
            vmem((wide, RUN), f32),
            vmem((table.shape[0], width), low),
            vmem((table.shape[0], width), low),
            vmem(de_shape, low),
            pltpu.SemaphoreType.DMA((8,)),
            pltpu.SemaphoreType.DMA,
        ]
        + (gather_scratch(2, sum(chunks)) if shards else []),
        compiler_params=pltpu.CompilerParams(
            dimension_semantics=("arbitrary",),
            vmem_limit_bytes=60 * 1024 * 1024,
            collective_id=2 if shards else None,
            has_side_effects=bool(shards),
        ),
        cost_estimate=pl.CostEstimate(
            flops=20_000_000_000, bytes_accessed=70_000_000, transcendentals=8_000_000
        ),
    )(pixels, keep, bands, gsd, table, rows, cols, de, gains, *views)
    z, band, a, gp, x2 = out[:5]
    pix, x, qkv, p, inv, oo, x1, o = out[5:13]
    saved = (x, qkv, p, inv, oo, x1, a, gp, x2, o)
    return z, pix, band, saved, [w.reshape(-1, w.shape[-1]) for w in out[13:]]


def encoder_back_kernel(
    heads, dz_ref, pix_ref, band_ref, x_ref, qkv_ref, p_ref, inv_ref, oo_ref, x1_ref, a_ref, gp_ref, x2_ref,
    rows_ref, cols_ref, de_ref, gains_ref,
    grows_ref, gcols_ref, gde_ref, ggains_ref,
    h_s, dx_s, dy_s, acc_s, do_s, dqkv_s, s_s, ds_s,
):
    low, f32 = jnp.bfloat16, jnp.float32
    step = pl.program_id(0)
    width = x_ref.shape[1]
    ee = width // heads
    groups = width // LANES
    runs = x_ref.shape[0] // RUN

    def gain(i):
        return gains_ref[i : i + 1, :]

    def back(x, grads, at):
        hat, scaled = unit_rows(x)
        ggains_ref[at : at + 1, :] = jnp.sum(grads * hat, 0, keepdims=True)
        ggains_ref[at + 1 : at + 2, :] = jnp.sum(grads, 0, keepdims=True)
        return unit_back(grads, hat, scaled, gain(at))

    def normed(x, at):
        hat, _ = unit_rows(x)
        h_s[...] = (hat * gain(at) + gain(at + 1)).astype(low)

    @pl.when(step == 0)
    def _():
        ggains_ref[...] = jnp.zeros_like(ggains_ref)
        normed(x2_ref[...], 4)
        gde_ref[...] = dot_tn(h_s[...], dz_ref[...]).astype(low)
        dx_s[...] = back(x2_ref[...], dot_nt(dz_ref[...], de_ref[...]), 4)
        dy_s[...] = dx_s[...].astype(low)
        normed(x1_ref[...], 2)
        acc_s[...] = jnp.zeros_like(acc_s)

    @pl.when(step < 4)
    def _():
        grows_ref[...] = dot_tn(a_ref[...], dy_s[...]).astype(low)
        du = (dot_nt(dy_s[...], rows_ref[...]) * gp_ref[...].astype(f32)).astype(low)
        do_s[...] = du
        gcols_ref[...] = dot_tn(h_s[...], du).astype(low)
        acc_s[...] += dot_nt(do_s[...], cols_ref[...])

    @pl.when(step == 4)
    def _():
        dx_s[...] += back(x1_ref[...], acc_s[...], 2)
        dy_s[...] = dx_s[...].astype(low)
        for run in range(runs):
            for g in range(groups):
                h_s[run * RUN : (run + 1) * RUN, g * LANES : (g + 1) * LANES] = oo_ref[
                    run * groups + g
                ].astype(low)
        gcols_ref[...] = dot_tn(h_s[...], dy_s[...]).astype(low)
        do_s[...] = dot_nt(dy_s[...], cols_ref[...]).astype(low)

        @pl.loop(0, runs * groups)
        def _(n):
            attend_back(
                n, n, groups, RUN, width, ee, ee ** (-0.5), qkv_ref, s_s, ds_s, p_ref, inv_ref, oo_ref, do_s,
                dqkv_s,
            )

        normed(x_ref[...], 0)
        acc_s[...] = jnp.zeros_like(acc_s)

    @pl.when((step >= 5) & (step < 8))
    def _():
        at = pl.ds(pl.multiple_of((step - 5) * width, width), width)
        gcols_ref[...] = dot_tn(h_s[...], dqkv_s[:, at]).astype(low)
        acc_s[...] += dot_nt(dqkv_s[:, at], cols_ref[...])

    @pl.when(step == 8)
    def _():
        dx_s[...] += back(x_ref[...], acc_s[...], 0)
        dy_s[...] = dx_s[...].astype(low)

    @pl.when(step >= 8)
    def _():
        pixel = pix_ref[...]
        h_s[...] = jnp.where(band_ref[...] == step - 8, pixel, jnp.zeros_like(pixel))
        grows_ref[...] = dot_tn(h_s[...], dy_s[...]).astype(low)


def encoder_back_call(dz, pixel, band, saved, rows, cols, de, gains, heads):
    x, qkv, p, inv, oo, x1, a, gp, x2, _ = saved
    tokens, width = x.shape
    low, f32 = jnp.bfloat16, jnp.float32
    wide = p.shape[2]
    one = pl.Buffered(1)

    def whole(array):
        return pl.BlockSpec(array.shape, lambda s: (0,) * len(array.shape), pipeline_mode=one)

    def row_block(s):
        return (jnp.minimum(s, 3), 0)

    def column_block(s):
        return (0, jnp.where(s < 4, s + 4, jnp.where(s == 4, 3, jnp.minimum(s - 5, 2))))

    def hidden_block(s):
        return (0, jnp.minimum(s, 3))

    def grow_block(s):
        return (jnp.where(s < 4, s, jnp.where(s < 8, 3, s - 4)), 0)

    hidden = pl.BlockSpec((tokens, width), hidden_block)
    square = (width, width)
    outs = (
        jax.ShapeDtypeStruct(rows.shape, low),
        jax.ShapeDtypeStruct(cols.shape, low),
        jax.ShapeDtypeStruct(de.shape, low),
        jax.ShapeDtypeStruct((8, width), f32),
    )
    vmem = pltpu.VMEM
    return pl.pallas_call(
        functools.partial(encoder_back_kernel, heads),
        grid=(12,),
        in_specs=[
            whole(dz), whole(pixel), whole(band), whole(x), whole(qkv), whole(p), whole(inv), whole(oo),
            whole(x1), hidden, hidden, whole(x2),
            pl.BlockSpec(square, row_block), pl.BlockSpec(square, column_block),
            whole(de), whole(gains),
        ],
        out_specs=(
            pl.BlockSpec(square, grow_block),
            pl.BlockSpec(square, column_block),
            whole(outs[2]),
            whole(outs[3]),
        ),
        out_shape=outs,
        scratch_shapes=[
            vmem((tokens, width), low),
            vmem((tokens, width), f32),
            vmem((tokens, width), low),
            vmem((tokens, width), f32),
            vmem((tokens, width), low),
            vmem((tokens, 3 * width), low),
            vmem((wide, RUN), f32),
            vmem((RUN, wide), low),
        ],
        compiler_params=pltpu.CompilerParams(
            dimension_semantics=("arbitrary",), vmem_limit_bytes=60 * 1024 * 1024
        ),
        cost_estimate=pl.CostEstimate(
            flops=40_000_000_000, bytes_accessed=110_000_000, transcendentals=1_000_000
        ),
    )(dz, pixel, band, x, qkv, p, inv, oo, x1, a, gp, x2, rows, cols, de, gains)


def back_reduce_kernel(heads, kinds, work, pieces, refs_in, refs_out, *refs):
    low, f32 = jnp.bfloat16, jnp.float32
    ref = dict(zip(refs_in + refs_out, refs))
    rest = refs[len(refs_in) + len(refs_out) :]
    per = 9
    bufs = [rest[per * i : per * i + per] for i in range(len(kinds))]
    (sm, ss, ssx, dx, acc, xin, h, dy, wide, wt, wu, out_r, out_c, out_e, p_t, inv_t, oo_t, s_s, ds_s, gsum,
     cs, cr, ls, os, x1s, x1r, x2s, x2r, z_s, z_r, ags, agr, ks, sms, smr, sss, ssr, dma, att_sem) = rest[
        per * len(kinds) :
    ]
    g, z, c, xn, yn = place()
    dg = (xn + 2) % 4
    here = 2 * z + c
    sib = (g, 2 * z + 1 - c)
    right, up = (xn, here), (yn, here)
    zto = [(z + j) % 4 for j in (1, 2, 3)]
    zpeer = [(g, 2 * t + c) for t in zto]
    greet([sib, right, up] + zpeer)
    steps = len(work)
    sent = []
    from_slot = [[] for _ in range(steps)]

    def send(src, dst, send_sem, recv_sem, peer):
        return pltpu.make_async_remote_copy(
            src_ref=src, dst_ref=dst, send_sem=send_sem, recv_sem=recv_sem,
            device_id=peer, device_id_type=MESH_ID,
        )

    def guarded(test, action):
        if test is None:
            action()
        else:
            pl.when(test)(action)

    def go(copies, keep=None, tests=None):
        for i, copy in enumerate(copies):
            test = tests[i] if tests else None
            guarded(test, copy.start)
            (sent if keep is None else keep).append((test, copy))

    def left(entries):
        for test, copy in entries:
            guarded(test, copy.wait_send)

    def got(copies):
        for copy in copies:
            copy.wait_recv()

    def mine(k, at=None):
        base = work[k][2]
        at = z if at is None else at
        return None if base is None else ((at >= base) & (at < base + 2))

    def buffers(k):
        kind, at = work[k][:2]
        return bufs[kind], at, at % kinds[kind][4], kinds[kind][2] // 2

    def c_copies(k):
        (_, crecv, *_), at, _, _ = buffers(k)
        return [
            send(
                ref[array].at[:, 1 - c, :, cut[0], cut[1]], crecv.at[at, pl.ds(z0, nz)],
                cs.at[k, i], cr.at[k, i], sib,
            )
            for i, (array, z0, nz, cut) in enumerate(work[k][3])
        ]

    def own_copies(k):
        (s, *_), _, slot, _ = buffers(k)
        return [
            pltpu.make_async_copy(
                ref[array].at[:, c, :, cut[0], cut[1]], s.at[slot, pl.ds(z0, nz)], os.at[k, i]
            )
            for i, (array, z0, nz, cut) in enumerate(work[k][3])
        ]

    def recv_load(k, i):
        (_, crecv, tmp, *_), at, _, _ = buffers(k)
        return pltpu.make_async_copy(crecv.at[at, i], tmp.at[i % 2], ls.at[k, i])

    def x1_copies(k):
        (s, _, _, xa, yb, *_), at, slot, half = buffers(k)
        lo, hi = pl.ds(0, half), pl.ds(half, half)
        return [
            send(s.at[slot, :, xn, :, lo], xa.at[at, 0], x1s.at[k, 0], x1r.at[k, 0], right),
            send(s.at[slot, :, dg, :, lo], xa.at[at, 1], x1s.at[k, 1], x1r.at[k, 1], right),
            send(s.at[slot, :, yn, :, hi], yb.at[at, 0], x1s.at[k, 2], x1r.at[k, 2], up),
            send(s.at[slot, :, dg, :, hi], yb.at[at, 1], x1s.at[k, 3], x1r.at[k, 3], up),
        ]

    def x2_copies(k):
        (s, _, _, _, _, xb, ya, *_), at, slot, half = buffers(k)
        lo, hi = pl.ds(0, half), pl.ds(half, half)
        return [
            send(s.at[slot, :, yn, :, lo], ya.at[at], x2s.at[k, 0], x2r.at[k, 0], up),
            send(s.at[slot, :, xn, :, hi], xb.at[at], x2s.at[k, 1], x2r.at[k, 1], right),
        ]

    def z_copies(k):
        (s, *_, zb, _), at, slot, _ = buffers(k)
        base = work[k][2] or 0
        return [
            send(
                s.at[slot, (zto[j] - base) % kinds[work[k][0]][0], g], zb.at[at, j],
                z_s.at[k, j], z_r.at[k, j], zpeer[j],
            )
            for j in range(3)
        ]

    def out_at(k, q, part=None):
        name, cut = work[k][4:6]
        if part is not None:
            cut = halves(cut)[part]
        return ref[name].at[q, cut[0], cut[1]]

    def ag_copies(k):
        (*_, fin), at, _, _ = buffers(k)
        return [
            send(fin.at[at], out_at(k, g), ags.at[k, 0], agr.at[k, 0], right),
            send(fin.at[at], out_at(k, g), ags.at[k, 1], agr.at[k, 1], up),
        ]

    def keep_copy(k):
        (*_, fin), at, _, _ = buffers(k)
        return pltpu.make_async_copy(fin.at[at], out_at(k, g), ks.at[k])

    def fwd_copies(k, of_x, of_y):
        return [
            send(out_at(k, of_x, 0), out_at(k, of_x, 0), ags.at[k, 2], agr.at[k, 2], up),
            send(out_at(k, of_y, 1), out_at(k, of_y, 1), ags.at[k, 3], agr.at[k, 3], right),
        ]

    def add_half(k, q, first, other):
        (s, *_), _, slot, half = buffers(k)
        part = pl.ds(0 if first else half, half)

        @pl.loop(0, kinds[work[k][0]][0])
        def _(i):
            s[slot, i, q, :, part] = (s[slot, i, q, :, part].astype(f32) + other[i].astype(f32)).astype(low)

    def load(k):
        kind, at = work[k][:2]
        slots = kinds[kind][4]
        if at >= slots:
            before = [j for j in range(steps) if work[j][:2] == (kind, at - slots)][0]
            left(from_slot[before])
            from_slot[before].clear()
        for copy in own_copies(k):
            copy.start()

    def pair(k):
        (s, _, tmp, *_), _, slot, _ = buffers(k)
        count = kinds[work[k][0]][0]
        got(c_copies(k))
        for i in range(2):
            recv_load(k, i).start()
        for copy in own_copies(k):
            copy.wait()
        for i in range(count):
            recv_load(k, i).wait()

            @pl.loop(0, 4)
            def _(q):
                s[slot, i, q] = (s[slot, i, q].astype(f32) + tmp[i % 2, q].astype(f32)).astype(low)

            if i + 2 < count:
                recv_load(k, i + 2).start()
        go(x1_copies(k), from_slot[k])

    def first_half(k):
        (_, _, _, xa, yb, *_), at, _, _ = buffers(k)
        got(x1_copies(k))
        add_half(k, yn, True, xa.at[at, 1])
        add_half(k, xn, False, yb.at[at, 1])
        go(x2_copies(k), from_slot[k])
        add_half(k, g, True, xa.at[at, 0])
        add_half(k, g, False, yb.at[at, 0])

    def second_half(k):
        (_, _, _, _, _, xb, ya, *_), at, _, _ = buffers(k)
        got(x2_copies(k))
        add_half(k, g, True, ya.at[at])
        add_half(k, g, False, xb.at[at])
        go(z_copies(k), from_slot[k], [mine(k, t) for t in zto])

    def finish(k):
        def act():
            (s, *_, zb, fin), at, slot, _ = buffers(k)
            got(z_copies(k))
            base = work[k][2] or 0
            total = s[slot, (z - base) % kinds[work[k][0]][0], g].astype(f32)
            for j in range(3):
                total = total + zb[at, j].astype(f32)
            fin[at] = total.astype(low)
            keep_copy(k).start()
            square = fin[at].astype(f32)
            square = square * square
            for i in range(square.shape[1] // ss.shape[1]):
                ss[...] += jnp.sum(
                    square[:, i * ss.shape[1] : (i + 1) * ss.shape[1]], 0, keepdims=True
                )

        guarded(mine(k), act)
        go(ag_copies(k), None, [mine(k)] * 2)

    def collect(k):
        guarded(mine(k), lambda: got(ag_copies(k)))
        go(fwd_copies(k, xn, yn), None, [mine(k)] * 2)

    def close(k):
        guarded(mine(k), lambda: got(fwd_copies(k, dg, dg)))

    stages = [load, pair, first_half, second_half, finish, collect, close]

    def share_rounds(value, sem_s, sem_r, store):
        def copy(i, slot, peer):
            return send(value.at[slot], value.at[4 + i], sem_s.at[i], sem_r.at[i], peer)

        def round_pair(i, peer, following):
            got([copy(i, i, peer)])
            value[i + 1] = value[i] + value[4 + i]
            go(following())

        def last():
            return [copy(3 + j, 3, zpeer[j]) for j in range(3)]

        def end():
            got(last())
            total = None
            for at in range(4):
                term = jnp.where(z == at, value[3], jnp.zeros_like(value[3]))
                for j in range(3):
                    term = term + jnp.where((z + 3 - j) % 4 == at, value[7 + j], jnp.zeros_like(value[3]))
                total = term if total is None else total + term
            store[...] = total

        return [
            lambda: go([copy(0, 0, sib)]),
            lambda: round_pair(0, sib, lambda: [copy(1, 1, right)]),
            lambda: round_pair(1, right, lambda: [copy(2, 2, up)]),
            lambda: round_pair(2, up, last),
            end,
        ]

    tokens, width = dx.shape
    ee = width // heads
    groups = width // LANES
    runs = tokens // RUN
    gains = ref["gains"]

    moving = {}

    def move(name, src, dst):
        copy = pltpu.make_async_copy(src, dst, dma.at[lanes_of.index(name)])
        copy.start()
        moving[name] = copy

    def done(*names):
        for name in names:
            if name in moving:
                moving.pop(name).wait()

    lanes_of = (
        "a", "gp", "rows", "cols", "x", "dz", "de", "o", "qkv", "pix", "out_r", "out_c", "out_e",
    )

    def tile(i):
        return pl.ds(i * width, width)

    def gain(i):
        return gains[i : i + 1, :]

    def back(grads, at):
        hat, scaled = unit_rows(xin[...])
        gsum[at : at + 1, :] = jnp.sum(grads * hat, 0, keepdims=True)
        gsum[at + 1 : at + 2, :] = jnp.sum(grads, 0, keepdims=True)
        return unit_back(grads, hat, scaled, gain(at))

    def normed(at):
        hat, _ = unit_rows(xin[...])
        h[...] = (hat * gain(at) + gain(at + 1)).astype(low)

    def column_grads(block, source):
        done("out_c")
        for d in range(8):
            value = dot_tn(h[:, d * 128 : (d + 1) * 128], source()).astype(low)
            out_c[d // 2, d % 2] = value.reshape(out_c.shape[2:])
        move("out_c", out_c, ref["g_cols"].at[:, :, :, :, tile(block)])

    def load_hidden(s):
        move("a", ref["a"].at[:, tile(s)], wide.at[:, tile(0)])
        move("gp", ref["gp"].at[:, tile(s)], wide.at[:, tile(1)])
        move("rows", ref["rows"].at[tile(s)], wt)

    def load_columns(block):
        move("cols", ref["cols"].at[:, tile(block)], wu)

    narrow = ref["dz"].shape[1]

    def first_loads():
        move("x", ref["x2"], xin)
        move("dz", ref["dz"], wide.at[:, pl.ds(2 * width, narrow)])
        move("de", ref["dec_rows"].at[pl.ds(2 * width, width)], wt.at[:, pl.ds(0, narrow)])
        move("a", ref["a"].at[:, tile(0)], wide.at[:, tile(0)])
        move("gp", ref["gp"].at[:, tile(0)], wide.at[:, tile(1)])
        load_columns(4)

    def head_piece(_):
        done("x", "dz", "de")
        dz = wide[:, 2 * width : 2 * width + narrow]
        normed(4)
        for d in range(8):
            out_e[0, d // 4, d % 4] = dot_tn(h[:, d * 128 : (d + 1) * 128], dz).astype(low)
        move("out_e", out_e, ref["g_de"])
        dx[...] = back(dot_nt(dz, wt[:, :narrow]), 4)
        move("rows", ref["rows"].at[tile(0)], wt)
        move("x", ref["x1"], xin)
        dy[...] = dx[...].astype(low)
        done("x")
        normed(2)
        acc[...] = jnp.zeros_like(acc)

    def hidden_piece(s):
        done("a", "gp", "rows", "out_r")
        wide[:, 2 * width :] = (dot_nt(dy[...], wt[...]) * wide[:, width : 2 * width].astype(f32)).astype(low)
        for q in range(4):
            out_r[q] = dot_tn(wide[:, q * 256 : (q + 1) * 256], dy[...]).astype(low)
        move("out_r", out_r, ref["g_down"].at[s // 2, s % 2])
        if s < 3:
            load_hidden(s + 1)
        column_grads(4 + s, lambda: wide[:, 2 * width :])
        done("cols")
        acc[...] += dot_nt(wide[:, 2 * width :], wu[...])
        load_columns(5 + s if s < 3 else 3)
        if s == 3:
            move("o", ref["o"], h)
            move("qkv", ref["qkv"], wide)

    def middle_piece(_):
        dx[...] += back(acc[...], 2)
        dy[...] = dx[...].astype(low)
        move("x", ref["x"], xin)
        done("o")
        column_grads(3, lambda: dy[...])
        done("cols")
        h[...] = dot_nt(dy[...], wu[...]).astype(low)
        load_columns(0)
        done("qkv")

    def attention_loads(n):
        slot = n % 2
        return [
            pltpu.make_async_copy(ref[name].at[n], buf.at[slot], att_sem.at[slot, i])
            for i, (name, buf) in enumerate((("p", p_t), ("inv", inv_t), ("oo", oo_t)))
        ]

    def attention_piece(part):
        count = runs * groups // 4
        first = part * count
        for copy in attention_loads(first):
            copy.start()

        @pl.loop(0, count)
        def _(i):
            n = first + i
            for copy in attention_loads(n):
                copy.wait()

            @pl.when(i + 1 < count)
            def _():
                for copy in attention_loads(n + 1):
                    copy.start()

            attend_back(
                n, n % 2, groups, RUN, width, ee, ee ** (-0.5), wide, s_s, ds_s, p_t, inv_t, oo_t, h, wide
            )

    def input_piece(t):
        if t == 0:
            done("x")
            normed(0)
            acc[...] = jnp.zeros_like(acc)
        column_grads(t, lambda: wide[:, t * width : (t + 1) * width])
        done("cols")
        acc[...] += dot_nt(wide[:, t * width : (t + 1) * width], wu[...])
        if t < 2:
            load_columns(t + 1)
        else:
            move("pix", ref["pix"], h)

    def first_piece(_):
        dx[...] += back(acc[...], 0)
        dy[...] = dx[...].astype(low)
        sm[0] = ref["small"][...]
        sm[0, 0:6, :] = gsum[0:6, :]

    def embed_piece(b):
        done("pix", "out_r")
        for q in range(4):
            part = h[:, q * 256 : (q + 1) * 256]
            part = jnp.where(ref["band"][...] == b, part, jnp.zeros_like(part))
            out_r[q] = dot_tn(part, dy[...]).astype(low)
        move("out_r", out_r, ref["g_emb"].at[b // 2, b % 2])

    action = {
        "head": head_piece, "hidden": hidden_piece, "middle": middle_piece, "attention": attention_piece,
        "input": input_piece, "first": first_piece, "embed": embed_piece,
    }

    ss[...] = jnp.zeros_like(ss)
    gsum[...] = jnp.zeros_like(gsum)
    small_rounds = share_rounds(sm, sms, smr, ref["small_out"])
    square_rounds = share_rounds(ssx, sss, ssr, ref["ss_out"])
    ends = [w[6] + 6 for w in work]
    last = max(ends)
    squared = max(w[6] + 4 for w in work)
    compute_end = max(t for t, _, _ in pieces)
    for t in range(last + 1):
        for i in (1, 6, 5, 4, 3, 2, 0):
            for k in range(steps):
                if work[k][6] + i == t:
                    stages[i](k)
        if t == 0:
            first_loads()
        done("out_r", "out_c", "out_e")
        for k in range(steps):
            if work[k][7] == t:
                go(c_copies(k))
        for at, name, argument in pieces:
            if at == t:
                action[name](argument)
        if compute_end < t <= compute_end + 5:
            small_rounds[t - compute_end - 1]()
        if t == squared:
            ssx[0] = jnp.broadcast_to(jnp.sum(ss[...], keepdims=True).reshape(1, 1), ssx.shape[1:])
            square_rounds[0]()
        if squared < t < last:
            square_rounds[t - squared]()
        if t == last:
            for following in square_rounds[last - squared :]:
                following()
    for k in range(steps):
        left(from_slot[k])
    left(sent)
    for k in range(steps):
        guarded(mine(k), keep_copy(k).wait)


def back_reduce_call(dz, pix, band, saved, rows, cols, dec_rows, gains, dcols, ddown, dhead, small, heads):
    x, qkv, p, inv, oo, x1, a, gp, x2, o = saved
    tokens, width = x.shape
    low, f32 = jnp.bfloat16, jnp.float32
    narrow = dec_rows.shape[1]
    ins = dict(
        dz=dz, pix=pix, band=band, x=x, x1=x1, x2=x2, qkv=qkv, p=p, inv=inv, oo=oo, o=o, a=a, gp=gp,
        rows=rows, cols=cols, dec_rows=dec_rows, gains=gains, small=small,
        d_cols=dcols.reshape(4, 2, 4, 16, dcols.shape[1]),
        d_down=ddown.reshape(2, 2, 4, 128, narrow),
        d_head=dhead.reshape(1, 2, 4, 128, narrow),
    )
    outs = dict(
        erows=((4, 256, width), low), ecols=((4, 32, cols.shape[1]), low),
        dcols=((4, 16, dcols.shape[1]), low), drows=((4, 128, narrow), low),
        small_out=(small.shape, f32), ss_out=((8, 128), f32),
        g_down=((2, 2, 4, 256, width), low), g_emb=((2, 2, 4, 256, width), low),
        g_cols=((4, 2, 4, 32, cols.shape[1]), low), g_de=((1, 2, 4, 128, narrow), low),
    )
    kinds = ((4, 32, 1024, 16, 6), (4, 16, 2048, 2, 2), (4, 64, 512, 2, 2))

    def column_chunk(at, block):
        cut = (slice(0, 32), slice(block * 1024, (block + 1) * 1024))
        return (0, at, None, (("g_cols", 0, 4, cut),), "ecols", cut)

    def row_chunk(at, i):
        cut = (slice(i * 32, (i + 1) * 32), slice(0, width))
        return (0, at, None, (("g_down", 0, 2, cut), ("g_emb", 2, 2, cut)), "erows", cut)

    chunks = []
    for i in range(2):
        cut = (slice(0, 16), slice(i * 2048, (i + 1) * 2048))
        chunks.append((1, i, None, (("d_cols", 0, 4, cut),), "dcols", cut))
    for i in range(2):
        cut = (slice(i * 64, (i + 1) * 64), slice(0, narrow))
        sources = (("d_down", 0, 2, cut), ("g_de", 2, 1, cut), ("d_head", 3, 1, cut))
        chunks.append((2, i, None, sources, "drows", cut))
    chunks += [column_chunk(i, 4 + i) for i in range(4)]
    chunks += [column_chunk(4 + i, block) for i, block in enumerate((3, 0, 1, 2))]
    chunks += [row_chunk(8 + i, i) for i in range(8)]
    starts = (0, 1, 3, 4, 5, 6, 7, 8, 9, 11, 12, 13) + tuple(range(14, 22))
    begins = (0, 0, 2, 2, 3, 4, 5, 6, 7, 10, 10, 11) + tuple(range(13, 21))
    work = tuple(chunk + (starts[i], begins[i]) for i, chunk in enumerate(chunks))
    pieces = [(1, "head", 0)] + [(2 + s, "hidden", s) for s in range(4)] + [(6, "middle", 0)]
    pieces += [(7 + i // 2, "attention", i) for i in range(4)]
    pieces += [(9, "input", 0), (9, "input", 1), (10, "input", 2), (10, "first", 0)]
    pieces += [(11 + i // 2, "embed", i) for i in range(4)]
    steps = len(work)
    hbm = pl.BlockSpec(memory_space=pl.ANY)
    vm = pl.BlockSpec(memory_space=pltpu.VMEM)
    vmem, sems = pltpu.VMEM, pltpu.SemaphoreType.DMA
    scratch, landing = [], {}
    for i, (nz, r, col, count, slots) in enumerate(kinds):
        landing[f"land{i}"] = ((count, nz, 4, r, col), low)
        half = col // 2
        scratch += [
            vmem((slots, nz, 4, r, col), low),
            None,
            vmem((2, 4, r, col), low),
            vmem((count, 2, nz, r, half), low),
            vmem((count, 2, nz, r, half), low),
            vmem((count, nz, r, half), low),
            vmem((count, nz, r, half), low),
            vmem((count, 3, r, col), low),
            vmem((count, r, col), low),
        ]
    outs.update(landing)
    in_names, out_names = tuple(ins), tuple(outs)

    def kernel(*refs):
        n = len(in_names) + len(out_names)
        ref = dict(zip(in_names + out_names, refs))
        kept = list(refs[n:])
        for i in range(len(kinds)):
            kept.insert(9 * i + 1, ref[f"land{i}"])
        back_reduce_kernel(heads, kinds, work, pieces, in_names, out_names, *refs[:n], *kept)

    result = pl.pallas_call(
        kernel,
        out_shape=tuple(jax.ShapeDtypeStruct(*outs[name]) for name in out_names),
        in_specs=[vm if name in ("band", "gains", "small") else hbm for name in in_names],
        out_specs=tuple(vm if name in ("small_out", "ss_out") else hbm for name in out_names),
        scratch_shapes=[s for s in scratch if s is not None]
        + [
            vmem((10,) + small.shape, f32),
            vmem((1, 512), f32),
            vmem((10, 8, 128), f32),
            vmem((tokens, width), f32),
            vmem((tokens, width), f32),
            vmem((tokens, width), f32),
            vmem((tokens, width), low),
            vmem((tokens, width), low),
            vmem((tokens, 3 * width), low),
            vmem((width, width), low),
            vmem((width, width), low),
            vmem((4, 256, width), low),
            vmem((4, 2, 4, 32, width), low),
            vmem((1, 2, 4, 128, narrow), low),
            vmem((2,) + p.shape[1:], low),
            vmem((2,) + inv.shape[1:], f32),
            vmem((2,) + oo.shape[1:], f32),
            vmem((p.shape[2], RUN), f32),
            vmem((RUN, p.shape[2]), low),
            vmem((8, width), f32),
            sems((steps, 3)), sems((steps, 3)), sems((steps, 4)), sems((steps, 3)),
            sems((steps, 4)), sems((steps, 4)),
            sems((steps, 2)), sems((steps, 2)),
            sems((steps, 3)), sems((steps, 3)),
            sems((steps, 4)), sems((steps, 4)),
            sems((steps,)), sems((6,)), sems((6,)), sems((6,)), sems((6,)), sems((13,)), sems((2, 3)),
        ],
        compiler_params=pltpu.CompilerParams(
            collective_id=1, has_side_effects=True, vmem_limit_bytes=63 * 1024 * 1024
        ),
    )(*ins.values())
    got = dict(zip(out_names, result))
    shards = [got[name].reshape(-1, got[name].shape[-1]) for name in ("ecols", "erows", "dcols", "drows")]
    return shards, got["small_out"], got["ss_out"]


def adam_step(master, moment, square, grad, factor, fix_one, fix_two, decay, rate):
    clipped = grad * factor
    moment_new = beta_first * moment + (1.0 - beta_first) * clipped
    square_new = beta_second * square + (1.0 - beta_second) * clipped * clipped
    direction = moment_new / fix_one / (jnp.sqrt(square_new / fix_two) + adam_eps) + decay * master
    return (clipped, square_new, master - rate * direction)


def adam_kernel(count_e, count_d, *refs):
    scal_ref, small_ref, ss_ref = refs[:3]
    ins, outs = refs[3:25], refs[25:]
    small = small_ref[...]
    width = small.shape[1]
    flat = lax.broadcasted_iota(jnp.int32, small.shape, 0) * width + lax.broadcasted_iota(
        jnp.int32, small.shape, 1
    )
    gains = jnp.where(flat < count_e + count_d, small, 0.0)
    norm = jnp.sqrt(ss_ref[0:1, 0:1] + jnp.sum(gains * gains, keepdims=True).reshape(1, 1))
    factor = clip_level / jnp.maximum(norm, clip_level)
    masked, fix_one, fix_two = scal_ref[0, 0], scal_ref[0, 1], scal_ref[0, 2]

    def update(grad, master, moment, square, decay, rate):
        return adam_step(master, moment, square, grad, factor, fix_one, fix_two, decay, rate)

    for i in range(4):
        grad, master, moment, square = ins[4 * i : 4 * i + 4]
        got = update(
            grad[...].astype(jnp.float32), master[...], moment[...], square[...], weight_decay, learn_rate
        )
        for target, value in zip(outs[3 * i : 3 * i + 3], got):
            target[...] = value

    @pl.when(pl.program_id(0) == 0)
    def _():
        at = 0
        for i in range(2):
            master, moment, square = ins[16 + 3 * i : 19 + 3 * i]
            rows, columns = master.shape
            for r in range(rows):
                row, lane = at // width, at % width
                grad = small[row : row + 1, lane : lane + columns]
                one = slice(r, r + 1)
                got = update(grad, master[one, :], moment[one, :], square[one, :], 0.0, gain_rate)
                for target, value in zip(outs[12 + 3 * i : 15 + 3 * i], got):
                    target[one, :] = value
                at += columns
        outs[18][...] = small[at // width : at // width + 1, at % width : at % width + 1] / masked
        outs[19][...] = norm


def adam_call(scal, small, squares, matrices, gains):
    steps = 4

    def block(array):
        rows, columns = array.shape
        if rows // steps % 16 == 0:
            return pl.BlockSpec((rows // steps, columns), lambda s: (s, 0))
        return pl.BlockSpec((rows, columns // steps), lambda s: (0, s))

    def whole(array):
        return pl.BlockSpec(array.shape, lambda s: (0, 0))

    struct = jax.ShapeDtypeStruct
    f32 = jnp.float32
    ins, in_specs, outs, out_specs = [], [], [], []
    for group in matrices:
        ins += group
        in_specs += [block(array) for array in group]
        outs += [struct(group[1].shape, f32)] * 3
        out_specs += [block(group[1])] * 3
    for group in gains:
        ins += group
        in_specs += [whole(array) for array in group]
        outs += [struct(group[0].shape, f32)] * 3
        out_specs += [whole(group[0])] * 3
    outs += [struct((1, 1), f32)] * 2
    out_specs += [pl.BlockSpec((1, 1), lambda s: (0, 0))] * 2
    out = pl.pallas_call(
        functools.partial(adam_kernel, gains[0][0].size, gains[1][0].size),
        grid=(steps,),
        in_specs=[pl.BlockSpec(memory_space=pltpu.SMEM), whole(small), whole(squares)] + in_specs,
        out_specs=tuple(out_specs),
        out_shape=tuple(outs),
        compiler_params=pltpu.CompilerParams(
            dimension_semantics=("arbitrary",), vmem_limit_bytes=56 * 1024 * 1024
        ),
    )(scal, small, squares, *ins)
    return tuple(out[:18]) + (out[18][0, 0], out[19][0, 0])


def body(
    pixels,
    keep_index,
    band_group,
    gsd_index,
    gsd_table,
    group_items,
    step_count,
    enc_cols,
    enc_rows,
    dec_cols,
    dec_rows,
    enc_gains,
    dec_gains,
    moment_ecols,
    moment_erows,
    moment_dcols,
    moment_drows,
    moment_egains,
    moment_dgains,
    square_ecols,
    square_erows,
    square_dcols,
    square_drows,
    square_egains,
    square_dgains,
):
    n_grp = lax.axis_size("grp")
    grp_at = lax.axis_index("grp")

    def gather_rows(master):
        rows = master.shape[0]
        if rows % (16 * n_grp):
            return lax.all_gather(to_low(master), "dp", axis=0, tiled=True)
        part = rows // n_grp
        mine = lax.dynamic_slice_in_dim(master, grp_at * part, part, 0)
        return lax.all_gather(to_low(mine), ("dp", "grp"), axis=0, tiled=True)

    direct = (n_grp, lax.axis_size("dp")) == (4, 8)
    own_count = jnp.sum(group_items.astype(jnp.float32))
    if direct:
        (whole_rows, whole_cols), total_count = gather_call(
            [to_low(enc_rows), to_low(enc_cols)], own_count, (4, 4), 2, 0
        )
    else:
        total_count = lax.psum(own_count, "grp")
        whole_rows, whole_cols = gather_rows(enc_rows), gather_rows(enc_cols)
    masked = total_count * (L - K)
    count_steps = step_count[0].astype(jnp.float32)
    fix_one = 1.0 - beta_first**count_steps
    fix_two = 1.0 - beta_second**count_steps
    keep_rows = keep_index[0]
    batch = keep_rows.shape[0]
    keep_column = keep_rows[..., None]
    band_row = band_group[0][:, None, :].astype(jnp.float32)
    gsd_row = gsd_index[0][:, None, :].astype(jnp.float32)
    if direct:
        shards, dec_embed = (to_low(dec_cols), to_low(dec_rows)), None
    else:
        dec_copy, dec_whole = gather_rows(dec_cols), gather_rows(dec_rows)
        shards, dec_embed = (), dec_whole[DFF : DFF + D]
    latent, kept_pixels, kept_bands, saved, gathered = encoder_call(
        pixels[0],
        keep_column,
        band_row,
        gsd_row,
        gsd_table[0],
        whole_rows,
        whole_cols,
        dec_embed,
        enc_gains,
        HEADS,
        shards,
    )
    if direct:
        dec_copy, dec_whole = gathered
    latent = latent.reshape(batch, K, -1)
    first_item = lax.axis_index("dp") * batch
    valid = (first_item + jnp.arange(batch, dtype=jnp.int32) < group_items[0]).astype(jnp.float32)
    scal = jnp.stack([valid / PIX, valid * (2.0 / PIX) / masked])
    grad_latent, grad_dcols, grad_ddown, grad_head, dec_sums, loss_local = decoder_call(
        scal,
        latent,
        keep_column,
        gsd_row,
        gsd_table[0],
        pixels[0],
        dec_copy,
        dec_whole,
        dec_gains,
        DHEADS,
    )
    loss_local = loss_local[0, 0]
    grad_latent = grad_latent.reshape(batch * K, -1)
    grad_dgains = dec_sums[:7]

    def reduce_rows(pieces, axis):
        whole = jnp.concatenate([to_low(piece) for piece in pieces], axis)
        return lax.psum_scatter(whole, "dp", scatter_dimension=0, tiled=True)

    if direct:
        count_e, count_d = enc_gains.size, grad_dgains.size
        flat = jnp.concatenate([grad_dgains.reshape(-1), loss_local[None]])
        small = jnp.pad(flat, (count_e, 16 * D - count_e - flat.shape[0])).reshape(16, D)
        shards, small, squares = back_reduce_call(
            grad_latent,
            kept_pixels,
            kept_bands,
            saved,
            whole_rows,
            whole_cols,
            dec_whole,
            enc_gains,
            grad_dcols,
            grad_ddown,
            grad_head,
            small,
            HEADS,
        )
        matrices = (
            [shards[0], enc_cols, moment_ecols, square_ecols],
            [shards[1], enc_rows, moment_erows, square_erows],
            [shards[2], dec_cols, moment_dcols, square_dcols],
            [shards[3], dec_rows, moment_drows, square_drows],
        )
        gains = ([enc_gains, moment_egains, square_egains], [dec_gains, moment_dgains, square_dgains])
        return adam_call(
            jnp.stack([masked, fix_one, fix_two]).reshape(1, 3), small, squares, matrices, gains
        )
    else:
        grad_erows, grad_ecols, grad_dembed, enc_sums = encoder_back_call(
            grad_latent,
            kept_pixels,
            kept_bands,
            saved,
            whole_rows,
            whole_cols,
            dec_embed,
            enc_gains,
            HEADS,
        )
        grad_egains = enc_sums[:6]
        drows = (grad_ddown, grad_dembed, grad_head)
        enc_sum, dec_sum, loss_sum = lax.psum((grad_egains, grad_dgains, loss_local), ("grp", "dp"))
        shards = tuple(
            lax.psum(reduce_rows(pieces, 0), "grp").astype(jnp.float32)
            for pieces in ((grad_ecols,), (grad_erows,), (grad_dcols,), drows)
        )
        shard_squares = lax.psum(sum((jnp.sum(piece * piece) for piece in shards)), "dp")
    loss = loss_sum / masked
    grad_norm = jnp.sqrt(shard_squares + jnp.sum(enc_sum * enc_sum) + jnp.sum(dec_sum * dec_sum))
    factor = clip_level / jnp.maximum(grad_norm, clip_level)
    clipped_ecols, squares_ecols, updated_ecols = adam_step(
        enc_cols,
        moment_ecols,
        square_ecols,
        shards[0],
        factor,
        fix_one,
        fix_two,
        weight_decay,
        learn_rate,
    )
    clipped_erows, squares_erows, updated_erows = adam_step(
        enc_rows,
        moment_erows,
        square_erows,
        shards[1],
        factor,
        fix_one,
        fix_two,
        weight_decay,
        learn_rate,
    )
    clipped_dcols, squares_dcols, updated_dcols = adam_step(
        dec_cols,
        moment_dcols,
        square_dcols,
        shards[2],
        factor,
        fix_one,
        fix_two,
        weight_decay,
        learn_rate,
    )
    clipped_drows, squares_drows, updated_drows = adam_step(
        dec_rows,
        moment_drows,
        square_drows,
        shards[3],
        factor,
        fix_one,
        fix_two,
        weight_decay,
        learn_rate,
    )
    clipped_egains, squares_egains, updated_egains = adam_step(
        enc_gains, moment_egains, square_egains, enc_sum, factor, fix_one, fix_two, 0.0, gain_rate
    )
    clipped_dgains, squares_dgains, updated_dgains = adam_step(
        dec_gains, moment_dgains, square_dgains, dec_sum, factor, fix_one, fix_two, 0.0, gain_rate
    )
    return (
        clipped_ecols,
        squares_ecols,
        updated_ecols,
        clipped_erows,
        squares_erows,
        updated_erows,
        clipped_dcols,
        squares_dcols,
        updated_dcols,
        clipped_drows,
        squares_drows,
        updated_drows,
        clipped_egains,
        squares_egains,
        updated_egains,
        clipped_dgains,
        squares_dgains,
        updated_dgains,
        loss,
        grad_norm,
    )


def solution(mesh):
    return jax.shard_map(
        body,
        mesh=mesh,
        in_specs=(
            P("grp", "dp", None, None),
            P("grp", "dp", None),
            P("grp", "dp", None),
            P("grp", "dp", None),
            P("grp", None, None),
            P("grp"),
            P(),
            P("dp", None),
            P("dp", None),
            P("dp", None),
            P("dp", None),
            P(),
            P(),
            P("dp", None),
            P("dp", None),
            P("dp", None),
            P("dp", None),
            P(),
            P(),
            P("dp", None),
            P("dp", None),
            P("dp", None),
            P("dp", None),
            P(),
            P(),
        ),
        out_specs=(
            P("dp", None),
            P("dp", None),
            P("dp", None),
            P("dp", None),
            P("dp", None),
            P("dp", None),
            P("dp", None),
            P("dp", None),
            P("dp", None),
            P("dp", None),
            P("dp", None),
            P("dp", None),
            P(),
            P(),
            P(),
            P(),
            P(),
            P(),
            P(),
            P(),
        ),
        check_vma=False,
    )
```

```python
import functools

import jax
import jax.numpy as jnp
from jax import lax
from jax.experimental import pallas as pl
from jax.experimental.pallas import tpu as pltpu
from jax.sharding import PartitionSpec as P

D = 1024
HEADS = 16
FF = 4096
DHEADS = 16
DFF = 2048
PIX = 1024
NBG = 4
L = 256
K = 64


norm_eps = 1e-06
clip_level = 0.005
learn_rate = 0.02
gain_rate = 0.25
weight_decay = 0.05
adam_eps = 1e-08
beta_first = 0.5
beta_second = 0.5


def to_low(value):
    return value.astype(jnp.bfloat16)


def project(inputs, matrix):
    return jnp.einsum("...n,nm->...m", inputs, matrix, preferred_element_type=jnp.float32)


def dot_nn(a, b):
    return lax.dot_general(a, b, (((1,), (0,)), ((), ())), preferred_element_type=jnp.float32)


def dot_nt(a, b):
    return lax.dot_general(a, b, (((1,), (1,)), ((), ())), preferred_element_type=jnp.float32)


def dot_tn(a, b):
    return lax.dot_general(a, b, (((0,), (0,)), ((), ())), preferred_element_type=jnp.float32)


def unit_rows(values):
    centred = values - jnp.mean(values, -1, keepdims=True)
    scaled = lax.rsqrt(jnp.mean(centred * centred, -1, keepdims=True) + norm_eps)
    return centred * scaled, scaled


def unit_back(grads, hat, scaled, gain):
    inner = grads * gain
    return scaled * (
        inner
        - jnp.mean(inner, -1, keepdims=True)
        - hat * jnp.mean(inner * hat, -1, keepdims=True)
    )

LANES = 128


def stack_rows(value, ee):
    head = lax.broadcasted_iota(jnp.int32, value.shape, 1) // ee
    return jnp.concatenate(
        [jnp.where(head == h, value, jnp.zeros_like(value)) for h in range(LANES // ee)], 0
    )


def stack_lanes(value, ee):
    head = lax.broadcasted_iota(jnp.int32, value.shape, 0) // ee
    return jnp.concatenate(
        [jnp.where(head == h, value, jnp.zeros_like(value)) for h in range(LANES // ee)], 1
    )


def span(at, size):
    return slice(at * size, (at + 1) * size)


def attend(n, groups, tokens, width, ee, expo, same, qkv_s, s_s, p_s, inv_s, oo_s, o_s):
    item = n // groups
    g = n % groups
    rs = span(item, tokens)
    qa = span(g, LANES)
    q = qkv_s[rs, qa]
    k = qkv_s[rs, span(width // LANES + g, LANES)]
    v = qkv_s[rs, span(2 * width // LANES + g, LANES)]
    s_s[...] = dot_nt(stack_rows(q, ee), k)
    for h in range(LANES // ee):
        at = slice(h * tokens, (h + 1) * tokens)
        s = s_s[at, :]
        if same is not None:
            s = jnp.where(same, s, -1e30)
        top = jnp.max(s, -1, keepdims=True)
        p_s[n, :, at] = jnp.exp2((s - top) * expo).astype(p_s.dtype)
    ones = jnp.ones_like(v)
    both = jnp.concatenate([stack_rows(v, ee), stack_rows(ones, ee)], 1)
    out = dot_nn(p_s[n], both)
    inv = 1.0 / out[:, LANES:]
    out = out[:, :LANES] * inv
    inv_s[n] = inv
    oo_s[n] = out
    o_s[rs, qa] = out.astype(o_s.dtype)


def attend_back(n, slot, groups, tokens, width, ee, scale, qkv_s, s_s, ds_s, p_s, inv_s, oo_s, do_s, dqkv_s):
    low = dqkv_s.dtype
    item = n // groups
    g = n % groups
    rs = span(item, tokens)
    qa = span(g, LANES)
    ka = span(width // LANES + g, LANES)
    va = span(2 * width // LANES + g, LANES)
    heads = range(LANES // ee)
    do = do_s[rs, qa].astype(jnp.float32) * inv_s[slot]
    rest = (-do * oo_s[slot]).astype(low)
    do_t = do.T.astype(low)
    do = do.astype(low)
    v = qkv_s[rs, va]
    s_s[...] = dot_nt(
        jnp.concatenate([stack_rows(do, ee), stack_rows(rest, ee)], 1),
        jnp.concatenate([v, jnp.ones_like(v)], 1),
    )
    for h in heads:
        at = slice(h * tokens, (h + 1) * tokens)
        ds_s[:, at] = (p_s[slot, :, at].astype(jnp.float32) * s_s[at, :]).astype(low)
    e_rows = jnp.concatenate([p_s[slot, :, h * tokens : (h + 1) * tokens] for h in heads], 0)
    ds_rows = jnp.concatenate([ds_s[:, h * tokens : (h + 1) * tokens] for h in heads], 0)
    dv_t = dot_nn(stack_lanes(do_t, ee), e_rows)
    dk_t = dot_nn(stack_lanes(qkv_s[rs, qa].T, ee), ds_rows)
    dq = dot_nn(ds_s[...], stack_rows(qkv_s[rs, ka], ee))
    dqkv_s[rs, qa] = (dq * scale).astype(low)
    dqkv_s[rs, ka] = (dk_t.T * scale).astype(low)
    dqkv_s[rs, va] = dv_t.T.astype(low)


def one_hot(index, count):
    places = lax.broadcasted_iota(jnp.int32, (index.shape[0], count), 1)
    return jnp.where(places.astype(jnp.float32) == index.astype(jnp.float32), 1.0, 0.0)


def split_table(table_ref, high_s, low_s):
    high = table_ref[...].astype(high_s.dtype)
    high_s[...] = high
    low_s[...] = (table_ref[...] - high.astype(jnp.float32)).astype(low_s.dtype)


def look_up(hot, index_row, high_s, low_s):
    index = jnp.sum(hot * index_row, -1, keepdims=True)
    rows = one_hot(index, high_s.shape[0]).astype(high_s.dtype)
    return dot_nn(rows, high_s[...]) + dot_nn(rows, low_s[...])


def decoder_kernel(
    items, heads, scal_ref, z_ref, keep_ref, gsd_ref, table_ref, pix_ref, cols_ref, down_ref, head_ref, gains_ref,
    dz_ref, gcols_out, gdown_out, ghead_out, ggains_ref, loss_ref,
    x_s, h1_s, qkv_s, p_s, o_s, x1_s, h2_s, a_s, gp_s, x2_s, hd_s, dx_s, dy_s, acc_s, dqkv_s, inv_s, oo_s, s_s, ds_s,
    high_s, low_s, pixel_s, gcols, gdown, ghead,
):
    low = jnp.bfloat16
    step = pl.program_id(0)
    width = x_s.shape[1]
    tokens = pix_ref.shape[1]
    hide = tokens - K
    rows = items * tokens
    tile = 512
    ee = width // heads
    scale = ee ** (-0.5)
    expo = scale * 1.4426950408889634

    @pl.when(step == 0)
    def _():
        gcols[...] = jnp.zeros_like(gcols)
        gdown[...] = jnp.zeros_like(gdown)
        ghead[...] = jnp.zeros_like(ghead)
        ggains_ref[...] = jnp.zeros_like(ggains_ref)
        loss_ref[...] = jnp.zeros_like(loss_ref)
        split_table(table_ref, high_s, low_s)

    def gain(i):
        return gains_ref[i : i + 1, :]

    f32 = jnp.float32
    before = lax.broadcasted_iota(jnp.int32, (tokens, tokens), 0) <= lax.broadcasted_iota(
        jnp.int32, (tokens, tokens), 1
    )
    before = before.astype(f32).astype(low)
    for i in range(items):
        base = i * tokens
        keep_hot = one_hot(keep_ref[i], tokens)
        shown = jnp.max(keep_hot, 0, keepdims=True)
        rank = dot_nn(jnp.broadcast_to(1.0 - shown, (8, tokens)).astype(low), before)[:1]
        slot = lax.broadcasted_iota(jnp.int32, (hide, tokens), 0).astype(f32) + 1.0
        hide_hot = jnp.where(slot == rank, 1.0 - shown, 0.0)
        position = look_up(jnp.concatenate([keep_hot, hide_hot], 0), gsd_ref[i], high_s, low_s)
        x_s[base : base + K, :] = position[:K] + z_ref[i]
        x_s[base + K : base + tokens, :] = position[K:] + gain(6)
        pixel_s[i] = dot_nn(hide_hot.astype(low), pix_ref[i]).astype(low)
    hat, _ = unit_rows(x_s[...])
    h1_s[...] = (hat * gain(0) + gain(1)).astype(low)

    for t in range(3):
        at = slice(t * width, (t + 1) * width)
        qkv_s[:, at] = dot_nn(h1_s[...], cols_ref[:, at]).astype(low)

    groups = width // LANES

    for n in range(items * groups):
        attend(n, groups, tokens, width, ee, expo, None, qkv_s, s_s.at[n % 2], p_s, inv_s, oo_s, o_s)

    x1_s[...] = x_s[...] + dot_nn(o_s[...], cols_ref[:, 3 * width : 4 * width])
    hat, _ = unit_rows(x1_s[...])
    h2_s[...] = (hat * gain(2) + gain(3)).astype(low)
    x2_s[...] = x1_s[...]

    for t in range(down_ref.shape[0] // tile):
        at = slice(t * tile, (t + 1) * tile)
        up = slice(4 * width + t * tile, 4 * width + (t + 1) * tile)
        u = dot_nn(h2_s[...], cols_ref[:, up])
        cumul = 0.5 * (1.0 + lax.erf(u * 0.7071067811865476))
        act = (u * cumul).astype(low)
        a_s[:, at] = act
        gp_s[:, at] = (cumul + u * jnp.exp(-0.5 * u * u) * 0.3989422804014327).astype(gp_s.dtype)
        x2_s[...] += dot_nn(act, down_ref[at, :])

    hat, _ = unit_rows(x2_s[...])
    hd_s[...] = (hat * gain(4) + gain(5)).astype(low)

    pixel_count = head_ref.shape[0]
    for i in range(items):
        base = i * tokens
        weight = scal_ref[0, step * items + i]
        coef = scal_ref[1, step * items + i]
        target, _ = unit_rows(pixel_s[i].astype(f32))
        hd = hd_s[base + K : base + tokens, :]
        back = jnp.zeros((hide, width), jnp.float32)
        for t in range(pixel_count // tile):
            at = slice(t * tile, (t + 1) * tile)
            err = dot_nt(hd, head_ref[at, :]) - target[:, at]
            loss_ref[...] += weight * jnp.sum(err * err, keepdims=True).reshape(1, 1)
            dpred = (err * coef).astype(low)
            ghead[at, :] += dot_tn(dpred, hd)
            back = back + dot_nn(dpred, head_ref[at, :])
        hat, scaled = unit_rows(x2_s[base + K : base + tokens, :])
        ggains_ref[4:5, :] += jnp.sum(back * hat, 0, keepdims=True)
        ggains_ref[5:6, :] += jnp.sum(back, 0, keepdims=True)
        dx = unit_back(back, hat, scaled, gain(4))
        dx_s[base : base + K, :] = jnp.zeros((K, width), jnp.float32)
        dx_s[base + K : base + tokens, :] = dx
        dy_s[base : base + K, :] = jnp.zeros((K, width), low)
        dy_s[base + K : base + tokens, :] = dx.astype(low)

    acc_s[...] = jnp.zeros_like(acc_s)

    for t in range(down_ref.shape[0] // tile):
        at = slice(t * tile, (t + 1) * tile)
        up = slice(4 * width + t * tile, 4 * width + (t + 1) * tile)
        gdown[at, :] += dot_tn(a_s[:, at], dy_s[...])
        du = (dot_nt(dy_s[...], down_ref[at, :]) * gp_s[:, at].astype(jnp.float32)).astype(low)
        gcols[:, up] += dot_tn(h2_s[...], du)
        acc_s[...] += dot_nt(du, cols_ref[:, up])

    hat, scaled = unit_rows(x1_s[...])
    grads = acc_s[...]
    ggains_ref[2:3, :] += jnp.sum(grads * hat, 0, keepdims=True)
    ggains_ref[3:4, :] += jnp.sum(grads, 0, keepdims=True)
    dx_s[...] += unit_back(grads, hat, scaled, gain(2))
    dy_s[...] = dx_s[...].astype(low)
    gcols[:, 3 * width : 4 * width] += dot_tn(o_s[...], dy_s[...])
    o_s[...] = dot_nt(dy_s[...], cols_ref[:, 3 * width : 4 * width]).astype(low)

    for n in range(items * groups):
        attend_back(
            n, n, groups, tokens, width, ee, scale, qkv_s, s_s.at[n % 2], ds_s.at[n % 2], p_s, inv_s, oo_s, o_s,
            dqkv_s,
        )

    acc_s[...] = jnp.zeros_like(acc_s)

    for t in range(3):
        at = slice(t * width, (t + 1) * width)
        gcols[:, at] += dot_tn(h1_s[...], dqkv_s[:, at])
        acc_s[...] += dot_nt(dqkv_s[:, at], cols_ref[:, at])

    hat, scaled = unit_rows(x_s[...])
    grads = acc_s[...]
    ggains_ref[0:1, :] += jnp.sum(grads * hat, 0, keepdims=True)
    ggains_ref[1:2, :] += jnp.sum(grads, 0, keepdims=True)
    dx_s[...] += unit_back(grads, hat, scaled, gain(0))
    for i in range(items):
        base = i * tokens
        dz_ref[i] = dx_s[base : base + K, :].astype(low)
        ggains_ref[6:7, :] += jnp.sum(dx_s[base + K : base + tokens, :], 0, keepdims=True)

    @pl.when(step == pl.num_programs(0) - 1)
    def _():
        gcols_out[...] = gcols[...].astype(low)
        gdown_out[...] = gdown[...].astype(low)
        ghead_out[...] = ghead[...].astype(low)


def decoder_call(scal, latent, keep, gsd, table, pixels, cols, rows, gains, heads):
    batch, tokens, pixel_count = pixels.shape
    width = cols.shape[0]
    down = jax.ShapeDtypeStruct((cols.shape[1] - 4 * width, width), rows.dtype)
    head = jax.ShapeDtypeStruct((pixel_count, width), rows.dtype)
    last = rows.shape[0] // pixel_count - 1
    items = 2
    run = items * tokens
    hide = tokens - K
    low = jnp.bfloat16
    full = pl.Buffered(1)

    def whole(array):
        return pl.BlockSpec(array.shape, lambda s: (0,) * len(array.shape), pipeline_mode=full)

    def by_item(shape):
        return pl.BlockSpec((items,) + shape, lambda s: (s, 0, 0))

    outs = (
        jax.ShapeDtypeStruct((batch, K, width), low),
        jax.ShapeDtypeStruct(cols.shape, low),
        jax.ShapeDtypeStruct(down.shape, low),
        jax.ShapeDtypeStruct(head.shape, low),
        jax.ShapeDtypeStruct((8, width), jnp.float32),
        jax.ShapeDtypeStruct((1, 1), jnp.float32),
    )
    vmem = pltpu.VMEM
    f32 = jnp.float32
    return pl.pallas_call(
        functools.partial(decoder_kernel, items, heads),
        grid=(batch // items,),
        in_specs=[
            pl.BlockSpec(memory_space=pltpu.SMEM),
            by_item((K, width)),
            by_item((K, 1)),
            by_item((1, tokens)),
            pl.BlockSpec((table.shape[0], width), lambda s: (0, table.shape[1] // width - 1), pipeline_mode=full),
            by_item((tokens, pixel_count)),
            whole(cols),
            whole(down),
            pl.BlockSpec(head.shape, lambda s: (last, 0), pipeline_mode=full),
            whole(gains),
        ],
        out_specs=(by_item((K, width)),) + tuple(whole(out) for out in outs[1:]),
        out_shape=outs,
        scratch_shapes=[
            vmem((run, width), f32),
            vmem((run, width), low),
            vmem((run, 3 * width), low),
            vmem((items * width // 128, tokens, 4 * tokens), low),
            vmem((run, width), low),
            vmem((run, width), f32),
            vmem((run, width), low),
            vmem((run, down.shape[0]), low),
            vmem((run, down.shape[0]), low),
            vmem((run, width), f32),
            vmem((run, width), low),
            vmem((run, width), f32),
            vmem((run, width), low),
            vmem((run, width), f32),
            vmem((run, 3 * width), low),
            vmem((items * width // 128, tokens, 128), f32),
            vmem((items * width // 128, tokens, 128), f32),
            vmem((2, 4 * tokens, tokens), f32),
            vmem((2, tokens, 4 * tokens), low),
            vmem((table.shape[0], width), low),
            vmem((table.shape[0], width), low),
            vmem((items, hide, pixel_count), low),
            vmem(cols.shape, f32),
            vmem(down.shape, f32),
            vmem(head.shape, f32),
        ],
        compiler_params=pltpu.CompilerParams(
            dimension_semantics=("arbitrary",), vmem_limit_bytes=63 * 1024 * 1024
        ),
        cost_estimate=pl.CostEstimate(
            flops=70_000_000_000, bytes_accessed=40_000_000, transcendentals=20_000_000
        ),
    )(scal, latent, keep, gsd, table, pixels, cols, rows, rows, gains)


MESH_ID = pl.DeviceIdType.MESH


def place():
    g = lax.axis_index("grp")
    d = lax.axis_index("dp")
    z, c = d // 2, d % 2
    xn = g + 1 - 2 * (g % 2)
    yn = (g + 2) % 4
    return g, z, c, xn, yn


def pieces(shape, parts):
    rows, columns = shape
    if rows // parts >= 32:
        n = rows // parts
        cut = [(slice(i * n, (i + 1) * n), slice(0, columns)) for i in range(parts)]
    else:
        n = columns // parts
        cut = [(slice(0, rows), slice(i * n, (i + 1) * n)) for i in range(parts)]
    return cut


def halves(cut):
    rows, columns = cut
    mid = (columns.start + columns.stop) // 2
    return (rows, slice(columns.start, mid)), (rows, slice(mid, columns.stop))


def greet(peers):
    barrier = pltpu.get_barrier_semaphore()
    for peer in peers:
        pl.semaphore_signal(barrier, inc=1, device_id=peer, device_id_type=MESH_ID)
    pl.semaphore_wait(barrier, len(peers))


GATHER_SEMS = 14


def gather_events(count, chunks, ahead, ins, outs, sems):
    zs, zr, xs, xr, ys, yr, fs, fr, gs, gr, cs, os, cr, ls = sems
    g, z, c, xn, yn = place()
    dg = (xn + 2) % 4
    here = 2 * z + c
    other = 1 - c
    sib = (g, 2 * z + 1 - c)
    right, up = (xn, here), (yn, here)
    zpeer = [(g, 2 * ((z + j) % 4) + c) for j in (1, 2, 3)]
    zfrom = [(z + 4 - j) % 4 for j in (1, 2, 3)]
    peers = [sib, right, up] + zpeer
    work = []
    for array in range(count):
        for cut in pieces(ins[array].shape[1:], chunks[array]):
            work.append((array, cut))
    steps = len(work)
    sent = []

    def send(src, dst, send_sem, recv_sem, peer):
        return pltpu.make_async_remote_copy(
            src_ref=src, dst_ref=dst, send_sem=send_sem, recv_sem=recv_sem,
            device_id=peer, device_id_type=MESH_ID,
        )

    def go(make):
        make().start()
        sent.append(make)

    def block(array, z_at, q, cut):
        return outs[array].at[z_at, c, q, cut[0], cut[1]]

    def zcopy(k, j):
        array, cut = work[k]
        return send(
            ins[array].at[g, cut[0], cut[1]], block(array, z, g, cut), zs.at[k, j], zr.at[k, j], zpeer[j]
        )

    def relay(k, j, q, cut, ssem, rsem, peer):
        at = block(work[k][0], zfrom[j], q, cut)
        return send(at, at, ssem, rsem, peer)

    def to_x(k, j):
        return relay(k, j, g, work[k][1], xs.at[k, j], xr.at[k, j], right)

    def to_y(k, j):
        return relay(k, j, g, work[k][1], ys.at[k, j], yr.at[k, j], up)

    def to_core(k, j, i, q):
        return relay(k, j, q, work[k][1], cs.at[k, j, i], cr.at[work[k][0]], sib)

    def on_y(k, j, q):
        return relay(k, j, q, halves(work[k][1])[0], fs.at[k, j], fr.at[k, j], up)

    def on_x(k, j, q):
        return relay(k, j, q, halves(work[k][1])[1], gs.at[k, j], gr.at[k, j], right)

    def own(array):
        return pltpu.make_async_copy(ins[array], outs[array].at[z, c], ls.at[array])

    def own_to_core(array):
        return send(ins[array], outs[array].at[z, c], os.at[array], cr.at[array], sib)

    def begin():
        for array in range(count):
            own(array).start()
        for k in range(min(ahead, steps)):
            for j in range(3):
                go(functools.partial(zcopy, k, j))
        for array in range(count):
            go(functools.partial(own_to_core, array))

    def event(t):
        if t < steps:
            for j in range(3):
                zcopy(t, j).wait_recv()
                go(functools.partial(to_x, t, j))
                go(functools.partial(to_y, t, j))
                go(functools.partial(to_core, t, j, 0, g))
            if t + ahead < steps:
                for j in range(3):
                    go(functools.partial(zcopy, t + ahead, j))
        if 1 <= t <= steps:
            k = t - 1
            for j in range(3):
                relay(k, j, xn, work[k][1], xs.at[k, j], xr.at[k, j], right).wait_recv()
                go(functools.partial(on_y, k, j, xn))
                go(functools.partial(to_core, k, j, 1, xn))
                relay(k, j, yn, work[k][1], ys.at[k, j], yr.at[k, j], up).wait_recv()
                go(functools.partial(on_x, k, j, yn))
                go(functools.partial(to_core, k, j, 2, yn))
        if 2 <= t:
            k = t - 2
            for j in range(3):
                on_y(k, j, dg).wait_recv()
                on_x(k, j, dg).wait_recv()
                go(functools.partial(to_core, k, j, 3, dg))

    def finish():
        for make in sent:
            make().wait_send()
        for array in range(count):
            whole = outs[array].at[:, other]
            send(whole, whole, os.at[array], cr.at[array], sib).wait_recv()
            own(array).wait()

    return peers, begin, [functools.partial(event, t) for t in range(steps + 2)], finish


def gather_scratch(count, steps):
    dma = pltpu.SemaphoreType.DMA
    return [dma((steps, 3))] * 10 + [dma((steps, 3, 4)), dma((count,)), dma((count,)), dma((count,))]


def gather_kernel(count, chunks, ahead, *refs):
    ins, items_ref = refs[:count], refs[count]
    outs, items_out = refs[count + 1 : 2 * count + 1], refs[2 * count + 1]
    sems = refs[2 * count + 2 :]
    it, its, itr = sems[GATHER_SEMS:]
    peers, begin, events, finish = gather_events(count, chunks, ahead, ins, outs, sems[:GATHER_SEMS])
    greet(peers)
    _, right, up = peers[:3]

    def items_copy(i, peer):
        return pltpu.make_async_remote_copy(
            src_ref=it.at[2 * i], dst_ref=it.at[2 * i + 1], send_sem=its.at[i], recv_sem=itr.at[i],
            device_id=peer, device_id_type=MESH_ID,
        )

    it[0] = items_ref[...]
    items_copy(0, right).start()
    begin()
    for t, event in enumerate(events):
        event()
        if t == 0:
            items_copy(0, right).wait_recv()
            it[2] = it[0] + it[1]
            items_copy(1, up).start()
        if t == 1:
            items_copy(1, up).wait_recv()
            items_out[...] = it[2] + it[3]
    finish()
    items_copy(0, right).wait_send()
    items_copy(1, up).wait_send()


def gather_call(shards, items, chunks, ahead=2, collective_id=0):
    count = len(shards)
    steps = sum(chunks)
    views = [s.reshape(4, s.shape[0] // 4, s.shape[1]) for s in shards]
    dma = pltpu.SemaphoreType.DMA
    hbm = pl.BlockSpec(memory_space=pl.ANY)
    vm = pl.BlockSpec(memory_space=pltpu.VMEM)
    *outs, total = pl.pallas_call(
        functools.partial(gather_kernel, count, chunks, ahead),
        out_shape=tuple(jax.ShapeDtypeStruct((4, 2) + v.shape, v.dtype) for v in views)
        + (jax.ShapeDtypeStruct((8, 128), jnp.float32),),
        in_specs=[hbm] * count + [vm],
        out_specs=tuple([hbm] * count + [vm]),
        scratch_shapes=gather_scratch(count, steps)
        + [pltpu.VMEM((4, 8, 128), jnp.float32), dma((2,)), dma((2,))],
        compiler_params=pltpu.CompilerParams(collective_id=collective_id, has_side_effects=True),
    )(*views, jnp.broadcast_to(items, (8, 128)))
    return [o.reshape(-1, o.shape[-1]) for o in outs], total[0, 0]


RUN = 256


def same_item():
    row = lax.broadcasted_iota(jnp.int32, (RUN, RUN), 0) // K
    column = lax.broadcasted_iota(jnp.int32, (RUN, RUN), 1) // K
    return row == column


def encoder_kernel(heads, chunks, *refs):
    count = 2 if chunks else 0
    (pixels_ref, keep_ref, bands_ref, gsd_ref, table_ref, rows_ref, cols_ref, de_ref, gains_ref) = refs[:9]
    shards = refs[9 : 9 + count]
    outs = refs[9 + count :]
    z_ref, band_ref, a_ref, gp_ref, x2_ref = outs[:5]
    stored = outs[5:13]
    gathered = outs[13 : 13 + count]
    rest = outs[13 + count :]
    pix_ref, x_ref, qkv_ref, p_ref, inv_ref, oo_ref, x1_ref, o_s = rest[:8]
    h_s, s_s, high_s, low_s, de_s, store_sem, de_sem = rest[8:15]
    low = jnp.bfloat16
    step = pl.program_id(0)
    width = x_ref.shape[1]
    ee = width // heads
    groups = width // LANES
    expo = ee ** (-0.5) * 1.4426950408889634
    if chunks:
        peers, begin, events, finish = gather_events(
            count, chunks, 2, shards, gathered, rest[15 : 15 + GATHER_SEMS]
        )

    def gain(i):
        return gains_ref[i : i + 1, :]

    def store(i):
        return pltpu.make_async_copy(rest[i], stored[i], store_sem.at[i])

    def load_de():
        return pltpu.make_async_copy(gathered[1].at[2] if chunks else de_ref, de_s, de_sem)

    if chunks:

        @pl.when(step == 0)
        def _():
            greet(peers)
            begin()

        for at, event in zip((3, 6, 7, 8, 9, 10), events):
            pl.when(step == at)(event)

    @pl.when(step == 11)
    def _():
        if chunks:
            finish()
        load_de().start()

    @pl.when(step == 0)
    def _():
        split_table(table_ref, high_s, low_s)

        @pl.loop(0, pixels_ref.shape[0])
        def _(i):
            at = pl.ds(pl.multiple_of(i * K, K), K)
            hot = one_hot(keep_ref[i], pixels_ref.shape[1])
            pix_ref[at, :] = dot_nn(hot.astype(low), pixels_ref[i]).astype(low)
            band_ref[at, :] = jnp.sum(hot * bands_ref[i], -1, keepdims=True).astype(jnp.int32)
            x_ref[at, :] = look_up(hot, gsd_ref[i], high_s, low_s)

        store(0).start()

    @pl.when(step < 4)
    def _():
        pixel = pix_ref[...]
        x_ref[...] += dot_nn(jnp.where(band_ref[...] == step, pixel, jnp.zeros_like(pixel)), rows_ref[...])

    @pl.when(step == 4)
    def _():
        store(1).start()
        hat, _ = unit_rows(x_ref[...])
        h_s[...] = (hat * gain(0) + gain(1)).astype(low)

    @pl.when((step >= 4) & (step < 7))
    def _():
        at = pl.ds(pl.multiple_of((step - 4) * width, width), width)
        qkv_ref[:, at] = dot_nn(h_s[...], cols_ref[...]).astype(low)

    @pl.when(step == 7)
    def _():
        store(2).start()
        same = same_item()

        for n in range(x_ref.shape[0] // RUN * groups):
            attend(n, groups, RUN, width, ee, expo, same, qkv_ref, s_s.at[n % 2], p_ref, inv_ref, oo_ref, o_s)

        for i in (3, 4, 5, 7):
            store(i).start()
        x1_ref[...] = x_ref[...] + dot_nn(o_s[...], cols_ref[...])
        store(6).start()
        hat, _ = unit_rows(x1_ref[...])
        h_s[...] = (hat * gain(2) + gain(3)).astype(low)
        x2_ref[...] = x1_ref[...]

    @pl.when(step >= 8)
    def _():
        half = width // 2
        for t in range(2):
            at = slice(t * half, (t + 1) * half)
            u = dot_nn(h_s[...], cols_ref[:, at])
            cumul = 0.5 * (1.0 + lax.erf(u * 0.7071067811865476))
            a_ref[:, at] = (u * cumul).astype(low)
            gp_ref[:, at] = (cumul + u * jnp.exp(-0.5 * u * u) * 0.3989422804014327).astype(low)

        x2_ref[...] += dot_nn(a_ref[...], rows_ref[...])

    @pl.when(step == 11)
    def _():
        hat, _ = unit_rows(x2_ref[...])
        h_s[...] = (hat * gain(4) + gain(5)).astype(low)
        load_de().wait()
        z_ref[...] = dot_nn(h_s[...], de_s[...].reshape(width, z_ref.shape[1]))
        for i in range(8):
            store(i).wait()


def encoder_call(pixels, keep, bands, gsd, table, rows, cols, de, gains, heads, shards=()):
    width = cols.shape[0]
    tokens = keep.shape[0] * K
    low, f32 = jnp.bfloat16, jnp.float32
    runs = tokens // RUN * (width // LANES)
    wide = LANES // (width // heads) * RUN
    one = pl.Buffered(1)
    hbm = pl.BlockSpec(memory_space=pl.ANY)
    vmem = pltpu.VMEM
    chunks = (2, 2) if shards else ()
    views = [s.reshape(4, s.shape[0] // 4, s.shape[1]) for s in shards]
    if shards:
        narrow = shards[1].shape[1]
        de, de_shape = jnp.zeros((8, 128), low), (2, 4, 128, narrow)
    else:
        narrow, de_shape = de.shape[1], de.shape

    def whole(shape):
        return pl.BlockSpec(shape, lambda s: (0,) * len(shape), pipeline_mode=one)

    def row_block(s):
        return (jnp.where(s < 4, s + 4, jnp.where(s < 8, 0, s - 8)), 0)

    def column_block(s):
        return (0, jnp.where(s < 4, 0, s - 4))

    def hidden_block(s):
        return (0, jnp.where(s < 8, 0, s - 8))

    hidden = pl.BlockSpec((tokens, width), hidden_block)
    blocks = [
        ((tokens, narrow), f32, whole((tokens, narrow))),
        ((tokens, 1), jnp.int32, whole((tokens, 1))),
        ((tokens, 4 * width), low, hidden),
        ((tokens, 4 * width), low, hidden),
        ((tokens, width), f32, whole((tokens, width))),
    ]
    held = [
        ((tokens, pixels.shape[2]), low),
        ((tokens, width), f32),
        ((tokens, 3 * width), low),
        ((runs, RUN, wide), low),
        ((runs, RUN, LANES), f32),
        ((runs, RUN, LANES), f32),
        ((tokens, width), f32),
        ((tokens, width), low),
    ]
    struct = jax.ShapeDtypeStruct
    out = pl.pallas_call(
        functools.partial(encoder_kernel, heads, chunks),
        grid=(12,),
        in_specs=[
            whole(pixels.shape),
            whole(keep.shape),
            whole(bands.shape),
            whole(gsd.shape),
            pl.BlockSpec((table.shape[0], width), lambda s: (0, 0), pipeline_mode=one),
            pl.BlockSpec((width, width), row_block),
            pl.BlockSpec((width, width), column_block),
            hbm,
            whole(gains.shape),
        ]
        + [hbm] * len(views),
        out_specs=tuple(b[2] for b in blocks) + (hbm,) * (len(held) + len(views)),
        out_shape=tuple(struct(b[0], b[1]) for b in blocks)
        + tuple(struct(*h) for h in held)
        + tuple(struct((4, 2) + v.shape, low) for v in views),
        scratch_shapes=[vmem(*h) for h in held]
        + [
            vmem((tokens, width), low),
            vmem((2, wide, RUN), f32),
            vmem((table.shape[0], width), low),
            vmem((table.shape[0], width), low),
            vmem(de_shape, low),
            pltpu.SemaphoreType.DMA((8,)),
            pltpu.SemaphoreType.DMA,
        ]
        + (gather_scratch(2, sum(chunks)) if shards else []),
        compiler_params=pltpu.CompilerParams(
            dimension_semantics=("arbitrary",),
            vmem_limit_bytes=60 * 1024 * 1024,
            collective_id=2 if shards else None,
            has_side_effects=bool(shards),
        ),
        cost_estimate=pl.CostEstimate(
            flops=20_000_000_000, bytes_accessed=70_000_000, transcendentals=8_000_000
        ),
    )(pixels, keep, bands, gsd, table, rows, cols, de, gains, *views)
    z, band, a, gp, x2 = out[:5]
    pix, x, qkv, p, inv, oo, x1, o = out[5:13]
    saved = (x, qkv, p, inv, oo, x1, a, gp, x2, o)
    return z, pix, band, saved, [w.reshape(-1, w.shape[-1]) for w in out[13:]]


def encoder_back_kernel(
    heads, dz_ref, pix_ref, band_ref, x_ref, qkv_ref, p_ref, inv_ref, oo_ref, x1_ref, a_ref, gp_ref, x2_ref,
    rows_ref, cols_ref, de_ref, gains_ref,
    grows_ref, gcols_ref, gde_ref, ggains_ref,
    h_s, dx_s, dy_s, acc_s, do_s, dqkv_s, s_s, ds_s,
):
    low, f32 = jnp.bfloat16, jnp.float32
    step = pl.program_id(0)
    width = x_ref.shape[1]
    ee = width // heads
    groups = width // LANES
    runs = x_ref.shape[0] // RUN

    def gain(i):
        return gains_ref[i : i + 1, :]

    def back(x, grads, at):
        hat, scaled = unit_rows(x)
        ggains_ref[at : at + 1, :] = jnp.sum(grads * hat, 0, keepdims=True)
        ggains_ref[at + 1 : at + 2, :] = jnp.sum(grads, 0, keepdims=True)
        return unit_back(grads, hat, scaled, gain(at))

    def normed(x, at):
        hat, _ = unit_rows(x)
        h_s[...] = (hat * gain(at) + gain(at + 1)).astype(low)

    @pl.when(step == 0)
    def _():
        ggains_ref[...] = jnp.zeros_like(ggains_ref)
        normed(x2_ref[...], 4)
        gde_ref[...] = dot_tn(h_s[...], dz_ref[...]).astype(low)
        dx_s[...] = back(x2_ref[...], dot_nt(dz_ref[...], de_ref[...]), 4)
        dy_s[...] = dx_s[...].astype(low)
        normed(x1_ref[...], 2)
        acc_s[...] = jnp.zeros_like(acc_s)

    @pl.when(step < 4)
    def _():
        grows_ref[...] = dot_tn(a_ref[...], dy_s[...]).astype(low)
        du = (dot_nt(dy_s[...], rows_ref[...]) * gp_ref[...].astype(f32)).astype(low)
        do_s[...] = du
        gcols_ref[...] = dot_tn(h_s[...], du).astype(low)
        acc_s[...] += dot_nt(do_s[...], cols_ref[...])

    @pl.when(step == 4)
    def _():
        dx_s[...] += back(x1_ref[...], acc_s[...], 2)
        dy_s[...] = dx_s[...].astype(low)
        for run in range(runs):
            for g in range(groups):
                h_s[run * RUN : (run + 1) * RUN, g * LANES : (g + 1) * LANES] = oo_ref[
                    run * groups + g
                ].astype(low)
        gcols_ref[...] = dot_tn(h_s[...], dy_s[...]).astype(low)
        do_s[...] = dot_nt(dy_s[...], cols_ref[...]).astype(low)

        for n in range(runs * groups):
            attend_back(
                n, n, groups, RUN, width, ee, ee ** (-0.5), qkv_ref, s_s, ds_s, p_ref, inv_ref, oo_ref, do_s,
                dqkv_s,
            )

        normed(x_ref[...], 0)
        acc_s[...] = jnp.zeros_like(acc_s)

    @pl.when((step >= 5) & (step < 8))
    def _():
        at = pl.ds(pl.multiple_of((step - 5) * width, width), width)
        gcols_ref[...] = dot_tn(h_s[...], dqkv_s[:, at]).astype(low)
        acc_s[...] += dot_nt(dqkv_s[:, at], cols_ref[...])

    @pl.when(step == 8)
    def _():
        dx_s[...] += back(x_ref[...], acc_s[...], 0)
        dy_s[...] = dx_s[...].astype(low)

    @pl.when(step >= 8)
    def _():
        pixel = pix_ref[...]
        h_s[...] = jnp.where(band_ref[...] == step - 8, pixel, jnp.zeros_like(pixel))
        grows_ref[...] = dot_tn(h_s[...], dy_s[...]).astype(low)


def encoder_back_call(dz, pixel, band, saved, rows, cols, de, gains, heads):
    x, qkv, p, inv, oo, x1, a, gp, x2, _ = saved
    tokens, width = x.shape
    low, f32 = jnp.bfloat16, jnp.float32
    wide = p.shape[2]
    one = pl.Buffered(1)

    def whole(array):
        return pl.BlockSpec(array.shape, lambda s: (0,) * len(array.shape), pipeline_mode=one)

    def row_block(s):
        return (jnp.minimum(s, 3), 0)

    def column_block(s):
        return (0, jnp.where(s < 4, s + 4, jnp.where(s == 4, 3, jnp.minimum(s - 5, 2))))

    def hidden_block(s):
        return (0, jnp.minimum(s, 3))

    def grow_block(s):
        return (jnp.where(s < 4, s, jnp.where(s < 8, 3, s - 4)), 0)

    hidden = pl.BlockSpec((tokens, width), hidden_block)
    square = (width, width)
    outs = (
        jax.ShapeDtypeStruct(rows.shape, low),
        jax.ShapeDtypeStruct(cols.shape, low),
        jax.ShapeDtypeStruct(de.shape, low),
        jax.ShapeDtypeStruct((8, width), f32),
    )
    vmem = pltpu.VMEM
    return pl.pallas_call(
        functools.partial(encoder_back_kernel, heads),
        grid=(12,),
        in_specs=[
            whole(dz), whole(pixel), whole(band), whole(x), whole(qkv), whole(p), whole(inv), whole(oo),
            whole(x1), hidden, hidden, whole(x2),
            pl.BlockSpec(square, row_block), pl.BlockSpec(square, column_block),
            whole(de), whole(gains),
        ],
        out_specs=(
            pl.BlockSpec(square, grow_block),
            pl.BlockSpec(square, column_block),
            whole(outs[2]),
            whole(outs[3]),
        ),
        out_shape=outs,
        scratch_shapes=[
            vmem((tokens, width), low),
            vmem((tokens, width), f32),
            vmem((tokens, width), low),
            vmem((tokens, width), f32),
            vmem((tokens, width), low),
            vmem((tokens, 3 * width), low),
            vmem((wide, RUN), f32),
            vmem((RUN, wide), low),
        ],
        compiler_params=pltpu.CompilerParams(
            dimension_semantics=("arbitrary",), vmem_limit_bytes=60 * 1024 * 1024
        ),
        cost_estimate=pl.CostEstimate(
            flops=40_000_000_000, bytes_accessed=110_000_000, transcendentals=1_000_000
        ),
    )(dz, pixel, band, x, qkv, p, inv, oo, x1, a, gp, x2, rows, cols, de, gains)


def back_reduce_kernel(heads, kinds, work, pieces, refs_in, refs_out, *refs):
    low, f32 = jnp.bfloat16, jnp.float32
    ref = dict(zip(refs_in + refs_out, refs))
    rest = refs[len(refs_in) + len(refs_out) :]
    per = 9
    bufs = [rest[per * i : per * i + per] for i in range(len(kinds))]
    (sm, ss, ssx, dx, acc, xin, h, dy, wide, wt, wu, out_r, out_c, out_e, p_t, inv_t, oo_t, s_s, ds_s, gsum,
     cs, cr, ls, os, x1s, x1r, x2s, x2r, z_s, z_r, ags, agr, ks, sms, smr, sss, ssr, dma, att_sem) = rest[
        per * len(kinds) :
    ]
    g, z, c, xn, yn = place()
    dg = (xn + 2) % 4
    here = 2 * z + c
    sib = (g, 2 * z + 1 - c)
    right, up = (xn, here), (yn, here)
    zto = [(z + j) % 4 for j in (1, 2, 3)]
    zpeer = [(g, 2 * t + c) for t in zto]
    greet([sib, right, up] + zpeer)
    steps = len(work)
    sent = []
    from_slot = [[] for _ in range(steps)]

    def send(src, dst, send_sem, recv_sem, peer):
        return pltpu.make_async_remote_copy(
            src_ref=src, dst_ref=dst, send_sem=send_sem, recv_sem=recv_sem,
            device_id=peer, device_id_type=MESH_ID,
        )

    def guarded(test, action):
        if test is None:
            action()
        else:
            pl.when(test)(action)

    def go(copies, keep=None, tests=None):
        for i, copy in enumerate(copies):
            test = tests[i] if tests else None
            guarded(test, copy.start)
            (sent if keep is None else keep).append((test, copy))

    def left(entries):
        for test, copy in entries:
            guarded(test, copy.wait_send)

    def got(copies):
        for copy in copies:
            copy.wait_recv()

    def mine(k, at=None):
        base = work[k][2]
        at = z if at is None else at
        return None if base is None else ((at >= base) & (at < base + 2))

    def buffers(k):
        kind, at = work[k][:2]
        return bufs[kind], at, at % kinds[kind][4], kinds[kind][2] // 2

    def c_copies(k):
        (_, crecv, *_), at, _, _ = buffers(k)
        return [
            send(
                ref[array].at[:, 1 - c, :, cut[0], cut[1]], crecv.at[at, pl.ds(z0, nz)],
                cs.at[k, i], cr.at[k, i], sib,
            )
            for i, (array, z0, nz, cut) in enumerate(work[k][3])
        ]

    def own_copies(k):
        (s, *_), _, slot, _ = buffers(k)
        return [
            pltpu.make_async_copy(
                ref[array].at[:, c, :, cut[0], cut[1]], s.at[slot, pl.ds(z0, nz)], os.at[k, i]
            )
            for i, (array, z0, nz, cut) in enumerate(work[k][3])
        ]

    def recv_load(k, i):
        (_, crecv, tmp, *_), at, _, _ = buffers(k)
        return pltpu.make_async_copy(crecv.at[at, i], tmp.at[i % 2], ls.at[k, i])

    def x1_copies(k):
        (s, _, _, xa, yb, *_), at, slot, half = buffers(k)
        lo, hi = pl.ds(0, half), pl.ds(half, half)
        return [
            send(s.at[slot, :, xn, :, lo], xa.at[at, 0], x1s.at[k, 0], x1r.at[k, 0], right),
            send(s.at[slot, :, dg, :, lo], xa.at[at, 1], x1s.at[k, 1], x1r.at[k, 1], right),
            send(s.at[slot, :, yn, :, hi], yb.at[at, 0], x1s.at[k, 2], x1r.at[k, 2], up),
            send(s.at[slot, :, dg, :, hi], yb.at[at, 1], x1s.at[k, 3], x1r.at[k, 3], up),
        ]

    def x2_copies(k):
        (s, _, _, _, _, xb, ya, *_), at, slot, half = buffers(k)
        lo, hi = pl.ds(0, half), pl.ds(half, half)
        return [
            send(s.at[slot, :, yn, :, lo], ya.at[at], x2s.at[k, 0], x2r.at[k, 0], up),
            send(s.at[slot, :, xn, :, hi], xb.at[at], x2s.at[k, 1], x2r.at[k, 1], right),
        ]

    def z_copies(k):
        (s, *_, zb, _), at, slot, _ = buffers(k)
        base = work[k][2] or 0
        return [
            send(
                s.at[slot, (zto[j] - base) % kinds[work[k][0]][0], g], zb.at[at, j],
                z_s.at[k, j], z_r.at[k, j], zpeer[j],
            )
            for j in range(3)
        ]

    def out_at(k, q, part=None):
        name, cut = work[k][4:6]
        if part is not None:
            cut = halves(cut)[part]
        return ref[name].at[q, cut[0], cut[1]]

    def ag_copies(k):
        (*_, fin), at, _, _ = buffers(k)
        return [
            send(fin.at[at], out_at(k, g), ags.at[k, 0], agr.at[k, 0], right),
            send(fin.at[at], out_at(k, g), ags.at[k, 1], agr.at[k, 1], up),
        ]

    def keep_copy(k):
        (*_, fin), at, _, _ = buffers(k)
        return pltpu.make_async_copy(fin.at[at], out_at(k, g), ks.at[k])

    def fwd_copies(k, of_x, of_y):
        return [
            send(out_at(k, of_x, 0), out_at(k, of_x, 0), ags.at[k, 2], agr.at[k, 2], up),
            send(out_at(k, of_y, 1), out_at(k, of_y, 1), ags.at[k, 3], agr.at[k, 3], right),
        ]

    def add_half(k, q, first, other):
        (s, *_), _, slot, half = buffers(k)
        part = pl.ds(0 if first else half, half)

        @pl.loop(0, kinds[work[k][0]][0])
        def _(i):
            s[slot, i, q, :, part] = (s[slot, i, q, :, part].astype(f32) + other[i].astype(f32)).astype(low)

    def load(k):
        kind, at = work[k][:2]
        slots = kinds[kind][4]
        if at >= slots:
            before = [j for j in range(steps) if work[j][:2] == (kind, at - slots)][0]
            left(from_slot[before])
            from_slot[before].clear()
        for copy in own_copies(k):
            copy.start()

    def pair(k):
        (s, _, tmp, *_), _, slot, _ = buffers(k)
        count = kinds[work[k][0]][0]
        got(c_copies(k))
        for i in range(2):
            recv_load(k, i).start()
        for copy in own_copies(k):
            copy.wait()
        for i in range(count):
            recv_load(k, i).wait()

            @pl.loop(0, 4)
            def _(q):
                s[slot, i, q] = (s[slot, i, q].astype(f32) + tmp[i % 2, q].astype(f32)).astype(low)

            if i + 2 < count:
                recv_load(k, i + 2).start()
        go(x1_copies(k), from_slot[k])

    def first_half(k):
        (_, _, _, xa, yb, *_), at, _, _ = buffers(k)
        got(x1_copies(k))
        add_half(k, yn, True, xa.at[at, 1])
        add_half(k, xn, False, yb.at[at, 1])
        go(x2_copies(k), from_slot[k])
        add_half(k, g, True, xa.at[at, 0])
        add_half(k, g, False, yb.at[at, 0])

    def second_half(k):
        (_, _, _, _, _, xb, ya, *_), at, _, _ = buffers(k)
        got(x2_copies(k))
        add_half(k, g, True, ya.at[at])
        add_half(k, g, False, xb.at[at])
        go(z_copies(k), from_slot[k], [mine(k, t) for t in zto])

    def finish(k):
        def act():
            (s, *_, zb, fin), at, slot, _ = buffers(k)
            got(z_copies(k))
            base = work[k][2] or 0
            total = s[slot, (z - base) % kinds[work[k][0]][0], g].astype(f32)
            for j in range(3):
                total = total + zb[at, j].astype(f32)
            fin[at] = total.astype(low)
            keep_copy(k).start()
            square = fin[at].astype(f32)
            square = square * square
            for i in range(square.shape[1] // ss.shape[1]):
                ss[...] += jnp.sum(
                    square[:, i * ss.shape[1] : (i + 1) * ss.shape[1]], 0, keepdims=True
                )

        guarded(mine(k), act)
        go(ag_copies(k), None, [mine(k)] * 2)

    def collect(k):
        guarded(mine(k), lambda: got(ag_copies(k)))
        go(fwd_copies(k, xn, yn), None, [mine(k)] * 2)

    def close(k):
        guarded(mine(k), lambda: got(fwd_copies(k, dg, dg)))

    stages = [load, pair, first_half, second_half, finish, collect, close]

    def share_rounds(value, sem_s, sem_r, store):
        def copy(i, slot, peer):
            return send(value.at[slot], value.at[4 + i], sem_s.at[i], sem_r.at[i], peer)

        def round_pair(i, peer, following):
            got([copy(i, i, peer)])
            value[i + 1] = value[i] + value[4 + i]
            go(following())

        def last():
            return [copy(3 + j, 3, zpeer[j]) for j in range(3)]

        def end():
            got(last())
            total = None
            for at in range(4):
                term = jnp.where(z == at, value[3], jnp.zeros_like(value[3]))
                for j in range(3):
                    term = term + jnp.where((z + 3 - j) % 4 == at, value[7 + j], jnp.zeros_like(value[3]))
                total = term if total is None else total + term
            store[...] = total

        return [
            lambda: go([copy(0, 0, sib)]),
            lambda: round_pair(0, sib, lambda: [copy(1, 1, right)]),
            lambda: round_pair(1, right, lambda: [copy(2, 2, up)]),
            lambda: round_pair(2, up, last),
            end,
        ]

    tokens, width = dx.shape
    ee = width // heads
    groups = width // LANES
    runs = tokens // RUN
    gains = ref["gains"]

    moving = {}

    def move(name, src, dst):
        copy = pltpu.make_async_copy(src, dst, dma.at[lanes_of.index(name)])
        copy.start()
        moving[name] = copy

    def done(*names):
        for name in names:
            if name in moving:
                moving.pop(name).wait()

    lanes_of = (
        "a", "gp", "rows", "cols", "x", "dz", "de", "o", "qkv", "pix", "out_r", "out_c", "out_e",
    )

    def tile(i):
        return pl.ds(i * width, width)

    def gain(i):
        return gains[i : i + 1, :]

    def back(grads, at):
        hat, scaled = unit_rows(xin[...])
        gsum[at : at + 1, :] = jnp.sum(grads * hat, 0, keepdims=True)
        gsum[at + 1 : at + 2, :] = jnp.sum(grads, 0, keepdims=True)
        return unit_back(grads, hat, scaled, gain(at))

    def normed(at):
        hat, _ = unit_rows(xin[...])
        h[...] = (hat * gain(at) + gain(at + 1)).astype(low)

    def column_grads(block, source):
        done("out_c")
        for d in range(8):
            value = dot_tn(h[:, d * 128 : (d + 1) * 128], source()).astype(low)
            out_c[d // 2, d % 2] = value.reshape(out_c.shape[2:])
        move("out_c", out_c, ref["g_cols"].at[:, :, :, :, tile(block)])

    def load_hidden(s):
        move("a", ref["a"].at[:, tile(s)], wide.at[:, tile(0)])
        move("gp", ref["gp"].at[:, tile(s)], wide.at[:, tile(1)])
        move("rows", ref["rows"].at[tile(s)], wt)

    def load_columns(block):
        move("cols", ref["cols"].at[:, tile(block)], wu)

    narrow = ref["dz"].shape[1]

    def first_loads():
        move("x", ref["x2"], xin)
        move("dz", ref["dz"], wide.at[:, pl.ds(2 * width, narrow)])
        move("de", ref["dec_rows"].at[pl.ds(2 * width, width)], wt.at[:, pl.ds(0, narrow)])
        move("a", ref["a"].at[:, tile(0)], wide.at[:, tile(0)])
        move("gp", ref["gp"].at[:, tile(0)], wide.at[:, tile(1)])
        load_columns(4)

    def head_piece(_):
        done("x", "dz", "de")
        dz = wide[:, 2 * width : 2 * width + narrow]
        normed(4)
        for d in range(8):
            out_e[0, d // 4, d % 4] = dot_tn(h[:, d * 128 : (d + 1) * 128], dz).astype(low)
        move("out_e", out_e, ref["g_de"])
        dx[...] = back(dot_nt(dz, wt[:, :narrow]), 4)
        move("rows", ref["rows"].at[tile(0)], wt)
        move("x", ref["x1"], xin)
        dy[...] = dx[...].astype(low)
        done("x")
        normed(2)
        acc[...] = jnp.zeros_like(acc)

    def hidden_piece(s):
        done("a", "gp", "rows", "out_r")
        wide[:, 2 * width :] = (dot_nt(dy[...], wt[...]) * wide[:, width : 2 * width].astype(f32)).astype(low)
        for q in range(4):
            out_r[q] = dot_tn(wide[:, q * 256 : (q + 1) * 256], dy[...]).astype(low)
        move("out_r", out_r, ref["g_down"].at[s // 2, s % 2])
        if s < 3:
            load_hidden(s + 1)
        column_grads(4 + s, lambda: wide[:, 2 * width :])
        done("cols")
        acc[...] += dot_nt(wide[:, 2 * width :], wu[...])
        load_columns(5 + s if s < 3 else 3)
        if s == 3:
            move("o", ref["o"], h)
            move("qkv", ref["qkv"], wide)

    def middle_piece(_):
        dx[...] += back(acc[...], 2)
        dy[...] = dx[...].astype(low)
        move("x", ref["x"], xin)
        done("o")
        column_grads(3, lambda: dy[...])
        done("cols")
        h[...] = dot_nt(dy[...], wu[...]).astype(low)
        load_columns(0)
        done("qkv")

    def attention_loads(n):
        slot = n % 2
        return [
            pltpu.make_async_copy(ref[name].at[n], buf.at[slot], att_sem.at[slot, i])
            for i, (name, buf) in enumerate((("p", p_t), ("inv", inv_t), ("oo", oo_t)))
        ]

    def attention_piece(part):
        count = runs * groups // 4
        first = part * count
        for copy in attention_loads(first):
            copy.start()

        for n in range(first, first + count):
            for copy in attention_loads(n):
                copy.wait()
            if n + 1 < first + count:
                for copy in attention_loads(n + 1):
                    copy.start()
            attend_back(
                n, n % 2, groups, RUN, width, ee, ee ** (-0.5), wide, s_s.at[n % 2], ds_s.at[n % 2], p_t, inv_t,
                oo_t, h, wide,
            )

    def input_piece(t):
        if t == 0:
            done("x")
            normed(0)
            acc[...] = jnp.zeros_like(acc)
        column_grads(t, lambda: wide[:, t * width : (t + 1) * width])
        done("cols")
        acc[...] += dot_nt(wide[:, t * width : (t + 1) * width], wu[...])
        if t < 2:
            load_columns(t + 1)
        else:
            move("pix", ref["pix"], h)

    def first_piece(_):
        dx[...] += back(acc[...], 0)
        dy[...] = dx[...].astype(low)
        sm[0] = ref["small"][...]
        sm[0, 0:6, :] = gsum[0:6, :]

    def embed_piece(b):
        done("pix", "out_r")
        for q in range(4):
            part = h[:, q * 256 : (q + 1) * 256]
            part = jnp.where(ref["band"][...] == b, part, jnp.zeros_like(part))
            out_r[q] = dot_tn(part, dy[...]).astype(low)
        move("out_r", out_r, ref["g_emb"].at[b // 2, b % 2])

    action = {
        "head": head_piece, "hidden": hidden_piece, "middle": middle_piece, "attention": attention_piece,
        "input": input_piece, "first": first_piece, "embed": embed_piece,
    }

    ss[...] = jnp.zeros_like(ss)
    gsum[...] = jnp.zeros_like(gsum)
    small_rounds = share_rounds(sm, sms, smr, ref["small_out"])
    square_rounds = share_rounds(ssx, sss, ssr, ref["ss_out"])
    ends = [w[6] + 6 for w in work]
    last = max(ends)
    squared = max(w[6] + 4 for w in work)
    compute_end = max(t for t, _, _ in pieces)
    for t in range(last + 1):
        for i in (1, 6, 5, 4, 3, 2, 0):
            for k in range(steps):
                if work[k][6] + i == t:
                    stages[i](k)
        if t == 0:
            first_loads()
        done("out_r", "out_c", "out_e")
        for k in range(steps):
            if work[k][7] == t:
                go(c_copies(k))
        for at, name, argument in pieces:
            if at == t:
                action[name](argument)
        if compute_end < t <= compute_end + 5:
            small_rounds[t - compute_end - 1]()
        if t == squared:
            ssx[0] = jnp.broadcast_to(jnp.sum(ss[...], keepdims=True).reshape(1, 1), ssx.shape[1:])
            square_rounds[0]()
        if squared < t < last:
            square_rounds[t - squared]()
        if t == last:
            for following in square_rounds[last - squared :]:
                following()
    for k in range(steps):
        left(from_slot[k])
    left(sent)
    for k in range(steps):
        guarded(mine(k), keep_copy(k).wait)


def back_reduce_call(dz, pix, band, saved, rows, cols, dec_rows, gains, dcols, ddown, dhead, small, heads):
    x, qkv, p, inv, oo, x1, a, gp, x2, o = saved
    tokens, width = x.shape
    low, f32 = jnp.bfloat16, jnp.float32
    narrow = dec_rows.shape[1]
    ins = dict(
        dz=dz, pix=pix, band=band, x=x, x1=x1, x2=x2, qkv=qkv, p=p, inv=inv, oo=oo, o=o, a=a, gp=gp,
        rows=rows, cols=cols, dec_rows=dec_rows, gains=gains, small=small,
        d_cols=dcols.reshape(4, 2, 4, 16, dcols.shape[1]),
        d_down=ddown.reshape(2, 2, 4, 128, narrow),
        d_head=dhead.reshape(1, 2, 4, 128, narrow),
    )
    outs = dict(
        erows=((4, 256, width), low), ecols=((4, 32, cols.shape[1]), low),
        dcols=((4, 16, dcols.shape[1]), low), drows=((4, 128, narrow), low),
        small_out=(small.shape, f32), ss_out=((8, 128), f32),
        g_down=((2, 2, 4, 256, width), low), g_emb=((2, 2, 4, 256, width), low),
        g_cols=((4, 2, 4, 32, cols.shape[1]), low), g_de=((1, 2, 4, 128, narrow), low),
    )
    kinds = ((4, 32, 1024, 16, 6), (4, 16, 2048, 2, 2), (4, 64, 512, 2, 2))

    def column_chunk(at, block):
        cut = (slice(0, 32), slice(block * 1024, (block + 1) * 1024))
        return (0, at, None, (("g_cols", 0, 4, cut),), "ecols", cut)

    def row_chunk(at, i):
        cut = (slice(i * 32, (i + 1) * 32), slice(0, width))
        return (0, at, None, (("g_down", 0, 2, cut), ("g_emb", 2, 2, cut)), "erows", cut)

    chunks = []
    for i in range(2):
        cut = (slice(0, 16), slice(i * 2048, (i + 1) * 2048))
        chunks.append((1, i, None, (("d_cols", 0, 4, cut),), "dcols", cut))
    for i in range(2):
        cut = (slice(i * 64, (i + 1) * 64), slice(0, narrow))
        sources = (("d_down", 0, 2, cut), ("g_de", 2, 1, cut), ("d_head", 3, 1, cut))
        chunks.append((2, i, None, sources, "drows", cut))
    chunks += [column_chunk(i, 4 + i) for i in range(4)]
    chunks += [column_chunk(4 + i, block) for i, block in enumerate((3, 0, 1, 2))]
    chunks += [row_chunk(8 + i, i) for i in range(8)]
    starts = (0, 1, 3, 4, 5, 6, 7, 8, 9, 11, 12, 13) + tuple(range(14, 22))
    begins = (0, 0, 2, 2, 3, 4, 5, 6, 7, 10, 10, 11) + tuple(range(13, 21))
    work = tuple(chunk + (starts[i], begins[i]) for i, chunk in enumerate(chunks))
    pieces = [(1, "head", 0)] + [(2 + s, "hidden", s) for s in range(4)] + [(6, "middle", 0)]
    pieces += [(7 + i // 2, "attention", i) for i in range(4)]
    pieces += [(9, "input", 0), (9, "input", 1), (10, "input", 2), (10, "first", 0)]
    pieces += [(11 + i // 2, "embed", i) for i in range(4)]
    steps = len(work)
    hbm = pl.BlockSpec(memory_space=pl.ANY)
    vm = pl.BlockSpec(memory_space=pltpu.VMEM)
    vmem, sems = pltpu.VMEM, pltpu.SemaphoreType.DMA
    scratch, landing = [], {}
    for i, (nz, r, col, count, slots) in enumerate(kinds):
        landing[f"land{i}"] = ((count, nz, 4, r, col), low)
        half = col // 2
        scratch += [
            vmem((slots, nz, 4, r, col), low),
            None,
            vmem((2, 4, r, col), low),
            vmem((count, 2, nz, r, half), low),
            vmem((count, 2, nz, r, half), low),
            vmem((count, nz, r, half), low),
            vmem((count, nz, r, half), low),
            vmem((count, 3, r, col), low),
            vmem((count, r, col), low),
        ]
    outs.update(landing)
    in_names, out_names = tuple(ins), tuple(outs)

    def kernel(*refs):
        n = len(in_names) + len(out_names)
        ref = dict(zip(in_names + out_names, refs))
        kept = list(refs[n:])
        for i in range(len(kinds)):
            kept.insert(9 * i + 1, ref[f"land{i}"])
        back_reduce_kernel(heads, kinds, work, pieces, in_names, out_names, *refs[:n], *kept)

    result = pl.pallas_call(
        kernel,
        out_shape=tuple(jax.ShapeDtypeStruct(*outs[name]) for name in out_names),
        in_specs=[vm if name in ("band", "gains", "small") else hbm for name in in_names],
        out_specs=tuple(vm if name in ("small_out", "ss_out") else hbm for name in out_names),
        scratch_shapes=[s for s in scratch if s is not None]
        + [
            vmem((10,) + small.shape, f32),
            vmem((1, 512), f32),
            vmem((10, 8, 128), f32),
            vmem((tokens, width), f32),
            vmem((tokens, width), f32),
            vmem((tokens, width), f32),
            vmem((tokens, width), low),
            vmem((tokens, width), low),
            vmem((tokens, 3 * width), low),
            vmem((width, width), low),
            vmem((width, width), low),
            vmem((4, 256, width), low),
            vmem((4, 2, 4, 32, width), low),
            vmem((1, 2, 4, 128, narrow), low),
            vmem((2,) + p.shape[1:], low),
            vmem((2,) + inv.shape[1:], f32),
            vmem((2,) + oo.shape[1:], f32),
            vmem((2, p.shape[2], RUN), f32),
            vmem((2, RUN, p.shape[2]), low),
            vmem((8, width), f32),
            sems((steps, 3)), sems((steps, 3)), sems((steps, 4)), sems((steps, 3)),
            sems((steps, 4)), sems((steps, 4)),
            sems((steps, 2)), sems((steps, 2)),
            sems((steps, 3)), sems((steps, 3)),
            sems((steps, 4)), sems((steps, 4)),
            sems((steps,)), sems((6,)), sems((6,)), sems((6,)), sems((6,)), sems((13,)), sems((2, 3)),
        ],
        compiler_params=pltpu.CompilerParams(
            collective_id=1, has_side_effects=True, vmem_limit_bytes=63 * 1024 * 1024
        ),
    )(*ins.values())
    got = dict(zip(out_names, result))
    shards = [got[name].reshape(-1, got[name].shape[-1]) for name in ("ecols", "erows", "dcols", "drows")]
    return shards, got["small_out"], got["ss_out"]


def adam_step(master, moment, square, grad, factor, fix_one, fix_two, decay, rate):
    clipped = grad * factor
    moment_new = beta_first * moment + (1.0 - beta_first) * clipped
    square_new = beta_second * square + (1.0 - beta_second) * clipped * clipped
    direction = moment_new / fix_one / (jnp.sqrt(square_new / fix_two) + adam_eps) + decay * master
    return (clipped, square_new, master - rate * direction)


def adam_kernel(count_e, count_d, *refs):
    scal_ref, small_ref, ss_ref = refs[:3]
    ins, outs = refs[3:25], refs[25:]
    small = small_ref[...]
    width = small.shape[1]
    flat = lax.broadcasted_iota(jnp.int32, small.shape, 0) * width + lax.broadcasted_iota(
        jnp.int32, small.shape, 1
    )
    gains = jnp.where(flat < count_e + count_d, small, 0.0)
    norm = jnp.sqrt(ss_ref[0:1, 0:1] + jnp.sum(gains * gains, keepdims=True).reshape(1, 1))
    factor = clip_level / jnp.maximum(norm, clip_level)
    masked, fix_one, fix_two = scal_ref[0, 0], scal_ref[0, 1], scal_ref[0, 2]

    def update(grad, master, moment, square, decay, rate):
        return adam_step(master, moment, square, grad, factor, fix_one, fix_two, decay, rate)

    for i in range(4):
        grad, master, moment, square = ins[4 * i : 4 * i + 4]
        got = update(
            grad[...].astype(jnp.float32), master[...], moment[...], square[...], weight_decay, learn_rate
        )
        for target, value in zip(outs[3 * i : 3 * i + 3], got):
            target[...] = value

    @pl.when(pl.program_id(0) == 0)
    def _():
        at = 0
        for i in range(2):
            master, moment, square = ins[16 + 3 * i : 19 + 3 * i]
            rows, columns = master.shape
            for r in range(rows):
                row, lane = at // width, at % width
                grad = small[row : row + 1, lane : lane + columns]
                one = slice(r, r + 1)
                got = update(grad, master[one, :], moment[one, :], square[one, :], 0.0, gain_rate)
                for target, value in zip(outs[12 + 3 * i : 15 + 3 * i], got):
                    target[one, :] = value
                at += columns
        outs[18][...] = small[at // width : at // width + 1, at % width : at % width + 1] / masked
        outs[19][...] = norm


def adam_call(scal, small, squares, matrices, gains):
    steps = 4

    def block(array):
        rows, columns = array.shape
        if rows // steps % 16 == 0:
            return pl.BlockSpec((rows // steps, columns), lambda s: (s, 0))
        return pl.BlockSpec((rows, columns // steps), lambda s: (0, s))

    def whole(array):
        return pl.BlockSpec(array.shape, lambda s: (0, 0))

    struct = jax.ShapeDtypeStruct
    f32 = jnp.float32
    ins, in_specs, outs, out_specs = [], [], [], []
    for group in matrices:
        ins += group
        in_specs += [block(array) for array in group]
        outs += [struct(group[1].shape, f32)] * 3
        out_specs += [block(group[1])] * 3
    for group in gains:
        ins += group
        in_specs += [whole(array) for array in group]
        outs += [struct(group[0].shape, f32)] * 3
        out_specs += [whole(group[0])] * 3
    outs += [struct((1, 1), f32)] * 2
    out_specs += [pl.BlockSpec((1, 1), lambda s: (0, 0))] * 2
    out = pl.pallas_call(
        functools.partial(adam_kernel, gains[0][0].size, gains[1][0].size),
        grid=(steps,),
        in_specs=[pl.BlockSpec(memory_space=pltpu.SMEM), whole(small), whole(squares)] + in_specs,
        out_specs=tuple(out_specs),
        out_shape=tuple(outs),
        compiler_params=pltpu.CompilerParams(
            dimension_semantics=("arbitrary",), vmem_limit_bytes=56 * 1024 * 1024
        ),
    )(scal, small, squares, *ins)
    return tuple(out[:18]) + (out[18][0, 0], out[19][0, 0])


def body(
    pixels,
    keep_index,
    band_group,
    gsd_index,
    gsd_table,
    group_items,
    step_count,
    enc_cols,
    enc_rows,
    dec_cols,
    dec_rows,
    enc_gains,
    dec_gains,
    moment_ecols,
    moment_erows,
    moment_dcols,
    moment_drows,
    moment_egains,
    moment_dgains,
    square_ecols,
    square_erows,
    square_dcols,
    square_drows,
    square_egains,
    square_dgains,
):
    n_grp = lax.axis_size("grp")
    grp_at = lax.axis_index("grp")

    def gather_rows(master):
        rows = master.shape[0]
        if rows % (16 * n_grp):
            return lax.all_gather(to_low(master), "dp", axis=0, tiled=True)
        part = rows // n_grp
        mine = lax.dynamic_slice_in_dim(master, grp_at * part, part, 0)
        return lax.all_gather(to_low(mine), ("dp", "grp"), axis=0, tiled=True)

    direct = (n_grp, lax.axis_size("dp")) == (4, 8)
    own_count = jnp.sum(group_items.astype(jnp.float32))
    if direct:
        (whole_rows, whole_cols), total_count = gather_call(
            [to_low(enc_rows), to_low(enc_cols)], own_count, (4, 4), 2, 0
        )
    else:
        total_count = lax.psum(own_count, "grp")
        whole_rows, whole_cols = gather_rows(enc_rows), gather_rows(enc_cols)
    masked = total_count * (L - K)
    count_steps = step_count[0].astype(jnp.float32)
    fix_one = 1.0 - beta_first**count_steps
    fix_two = 1.0 - beta_second**count_steps
    keep_rows = keep_index[0]
    batch = keep_rows.shape[0]
    keep_column = keep_rows[..., None]
    band_row = band_group[0][:, None, :].astype(jnp.float32)
    gsd_row = gsd_index[0][:, None, :].astype(jnp.float32)
    if direct:
        shards, dec_embed = (to_low(dec_cols), to_low(dec_rows)), None
    else:
        dec_copy, dec_whole = gather_rows(dec_cols), gather_rows(dec_rows)
        shards, dec_embed = (), dec_whole[DFF : DFF + D]
    latent, kept_pixels, kept_bands, saved, gathered = encoder_call(
        pixels[0],
        keep_column,
        band_row,
        gsd_row,
        gsd_table[0],
        whole_rows,
        whole_cols,
        dec_embed,
        enc_gains,
        HEADS,
        shards,
    )
    if direct:
        dec_copy, dec_whole = gathered
    latent = latent.reshape(batch, K, -1)
    first_item = lax.axis_index("dp") * batch
    valid = (first_item + jnp.arange(batch, dtype=jnp.int32) < group_items[0]).astype(jnp.float32)
    scal = jnp.stack([valid / PIX, valid * (2.0 / PIX) / masked])
    grad_latent, grad_dcols, grad_ddown, grad_head, dec_sums, loss_local = decoder_call(
        scal,
        latent,
        keep_column,
        gsd_row,
        gsd_table[0],
        pixels[0],
        dec_copy,
        dec_whole,
        dec_gains,
        DHEADS,
    )
    loss_local = loss_local[0, 0]
    grad_latent = grad_latent.reshape(batch * K, -1)
    grad_dgains = dec_sums[:7]

    def reduce_rows(pieces, axis):
        whole = jnp.concatenate([to_low(piece) for piece in pieces], axis)
        return lax.psum_scatter(whole, "dp", scatter_dimension=0, tiled=True)

    if direct:
        count_e, count_d = enc_gains.size, grad_dgains.size
        flat = jnp.concatenate([grad_dgains.reshape(-1), loss_local[None]])
        small = jnp.pad(flat, (count_e, 16 * D - count_e - flat.shape[0])).reshape(16, D)
        shards, small, squares = back_reduce_call(
            grad_latent,
            kept_pixels,
            kept_bands,
            saved,
            whole_rows,
            whole_cols,
            dec_whole,
            enc_gains,
            grad_dcols,
            grad_ddown,
            grad_head,
            small,
            HEADS,
        )
        matrices = (
            [shards[0], enc_cols, moment_ecols, square_ecols],
            [shards[1], enc_rows, moment_erows, square_erows],
            [shards[2], dec_cols, moment_dcols, square_dcols],
            [shards[3], dec_rows, moment_drows, square_drows],
        )
        gains = ([enc_gains, moment_egains, square_egains], [dec_gains, moment_dgains, square_dgains])
        return adam_call(
            jnp.stack([masked, fix_one, fix_two]).reshape(1, 3), small, squares, matrices, gains
        )
    else:
        grad_erows, grad_ecols, grad_dembed, enc_sums = encoder_back_call(
            grad_latent,
            kept_pixels,
            kept_bands,
            saved,
            whole_rows,
            whole_cols,
            dec_embed,
            enc_gains,
            HEADS,
        )
        grad_egains = enc_sums[:6]
        drows = (grad_ddown, grad_dembed, grad_head)
        enc_sum, dec_sum, loss_sum = lax.psum((grad_egains, grad_dgains, loss_local), ("grp", "dp"))
        shards = tuple(
            lax.psum(reduce_rows(pieces, 0), "grp").astype(jnp.float32)
            for pieces in ((grad_ecols,), (grad_erows,), (grad_dcols,), drows)
        )
        shard_squares = lax.psum(sum((jnp.sum(piece * piece) for piece in shards)), "dp")
    loss = loss_sum / masked
    grad_norm = jnp.sqrt(shard_squares + jnp.sum(enc_sum * enc_sum) + jnp.sum(dec_sum * dec_sum))
    factor = clip_level / jnp.maximum(grad_norm, clip_level)
    clipped_ecols, squares_ecols, updated_ecols = adam_step(
        enc_cols,
        moment_ecols,
        square_ecols,
        shards[0],
        factor,
        fix_one,
        fix_two,
        weight_decay,
        learn_rate,
    )
    clipped_erows, squares_erows, updated_erows = adam_step(
        enc_rows,
        moment_erows,
        square_erows,
        shards[1],
        factor,
        fix_one,
        fix_two,
        weight_decay,
        learn_rate,
    )
    clipped_dcols, squares_dcols, updated_dcols = adam_step(
        dec_cols,
        moment_dcols,
        square_dcols,
        shards[2],
        factor,
        fix_one,
        fix_two,
        weight_decay,
        learn_rate,
    )
    clipped_drows, squares_drows, updated_drows = adam_step(
        dec_rows,
        moment_drows,
        square_drows,
        shards[3],
        factor,
        fix_one,
        fix_two,
        weight_decay,
        learn_rate,
    )
    clipped_egains, squares_egains, updated_egains = adam_step(
        enc_gains, moment_egains, square_egains, enc_sum, factor, fix_one, fix_two, 0.0, gain_rate
    )
    clipped_dgains, squares_dgains, updated_dgains = adam_step(
        dec_gains, moment_dgains, square_dgains, dec_sum, factor, fix_one, fix_two, 0.0, gain_rate
    )
    return (
        clipped_ecols,
        squares_ecols,
        updated_ecols,
        clipped_erows,
        squares_erows,
        updated_erows,
        clipped_dcols,
        squares_dcols,
        updated_dcols,
        clipped_drows,
        squares_drows,
        updated_drows,
        clipped_egains,
        squares_egains,
        updated_egains,
        clipped_dgains,
        squares_dgains,
        updated_dgains,
        loss,
        grad_norm,
    )


def solution(mesh):
    return jax.shard_map(
        body,
        mesh=mesh,
        in_specs=(
            P("grp", "dp", None, None),
            P("grp", "dp", None),
            P("grp", "dp", None),
            P("grp", "dp", None),
            P("grp", None, None),
            P("grp"),
            P(),
            P("dp", None),
            P("dp", None),
            P("dp", None),
            P("dp", None),
            P(),
            P(),
            P("dp", None),
            P("dp", None),
            P("dp", None),
            P("dp", None),
            P(),
            P(),
            P("dp", None),
            P("dp", None),
            P("dp", None),
            P("dp", None),
            P(),
            P(),
        ),
        out_specs=(
            P("dp", None),
            P("dp", None),
            P("dp", None),
            P("dp", None),
            P("dp", None),
            P("dp", None),
            P("dp", None),
            P("dp", None),
            P("dp", None),
            P("dp", None),
            P("dp", None),
            P("dp", None),
            P(),
            P(),
            P(),
            P(),
            P(),
            P(),
            P(),
            P(),
        ),
        check_vma=False,
    )
```

```python
import functools

import jax
import jax.numpy as jnp
from jax import lax
from jax.experimental import pallas as pl
from jax.experimental.pallas import tpu as pltpu
from jax.sharding import PartitionSpec as P

D = 1024
HEADS = 16
FF = 4096
DHEADS = 16
DFF = 2048
PIX = 1024
NBG = 4
L = 256
K = 64


norm_eps = 1e-06
clip_level = 0.005
learn_rate = 0.02
gain_rate = 0.25
weight_decay = 0.05
adam_eps = 1e-08
beta_first = 0.5
beta_second = 0.5


def to_low(value):
    return value.astype(jnp.bfloat16)


def project(inputs, matrix):
    return jnp.einsum("...n,nm->...m", inputs, matrix, preferred_element_type=jnp.float32)


def dot_nn(a, b):
    return lax.dot_general(a, b, (((1,), (0,)), ((), ())), preferred_element_type=jnp.float32)


def dot_nt(a, b):
    return lax.dot_general(a, b, (((1,), (1,)), ((), ())), preferred_element_type=jnp.float32)


def dot_tn(a, b):
    return lax.dot_general(a, b, (((0,), (0,)), ((), ())), preferred_element_type=jnp.float32)


def unit_rows(values):
    centred = values - jnp.mean(values, -1, keepdims=True)
    scaled = lax.rsqrt(jnp.mean(centred * centred, -1, keepdims=True) + norm_eps)
    return centred * scaled, scaled


def unit_back(grads, hat, scaled, gain):
    inner = grads * gain
    return scaled * (
        inner
        - jnp.mean(inner, -1, keepdims=True)
        - hat * jnp.mean(inner * hat, -1, keepdims=True)
    )

LANES = 128


def stack_rows(value, ee):
    head = lax.broadcasted_iota(jnp.int32, value.shape, 1) // ee
    return jnp.concatenate(
        [jnp.where(head == h, value, jnp.zeros_like(value)) for h in range(LANES // ee)], 0
    )


def stack_lanes(value, ee):
    head = lax.broadcasted_iota(jnp.int32, value.shape, 0) // ee
    return jnp.concatenate(
        [jnp.where(head == h, value, jnp.zeros_like(value)) for h in range(LANES // ee)], 1
    )


def span(at, size):
    return slice(at * size, (at + 1) * size)


def attend(n, groups, tokens, width, ee, expo, same, qkv_s, s_s, p_s, inv_s, oo_s, o_s):
    item = n // groups
    g = n % groups
    rs = span(item, tokens)
    qa = span(g, LANES)
    q = qkv_s[rs, qa]
    k = qkv_s[rs, span(width // LANES + g, LANES)]
    v = qkv_s[rs, span(2 * width // LANES + g, LANES)]
    s_s[...] = dot_nt(stack_rows(q, ee), k)
    for h in range(LANES // ee):
        at = slice(h * tokens, (h + 1) * tokens)
        s = s_s[at, :]
        if same is not None:
            s = jnp.where(same, s, -1e30)
        top = jnp.max(s, -1, keepdims=True)
        p_s[n, :, at] = jnp.exp2((s - top) * expo).astype(p_s.dtype)
    ones = jnp.ones_like(v)
    both = jnp.concatenate([stack_rows(v, ee), stack_rows(ones, ee)], 1)
    out = dot_nn(p_s[n], both)
    inv = 1.0 / out[:, LANES:]
    out = out[:, :LANES] * inv
    inv_s[n] = inv
    oo_s[n] = out
    o_s[rs, qa] = out.astype(o_s.dtype)


def attend_back(n, slot, groups, tokens, width, ee, scale, qkv_s, s_s, ds_s, p_s, inv_s, oo_s, do_s, dqkv_s):
    low = dqkv_s.dtype
    item = n // groups
    g = n % groups
    rs = span(item, tokens)
    qa = span(g, LANES)
    ka = span(width // LANES + g, LANES)
    va = span(2 * width // LANES + g, LANES)
    heads = range(LANES // ee)
    do = do_s[rs, qa].astype(jnp.float32) * inv_s[slot]
    rest = (-do * oo_s[slot]).astype(low)
    do_t = do.T.astype(low)
    do = do.astype(low)
    v = qkv_s[rs, va]
    s_s[...] = dot_nt(
        jnp.concatenate([stack_rows(do, ee), stack_rows(rest, ee)], 1),
        jnp.concatenate([v, jnp.ones_like(v)], 1),
    )
    for h in heads:
        at = slice(h * tokens, (h + 1) * tokens)
        ds_s[:, at] = (p_s[slot, :, at].astype(jnp.float32) * s_s[at, :]).astype(low)
    e_rows = jnp.concatenate([p_s[slot, :, h * tokens : (h + 1) * tokens] for h in heads], 0)
    ds_rows = jnp.concatenate([ds_s[:, h * tokens : (h + 1) * tokens] for h in heads], 0)
    dv_t = dot_nn(stack_lanes(do_t, ee), e_rows)
    dk_t = dot_nn(stack_lanes(qkv_s[rs, qa].T, ee), ds_rows)
    dq = dot_nn(ds_s[...], stack_rows(qkv_s[rs, ka], ee))
    dqkv_s[rs, qa] = (dq * scale).astype(low)
    dqkv_s[rs, ka] = (dk_t.T * scale).astype(low)
    dqkv_s[rs, va] = dv_t.T.astype(low)


def one_hot(index, count):
    places = lax.broadcasted_iota(jnp.int32, (index.shape[0], count), 1)
    return jnp.where(places.astype(jnp.float32) == index.astype(jnp.float32), 1.0, 0.0)


def split_table(table_ref, high_s, low_s):
    high = table_ref[...].astype(high_s.dtype)
    high_s[...] = high
    low_s[...] = (table_ref[...] - high.astype(jnp.float32)).astype(low_s.dtype)


def look_up(hot, index_row, high_s, low_s):
    index = jnp.sum(hot * index_row, -1, keepdims=True)
    rows = one_hot(index, high_s.shape[0]).astype(high_s.dtype)
    return dot_nn(rows, high_s[...]) + dot_nn(rows, low_s[...])


def decoder_kernel(
    items, heads, scal_ref, z_ref, keep_ref, gsd_ref, table_ref, pix_ref, cols_ref, down_ref, head_ref, gains_ref,
    dz_ref, gcols_out, gdown_out, ghead_out, ggains_ref, loss_ref,
    x_s, h1_s, qkv_s, p_s, o_s, x1_s, h2_s, a_s, gp_s, x2_s, hd_s, dx_s, dy_s, acc_s, dqkv_s, inv_s, oo_s, s_s, ds_s,
    high_s, low_s, pixel_s, gcols, gdown, ghead,
):
    low = jnp.bfloat16
    step = pl.program_id(0)
    width = x_s.shape[1]
    tokens = pix_ref.shape[1]
    hide = tokens - K
    rows = items * tokens
    tile = 512
    ee = width // heads
    scale = ee ** (-0.5)
    expo = scale * 1.4426950408889634

    @pl.when(step == 0)
    def _():
        gcols[...] = jnp.zeros_like(gcols)
        gdown[...] = jnp.zeros_like(gdown)
        ghead[...] = jnp.zeros_like(ghead)
        ggains_ref[...] = jnp.zeros_like(ggains_ref)
        loss_ref[...] = jnp.zeros_like(loss_ref)
        split_table(table_ref, high_s, low_s)

    def gain(i):
        return gains_ref[i : i + 1, :]

    f32 = jnp.float32
    before = lax.broadcasted_iota(jnp.int32, (tokens, tokens), 0) <= lax.broadcasted_iota(
        jnp.int32, (tokens, tokens), 1
    )
    before = before.astype(f32).astype(low)
    for i in range(items):
        base = i * tokens
        keep_hot = one_hot(keep_ref[i], tokens)
        shown = jnp.max(keep_hot, 0, keepdims=True)
        rank = dot_nn(jnp.broadcast_to(1.0 - shown, (8, tokens)).astype(low), before)[:1]
        slot = lax.broadcasted_iota(jnp.int32, (hide, tokens), 0).astype(f32) + 1.0
        hide_hot = jnp.where(slot == rank, 1.0 - shown, 0.0)
        position = look_up(jnp.concatenate([keep_hot, hide_hot], 0), gsd_ref[i].astype(f32), high_s, low_s)
        x_s[base : base + K, :] = position[:K] + z_ref[i]
        x_s[base + K : base + tokens, :] = position[K:] + gain(6)
        pixel_s[i] = dot_nn(hide_hot.astype(low), pix_ref[i]).astype(low)
    hat, _ = unit_rows(x_s[...])
    h1_s[...] = (hat * gain(0) + gain(1)).astype(low)

    for t in range(3):
        at = slice(t * width, (t + 1) * width)
        qkv_s[:, at] = dot_nn(h1_s[...], cols_ref[:, at]).astype(low)

    groups = width // LANES

    for n in range(items * groups):
        attend(n, groups, tokens, width, ee, expo, None, qkv_s, s_s.at[n % 2], p_s, inv_s, oo_s, o_s)

    x1_s[...] = x_s[...] + dot_nn(o_s[...], cols_ref[:, 3 * width : 4 * width])
    hat, _ = unit_rows(x1_s[...])
    h2_s[...] = (hat * gain(2) + gain(3)).astype(low)
    x2_s[...] = x1_s[...]

    for t in range(down_ref.shape[0] // tile):
        at = slice(t * tile, (t + 1) * tile)
        up = slice(4 * width + t * tile, 4 * width + (t + 1) * tile)
        u = dot_nn(h2_s[...], cols_ref[:, up])
        cumul = 0.5 * (1.0 + lax.erf(u * 0.7071067811865476))
        act = (u * cumul).astype(low)
        a_s[:, at] = act
        gp_s[:, at] = (cumul + u * jnp.exp(-0.5 * u * u) * 0.3989422804014327).astype(gp_s.dtype)
        x2_s[...] += dot_nn(act, down_ref[at, :])

    hat, _ = unit_rows(x2_s[...])
    hd_s[...] = (hat * gain(4) + gain(5)).astype(low)

    pixel_count = head_ref.shape[0]
    for i in range(items):
        base = i * tokens
        weight = scal_ref[0, step * items + i]
        coef = scal_ref[1, step * items + i]
        target, _ = unit_rows(pixel_s[i].astype(f32))
        hd = hd_s[base + K : base + tokens, :]
        back = jnp.zeros((hide, width), jnp.float32)
        for t in range(pixel_count // tile):
            at = slice(t * tile, (t + 1) * tile)
            err = dot_nt(hd, head_ref[at, :]) - target[:, at]
            loss_ref[...] += weight * jnp.sum(err * err, keepdims=True).reshape(1, 1)
            dpred = (err * coef).astype(low)
            ghead[at, :] += dot_tn(dpred, hd)
            back = back + dot_nn(dpred, head_ref[at, :])
        hat, scaled = unit_rows(x2_s[base + K : base + tokens, :])
        ggains_ref[4:5, :] += jnp.sum(back * hat, 0, keepdims=True)
        ggains_ref[5:6, :] += jnp.sum(back, 0, keepdims=True)
        dx = unit_back(back, hat, scaled, gain(4))
        dx_s[base : base + K, :] = jnp.zeros((K, width), jnp.float32)
        dx_s[base + K : base + tokens, :] = dx
        dy_s[base : base + K, :] = jnp.zeros((K, width), low)
        dy_s[base + K : base + tokens, :] = dx.astype(low)

    acc_s[...] = jnp.zeros_like(acc_s)

    for t in range(down_ref.shape[0] // tile):
        at = slice(t * tile, (t + 1) * tile)
        up = slice(4 * width + t * tile, 4 * width + (t + 1) * tile)
        gdown[at, :] += dot_tn(a_s[:, at], dy_s[...])
        du = (dot_nt(dy_s[...], down_ref[at, :]) * gp_s[:, at].astype(jnp.float32)).astype(low)
        gcols[:, up] += dot_tn(h2_s[...], du)
        acc_s[...] += dot_nt(du, cols_ref[:, up])

    hat, scaled = unit_rows(x1_s[...])
    grads = acc_s[...]
    ggains_ref[2:3, :] += jnp.sum(grads * hat, 0, keepdims=True)
    ggains_ref[3:4, :] += jnp.sum(grads, 0, keepdims=True)
    dx_s[...] += unit_back(grads, hat, scaled, gain(2))
    dy_s[...] = dx_s[...].astype(low)
    gcols[:, 3 * width : 4 * width] += dot_tn(o_s[...], dy_s[...])
    o_s[...] = dot_nt(dy_s[...], cols_ref[:, 3 * width : 4 * width]).astype(low)

    for n in range(items * groups):
        attend_back(
            n, n, groups, tokens, width, ee, scale, qkv_s, s_s.at[n % 2], ds_s.at[n % 2], p_s, inv_s, oo_s, o_s,
            dqkv_s,
        )

    acc_s[...] = jnp.zeros_like(acc_s)

    for t in range(3):
        at = slice(t * width, (t + 1) * width)
        gcols[:, at] += dot_tn(h1_s[...], dqkv_s[:, at])
        acc_s[...] += dot_nt(dqkv_s[:, at], cols_ref[:, at])

    hat, scaled = unit_rows(x_s[...])
    grads = acc_s[...]
    ggains_ref[0:1, :] += jnp.sum(grads * hat, 0, keepdims=True)
    ggains_ref[1:2, :] += jnp.sum(grads, 0, keepdims=True)
    dx_s[...] += unit_back(grads, hat, scaled, gain(0))
    for i in range(items):
        base = i * tokens
        dz_ref[i] = dx_s[base : base + K, :].astype(low)
        ggains_ref[6:7, :] += jnp.sum(dx_s[base + K : base + tokens, :], 0, keepdims=True)

    @pl.when(step == pl.num_programs(0) - 1)
    def _():
        gcols_out[...] = gcols[...].astype(low)
        gdown_out[...] = gdown[...].astype(low)
        ghead_out[...] = ghead[...].astype(low)


def decoder_call(scal, latent, keep, gsd, table, pixels, cols, rows, gains, heads):
    batch, tokens, pixel_count = pixels.shape
    width = cols.shape[0]
    down = jax.ShapeDtypeStruct((cols.shape[1] - 4 * width, width), rows.dtype)
    head = jax.ShapeDtypeStruct((pixel_count, width), rows.dtype)
    last = rows.shape[0] // pixel_count - 1
    items = 2
    run = items * tokens
    hide = tokens - K
    low = jnp.bfloat16
    full = pl.Buffered(1)

    def whole(array):
        return pl.BlockSpec(array.shape, lambda s: (0,) * len(array.shape), pipeline_mode=full)

    def by_item(shape):
        return pl.BlockSpec((items,) + shape, lambda s: (s, 0, 0))

    outs = (
        jax.ShapeDtypeStruct((batch, K, width), low),
        jax.ShapeDtypeStruct(cols.shape, low),
        jax.ShapeDtypeStruct(down.shape, low),
        jax.ShapeDtypeStruct(head.shape, low),
        jax.ShapeDtypeStruct((8, width), jnp.float32),
        jax.ShapeDtypeStruct((1, 1), jnp.float32),
    )
    vmem = pltpu.VMEM
    f32 = jnp.float32
    return pl.pallas_call(
        functools.partial(decoder_kernel, items, heads),
        grid=(batch // items,),
        in_specs=[
            pl.BlockSpec(memory_space=pltpu.SMEM),
            by_item((K, width)),
            by_item((K, 1)),
            by_item((1, tokens)),
            pl.BlockSpec((table.shape[0], width), lambda s: (0, table.shape[1] // width - 1), pipeline_mode=full),
            by_item((tokens, pixel_count)),
            whole(cols),
            whole(down),
            pl.BlockSpec(head.shape, lambda s: (last, 0), pipeline_mode=full),
            whole(gains),
        ],
        out_specs=(by_item((K, width)),) + tuple(whole(out) for out in outs[1:]),
        out_shape=outs,
        scratch_shapes=[
            vmem((run, width), f32),
            vmem((run, width), low),
            vmem((run, 3 * width), low),
            vmem((items * width // 128, tokens, 4 * tokens), low),
            vmem((run, width), low),
            vmem((run, width), f32),
            vmem((run, width), low),
            vmem((run, down.shape[0]), low),
            vmem((run, down.shape[0]), low),
            vmem((run, width), f32),
            vmem((run, width), low),
            vmem((run, width), f32),
            vmem((run, width), low),
            vmem((run, width), f32),
            vmem((run, 3 * width), low),
            vmem((items * width // 128, tokens, 128), f32),
            vmem((items * width // 128, tokens, 128), f32),
            vmem((2, 4 * tokens, tokens), f32),
            vmem((2, tokens, 4 * tokens), low),
            vmem((table.shape[0], width), low),
            vmem((table.shape[0], width), low),
            vmem((items, hide, pixel_count), low),
            vmem(cols.shape, f32),
            vmem(down.shape, f32),
            vmem(head.shape, f32),
        ],
        compiler_params=pltpu.CompilerParams(
            dimension_semantics=("arbitrary",), vmem_limit_bytes=63 * 1024 * 1024
        ),
        cost_estimate=pl.CostEstimate(
            flops=70_000_000_000, bytes_accessed=40_000_000, transcendentals=20_000_000
        ),
    )(scal, latent, keep, gsd, table, pixels, cols, rows, rows, gains)


MESH_ID = pl.DeviceIdType.MESH


def place():
    g = lax.axis_index("grp")
    d = lax.axis_index("dp")
    z, c = d // 2, d % 2
    xn = g + 1 - 2 * (g % 2)
    yn = (g + 2) % 4
    return g, z, c, xn, yn


def pieces(shape, parts):
    rows, columns = shape
    if rows // parts >= 32:
        n = rows // parts
        cut = [(slice(i * n, (i + 1) * n), slice(0, columns)) for i in range(parts)]
    else:
        n = columns // parts
        cut = [(slice(0, rows), slice(i * n, (i + 1) * n)) for i in range(parts)]
    return cut


def halves(cut):
    rows, columns = cut
    mid = (columns.start + columns.stop) // 2
    return (rows, slice(columns.start, mid)), (rows, slice(mid, columns.stop))


def greet(peers):
    barrier = pltpu.get_barrier_semaphore()
    for peer in peers:
        pl.semaphore_signal(barrier, inc=1, device_id=peer, device_id_type=MESH_ID)
    pl.semaphore_wait(barrier, len(peers))


GATHER_SEMS = 14


def gather_events(count, chunks, ahead, ins, outs, sems):
    zs, zr, xs, xr, ys, yr, fs, fr, gs, gr, cs, os, cr, ls = sems
    g, z, c, xn, yn = place()
    dg = (xn + 2) % 4
    here = 2 * z + c
    other = 1 - c
    sib = (g, 2 * z + 1 - c)
    right, up = (xn, here), (yn, here)
    zpeer = [(g, 2 * ((z + j) % 4) + c) for j in (1, 2, 3)]
    zfrom = [(z + 4 - j) % 4 for j in (1, 2, 3)]
    peers = [sib, right, up] + zpeer
    work = []
    for array in range(count):
        for cut in pieces(ins[array].shape[1:], chunks[array]):
            work.append((array, cut))
    steps = len(work)
    sent = []

    def send(src, dst, send_sem, recv_sem, peer):
        return pltpu.make_async_remote_copy(
            src_ref=src, dst_ref=dst, send_sem=send_sem, recv_sem=recv_sem,
            device_id=peer, device_id_type=MESH_ID,
        )

    def go(make):
        make().start()
        sent.append(make)

    def block(array, z_at, q, cut):
        return outs[array].at[z_at, c, q, cut[0], cut[1]]

    def zcopy(k, j):
        array, cut = work[k]
        return send(
            ins[array].at[g, cut[0], cut[1]], block(array, z, g, cut), zs.at[k, j], zr.at[k, j], zpeer[j]
        )

    def relay(k, j, q, cut, ssem, rsem, peer):
        at = block(work[k][0], zfrom[j], q, cut)
        return send(at, at, ssem, rsem, peer)

    def to_x(k, j):
        return relay(k, j, g, work[k][1], xs.at[k, j], xr.at[k, j], right)

    def to_y(k, j):
        return relay(k, j, g, work[k][1], ys.at[k, j], yr.at[k, j], up)

    def to_core(k, j, i, q):
        return relay(k, j, q, work[k][1], cs.at[k, j, i], cr.at[work[k][0]], sib)

    def on_y(k, j, q):
        return relay(k, j, q, halves(work[k][1])[0], fs.at[k, j], fr.at[k, j], up)

    def on_x(k, j, q):
        return relay(k, j, q, halves(work[k][1])[1], gs.at[k, j], gr.at[k, j], right)

    def own(array):
        return pltpu.make_async_copy(ins[array], outs[array].at[z, c], ls.at[array])

    def own_to_core(array):
        return send(ins[array], outs[array].at[z, c], os.at[array], cr.at[array], sib)

    def begin():
        for k in range(min(ahead, steps)):
            for j in range(3):
                go(functools.partial(zcopy, k, j))

    def begin_own():
        for array in range(count):
            own(array).start()
        for array in range(count):
            go(functools.partial(own_to_core, array))

    def event(t):
        if t < steps:
            for j in range(3):
                zcopy(t, j).wait_recv()
                go(functools.partial(to_x, t, j))
                go(functools.partial(to_y, t, j))
                go(functools.partial(to_core, t, j, 0, g))
            if t + ahead < steps:
                for j in range(3):
                    go(functools.partial(zcopy, t + ahead, j))
        if 1 <= t <= steps:
            k = t - 1
            for j in range(3):
                relay(k, j, xn, work[k][1], xs.at[k, j], xr.at[k, j], right).wait_recv()
                go(functools.partial(on_y, k, j, xn))
                go(functools.partial(to_core, k, j, 1, xn))
                relay(k, j, yn, work[k][1], ys.at[k, j], yr.at[k, j], up).wait_recv()
                go(functools.partial(on_x, k, j, yn))
                go(functools.partial(to_core, k, j, 2, yn))
        if 2 <= t:
            k = t - 2
            for j in range(3):
                on_y(k, j, dg).wait_recv()
                on_x(k, j, dg).wait_recv()
                go(functools.partial(to_core, k, j, 3, dg))

    def finish():
        for make in sent:
            make().wait_send()
        for array in range(count):
            whole = outs[array].at[:, other]
            send(whole, whole, os.at[array], cr.at[array], sib).wait_recv()
            own(array).wait()

    return peers, begin, begin_own, [functools.partial(event, t) for t in range(steps + 2)], finish


def gather_scratch(count, steps):
    dma = pltpu.SemaphoreType.DMA
    return [dma((steps, 3))] * 10 + [dma((steps, 3, 4)), dma((count,)), dma((count,)), dma((count,))]


def gather_kernel(count, chunks, ahead, *refs):
    ins, items_ref = refs[:count], refs[count]
    outs, items_out = refs[count + 1 : 2 * count + 1], refs[2 * count + 1]
    sems = refs[2 * count + 2 :]
    it, its, itr, load_sem = sems[GATHER_SEMS : GATHER_SEMS + 4]
    wide = sems[GATHER_SEMS + 4 : GATHER_SEMS + 4 + count]
    masters, ins = ins, sems[GATHER_SEMS + 4 + count :]
    parts = [(array, cut) for array in range(count) for cut in pieces(ins[array].shape[1:], chunks[array])]
    loads = [
        pltpu.make_async_copy(
            masters[array].at[:, cut[0], cut[1]], wide[array].at[:, cut[0], cut[1]], load_sem.at[i]
        )
        for i, (array, cut) in enumerate(parts)
    ]
    for load in loads:
        load.start()
    peers, begin, begin_own, events, finish = gather_events(
        count, chunks, ahead, ins, outs, sems[:GATHER_SEMS]
    )

    def narrow(i):
        array, cut = parts[i]
        loads[i].wait()
        ins[array][:, cut[0], cut[1]] = wide[array][:, cut[0], cut[1]].astype(ins[array].dtype)

    greet(peers)
    _, right, up = peers[:3]

    def items_copy(i, peer):
        return pltpu.make_async_remote_copy(
            src_ref=it.at[2 * i], dst_ref=it.at[2 * i + 1], send_sem=its.at[i], recv_sem=itr.at[i],
            device_id=peer, device_id_type=MESH_ID,
        )

    it[0] = items_ref[...]
    items_copy(0, right).start()
    for i in range(ahead):
        narrow(i)
    begin()
    for i in range(ahead, len(parts)):
        narrow(i)
    begin_own()
    for t, event in enumerate(events):
        event()
        if t == 0:
            items_copy(0, right).wait_recv()
            it[2] = it[0] + it[1]
            items_copy(1, up).start()
        if t == 1:
            items_copy(1, up).wait_recv()
            items_out[...] = it[2] + it[3]
    finish()
    items_copy(0, right).wait_send()
    items_copy(1, up).wait_send()


def gather_call(shards, items, chunks, ahead=2, collective_id=0):
    count = len(shards)
    steps = sum(chunks)
    views = [s.reshape(4, s.shape[0] // 4, s.shape[1]) for s in shards]
    dma = pltpu.SemaphoreType.DMA
    hbm = pl.BlockSpec(memory_space=pl.ANY)
    vm = pl.BlockSpec(memory_space=pltpu.VMEM)
    *outs, total = pl.pallas_call(
        functools.partial(gather_kernel, count, chunks, ahead),
        out_shape=tuple(jax.ShapeDtypeStruct((4, 2) + v.shape, jnp.bfloat16) for v in views)
        + (jax.ShapeDtypeStruct((8, 128), jnp.float32),),
        in_specs=[hbm] * count + [vm],
        out_specs=tuple([hbm] * count + [vm]),
        scratch_shapes=gather_scratch(count, steps)
        + [pltpu.VMEM((4, 8, 128), jnp.float32), dma((2,)), dma((2,)), dma((steps,))]
        + [pltpu.VMEM(v.shape, jnp.float32) for v in views]
        + [pltpu.VMEM(v.shape, jnp.bfloat16) for v in views],
        compiler_params=pltpu.CompilerParams(
            collective_id=collective_id, has_side_effects=True, vmem_limit_bytes=60 * 1024 * 1024
        ),
    )(*views, jnp.broadcast_to(items, (8, 128)))
    return [o.reshape(-1, o.shape[-1]) for o in outs], total[0, 0]


RUN = 256


def same_item():
    row = lax.broadcasted_iota(jnp.int32, (RUN, RUN), 0) // K
    column = lax.broadcasted_iota(jnp.int32, (RUN, RUN), 1) // K
    return row == column


def encoder_kernel(heads, chunks, *refs):
    count = 2 if chunks else 0
    (pixels_ref, keep_ref, bands_ref, gsd_ref, table_ref, rows_ref, cols_ref, de_ref, gains_ref) = refs[:9]
    shards = refs[9 : 9 + count]
    outs = refs[9 + count :]
    z_ref, band_ref, a_ref, gp_ref, x2_ref = outs[:5]
    stored = outs[5:13]
    gathered = outs[13 : 13 + count]
    rest = outs[13 + count :]
    pix_ref, x_ref, qkv_ref, p_ref, inv_ref, oo_ref, x1_ref, o_s = rest[:8]
    h_s, s_s, high_s, low_s, de_s, store_sem, de_sem = rest[8:15]
    low = jnp.bfloat16
    step = pl.program_id(0)
    width = x_ref.shape[1]
    ee = width // heads
    groups = width // LANES
    expo = ee ** (-0.5) * 1.4426950408889634
    if chunks:
        low_shards = rest[15 + GATHER_SEMS : 17 + GATHER_SEMS]
        wide_shards = rest[17 + GATHER_SEMS : 19 + GATHER_SEMS]
        shard_sem = rest[19 + GATHER_SEMS]
        peers, begin, begin_own, events, finish = gather_events(
            count, chunks, 2, low_shards, gathered, rest[15 : 15 + GATHER_SEMS]
        )

    def gain(i):
        return gains_ref[i : i + 1, :]

    def store(i):
        return pltpu.make_async_copy(rest[i], stored[i], store_sem.at[i])

    def load_de():
        return pltpu.make_async_copy(gathered[1].at[2] if chunks else de_ref, de_s, de_sem)

    if chunks:

        @pl.when(step == 0)
        def _():
            loads = [
                pltpu.make_async_copy(shards[i], wide_shards[i], shard_sem.at[i]) for i in range(count)
            ]
            for load in loads:
                load.start()
            greet(peers)
            for i in range(count):
                loads[i].wait()
                low_shards[i][...] = wide_shards[i][...].astype(low)
            begin()
            begin_own()

        for at, event in zip((3, 6, 7, 8, 9, 10), events):
            pl.when(step == at)(event)

    @pl.when(step == 11)
    def _():
        if chunks:
            finish()
        load_de().start()

    @pl.when(step == 0)
    def _():
        split_table(table_ref, high_s, low_s)

        @pl.loop(0, pixels_ref.shape[0])
        def _(i):
            at = pl.ds(pl.multiple_of(i * K, K), K)
            hot = one_hot(keep_ref[i], pixels_ref.shape[1])
            pix_ref[at, :] = dot_nn(hot.astype(low), pixels_ref[i]).astype(low)
            band_ref[at, :] = jnp.sum(hot * bands_ref[i].astype(jnp.float32), -1, keepdims=True).astype(jnp.int32)
            x_ref[at, :] = look_up(hot, gsd_ref[i].astype(jnp.float32), high_s, low_s)

        store(0).start()

    @pl.when(step < 4)
    def _():
        pixel = pix_ref[...]
        x_ref[...] += dot_nn(jnp.where(band_ref[...] == step, pixel, jnp.zeros_like(pixel)), rows_ref[...])

    @pl.when(step == 4)
    def _():
        store(1).start()
        hat, _ = unit_rows(x_ref[...])
        h_s[...] = (hat * gain(0) + gain(1)).astype(low)

    @pl.when((step >= 4) & (step < 7))
    def _():
        at = pl.ds(pl.multiple_of((step - 4) * width, width), width)
        qkv_ref[:, at] = dot_nn(h_s[...], cols_ref[...]).astype(low)

    @pl.when(step == 7)
    def _():
        store(2).start()
        same = same_item()

        for n in range(x_ref.shape[0] // RUN * groups):
            attend(n, groups, RUN, width, ee, expo, same, qkv_ref, s_s.at[n % 2], p_ref, inv_ref, oo_ref, o_s)

        for i in (3, 4, 5, 7):
            store(i).start()
        x1_ref[...] = x_ref[...] + dot_nn(o_s[...], cols_ref[...])
        store(6).start()
        hat, _ = unit_rows(x1_ref[...])
        h_s[...] = (hat * gain(2) + gain(3)).astype(low)
        x2_ref[...] = x1_ref[...]

    @pl.when(step >= 8)
    def _():
        half = width // 2
        for t in range(2):
            at = slice(t * half, (t + 1) * half)
            u = dot_nn(h_s[...], cols_ref[:, at])
            cumul = 0.5 * (1.0 + lax.erf(u * 0.7071067811865476))
            a_ref[:, at] = (u * cumul).astype(low)
            gp_ref[:, at] = (cumul + u * jnp.exp(-0.5 * u * u) * 0.3989422804014327).astype(low)

        x2_ref[...] += dot_nn(a_ref[...], rows_ref[...])

    @pl.when(step == 11)
    def _():
        hat, _ = unit_rows(x2_ref[...])
        h_s[...] = (hat * gain(4) + gain(5)).astype(low)
        load_de().wait()
        z_ref[...] = dot_nn(h_s[...], de_s[...].reshape(width, z_ref.shape[1]))
        for i in range(8):
            store(i).wait()


def encoder_call(pixels, keep, bands, gsd, table, rows, cols, de, gains, heads, shards=()):
    width = cols.shape[0]
    tokens = keep.shape[0] * K
    low, f32 = jnp.bfloat16, jnp.float32
    runs = tokens // RUN * (width // LANES)
    wide = LANES // (width // heads) * RUN
    one = pl.Buffered(1)
    hbm = pl.BlockSpec(memory_space=pl.ANY)
    vmem = pltpu.VMEM
    chunks = (2, 2) if shards else ()
    views = [s.reshape(4, s.shape[0] // 4, s.shape[1]) for s in shards]
    if shards:
        narrow = shards[1].shape[1]
        de, de_shape = jnp.zeros((8, 128), low), (2, 4, 128, narrow)
    else:
        narrow, de_shape = de.shape[1], de.shape

    def whole(shape):
        return pl.BlockSpec(shape, lambda s: (0,) * len(shape), pipeline_mode=one)

    def row_block(s):
        return (jnp.where(s < 4, s + 4, jnp.where(s < 8, 0, s - 8)), 0)

    def column_block(s):
        return (0, jnp.where(s < 4, 0, s - 4))

    def hidden_block(s):
        return (0, jnp.where(s < 8, 0, s - 8))

    hidden = pl.BlockSpec((tokens, width), hidden_block)
    blocks = [
        ((tokens, narrow), f32, whole((tokens, narrow))),
        ((tokens, 1), jnp.int32, whole((tokens, 1))),
        ((tokens, 4 * width), low, hidden),
        ((tokens, 4 * width), low, hidden),
        ((tokens, width), f32, whole((tokens, width))),
    ]
    held = [
        ((tokens, pixels.shape[2]), low),
        ((tokens, width), f32),
        ((tokens, 3 * width), low),
        ((runs, RUN, wide), low),
        ((runs, RUN, LANES), f32),
        ((runs, RUN, LANES), f32),
        ((tokens, width), f32),
        ((tokens, width), low),
    ]
    struct = jax.ShapeDtypeStruct
    out = pl.pallas_call(
        functools.partial(encoder_kernel, heads, chunks),
        grid=(12,),
        in_specs=[
            whole(pixels.shape),
            whole(keep.shape),
            whole(bands.shape),
            whole(gsd.shape),
            pl.BlockSpec((table.shape[0], width), lambda s: (0, 0), pipeline_mode=one),
            pl.BlockSpec((width, width), row_block),
            pl.BlockSpec((width, width), column_block),
            hbm,
            whole(gains.shape),
        ]
        + [hbm] * len(views),
        out_specs=tuple(b[2] for b in blocks) + (hbm,) * (len(held) + len(views)),
        out_shape=tuple(struct(b[0], b[1]) for b in blocks)
        + tuple(struct(*h) for h in held)
        + tuple(struct((4, 2) + v.shape, low) for v in views),
        scratch_shapes=[vmem(*h) for h in held]
        + [
            vmem((tokens, width), low),
            vmem((2, wide, RUN), f32),
            vmem((table.shape[0], width), low),
            vmem((table.shape[0], width), low),
            vmem(de_shape, low),
            pltpu.SemaphoreType.DMA((8,)),
            pltpu.SemaphoreType.DMA,
        ]
        + (gather_scratch(2, sum(chunks)) if shards else [])
        + [vmem(v.shape, low) for v in views]
        + [vmem(v.shape, f32) for v in views]
        + ([pltpu.SemaphoreType.DMA((2,))] if shards else []),
        compiler_params=pltpu.CompilerParams(
            dimension_semantics=("arbitrary",),
            vmem_limit_bytes=60 * 1024 * 1024,
            collective_id=2 if shards else None,
            has_side_effects=bool(shards),
        ),
        cost_estimate=pl.CostEstimate(
            flops=20_000_000_000, bytes_accessed=70_000_000, transcendentals=8_000_000
        ),
    )(pixels, keep, bands, gsd, table, rows, cols, de, gains, *views)
    z, band, a, gp, x2 = out[:5]
    pix, x, qkv, p, inv, oo, x1, o = out[5:13]
    saved = (x, qkv, p, inv, oo, x1, a, gp, x2, o)
    return z, pix, band, saved, [w.reshape(-1, w.shape[-1]) for w in out[13:]]


def encoder_back_kernel(
    heads, dz_ref, pix_ref, band_ref, x_ref, qkv_ref, p_ref, inv_ref, oo_ref, x1_ref, a_ref, gp_ref, x2_ref,
    rows_ref, cols_ref, de_ref, gains_ref,
    grows_ref, gcols_ref, gde_ref, ggains_ref,
    h_s, dx_s, dy_s, acc_s, do_s, dqkv_s, s_s, ds_s,
):
    low, f32 = jnp.bfloat16, jnp.float32
    step = pl.program_id(0)
    width = x_ref.shape[1]
    ee = width // heads
    groups = width // LANES
    runs = x_ref.shape[0] // RUN

    def gain(i):
        return gains_ref[i : i + 1, :]

    def back(x, grads, at):
        hat, scaled = unit_rows(x)
        ggains_ref[at : at + 1, :] = jnp.sum(grads * hat, 0, keepdims=True)
        ggains_ref[at + 1 : at + 2, :] = jnp.sum(grads, 0, keepdims=True)
        return unit_back(grads, hat, scaled, gain(at))

    def normed(x, at):
        hat, _ = unit_rows(x)
        h_s[...] = (hat * gain(at) + gain(at + 1)).astype(low)

    @pl.when(step == 0)
    def _():
        ggains_ref[...] = jnp.zeros_like(ggains_ref)
        normed(x2_ref[...], 4)
        gde_ref[...] = dot_tn(h_s[...], dz_ref[...]).astype(low)
        dx_s[...] = back(x2_ref[...], dot_nt(dz_ref[...], de_ref[...]), 4)
        dy_s[...] = dx_s[...].astype(low)
        normed(x1_ref[...], 2)
        acc_s[...] = jnp.zeros_like(acc_s)

    @pl.when(step < 4)
    def _():
        grows_ref[...] = dot_tn(a_ref[...], dy_s[...]).astype(low)
        du = (dot_nt(dy_s[...], rows_ref[...]) * gp_ref[...].astype(f32)).astype(low)
        do_s[...] = du
        gcols_ref[...] = dot_tn(h_s[...], du).astype(low)
        acc_s[...] += dot_nt(do_s[...], cols_ref[...])

    @pl.when(step == 4)
    def _():
        dx_s[...] += back(x1_ref[...], acc_s[...], 2)
        dy_s[...] = dx_s[...].astype(low)
        for run in range(runs):
            for g in range(groups):
                h_s[run * RUN : (run + 1) * RUN, g * LANES : (g + 1) * LANES] = oo_ref[
                    run * groups + g
                ].astype(low)
        gcols_ref[...] = dot_tn(h_s[...], dy_s[...]).astype(low)
        do_s[...] = dot_nt(dy_s[...], cols_ref[...]).astype(low)

        for n in range(runs * groups):
            attend_back(
                n, n, groups, RUN, width, ee, ee ** (-0.5), qkv_ref, s_s, ds_s, p_ref, inv_ref, oo_ref, do_s,
                dqkv_s,
            )

        normed(x_ref[...], 0)
        acc_s[...] = jnp.zeros_like(acc_s)

    @pl.when((step >= 5) & (step < 8))
    def _():
        at = pl.ds(pl.multiple_of((step - 5) * width, width), width)
        gcols_ref[...] = dot_tn(h_s[...], dqkv_s[:, at]).astype(low)
        acc_s[...] += dot_nt(dqkv_s[:, at], cols_ref[...])

    @pl.when(step == 8)
    def _():
        dx_s[...] += back(x_ref[...], acc_s[...], 0)
        dy_s[...] = dx_s[...].astype(low)

    @pl.when(step >= 8)
    def _():
        pixel = pix_ref[...]
        h_s[...] = jnp.where(band_ref[...] == step - 8, pixel, jnp.zeros_like(pixel))
        grows_ref[...] = dot_tn(h_s[...], dy_s[...]).astype(low)


def encoder_back_call(dz, pixel, band, saved, rows, cols, de, gains, heads):
    x, qkv, p, inv, oo, x1, a, gp, x2, _ = saved
    tokens, width = x.shape
    low, f32 = jnp.bfloat16, jnp.float32
    wide = p.shape[2]
    one = pl.Buffered(1)

    def whole(array):
        return pl.BlockSpec(array.shape, lambda s: (0,) * len(array.shape), pipeline_mode=one)

    def row_block(s):
        return (jnp.minimum(s, 3), 0)

    def column_block(s):
        return (0, jnp.where(s < 4, s + 4, jnp.where(s == 4, 3, jnp.minimum(s - 5, 2))))

    def hidden_block(s):
        return (0, jnp.minimum(s, 3))

    def grow_block(s):
        return (jnp.where(s < 4, s, jnp.where(s < 8, 3, s - 4)), 0)

    hidden = pl.BlockSpec((tokens, width), hidden_block)
    square = (width, width)
    outs = (
        jax.ShapeDtypeStruct(rows.shape, low),
        jax.ShapeDtypeStruct(cols.shape, low),
        jax.ShapeDtypeStruct(de.shape, low),
        jax.ShapeDtypeStruct((8, width), f32),
    )
    vmem = pltpu.VMEM
    return pl.pallas_call(
        functools.partial(encoder_back_kernel, heads),
        grid=(12,),
        in_specs=[
            whole(dz), whole(pixel), whole(band), whole(x), whole(qkv), whole(p), whole(inv), whole(oo),
            whole(x1), hidden, hidden, whole(x2),
            pl.BlockSpec(square, row_block), pl.BlockSpec(square, column_block),
            whole(de), whole(gains),
        ],
        out_specs=(
            pl.BlockSpec(square, grow_block),
            pl.BlockSpec(square, column_block),
            whole(outs[2]),
            whole(outs[3]),
        ),
        out_shape=outs,
        scratch_shapes=[
            vmem((tokens, width), low),
            vmem((tokens, width), f32),
            vmem((tokens, width), low),
            vmem((tokens, width), f32),
            vmem((tokens, width), low),
            vmem((tokens, 3 * width), low),
            vmem((wide, RUN), f32),
            vmem((RUN, wide), low),
        ],
        compiler_params=pltpu.CompilerParams(
            dimension_semantics=("arbitrary",), vmem_limit_bytes=60 * 1024 * 1024
        ),
        cost_estimate=pl.CostEstimate(
            flops=40_000_000_000, bytes_accessed=110_000_000, transcendentals=1_000_000
        ),
    )(dz, pixel, band, x, qkv, p, inv, oo, x1, a, gp, x2, rows, cols, de, gains)


def back_reduce_kernel(heads, kinds, work, pieces, refs_in, refs_out, *refs):
    low, f32 = jnp.bfloat16, jnp.float32
    ref = dict(zip(refs_in + refs_out, refs))
    rest = refs[len(refs_in) + len(refs_out) :]
    per = 9
    bufs = [rest[per * i : per * i + per] for i in range(len(kinds))]
    (sm, ss, ssx, dx, acc, xin, h, dy, wide, wt, wu, out_r, out_c, out_e, p_t, inv_t, oo_t, s_s, ds_s, gsum,
     cs, cr, ls, os, x1s, x1r, x2s, x2r, z_s, z_r, ags, agr, ks, sms, smr, sss, ssr, dma, att_sem) = rest[
        per * len(kinds) :
    ]
    g, z, c, xn, yn = place()
    dg = (xn + 2) % 4
    here = 2 * z + c
    sib = (g, 2 * z + 1 - c)
    right, up = (xn, here), (yn, here)
    zto = [(z + j) % 4 for j in (1, 2, 3)]
    zpeer = [(g, 2 * t + c) for t in zto]
    greet([sib, right, up] + zpeer)
    steps = len(work)
    sent = []
    from_slot = [[] for _ in range(steps)]

    def send(src, dst, send_sem, recv_sem, peer):
        return pltpu.make_async_remote_copy(
            src_ref=src, dst_ref=dst, send_sem=send_sem, recv_sem=recv_sem,
            device_id=peer, device_id_type=MESH_ID,
        )

    def guarded(test, action):
        if test is None:
            action()
        else:
            pl.when(test)(action)

    def go(copies, keep=None, tests=None):
        for i, copy in enumerate(copies):
            test = tests[i] if tests else None
            guarded(test, copy.start)
            (sent if keep is None else keep).append((test, copy))

    def left(entries):
        for test, copy in entries:
            guarded(test, copy.wait_send)

    def got(copies):
        for copy in copies:
            copy.wait_recv()

    def mine(k, at=None):
        base = work[k][2]
        at = z if at is None else at
        return None if base is None else ((at >= base) & (at < base + 2))

    def buffers(k):
        kind, at = work[k][:2]
        return bufs[kind], at, at % kinds[kind][4], kinds[kind][2] // 2

    def c_copies(k):
        (_, crecv, *_), at, _, _ = buffers(k)
        return [
            send(
                ref[array].at[:, 1 - c, :, cut[0], cut[1]], crecv.at[at, pl.ds(z0, nz)],
                cs.at[k, i], cr.at[k, i], sib,
            )
            for i, (array, z0, nz, cut) in enumerate(work[k][3])
        ]

    def own_copies(k):
        (s, *_), _, slot, _ = buffers(k)
        return [
            pltpu.make_async_copy(
                ref[array].at[:, c, :, cut[0], cut[1]], s.at[slot, pl.ds(z0, nz)], os.at[k, i]
            )
            for i, (array, z0, nz, cut) in enumerate(work[k][3])
        ]

    def recv_load(k, i):
        (_, crecv, tmp, *_), at, _, _ = buffers(k)
        return pltpu.make_async_copy(crecv.at[at, i], tmp.at[i % 2], ls.at[k, i])

    def x1_copies(k):
        (s, _, _, xa, yb, *_), at, slot, half = buffers(k)
        lo, hi = pl.ds(0, half), pl.ds(half, half)
        return [
            send(s.at[slot, :, xn, :, lo], xa.at[at, 0], x1s.at[k, 0], x1r.at[k, 0], right),
            send(s.at[slot, :, dg, :, lo], xa.at[at, 1], x1s.at[k, 1], x1r.at[k, 1], right),
            send(s.at[slot, :, yn, :, hi], yb.at[at, 0], x1s.at[k, 2], x1r.at[k, 2], up),
            send(s.at[slot, :, dg, :, hi], yb.at[at, 1], x1s.at[k, 3], x1r.at[k, 3], up),
        ]

    def x2_copies(k):
        (s, _, _, _, _, xb, ya, *_), at, slot, half = buffers(k)
        lo, hi = pl.ds(0, half), pl.ds(half, half)
        return [
            send(s.at[slot, :, yn, :, lo], ya.at[at], x2s.at[k, 0], x2r.at[k, 0], up),
            send(s.at[slot, :, xn, :, hi], xb.at[at], x2s.at[k, 1], x2r.at[k, 1], right),
        ]

    def z_copies(k):
        (s, *_, zb, _), at, slot, _ = buffers(k)
        base = work[k][2] or 0
        return [
            send(
                s.at[slot, (zto[j] - base) % kinds[work[k][0]][0], g], zb.at[at, j],
                z_s.at[k, j], z_r.at[k, j], zpeer[j],
            )
            for j in range(3)
        ]

    def out_at(k, q, part=None):
        name, cut = work[k][4:6]
        if part is not None:
            cut = halves(cut)[part]
        return ref[name].at[q, cut[0], cut[1]]

    def ag_copies(k):
        (*_, fin), at, _, _ = buffers(k)
        return [
            send(fin.at[at], out_at(k, g), ags.at[k, 0], agr.at[k, 0], right),
            send(fin.at[at], out_at(k, g), ags.at[k, 1], agr.at[k, 1], up),
        ]

    def keep_copy(k):
        (*_, fin), at, _, _ = buffers(k)
        return pltpu.make_async_copy(fin.at[at], out_at(k, g), ks.at[k])

    def fwd_copies(k, of_x, of_y):
        return [
            send(out_at(k, of_x, 0), out_at(k, of_x, 0), ags.at[k, 2], agr.at[k, 2], up),
            send(out_at(k, of_y, 1), out_at(k, of_y, 1), ags.at[k, 3], agr.at[k, 3], right),
        ]

    def add_half(k, q, first, other):
        (s, *_), _, slot, half = buffers(k)
        part = pl.ds(0 if first else half, half)

        @pl.loop(0, kinds[work[k][0]][0])
        def _(i):
            s[slot, i, q, :, part] = (s[slot, i, q, :, part].astype(f32) + other[i].astype(f32)).astype(low)

    def load(k):
        kind, at = work[k][:2]
        slots = kinds[kind][4]
        if at >= slots:
            before = [j for j in range(steps) if work[j][:2] == (kind, at - slots)][0]
            left(from_slot[before])
            from_slot[before].clear()
        for copy in own_copies(k):
            copy.start()

    def pair(k):
        (s, _, tmp, *_), _, slot, _ = buffers(k)
        count = kinds[work[k][0]][0]
        got(c_copies(k))
        for i in range(2):
            recv_load(k, i).start()
        for copy in own_copies(k):
            copy.wait()
        for i in range(count):
            recv_load(k, i).wait()

            @pl.loop(0, 4)
            def _(q):
                s[slot, i, q] = (s[slot, i, q].astype(f32) + tmp[i % 2, q].astype(f32)).astype(low)

            if i + 2 < count:
                recv_load(k, i + 2).start()
        go(x1_copies(k), from_slot[k])

    def first_half(k):
        (_, _, _, xa, yb, *_), at, _, _ = buffers(k)
        got(x1_copies(k))
        add_half(k, yn, True, xa.at[at, 1])
        add_half(k, xn, False, yb.at[at, 1])
        go(x2_copies(k), from_slot[k])
        add_half(k, g, True, xa.at[at, 0])
        add_half(k, g, False, yb.at[at, 0])

    def second_half(k):
        (_, _, _, _, _, xb, ya, *_), at, _, _ = buffers(k)
        got(x2_copies(k))
        add_half(k, g, True, ya.at[at])
        add_half(k, g, False, xb.at[at])
        go(z_copies(k), from_slot[k], [mine(k, t) for t in zto])

    def finish(k):
        def act():
            (s, *_, zb, fin), at, slot, _ = buffers(k)
            got(z_copies(k))
            base = work[k][2] or 0
            total = s[slot, (z - base) % kinds[work[k][0]][0], g].astype(f32)
            for j in range(3):
                total = total + zb[at, j].astype(f32)
            fin[at] = total.astype(low)
            keep_copy(k).start()
            square = fin[at].astype(f32)
            square = square * square
            for i in range(square.shape[1] // ss.shape[1]):
                ss[...] += jnp.sum(
                    square[:, i * ss.shape[1] : (i + 1) * ss.shape[1]], 0, keepdims=True
                )

        guarded(mine(k), act)
        go(ag_copies(k), None, [mine(k)] * 2)

    def collect(k):
        guarded(mine(k), lambda: got(ag_copies(k)))
        go(fwd_copies(k, xn, yn), None, [mine(k)] * 2)

    def close(k):
        guarded(mine(k), lambda: got(fwd_copies(k, dg, dg)))

    stages = [load, pair, first_half, second_half, finish, collect, close]

    def share_rounds(value, sem_s, sem_r, store):
        def copy(i, slot, peer):
            return send(value.at[slot], value.at[4 + i], sem_s.at[i], sem_r.at[i], peer)

        def round_pair(i, peer, following):
            got([copy(i, i, peer)])
            value[i + 1] = value[i] + value[4 + i]
            go(following())

        def last():
            return [copy(3 + j, 3, zpeer[j]) for j in range(3)]

        def end():
            got(last())
            total = None
            for at in range(4):
                term = jnp.where(z == at, value[3], jnp.zeros_like(value[3]))
                for j in range(3):
                    term = term + jnp.where((z + 3 - j) % 4 == at, value[7 + j], jnp.zeros_like(value[3]))
                total = term if total is None else total + term
            store[...] = total

        return [
            lambda: go([copy(0, 0, sib)]),
            lambda: round_pair(0, sib, lambda: [copy(1, 1, right)]),
            lambda: round_pair(1, right, lambda: [copy(2, 2, up)]),
            lambda: round_pair(2, up, last),
            end,
        ]

    tokens, width = dx.shape
    ee = width // heads
    groups = width // LANES
    runs = tokens // RUN
    gains = ref["gains"]

    moving = {}

    def move(name, src, dst):
        copy = pltpu.make_async_copy(src, dst, dma.at[lanes_of.index(name)])
        copy.start()
        moving[name] = copy

    def done(*names):
        for name in names:
            if name in moving:
                moving.pop(name).wait()

    lanes_of = (
        "a", "gp", "rows", "cols", "x", "dz", "de", "o", "qkv", "pix", "out_r", "out_c", "out_e",
    )

    def tile(i):
        return pl.ds(i * width, width)

    def gain(i):
        return gains[i : i + 1, :]

    def back(grads, at):
        hat, scaled = unit_rows(xin[...])
        gsum[at : at + 1, :] = jnp.sum(grads * hat, 0, keepdims=True)
        gsum[at + 1 : at + 2, :] = jnp.sum(grads, 0, keepdims=True)
        return unit_back(grads, hat, scaled, gain(at))

    def normed(at):
        hat, _ = unit_rows(xin[...])
        h[...] = (hat * gain(at) + gain(at + 1)).astype(low)

    def column_grads(block, source):
        done("out_c")
        for d in range(8):
            value = dot_tn(h[:, d * 128 : (d + 1) * 128], source()).astype(low)
            out_c[d // 2, d % 2] = value.reshape(out_c.shape[2:])
        move("out_c", out_c, ref["g_cols"].at[:, :, :, :, tile(block)])

    def load_hidden(s):
        move("a", ref["a"].at[:, tile(s)], wide.at[:, tile(0)])
        move("gp", ref["gp"].at[:, tile(s)], wide.at[:, tile(1)])
        move("rows", ref["rows"].at[tile(s)], wt)

    def load_columns(block):
        move("cols", ref["cols"].at[:, tile(block)], wu)

    narrow = ref["dz"].shape[1]

    def first_loads():
        move("x", ref["x2"], xin)
        move("dz", ref["dz"], wide.at[:, pl.ds(2 * width, narrow)])
        move("de", ref["dec_rows"].at[pl.ds(2 * width, width)], wt.at[:, pl.ds(0, narrow)])
        move("a", ref["a"].at[:, tile(0)], wide.at[:, tile(0)])
        move("gp", ref["gp"].at[:, tile(0)], wide.at[:, tile(1)])
        load_columns(4)

    def head_piece(_):
        done("x", "dz", "de")
        dz = wide[:, 2 * width : 2 * width + narrow]
        normed(4)
        for d in range(8):
            out_e[0, d // 4, d % 4] = dot_tn(h[:, d * 128 : (d + 1) * 128], dz).astype(low)
        move("out_e", out_e, ref["g_de"])
        dx[...] = back(dot_nt(dz, wt[:, :narrow]), 4)
        move("rows", ref["rows"].at[tile(0)], wt)
        move("x", ref["x1"], xin)
        dy[...] = dx[...].astype(low)
        done("x")
        normed(2)
        acc[...] = jnp.zeros_like(acc)

    def hidden_piece(s):
        done("a", "gp", "rows", "out_r")
        wide[:, 2 * width :] = (dot_nt(dy[...], wt[...]) * wide[:, width : 2 * width].astype(f32)).astype(low)
        for q in range(4):
            out_r[q] = dot_tn(wide[:, q * 256 : (q + 1) * 256], dy[...]).astype(low)
        move("out_r", out_r, ref["g_down"].at[s // 2, s % 2])
        if s < 3:
            load_hidden(s + 1)
        column_grads(4 + s, lambda: wide[:, 2 * width :])
        done("cols")
        acc[...] += dot_nt(wide[:, 2 * width :], wu[...])
        load_columns(5 + s if s < 3 else 3)
        if s == 3:
            move("o", ref["o"], h)
            move("qkv", ref["qkv"], wide)

    def middle_piece(_):
        dx[...] += back(acc[...], 2)
        dy[...] = dx[...].astype(low)
        move("x", ref["x"], xin)
        done("o")
        column_grads(3, lambda: dy[...])
        done("cols")
        h[...] = dot_nt(dy[...], wu[...]).astype(low)
        load_columns(0)
        done("qkv")

    def attention_loads(n):
        slot = n % 2
        return [
            pltpu.make_async_copy(ref[name].at[n], buf.at[slot], att_sem.at[slot, i])
            for i, (name, buf) in enumerate((("p", p_t), ("inv", inv_t), ("oo", oo_t)))
        ]

    def attention_piece(part):
        count = runs * groups // 4
        first = part * count
        for copy in attention_loads(first):
            copy.start()

        for n in range(first, first + count):
            for copy in attention_loads(n):
                copy.wait()
            if n + 1 < first + count:
                for copy in attention_loads(n + 1):
                    copy.start()
            attend_back(
                n, n % 2, groups, RUN, width, ee, ee ** (-0.5), wide, s_s.at[n % 2], ds_s.at[n % 2], p_t, inv_t,
                oo_t, h, wide,
            )

    def input_piece(t):
        if t == 0:
            done("x")
            normed(0)
            acc[...] = jnp.zeros_like(acc)
        column_grads(t, lambda: wide[:, t * width : (t + 1) * width])
        done("cols")
        acc[...] += dot_nt(wide[:, t * width : (t + 1) * width], wu[...])
        if t < 2:
            load_columns(t + 1)
        else:
            move("pix", ref["pix"], h)

    def first_piece(_):
        dx[...] += back(acc[...], 0)
        dy[...] = dx[...].astype(low)
        sm[0] = ref["small"][...]
        sm[0, 0:6, :] = gsum[0:6, :]

    def embed_piece(b):
        done("pix", "out_r")
        for q in range(4):
            part = h[:, q * 256 : (q + 1) * 256]
            part = jnp.where(ref["band"][...] == b, part, jnp.zeros_like(part))
            out_r[q] = dot_tn(part, dy[...]).astype(low)
        move("out_r", out_r, ref["g_emb"].at[b // 2, b % 2])

    action = {
        "head": head_piece, "hidden": hidden_piece, "middle": middle_piece, "attention": attention_piece,
        "input": input_piece, "first": first_piece, "embed": embed_piece,
    }

    ss[...] = jnp.zeros_like(ss)
    gsum[...] = jnp.zeros_like(gsum)
    small_rounds = share_rounds(sm, sms, smr, ref["small_out"])
    square_rounds = share_rounds(ssx, sss, ssr, ref["ss_out"])
    ends = [w[6] + 6 for w in work]
    last = max(ends)
    squared = max(w[6] + 4 for w in work)
    compute_end = max(t for t, _, _ in pieces)
    for t in range(last + 1):
        for i in (1, 6, 5, 4, 3, 2, 0):
            for k in range(steps):
                if work[k][6] + i == t:
                    stages[i](k)
        if t == 0:
            first_loads()
        done("out_r", "out_c", "out_e")
        for k in range(steps):
            if work[k][7] == t:
                go(c_copies(k))
        for at, name, argument in pieces:
            if at == t:
                action[name](argument)
        if compute_end < t <= compute_end + 5:
            small_rounds[t - compute_end - 1]()
        if t == squared:
            ssx[0] = jnp.broadcast_to(jnp.sum(ss[...], keepdims=True).reshape(1, 1), ssx.shape[1:])
            square_rounds[0]()
        if squared < t < last:
            square_rounds[t - squared]()
        if t == last:
            for following in square_rounds[last - squared :]:
                following()
    for k in range(steps):
        left(from_slot[k])
    left(sent)
    for k in range(steps):
        guarded(mine(k), keep_copy(k).wait)


def back_reduce_call(dz, pix, band, saved, rows, cols, dec_rows, gains, dcols, ddown, dhead, small, heads):
    x, qkv, p, inv, oo, x1, a, gp, x2, o = saved
    tokens, width = x.shape
    low, f32 = jnp.bfloat16, jnp.float32
    narrow = dec_rows.shape[1]
    ins = dict(
        dz=dz, pix=pix, band=band, x=x, x1=x1, x2=x2, qkv=qkv, p=p, inv=inv, oo=oo, o=o, a=a, gp=gp,
        rows=rows, cols=cols, dec_rows=dec_rows, gains=gains, small=small,
        d_cols=dcols.reshape(4, 2, 4, 16, dcols.shape[1]),
        d_down=ddown.reshape(2, 2, 4, 128, narrow),
        d_head=dhead.reshape(1, 2, 4, 128, narrow),
    )
    outs = dict(
        erows=((4, 256, width), low), ecols=((4, 32, cols.shape[1]), low),
        dcols=((4, 16, dcols.shape[1]), low), drows=((4, 128, narrow), low),
        small_out=(small.shape, f32), ss_out=((8, 128), f32),
        g_down=((2, 2, 4, 256, width), low), g_emb=((2, 2, 4, 256, width), low),
        g_cols=((4, 2, 4, 32, cols.shape[1]), low), g_de=((1, 2, 4, 128, narrow), low),
    )
    kinds = ((4, 32, 1024, 16, 6), (4, 16, 2048, 2, 2), (4, 64, 512, 2, 2))

    def column_chunk(at, block):
        cut = (slice(0, 32), slice(block * 1024, (block + 1) * 1024))
        return (0, at, None, (("g_cols", 0, 4, cut),), "ecols", cut)

    def row_chunk(at, i):
        cut = (slice(i * 32, (i + 1) * 32), slice(0, width))
        return (0, at, None, (("g_down", 0, 2, cut), ("g_emb", 2, 2, cut)), "erows", cut)

    chunks = []
    for i in range(2):
        cut = (slice(0, 16), slice(i * 2048, (i + 1) * 2048))
        chunks.append((1, i, None, (("d_cols", 0, 4, cut),), "dcols", cut))
    for i in range(2):
        cut = (slice(i * 64, (i + 1) * 64), slice(0, narrow))
        sources = (("d_down", 0, 2, cut), ("g_de", 2, 1, cut), ("d_head", 3, 1, cut))
        chunks.append((2, i, None, sources, "drows", cut))
    chunks += [column_chunk(i, 4 + i) for i in range(4)]
    chunks += [column_chunk(4 + i, block) for i, block in enumerate((3, 0, 1, 2))]
    chunks += [row_chunk(8 + i, i) for i in range(8)]
    starts = (0, 1, 3, 4, 5, 6, 7, 8, 9, 11, 12, 13) + tuple(range(14, 22))
    begins = (0, 0, 2, 2, 3, 4, 5, 6, 7, 10, 10, 11) + tuple(range(13, 21))
    work = tuple(chunk + (starts[i], begins[i]) for i, chunk in enumerate(chunks))
    pieces = [(1, "head", 0)] + [(2 + s, "hidden", s) for s in range(4)] + [(6, "middle", 0)]
    pieces += [(7 + i // 2, "attention", i) for i in range(4)]
    pieces += [(9, "input", 0), (9, "input", 1), (10, "input", 2), (10, "first", 0)]
    pieces += [(11 + i // 2, "embed", i) for i in range(4)]
    steps = len(work)
    hbm = pl.BlockSpec(memory_space=pl.ANY)
    vm = pl.BlockSpec(memory_space=pltpu.VMEM)
    vmem, sems = pltpu.VMEM, pltpu.SemaphoreType.DMA
    scratch, landing = [], {}
    for i, (nz, r, col, count, slots) in enumerate(kinds):
        landing[f"land{i}"] = ((count, nz, 4, r, col), low)
        half = col // 2
        scratch += [
            vmem((slots, nz, 4, r, col), low),
            None,
            vmem((2, 4, r, col), low),
            vmem((count, 2, nz, r, half), low),
            vmem((count, 2, nz, r, half), low),
            vmem((count, nz, r, half), low),
            vmem((count, nz, r, half), low),
            vmem((count, 3, r, col), low),
            vmem((count, r, col), low),
        ]
    outs.update(landing)
    in_names, out_names = tuple(ins), tuple(outs)

    def kernel(*refs):
        n = len(in_names) + len(out_names)
        ref = dict(zip(in_names + out_names, refs))
        kept = list(refs[n:])
        for i in range(len(kinds)):
            kept.insert(9 * i + 1, ref[f"land{i}"])
        back_reduce_kernel(heads, kinds, work, pieces, in_names, out_names, *refs[:n], *kept)

    result = pl.pallas_call(
        kernel,
        out_shape=tuple(jax.ShapeDtypeStruct(*outs[name]) for name in out_names),
        in_specs=[vm if name in ("band", "gains", "small") else hbm for name in in_names],
        out_specs=tuple(vm if name in ("small_out", "ss_out") else hbm for name in out_names),
        scratch_shapes=[s for s in scratch if s is not None]
        + [
            vmem((10,) + small.shape, f32),
            vmem((1, 512), f32),
            vmem((10, 8, 128), f32),
            vmem((tokens, width), f32),
            vmem((tokens, width), f32),
            vmem((tokens, width), f32),
            vmem((tokens, width), low),
            vmem((tokens, width), low),
            vmem((tokens, 3 * width), low),
            vmem((width, width), low),
            vmem((width, width), low),
            vmem((4, 256, width), low),
            vmem((4, 2, 4, 32, width), low),
            vmem((1, 2, 4, 128, narrow), low),
            vmem((2,) + p.shape[1:], low),
            vmem((2,) + inv.shape[1:], f32),
            vmem((2,) + oo.shape[1:], f32),
            vmem((2, p.shape[2], RUN), f32),
            vmem((2, RUN, p.shape[2]), low),
            vmem((8, width), f32),
            sems((steps, 3)), sems((steps, 3)), sems((steps, 4)), sems((steps, 3)),
            sems((steps, 4)), sems((steps, 4)),
            sems((steps, 2)), sems((steps, 2)),
            sems((steps, 3)), sems((steps, 3)),
            sems((steps, 4)), sems((steps, 4)),
            sems((steps,)), sems((6,)), sems((6,)), sems((6,)), sems((6,)), sems((13,)), sems((2, 3)),
        ],
        compiler_params=pltpu.CompilerParams(
            collective_id=1, has_side_effects=True, vmem_limit_bytes=63 * 1024 * 1024
        ),
    )(*ins.values())
    got = dict(zip(out_names, result))
    shards = [got[name].reshape(-1, got[name].shape[-1]) for name in ("ecols", "erows", "dcols", "drows")]
    return shards, got["small_out"], got["ss_out"]


def adam_step(master, moment, square, grad, factor, fix_one, fix_two, decay, rate):
    clipped = grad * factor
    moment_new = beta_first * moment + (1.0 - beta_first) * clipped
    square_new = beta_second * square + (1.0 - beta_second) * clipped * clipped
    direction = moment_new / fix_one / (jnp.sqrt(square_new / fix_two) + adam_eps) + decay * master
    return (clipped, square_new, master - rate * direction)


def adam_kernel(count_e, count_d, *refs):
    scal_ref, small_ref, ss_ref = refs[:3]
    ins, outs = refs[3:25], refs[25:]
    small = small_ref[...]
    width = small.shape[1]
    flat = lax.broadcasted_iota(jnp.int32, small.shape, 0) * width + lax.broadcasted_iota(
        jnp.int32, small.shape, 1
    )
    gains = jnp.where(flat < count_e + count_d, small, 0.0)
    norm = jnp.sqrt(ss_ref[0:1, 0:1] + jnp.sum(gains * gains, keepdims=True).reshape(1, 1))
    factor = clip_level / jnp.maximum(norm, clip_level)
    masked, fix_one, fix_two = scal_ref[0, 0], scal_ref[0, 1], scal_ref[0, 2]

    def update(grad, master, moment, square, decay, rate):
        return adam_step(master, moment, square, grad, factor, fix_one, fix_two, decay, rate)

    for i in range(4):
        grad, master, moment, square = ins[4 * i : 4 * i + 4]
        got = update(
            grad[...].astype(jnp.float32), master[...], moment[...], square[...], weight_decay, learn_rate
        )
        for target, value in zip(outs[3 * i : 3 * i + 3], got):
            target[...] = value

    @pl.when(pl.program_id(0) == 0)
    def _():
        at = 0
        for i in range(2):
            master, moment, square = ins[16 + 3 * i : 19 + 3 * i]
            rows, columns = master.shape
            for r in range(rows):
                row, lane = at // width, at % width
                grad = small[row : row + 1, lane : lane + columns]
                one = slice(r, r + 1)
                got = update(grad, master[one, :], moment[one, :], square[one, :], 0.0, gain_rate)
                for target, value in zip(outs[12 + 3 * i : 15 + 3 * i], got):
                    target[one, :] = value
                at += columns
        outs[18][...] = small[at // width : at // width + 1, at % width : at % width + 1] / masked
        outs[19][...] = norm


def adam_call(scal, small, squares, matrices, gains):
    steps = 4

    def block(array):
        rows, columns = array.shape
        if rows // steps % 16 == 0:
            return pl.BlockSpec((rows // steps, columns), lambda s: (s, 0))
        return pl.BlockSpec((rows, columns // steps), lambda s: (0, s))

    def whole(array):
        return pl.BlockSpec(array.shape, lambda s: (0, 0))

    struct = jax.ShapeDtypeStruct
    f32 = jnp.float32
    ins, in_specs, outs, out_specs = [], [], [], []
    for group in matrices:
        ins += group
        in_specs += [block(array) for array in group]
        outs += [struct(group[1].shape, f32)] * 3
        out_specs += [block(group[1])] * 3
    for group in gains:
        ins += group
        in_specs += [whole(array) for array in group]
        outs += [struct(group[0].shape, f32)] * 3
        out_specs += [whole(group[0])] * 3
    outs += [struct((1, 1), f32)] * 2
    out_specs += [pl.BlockSpec((1, 1), lambda s: (0, 0))] * 2
    out = pl.pallas_call(
        functools.partial(adam_kernel, gains[0][0].size, gains[1][0].size),
        grid=(steps,),
        in_specs=[pl.BlockSpec(memory_space=pltpu.SMEM), whole(small), whole(squares)] + in_specs,
        out_specs=tuple(out_specs),
        out_shape=tuple(outs),
        compiler_params=pltpu.CompilerParams(
            dimension_semantics=("arbitrary",), vmem_limit_bytes=56 * 1024 * 1024
        ),
    )(scal, small, squares, *ins)
    return tuple(out[:18]) + (out[18][0, 0], out[19][0, 0])


def body(
    pixels,
    keep_index,
    band_group,
    gsd_index,
    gsd_table,
    group_items,
    step_count,
    enc_cols,
    enc_rows,
    dec_cols,
    dec_rows,
    enc_gains,
    dec_gains,
    moment_ecols,
    moment_erows,
    moment_dcols,
    moment_drows,
    moment_egains,
    moment_dgains,
    square_ecols,
    square_erows,
    square_dcols,
    square_drows,
    square_egains,
    square_dgains,
):
    n_grp = lax.axis_size("grp")
    grp_at = lax.axis_index("grp")

    def gather_rows(master):
        rows = master.shape[0]
        if rows % (16 * n_grp):
            return lax.all_gather(to_low(master), "dp", axis=0, tiled=True)
        part = rows // n_grp
        mine = lax.dynamic_slice_in_dim(master, grp_at * part, part, 0)
        return lax.all_gather(to_low(mine), ("dp", "grp"), axis=0, tiled=True)

    direct = (n_grp, lax.axis_size("dp")) == (4, 8)
    own_count = jnp.sum(group_items.astype(jnp.float32))
    if direct:
        (whole_rows, whole_cols), total_count = gather_call(
            [enc_rows, enc_cols], own_count, (4, 4), 2, 0
        )
    else:
        total_count = lax.psum(own_count, "grp")
        whole_rows, whole_cols = gather_rows(enc_rows), gather_rows(enc_cols)
    masked = total_count * (L - K)
    count_steps = step_count[0].astype(jnp.float32)
    fix_one = 1.0 - beta_first**count_steps
    fix_two = 1.0 - beta_second**count_steps
    keep_rows = keep_index[0]
    batch = keep_rows.shape[0]
    keep_column = keep_rows[..., None]
    band_row = band_group[0][:, None, :]
    gsd_row = gsd_index[0][:, None, :]
    if direct:
        shards, dec_embed = (dec_cols, dec_rows), None
    else:
        dec_copy, dec_whole = gather_rows(dec_cols), gather_rows(dec_rows)
        shards, dec_embed = (), dec_whole[DFF : DFF + D]
    latent, kept_pixels, kept_bands, saved, gathered = encoder_call(
        pixels[0],
        keep_column,
        band_row,
        gsd_row,
        gsd_table[0],
        whole_rows,
        whole_cols,
        dec_embed,
        enc_gains,
        HEADS,
        shards,
    )
    if direct:
        dec_copy, dec_whole = gathered
    latent = latent.reshape(batch, K, -1)
    first_item = lax.axis_index("dp") * batch
    valid = (first_item + jnp.arange(batch, dtype=jnp.int32) < group_items[0]).astype(jnp.float32)
    scal = jnp.stack([valid / PIX, valid * (2.0 / PIX) / masked])
    grad_latent, grad_dcols, grad_ddown, grad_head, dec_sums, loss_local = decoder_call(
        scal,
        latent,
        keep_column,
        gsd_row,
        gsd_table[0],
        pixels[0],
        dec_copy,
        dec_whole,
        dec_gains,
        DHEADS,
    )
    loss_local = loss_local[0, 0]
    grad_latent = grad_latent.reshape(batch * K, -1)
    grad_dgains = dec_sums[:7]

    def reduce_rows(pieces, axis):
        whole = jnp.concatenate([to_low(piece) for piece in pieces], axis)
        return lax.psum_scatter(whole, "dp", scatter_dimension=0, tiled=True)

    if direct:
        count_e, count_d = enc_gains.size, grad_dgains.size
        flat = jnp.concatenate([grad_dgains.reshape(-1), loss_local[None]])
        small = jnp.pad(flat, (count_e, 16 * D - count_e - flat.shape[0])).reshape(16, D)
        shards, small, squares = back_reduce_call(
            grad_latent,
            kept_pixels,
            kept_bands,
            saved,
            whole_rows,
            whole_cols,
            dec_whole,
            enc_gains,
            grad_dcols,
            grad_ddown,
            grad_head,
            small,
            HEADS,
        )
        matrices = (
            [shards[0], enc_cols, moment_ecols, square_ecols],
            [shards[1], enc_rows, moment_erows, square_erows],
            [shards[2], dec_cols, moment_dcols, square_dcols],
            [shards[3], dec_rows, moment_drows, square_drows],
        )
        gains = ([enc_gains, moment_egains, square_egains], [dec_gains, moment_dgains, square_dgains])
        return adam_call(
            jnp.stack([masked, fix_one, fix_two]).reshape(1, 3), small, squares, matrices, gains
        )
    else:
        grad_erows, grad_ecols, grad_dembed, enc_sums = encoder_back_call(
            grad_latent,
            kept_pixels,
            kept_bands,
            saved,
            whole_rows,
            whole_cols,
            dec_embed,
            enc_gains,
            HEADS,
        )
        grad_egains = enc_sums[:6]
        drows = (grad_ddown, grad_dembed, grad_head)
        enc_sum, dec_sum, loss_sum = lax.psum((grad_egains, grad_dgains, loss_local), ("grp", "dp"))
        shards = tuple(
            lax.psum(reduce_rows(pieces, 0), "grp").astype(jnp.float32)
            for pieces in ((grad_ecols,), (grad_erows,), (grad_dcols,), drows)
        )
        shard_squares = lax.psum(sum((jnp.sum(piece * piece) for piece in shards)), "dp")
    loss = loss_sum / masked
    grad_norm = jnp.sqrt(shard_squares + jnp.sum(enc_sum * enc_sum) + jnp.sum(dec_sum * dec_sum))
    factor = clip_level / jnp.maximum(grad_norm, clip_level)
    clipped_ecols, squares_ecols, updated_ecols = adam_step(
        enc_cols,
        moment_ecols,
        square_ecols,
        shards[0],
        factor,
        fix_one,
        fix_two,
        weight_decay,
        learn_rate,
    )
    clipped_erows, squares_erows, updated_erows = adam_step(
        enc_rows,
        moment_erows,
        square_erows,
        shards[1],
        factor,
        fix_one,
        fix_two,
        weight_decay,
        learn_rate,
    )
    clipped_dcols, squares_dcols, updated_dcols = adam_step(
        dec_cols,
        moment_dcols,
        square_dcols,
        shards[2],
        factor,
        fix_one,
        fix_two,
        weight_decay,
        learn_rate,
    )
    clipped_drows, squares_drows, updated_drows = adam_step(
        dec_rows,
        moment_drows,
        square_drows,
        shards[3],
        factor,
        fix_one,
        fix_two,
        weight_decay,
        learn_rate,
    )
    clipped_egains, squares_egains, updated_egains = adam_step(
        enc_gains, moment_egains, square_egains, enc_sum, factor, fix_one, fix_two, 0.0, gain_rate
    )
    clipped_dgains, squares_dgains, updated_dgains = adam_step(
        dec_gains, moment_dgains, square_dgains, dec_sum, factor, fix_one, fix_two, 0.0, gain_rate
    )
    return (
        clipped_ecols,
        squares_ecols,
        updated_ecols,
        clipped_erows,
        squares_erows,
        updated_erows,
        clipped_dcols,
        squares_dcols,
        updated_dcols,
        clipped_drows,
        squares_drows,
        updated_drows,
        clipped_egains,
        squares_egains,
        updated_egains,
        clipped_dgains,
        squares_dgains,
        updated_dgains,
        loss,
        grad_norm,
    )


def solution(mesh):
    return jax.shard_map(
        body,
        mesh=mesh,
        in_specs=(
            P("grp", "dp", None, None),
            P("grp", "dp", None),
            P("grp", "dp", None),
            P("grp", "dp", None),
            P("grp", None, None),
            P("grp"),
            P(),
            P("dp", None),
            P("dp", None),
            P("dp", None),
            P("dp", None),
            P(),
            P(),
            P("dp", None),
            P("dp", None),
            P("dp", None),
            P("dp", None),
            P(),
            P(),
            P("dp", None),
            P("dp", None),
            P("dp", None),
            P("dp", None),
            P(),
            P(),
        ),
        out_specs=(
            P("dp", None),
            P("dp", None),
            P("dp", None),
            P("dp", None),
            P("dp", None),
            P("dp", None),
            P("dp", None),
            P("dp", None),
            P("dp", None),
            P("dp", None),
            P("dp", None),
            P("dp", None),
            P(),
            P(),
            P(),
            P(),
            P(),
            P(),
            P(),
            P(),
        ),
        check_vma=False,
    )
```

```python
import functools

import jax
import jax.numpy as jnp
from jax import lax
from jax.experimental import pallas as pl
from jax.experimental.pallas import tpu as pltpu
from jax.sharding import PartitionSpec as P

D = 1024
HEADS = 16
FF = 4096
DHEADS = 16
DFF = 2048
PIX = 1024
NBG = 4
L = 256
K = 64


norm_eps = 1e-06
clip_level = 0.005
learn_rate = 0.02
gain_rate = 0.25
weight_decay = 0.05
adam_eps = 1e-08
beta_first = 0.5
beta_second = 0.5


def to_low(value):
    return value.astype(jnp.bfloat16)


def project(inputs, matrix):
    return jnp.einsum("...n,nm->...m", inputs, matrix, preferred_element_type=jnp.float32)


def dot_nn(a, b):
    return lax.dot_general(a, b, (((1,), (0,)), ((), ())), preferred_element_type=jnp.float32)


def dot_nt(a, b):
    return lax.dot_general(a, b, (((1,), (1,)), ((), ())), preferred_element_type=jnp.float32)


def dot_tn(a, b):
    return lax.dot_general(a, b, (((0,), (0,)), ((), ())), preferred_element_type=jnp.float32)


def unit_rows(values):
    centred = values - jnp.mean(values, -1, keepdims=True)
    scaled = lax.rsqrt(jnp.mean(centred * centred, -1, keepdims=True) + norm_eps)
    return centred * scaled, scaled


def unit_back(grads, hat, scaled, gain):
    inner = grads * gain
    return scaled * (
        inner
        - jnp.mean(inner, -1, keepdims=True)
        - hat * jnp.mean(inner * hat, -1, keepdims=True)
    )

LANES = 128


def stack_rows(value, ee):
    head = lax.broadcasted_iota(jnp.int32, value.shape, 1) // ee
    return jnp.concatenate(
        [jnp.where(head == h, value, jnp.zeros_like(value)) for h in range(LANES // ee)], 0
    )


def stack_lanes(value, ee):
    head = lax.broadcasted_iota(jnp.int32, value.shape, 0) // ee
    return jnp.concatenate(
        [jnp.where(head == h, value, jnp.zeros_like(value)) for h in range(LANES // ee)], 1
    )


def span(at, size):
    return slice(at * size, (at + 1) * size)


def attend(n, groups, tokens, width, ee, expo, same, qkv_s, s_s, p_s, inv_s, oo_s, o_s):
    item = n // groups
    g = n % groups
    rs = span(item, tokens)
    qa = span(g, LANES)
    q = qkv_s[rs, qa]
    k = qkv_s[rs, span(width // LANES + g, LANES)]
    v = qkv_s[rs, span(2 * width // LANES + g, LANES)]
    s_s[...] = dot_nt(stack_rows(q, ee), k)
    for h in range(LANES // ee):
        at = slice(h * tokens, (h + 1) * tokens)
        s = s_s[at, :]
        if same is not None:
            s = jnp.where(same, s, -1e30)
        top = jnp.max(s, -1, keepdims=True)
        p_s[n, :, at] = jnp.exp2((s - top) * expo).astype(p_s.dtype)
    ones = jnp.ones_like(v)
    both = jnp.concatenate([stack_rows(v, ee), stack_rows(ones, ee)], 1)
    out = dot_nn(p_s[n], both)
    inv = 1.0 / out[:, LANES:]
    out = out[:, :LANES] * inv
    inv_s[n] = inv
    oo_s[n] = out
    o_s[rs, qa] = out.astype(o_s.dtype)


def attend_back(n, slot, groups, tokens, width, ee, scale, qkv_s, s_s, ds_s, p_s, inv_s, oo_s, do_s, dqkv_s):
    low = dqkv_s.dtype
    item = n // groups
    g = n % groups
    rs = span(item, tokens)
    qa = span(g, LANES)
    ka = span(width // LANES + g, LANES)
    va = span(2 * width // LANES + g, LANES)
    heads = range(LANES // ee)
    do = do_s[rs, qa].astype(jnp.float32) * inv_s[slot]
    rest = (-do * oo_s[slot]).astype(low)
    do_t = do.T.astype(low)
    do = do.astype(low)
    v = qkv_s[rs, va]
    s_s[...] = dot_nt(
        jnp.concatenate([stack_rows(do, ee), stack_rows(rest, ee)], 1),
        jnp.concatenate([v, jnp.ones_like(v)], 1),
    )
    for h in heads:
        at = slice(h * tokens, (h + 1) * tokens)
        ds_s[:, at] = (p_s[slot, :, at].astype(jnp.float32) * s_s[at, :]).astype(low)
    e_rows = jnp.concatenate([p_s[slot, :, h * tokens : (h + 1) * tokens] for h in heads], 0)
    ds_rows = jnp.concatenate([ds_s[:, h * tokens : (h + 1) * tokens] for h in heads], 0)
    dv_t = dot_nn(stack_lanes(do_t, ee), e_rows)
    dk_t = dot_nn(stack_lanes(qkv_s[rs, qa].T, ee), ds_rows)
    dq = dot_nn(ds_s[...], stack_rows(qkv_s[rs, ka], ee))
    dqkv_s[rs, qa] = (dq * scale).astype(low)
    dqkv_s[rs, ka] = (dk_t.T * scale).astype(low)
    dqkv_s[rs, va] = dv_t.T.astype(low)


def one_hot(index, count):
    places = lax.broadcasted_iota(jnp.int32, (index.shape[0], count), 1)
    return jnp.where(places.astype(jnp.float32) == index.astype(jnp.float32), 1.0, 0.0)


def split_table(table_ref, high_s, low_s):
    high = table_ref[...].astype(high_s.dtype)
    high_s[...] = high
    low_s[...] = (table_ref[...] - high.astype(jnp.float32)).astype(low_s.dtype)


def look_up(hot, index_row, high_s, low_s):
    index = jnp.sum(hot * index_row, -1, keepdims=True)
    rows = one_hot(index, high_s.shape[0]).astype(high_s.dtype)
    return dot_nn(rows, high_s[...]) + dot_nn(rows, low_s[...])


def decoder_kernel(
    items, heads, scal_ref, z_ref, keep_ref, gsd_ref, table_ref, pix_ref, cols_ref, down_ref, head_ref, gains_ref,
    dz_ref, gcols_out, gdown_out, ghead_out, ggains_ref, loss_ref,
    x_s, h1_s, qkv_s, p_s, o_s, x1_s, h2_s, a_s, gp_s, x2_s, hd_s, dx_s, dy_s, acc_s, dqkv_s, inv_s, oo_s, s_s, ds_s,
    high_s, low_s, pixel_s, gcols, gdown, ghead,
):
    low = jnp.bfloat16
    step = pl.program_id(0)
    width = x_s.shape[1]
    tokens = pix_ref.shape[1]
    hide = tokens - K
    rows = items * tokens
    tile = 512
    ee = width // heads
    scale = ee ** (-0.5)
    expo = scale * 1.4426950408889634

    @pl.when(step == 0)
    def _():
        gcols[...] = jnp.zeros_like(gcols)
        gdown[...] = jnp.zeros_like(gdown)
        ghead[...] = jnp.zeros_like(ghead)
        ggains_ref[...] = jnp.zeros_like(ggains_ref)
        loss_ref[...] = jnp.zeros_like(loss_ref)
        split_table(table_ref, high_s, low_s)

    def gain(i):
        return gains_ref[i : i + 1, :]

    f32 = jnp.float32
    before = lax.broadcasted_iota(jnp.int32, (tokens, tokens), 0) <= lax.broadcasted_iota(
        jnp.int32, (tokens, tokens), 1
    )
    before = before.astype(f32).astype(low)
    for i in range(items):
        base = i * tokens
        keep_hot = one_hot(keep_ref[i], tokens)
        shown = jnp.max(keep_hot, 0, keepdims=True)
        rank = dot_nn(jnp.broadcast_to(1.0 - shown, (8, tokens)).astype(low), before)[:1]
        slot = lax.broadcasted_iota(jnp.int32, (hide, tokens), 0).astype(f32) + 1.0
        hide_hot = jnp.where(slot == rank, 1.0 - shown, 0.0)
        position = look_up(jnp.concatenate([keep_hot, hide_hot], 0), gsd_ref[i].astype(f32), high_s, low_s)
        x_s[base : base + K, :] = position[:K] + z_ref[i]
        x_s[base + K : base + tokens, :] = position[K:] + gain(6)
        pixel_s[i] = dot_nn(hide_hot.astype(low), pix_ref[i]).astype(low)
    hat, _ = unit_rows(x_s[...])
    h1_s[...] = (hat * gain(0) + gain(1)).astype(low)

    for t in range(3):
        at = slice(t * width, (t + 1) * width)
        qkv_s[:, at] = dot_nn(h1_s[...], cols_ref[:, at]).astype(low)

    groups = width // LANES

    for n in range(items * groups):
        attend(n, groups, tokens, width, ee, expo, None, qkv_s, s_s.at[n % 2], p_s, inv_s, oo_s, o_s)

    x1_s[...] = x_s[...] + dot_nn(o_s[...], cols_ref[:, 3 * width : 4 * width])
    hat, _ = unit_rows(x1_s[...])
    h2_s[...] = (hat * gain(2) + gain(3)).astype(low)
    x2_s[...] = x1_s[...]

    for t in range(down_ref.shape[0] // tile):
        at = slice(t * tile, (t + 1) * tile)
        up = slice(4 * width + t * tile, 4 * width + (t + 1) * tile)
        u = dot_nn(h2_s[...], cols_ref[:, up])
        cumul = 0.5 * (1.0 + lax.erf(u * 0.7071067811865476))
        act = (u * cumul).astype(low)
        a_s[:, at] = act
        gp_s[:, at] = (cumul + u * jnp.exp(-0.5 * u * u) * 0.3989422804014327).astype(gp_s.dtype)
        x2_s[...] += dot_nn(act, down_ref[at, :])

    hat, _ = unit_rows(x2_s[...])
    hd_s[...] = (hat * gain(4) + gain(5)).astype(low)

    pixel_count = head_ref.shape[0]
    for i in range(items):
        base = i * tokens
        weight = scal_ref[0, step * items + i]
        coef = scal_ref[1, step * items + i]
        target, _ = unit_rows(pixel_s[i].astype(f32))
        hd = hd_s[base + K : base + tokens, :]
        back = jnp.zeros((hide, width), jnp.float32)
        for t in range(pixel_count // tile):
            at = slice(t * tile, (t + 1) * tile)
            err = dot_nt(hd, head_ref[at, :]) - target[:, at]
            loss_ref[...] += weight * jnp.sum(err * err, keepdims=True).reshape(1, 1)
            dpred = (err * coef).astype(low)
            ghead[at, :] += dot_tn(dpred, hd)
            back = back + dot_nn(dpred, head_ref[at, :])
        hat, scaled = unit_rows(x2_s[base + K : base + tokens, :])
        ggains_ref[4:5, :] += jnp.sum(back * hat, 0, keepdims=True)
        ggains_ref[5:6, :] += jnp.sum(back, 0, keepdims=True)
        dx = unit_back(back, hat, scaled, gain(4))
        dx_s[base : base + K, :] = jnp.zeros((K, width), jnp.float32)
        dx_s[base + K : base + tokens, :] = dx
        dy_s[base : base + K, :] = jnp.zeros((K, width), low)
        dy_s[base + K : base + tokens, :] = dx.astype(low)

    acc_s[...] = jnp.zeros_like(acc_s)

    for t in range(down_ref.shape[0] // tile):
        at = slice(t * tile, (t + 1) * tile)
        up = slice(4 * width + t * tile, 4 * width + (t + 1) * tile)
        gdown[at, :] += dot_tn(a_s[:, at], dy_s[...])
        du = (dot_nt(dy_s[...], down_ref[at, :]) * gp_s[:, at].astype(jnp.float32)).astype(low)
        gcols[:, up] += dot_tn(h2_s[...], du)
        acc_s[...] += dot_nt(du, cols_ref[:, up])

    hat, scaled = unit_rows(x1_s[...])
    grads = acc_s[...]
    ggains_ref[2:3, :] += jnp.sum(grads * hat, 0, keepdims=True)
    ggains_ref[3:4, :] += jnp.sum(grads, 0, keepdims=True)
    dx_s[...] += unit_back(grads, hat, scaled, gain(2))
    dy_s[...] = dx_s[...].astype(low)
    gcols[:, 3 * width : 4 * width] += dot_tn(o_s[...], dy_s[...])
    o_s[...] = dot_nt(dy_s[...], cols_ref[:, 3 * width : 4 * width]).astype(low)

    for n in range(items * groups):
        attend_back(
            n, n, groups, tokens, width, ee, scale, qkv_s, s_s.at[n % 2], ds_s.at[n % 2], p_s, inv_s, oo_s, o_s,
            dqkv_s,
        )

    acc_s[...] = jnp.zeros_like(acc_s)

    for t in range(3):
        at = slice(t * width, (t + 1) * width)
        gcols[:, at] += dot_tn(h1_s[...], dqkv_s[:, at])
        acc_s[...] += dot_nt(dqkv_s[:, at], cols_ref[:, at])

    hat, scaled = unit_rows(x_s[...])
    grads = acc_s[...]
    ggains_ref[0:1, :] += jnp.sum(grads * hat, 0, keepdims=True)
    ggains_ref[1:2, :] += jnp.sum(grads, 0, keepdims=True)
    dx_s[...] += unit_back(grads, hat, scaled, gain(0))
    for i in range(items):
        base = i * tokens
        dz_ref[i] = dx_s[base : base + K, :].astype(low)
        ggains_ref[6:7, :] += jnp.sum(dx_s[base + K : base + tokens, :], 0, keepdims=True)

    @pl.when(step == pl.num_programs(0) - 1)
    def _():
        gcols_out[...] = gcols[...].astype(low)
        gdown_out[...] = gdown[...].astype(low)
        ghead_out[...] = ghead[...].astype(low)


def decoder_call(scal, latent, keep, gsd, table, pixels, cols, rows, gains, heads):
    batch, tokens, pixel_count = pixels.shape
    width = cols.shape[0]
    down = jax.ShapeDtypeStruct((cols.shape[1] - 4 * width, width), rows.dtype)
    head = jax.ShapeDtypeStruct((pixel_count, width), rows.dtype)
    last = rows.shape[0] // pixel_count - 1
    items = 2
    run = items * tokens
    hide = tokens - K
    low = jnp.bfloat16
    full = pl.Buffered(1)

    def whole(array):
        return pl.BlockSpec(array.shape, lambda s: (0,) * len(array.shape), pipeline_mode=full)

    def by_item(shape):
        return pl.BlockSpec((items,) + shape, lambda s: (s, 0, 0))

    outs = (
        jax.ShapeDtypeStruct((batch, K, width), low),
        jax.ShapeDtypeStruct(cols.shape, low),
        jax.ShapeDtypeStruct(down.shape, low),
        jax.ShapeDtypeStruct(head.shape, low),
        jax.ShapeDtypeStruct((8, width), jnp.float32),
        jax.ShapeDtypeStruct((1, 1), jnp.float32),
    )
    vmem = pltpu.VMEM
    f32 = jnp.float32
    return pl.pallas_call(
        functools.partial(decoder_kernel, items, heads),
        grid=(batch // items,),
        in_specs=[
            pl.BlockSpec(memory_space=pltpu.SMEM),
            by_item((K, width)),
            by_item((K, 1)),
            by_item((1, tokens)),
            pl.BlockSpec((table.shape[0], width), lambda s: (0, table.shape[1] // width - 1), pipeline_mode=full),
            by_item((tokens, pixel_count)),
            whole(cols),
            whole(down),
            pl.BlockSpec(head.shape, lambda s: (last, 0), pipeline_mode=full),
            whole(gains),
        ],
        out_specs=(by_item((K, width)),) + tuple(whole(out) for out in outs[1:]),
        out_shape=outs,
        scratch_shapes=[
            vmem((run, width), f32),
            vmem((run, width), low),
            vmem((run, 3 * width), low),
            vmem((items * width // 128, tokens, 4 * tokens), low),
            vmem((run, width), low),
            vmem((run, width), f32),
            vmem((run, width), low),
            vmem((run, down.shape[0]), low),
            vmem((run, down.shape[0]), low),
            vmem((run, width), f32),
            vmem((run, width), low),
            vmem((run, width), f32),
            vmem((run, width), low),
            vmem((run, width), f32),
            vmem((run, 3 * width), low),
            vmem((items * width // 128, tokens, 128), f32),
            vmem((items * width // 128, tokens, 128), f32),
            vmem((2, 4 * tokens, tokens), f32),
            vmem((2, tokens, 4 * tokens), low),
            vmem((table.shape[0], width), low),
            vmem((table.shape[0], width), low),
            vmem((items, hide, pixel_count), low),
            vmem(cols.shape, f32),
            vmem(down.shape, f32),
            vmem(head.shape, f32),
        ],
        compiler_params=pltpu.CompilerParams(
            dimension_semantics=("arbitrary",), vmem_limit_bytes=63 * 1024 * 1024
        ),
        cost_estimate=pl.CostEstimate(
            flops=70_000_000_000, bytes_accessed=40_000_000, transcendentals=20_000_000
        ),
    )(scal, latent, keep, gsd, table, pixels, cols, rows, rows, gains)


MESH_ID = pl.DeviceIdType.MESH


def place():
    g = lax.axis_index("grp")
    d = lax.axis_index("dp")
    z, c = d // 2, d % 2
    xn = g + 1 - 2 * (g % 2)
    yn = (g + 2) % 4
    return g, z, c, xn, yn


def pieces(shape, parts):
    rows, columns = shape
    if rows // parts >= 32:
        n = rows // parts
        cut = [(slice(i * n, (i + 1) * n), slice(0, columns)) for i in range(parts)]
    else:
        n = columns // parts
        cut = [(slice(0, rows), slice(i * n, (i + 1) * n)) for i in range(parts)]
    return cut


def halves(cut):
    rows, columns = cut
    mid = (columns.start + columns.stop) // 2
    return (rows, slice(columns.start, mid)), (rows, slice(mid, columns.stop))


def greet(peers):
    barrier = pltpu.get_barrier_semaphore()
    for peer in peers:
        pl.semaphore_signal(barrier, inc=1, device_id=peer, device_id_type=MESH_ID)
    pl.semaphore_wait(barrier, len(peers))


GATHER_SEMS = 14


def gather_events(count, chunks, ahead, ins, outs, sems):
    zs, zr, xs, xr, ys, yr, fs, fr, gs, gr, cs, os, cr, ls = sems
    g, z, c, xn, yn = place()
    dg = (xn + 2) % 4
    here = 2 * z + c
    other = 1 - c
    sib = (g, 2 * z + 1 - c)
    right, up = (xn, here), (yn, here)
    zpeer = [(g, 2 * ((z + j) % 4) + c) for j in (1, 2, 3)]
    zfrom = [(z + 4 - j) % 4 for j in (1, 2, 3)]
    peers = [sib, right, up] + zpeer
    work = []
    for array in range(count):
        for cut in pieces(ins[array].shape[1:], chunks[array]):
            work.append((array, cut))
    steps = len(work)
    sent = []

    def send(src, dst, send_sem, recv_sem, peer):
        return pltpu.make_async_remote_copy(
            src_ref=src, dst_ref=dst, send_sem=send_sem, recv_sem=recv_sem,
            device_id=peer, device_id_type=MESH_ID,
        )

    def go(make):
        make().start()
        sent.append(make)

    def block(array, z_at, q, cut):
        return outs[array].at[z_at, c, q, cut[0], cut[1]]

    def zcopy(k, j):
        array, cut = work[k]
        return send(
            ins[array].at[g, cut[0], cut[1]], block(array, z, g, cut), zs.at[k, j], zr.at[k, j], zpeer[j]
        )

    def relay(k, j, q, cut, ssem, rsem, peer):
        at = block(work[k][0], zfrom[j], q, cut)
        return send(at, at, ssem, rsem, peer)

    def to_x(k, j):
        return relay(k, j, g, work[k][1], xs.at[k, j], xr.at[k, j], right)

    def to_y(k, j):
        return relay(k, j, g, work[k][1], ys.at[k, j], yr.at[k, j], up)

    def to_core(k, j, i, q):
        return relay(k, j, q, work[k][1], cs.at[k, j, i], cr.at[work[k][0]], sib)

    def on_y(k, j, q):
        return relay(k, j, q, halves(work[k][1])[0], fs.at[k, j], fr.at[k, j], up)

    def on_x(k, j, q):
        return relay(k, j, q, halves(work[k][1])[1], gs.at[k, j], gr.at[k, j], right)

    def own(array):
        return pltpu.make_async_copy(ins[array], outs[array].at[z, c], ls.at[array])

    def own_to_core(array):
        return send(ins[array], outs[array].at[z, c], os.at[array], cr.at[array], sib)

    def begin():
        for k in range(min(ahead, steps)):
            for j in range(3):
                go(functools.partial(zcopy, k, j))

    def begin_own():
        for array in range(count):
            own(array).start()
        for array in range(count):
            go(functools.partial(own_to_core, array))

    def event(t):
        if t < steps:
            for j in range(3):
                zcopy(t, j).wait_recv()
                go(functools.partial(to_x, t, j))
                go(functools.partial(to_y, t, j))
                go(functools.partial(to_core, t, j, 0, g))
            if t + ahead < steps:
                for j in range(3):
                    go(functools.partial(zcopy, t + ahead, j))
        if 1 <= t <= steps:
            k = t - 1
            for j in range(3):
                relay(k, j, xn, work[k][1], xs.at[k, j], xr.at[k, j], right).wait_recv()
                go(functools.partial(on_y, k, j, xn))
                go(functools.partial(to_core, k, j, 1, xn))
                relay(k, j, yn, work[k][1], ys.at[k, j], yr.at[k, j], up).wait_recv()
                go(functools.partial(on_x, k, j, yn))
                go(functools.partial(to_core, k, j, 2, yn))
        if 2 <= t:
            k = t - 2
            for j in range(3):
                on_y(k, j, dg).wait_recv()
                on_x(k, j, dg).wait_recv()
                go(functools.partial(to_core, k, j, 3, dg))

    def finish():
        for make in sent:
            make().wait_send()
        for array in range(count):
            whole = outs[array].at[:, other]
            send(whole, whole, os.at[array], cr.at[array], sib).wait_recv()
            own(array).wait()

    return peers, begin, begin_own, [functools.partial(event, t) for t in range(steps + 2)], finish


def gather_scratch(count, steps):
    dma = pltpu.SemaphoreType.DMA
    return [dma((steps, 3))] * 10 + [dma((steps, 3, 4)), dma((count,)), dma((count,)), dma((count,))]


def gather_kernel(count, chunks, ahead, *refs):
    ins, items_ref = refs[:count], refs[count]
    outs, items_out = refs[count + 1 : 2 * count + 1], refs[2 * count + 1]
    sems = refs[2 * count + 2 :]
    it, its, itr, load_sem = sems[GATHER_SEMS : GATHER_SEMS + 4]
    wide = sems[GATHER_SEMS + 4 : GATHER_SEMS + 4 + count]
    masters, ins = ins, sems[GATHER_SEMS + 4 + count :]
    parts = [(array, cut) for array in range(count) for cut in pieces(ins[array].shape[1:], chunks[array])]
    loads = [
        pltpu.make_async_copy(
            masters[array].at[:, cut[0], cut[1]], wide[array].at[:, cut[0], cut[1]], load_sem.at[i]
        )
        for i, (array, cut) in enumerate(parts)
    ]
    for load in loads:
        load.start()
    peers, begin, begin_own, events, finish = gather_events(
        count, chunks, ahead, ins, outs, sems[:GATHER_SEMS]
    )

    def narrow(i):
        array, cut = parts[i]
        loads[i].wait()
        ins[array][:, cut[0], cut[1]] = wide[array][:, cut[0], cut[1]].astype(ins[array].dtype)

    greet(peers)
    _, right, up = peers[:3]

    def items_copy(i, peer):
        return pltpu.make_async_remote_copy(
            src_ref=it.at[2 * i], dst_ref=it.at[2 * i + 1], send_sem=its.at[i], recv_sem=itr.at[i],
            device_id=peer, device_id_type=MESH_ID,
        )

    it[0] = items_ref[...]
    items_copy(0, right).start()
    for i in range(ahead):
        narrow(i)
    begin()
    for i in range(ahead, len(parts)):
        narrow(i)
    begin_own()
    for t, event in enumerate(events):
        event()
        if t == 0:
            items_copy(0, right).wait_recv()
            it[2] = it[0] + it[1]
            items_copy(1, up).start()
        if t == 1:
            items_copy(1, up).wait_recv()
            items_out[...] = it[2] + it[3]
    finish()
    items_copy(0, right).wait_send()
    items_copy(1, up).wait_send()


def gather_call(shards, items, chunks, ahead=2, collective_id=0):
    count = len(shards)
    steps = sum(chunks)
    views = [s.reshape(4, s.shape[0] // 4, s.shape[1]) for s in shards]
    dma = pltpu.SemaphoreType.DMA
    hbm = pl.BlockSpec(memory_space=pl.ANY)
    vm = pl.BlockSpec(memory_space=pltpu.VMEM)
    *outs, total = pl.pallas_call(
        functools.partial(gather_kernel, count, chunks, ahead),
        out_shape=tuple(jax.ShapeDtypeStruct((4, 2) + v.shape, jnp.bfloat16) for v in views)
        + (jax.ShapeDtypeStruct((8, 128), jnp.float32),),
        in_specs=[hbm] * count + [vm],
        out_specs=tuple([hbm] * count + [vm]),
        scratch_shapes=gather_scratch(count, steps)
        + [pltpu.VMEM((4, 8, 128), jnp.float32), dma((2,)), dma((2,)), dma((steps,))]
        + [pltpu.VMEM(v.shape, jnp.float32) for v in views]
        + [pltpu.VMEM(v.shape, jnp.bfloat16) for v in views],
        compiler_params=pltpu.CompilerParams(
            collective_id=collective_id, has_side_effects=True, vmem_limit_bytes=60 * 1024 * 1024
        ),
    )(*views, jnp.broadcast_to(items, (8, 128)))
    return [o.reshape(-1, o.shape[-1]) for o in outs], total[0, 0]


RUN = 256


def same_item():
    row = lax.broadcasted_iota(jnp.int32, (RUN, RUN), 0) // K
    column = lax.broadcasted_iota(jnp.int32, (RUN, RUN), 1) // K
    return row == column


def encoder_kernel(heads, chunks, *refs):
    count = 2 if chunks else 0
    (pixels_ref, keep_ref, bands_ref, gsd_ref, table_ref, rows_ref, cols_ref, de_ref, gains_ref) = refs[:9]
    shards = refs[9 : 9 + count]
    outs = refs[9 + count :]
    z_ref, band_ref, a_ref, gp_ref, x2_ref = outs[:5]
    stored = outs[5:13]
    gathered = outs[13 : 13 + count]
    rest = outs[13 + count :]
    pix_ref, x_ref, qkv_ref, p_ref, inv_ref, oo_ref, x1_ref, o_s = rest[:8]
    h_s, s_s, high_s, low_s, de_s, store_sem, de_sem = rest[8:15]
    low = jnp.bfloat16
    step = pl.program_id(0)
    width = x_ref.shape[1]
    ee = width // heads
    groups = width // LANES
    expo = ee ** (-0.5) * 1.4426950408889634
    if chunks:
        low_shards = rest[15 + GATHER_SEMS : 17 + GATHER_SEMS]
        wide_shards = rest[17 + GATHER_SEMS : 19 + GATHER_SEMS]
        shard_sem = rest[19 + GATHER_SEMS]
        peers, begin, begin_own, events, finish = gather_events(
            count, chunks, 2, low_shards, gathered, rest[15 : 15 + GATHER_SEMS]
        )

    def gain(i):
        return gains_ref[i : i + 1, :]

    def store(i):
        return pltpu.make_async_copy(rest[i], stored[i], store_sem.at[i])

    def load_de():
        return pltpu.make_async_copy(gathered[1].at[2] if chunks else de_ref, de_s, de_sem)

    if chunks:

        @pl.when(step == 0)
        def _():
            loads = [
                pltpu.make_async_copy(shards[i], wide_shards[i], shard_sem.at[i]) for i in range(count)
            ]
            for load in loads:
                load.start()
            greet(peers)
            for i in range(count):
                loads[i].wait()
                low_shards[i][...] = wide_shards[i][...].astype(low)
            begin()
            begin_own()

        for at, event in zip((3, 5, 7, 8, 9, 10), events):
            pl.when(step == at)(event)

    @pl.when(step == 11)
    def _():
        if chunks:
            finish()
        load_de().start()

    @pl.when(step == 0)
    def _():
        split_table(table_ref, high_s, low_s)

        @pl.loop(0, pixels_ref.shape[0])
        def _(i):
            at = pl.ds(pl.multiple_of(i * K, K), K)
            hot = one_hot(keep_ref[i], pixels_ref.shape[1])
            pix_ref[at, :] = dot_nn(hot.astype(low), pixels_ref[i]).astype(low)
            band_ref[at, :] = jnp.sum(hot * bands_ref[i].astype(jnp.float32), -1, keepdims=True).astype(jnp.int32)
            x_ref[at, :] = look_up(hot, gsd_ref[i].astype(jnp.float32), high_s, low_s)

        store(0).start()

    @pl.when(step < 4)
    def _():
        pixel = pix_ref[...]
        x_ref[...] += dot_nn(jnp.where(band_ref[...] == step, pixel, jnp.zeros_like(pixel)), rows_ref[...])

    @pl.when(step == 4)
    def _():
        store(1).start()
        hat, _ = unit_rows(x_ref[...])
        h_s[...] = (hat * gain(0) + gain(1)).astype(low)

    @pl.when((step >= 4) & (step < 7))
    def _():
        at = pl.ds(pl.multiple_of((step - 4) * width, width), width)
        qkv_ref[:, at] = dot_nn(h_s[...], cols_ref[...]).astype(low)

    @pl.when(step == 7)
    def _():
        store(2).start()
        same = same_item()

        for n in range(x_ref.shape[0] // RUN * groups):
            attend(n, groups, RUN, width, ee, expo, same, qkv_ref, s_s.at[n % 2], p_ref, inv_ref, oo_ref, o_s)

        for i in (3, 4, 5, 7):
            store(i).start()
        x1_ref[...] = x_ref[...] + dot_nn(o_s[...], cols_ref[...])
        store(6).start()
        hat, _ = unit_rows(x1_ref[...])
        h_s[...] = (hat * gain(2) + gain(3)).astype(low)
        x2_ref[...] = x1_ref[...]

    @pl.when(step >= 8)
    def _():
        half = width // 2
        for t in range(2):
            at = slice(t * half, (t + 1) * half)
            u = dot_nn(h_s[...], cols_ref[:, at])
            cumul = 0.5 * (1.0 + lax.erf(u * 0.7071067811865476))
            a_ref[:, at] = (u * cumul).astype(low)
            gp_ref[:, at] = (cumul + u * jnp.exp(-0.5 * u * u) * 0.3989422804014327).astype(low)

        x2_ref[...] += dot_nn(a_ref[...], rows_ref[...])

    @pl.when(step == 11)
    def _():
        hat, _ = unit_rows(x2_ref[...])
        h_s[...] = (hat * gain(4) + gain(5)).astype(low)
        load_de().wait()
        z_ref[...] = dot_nn(h_s[...], de_s[...].reshape(width, z_ref.shape[1]))
        for i in range(8):
            store(i).wait()


def encoder_call(pixels, keep, bands, gsd, table, rows, cols, de, gains, heads, shards=()):
    width = cols.shape[0]
    tokens = keep.shape[0] * K
    low, f32 = jnp.bfloat16, jnp.float32
    runs = tokens // RUN * (width // LANES)
    wide = LANES // (width // heads) * RUN
    one = pl.Buffered(1)
    hbm = pl.BlockSpec(memory_space=pl.ANY)
    vmem = pltpu.VMEM
    chunks = (2, 2) if shards else ()
    views = [s.reshape(4, s.shape[0] // 4, s.shape[1]) for s in shards]
    if shards:
        narrow = shards[1].shape[1]
        de, de_shape = jnp.zeros((8, 128), low), (2, 4, 128, narrow)
    else:
        narrow, de_shape = de.shape[1], de.shape

    def whole(shape):
        return pl.BlockSpec(shape, lambda s: (0,) * len(shape), pipeline_mode=one)

    def row_block(s):
        return (jnp.where(s < 4, s + 4, jnp.where(s < 8, 0, s - 8)), 0)

    def column_block(s):
        return (0, jnp.where(s < 4, 0, s - 4))

    def hidden_block(s):
        return (0, jnp.where(s < 8, 0, s - 8))

    hidden = pl.BlockSpec((tokens, width), hidden_block)
    blocks = [
        ((tokens, narrow), f32, whole((tokens, narrow))),
        ((tokens, 1), jnp.int32, whole((tokens, 1))),
        ((tokens, 4 * width), low, hidden),
        ((tokens, 4 * width), low, hidden),
        ((tokens, width), f32, whole((tokens, width))),
    ]
    held = [
        ((tokens, pixels.shape[2]), low),
        ((tokens, width), f32),
        ((tokens, 3 * width), low),
        ((runs, RUN, wide), low),
        ((runs, RUN, LANES), f32),
        ((runs, RUN, LANES), f32),
        ((tokens, width), f32),
        ((tokens, width), low),
    ]
    struct = jax.ShapeDtypeStruct
    out = pl.pallas_call(
        functools.partial(encoder_kernel, heads, chunks),
        grid=(12,),
        in_specs=[
            whole(pixels.shape),
            whole(keep.shape),
            whole(bands.shape),
            whole(gsd.shape),
            pl.BlockSpec((table.shape[0], width), lambda s: (0, 0), pipeline_mode=one),
            pl.BlockSpec((width, width), row_block),
            pl.BlockSpec((width, width), column_block),
            hbm,
            whole(gains.shape),
        ]
        + [hbm] * len(views),
        out_specs=tuple(b[2] for b in blocks) + (hbm,) * (len(held) + len(views)),
        out_shape=tuple(struct(b[0], b[1]) for b in blocks)
        + tuple(struct(*h) for h in held)
        + tuple(struct((4, 2) + v.shape, low) for v in views),
        scratch_shapes=[vmem(*h) for h in held]
        + [
            vmem((tokens, width), low),
            vmem((2, wide, RUN), f32),
            vmem((table.shape[0], width), low),
            vmem((table.shape[0], width), low),
            vmem(de_shape, low),
            pltpu.SemaphoreType.DMA((8,)),
            pltpu.SemaphoreType.DMA,
        ]
        + (gather_scratch(2, sum(chunks)) if shards else [])
        + [vmem(v.shape, low) for v in views]
        + [vmem(v.shape, f32) for v in views]
        + ([pltpu.SemaphoreType.DMA((2,))] if shards else []),
        compiler_params=pltpu.CompilerParams(
            dimension_semantics=("arbitrary",),
            vmem_limit_bytes=60 * 1024 * 1024,
            collective_id=2 if shards else None,
            has_side_effects=bool(shards),
        ),
        cost_estimate=pl.CostEstimate(
            flops=20_000_000_000, bytes_accessed=70_000_000, transcendentals=8_000_000
        ),
    )(pixels, keep, bands, gsd, table, rows, cols, de, gains, *views)
    z, band, a, gp, x2 = out[:5]
    pix, x, qkv, p, inv, oo, x1, o = out[5:13]
    saved = (x, qkv, p, inv, oo, x1, a, gp, x2, o)
    return z, pix, band, saved, [w.reshape(-1, w.shape[-1]) for w in out[13:]]


def encoder_back_kernel(
    heads, dz_ref, pix_ref, band_ref, x_ref, qkv_ref, p_ref, inv_ref, oo_ref, x1_ref, a_ref, gp_ref, x2_ref,
    rows_ref, cols_ref, de_ref, gains_ref,
    grows_ref, gcols_ref, gde_ref, ggains_ref,
    h_s, dx_s, dy_s, acc_s, do_s, dqkv_s, s_s, ds_s,
):
    low, f32 = jnp.bfloat16, jnp.float32
    step = pl.program_id(0)
    width = x_ref.shape[1]
    ee = width // heads
    groups = width // LANES
    runs = x_ref.shape[0] // RUN

    def gain(i):
        return gains_ref[i : i + 1, :]

    def back(x, grads, at):
        hat, scaled = unit_rows(x)
        ggains_ref[at : at + 1, :] = jnp.sum(grads * hat, 0, keepdims=True)
        ggains_ref[at + 1 : at + 2, :] = jnp.sum(grads, 0, keepdims=True)
        return unit_back(grads, hat, scaled, gain(at))

    def normed(x, at):
        hat, _ = unit_rows(x)
        h_s[...] = (hat * gain(at) + gain(at + 1)).astype(low)

    @pl.when(step == 0)
    def _():
        ggains_ref[...] = jnp.zeros_like(ggains_ref)
        normed(x2_ref[...], 4)
        gde_ref[...] = dot_tn(h_s[...], dz_ref[...]).astype(low)
        dx_s[...] = back(x2_ref[...], dot_nt(dz_ref[...], de_ref[...]), 4)
        dy_s[...] = dx_s[...].astype(low)
        normed(x1_ref[...], 2)
        acc_s[...] = jnp.zeros_like(acc_s)

    @pl.when(step < 4)
    def _():
        grows_ref[...] = dot_tn(a_ref[...], dy_s[...]).astype(low)
        du = (dot_nt(dy_s[...], rows_ref[...]) * gp_ref[...].astype(f32)).astype(low)
        do_s[...] = du
        gcols_ref[...] = dot_tn(h_s[...], du).astype(low)
        acc_s[...] += dot_nt(do_s[...], cols_ref[...])

    @pl.when(step == 4)
    def _():
        dx_s[...] += back(x1_ref[...], acc_s[...], 2)
        dy_s[...] = dx_s[...].astype(low)
        for run in range(runs):
            for g in range(groups):
                h_s[run * RUN : (run + 1) * RUN, g * LANES : (g + 1) * LANES] = oo_ref[
                    run * groups + g
                ].astype(low)
        gcols_ref[...] = dot_tn(h_s[...], dy_s[...]).astype(low)
        do_s[...] = dot_nt(dy_s[...], cols_ref[...]).astype(low)

        for n in range(runs * groups):
            attend_back(
                n, n, groups, RUN, width, ee, ee ** (-0.5), qkv_ref, s_s, ds_s, p_ref, inv_ref, oo_ref, do_s,
                dqkv_s,
            )

        normed(x_ref[...], 0)
        acc_s[...] = jnp.zeros_like(acc_s)

    @pl.when((step >= 5) & (step < 8))
    def _():
        at = pl.ds(pl.multiple_of((step - 5) * width, width), width)
        gcols_ref[...] = dot_tn(h_s[...], dqkv_s[:, at]).astype(low)
        acc_s[...] += dot_nt(dqkv_s[:, at], cols_ref[...])

    @pl.when(step == 8)
    def _():
        dx_s[...] += back(x_ref[...], acc_s[...], 0)
        dy_s[...] = dx_s[...].astype(low)

    @pl.when(step >= 8)
    def _():
        pixel = pix_ref[...]
        h_s[...] = jnp.where(band_ref[...] == step - 8, pixel, jnp.zeros_like(pixel))
        grows_ref[...] = dot_tn(h_s[...], dy_s[...]).astype(low)


def encoder_back_call(dz, pixel, band, saved, rows, cols, de, gains, heads):
    x, qkv, p, inv, oo, x1, a, gp, x2, _ = saved
    tokens, width = x.shape
    low, f32 = jnp.bfloat16, jnp.float32
    wide = p.shape[2]
    one = pl.Buffered(1)

    def whole(array):
        return pl.BlockSpec(array.shape, lambda s: (0,) * len(array.shape), pipeline_mode=one)

    def row_block(s):
        return (jnp.minimum(s, 3), 0)

    def column_block(s):
        return (0, jnp.where(s < 4, s + 4, jnp.where(s == 4, 3, jnp.minimum(s - 5, 2))))

    def hidden_block(s):
        return (0, jnp.minimum(s, 3))

    def grow_block(s):
        return (jnp.where(s < 4, s, jnp.where(s < 8, 3, s - 4)), 0)

    hidden = pl.BlockSpec((tokens, width), hidden_block)
    square = (width, width)
    outs = (
        jax.ShapeDtypeStruct(rows.shape, low),
        jax.ShapeDtypeStruct(cols.shape, low),
        jax.ShapeDtypeStruct(de.shape, low),
        jax.ShapeDtypeStruct((8, width), f32),
    )
    vmem = pltpu.VMEM
    return pl.pallas_call(
        functools.partial(encoder_back_kernel, heads),
        grid=(12,),
        in_specs=[
            whole(dz), whole(pixel), whole(band), whole(x), whole(qkv), whole(p), whole(inv), whole(oo),
            whole(x1), hidden, hidden, whole(x2),
            pl.BlockSpec(square, row_block), pl.BlockSpec(square, column_block),
            whole(de), whole(gains),
        ],
        out_specs=(
            pl.BlockSpec(square, grow_block),
            pl.BlockSpec(square, column_block),
            whole(outs[2]),
            whole(outs[3]),
        ),
        out_shape=outs,
        scratch_shapes=[
            vmem((tokens, width), low),
            vmem((tokens, width), f32),
            vmem((tokens, width), low),
            vmem((tokens, width), f32),
            vmem((tokens, width), low),
            vmem((tokens, 3 * width), low),
            vmem((wide, RUN), f32),
            vmem((RUN, wide), low),
        ],
        compiler_params=pltpu.CompilerParams(
            dimension_semantics=("arbitrary",), vmem_limit_bytes=60 * 1024 * 1024
        ),
        cost_estimate=pl.CostEstimate(
            flops=40_000_000_000, bytes_accessed=110_000_000, transcendentals=1_000_000
        ),
    )(dz, pixel, band, x, qkv, p, inv, oo, x1, a, gp, x2, rows, cols, de, gains)


def back_reduce_kernel(heads, kinds, work, pieces, refs_in, refs_out, *refs):
    low, f32 = jnp.bfloat16, jnp.float32
    ref = dict(zip(refs_in + refs_out, refs))
    rest = refs[len(refs_in) + len(refs_out) :]
    per = 9
    bufs = [rest[per * i : per * i + per] for i in range(len(kinds))]
    (sm, ss, ssx, dx, acc, xin, h, dy, wide, wt, wu, out_r, out_c, out_e, p_t, inv_t, oo_t, s_s, ds_s, gsum,
     cs, cr, ls, os, x1s, x1r, x2s, x2r, z_s, z_r, ags, agr, ks, sms, smr, sss, ssr, dma, att_sem) = rest[
        per * len(kinds) :
    ]
    g, z, c, xn, yn = place()
    dg = (xn + 2) % 4
    here = 2 * z + c
    sib = (g, 2 * z + 1 - c)
    right, up = (xn, here), (yn, here)
    zto = [(z + j) % 4 for j in (1, 2, 3)]
    zpeer = [(g, 2 * t + c) for t in zto]
    greet([sib, right, up] + zpeer)
    steps = len(work)
    sent = []
    from_slot = [[] for _ in range(steps)]

    def send(src, dst, send_sem, recv_sem, peer):
        return pltpu.make_async_remote_copy(
            src_ref=src, dst_ref=dst, send_sem=send_sem, recv_sem=recv_sem,
            device_id=peer, device_id_type=MESH_ID,
        )

    def guarded(test, action):
        if test is None:
            action()
        else:
            pl.when(test)(action)

    def go(copies, keep=None, tests=None):
        for i, copy in enumerate(copies):
            test = tests[i] if tests else None
            guarded(test, copy.start)
            (sent if keep is None else keep).append((test, copy))

    def left(entries):
        for test, copy in entries:
            guarded(test, copy.wait_send)

    def got(copies):
        for copy in copies:
            copy.wait_recv()

    def mine(k, at=None):
        base = work[k][2]
        at = z if at is None else at
        return None if base is None else ((at >= base) & (at < base + 2))

    def buffers(k):
        kind, at = work[k][:2]
        return bufs[kind], at, at % kinds[kind][4], kinds[kind][2] // 2

    def c_copies(k):
        (_, crecv, *_), at, _, _ = buffers(k)
        return [
            send(
                ref[array].at[:, 1 - c, :, cut[0], cut[1]], crecv.at[at, pl.ds(z0, nz)],
                cs.at[k, i], cr.at[k, i], sib,
            )
            for i, (array, z0, nz, cut) in enumerate(work[k][3])
        ]

    def own_copies(k):
        (s, *_), _, slot, _ = buffers(k)
        return [
            pltpu.make_async_copy(
                ref[array].at[:, c, :, cut[0], cut[1]], s.at[slot, pl.ds(z0, nz)], os.at[k, i]
            )
            for i, (array, z0, nz, cut) in enumerate(work[k][3])
        ]

    def recv_load(k, i):
        (_, crecv, tmp, *_), at, _, _ = buffers(k)
        return pltpu.make_async_copy(crecv.at[at, i], tmp.at[i % 2], ls.at[k, i])

    def x1_copies(k):
        (s, _, _, xa, yb, *_), at, slot, half = buffers(k)
        lo, hi = pl.ds(0, half), pl.ds(half, half)
        return [
            send(s.at[slot, :, xn, :, lo], xa.at[at, 0], x1s.at[k, 0], x1r.at[k, 0], right),
            send(s.at[slot, :, dg, :, lo], xa.at[at, 1], x1s.at[k, 1], x1r.at[k, 1], right),
            send(s.at[slot, :, yn, :, hi], yb.at[at, 0], x1s.at[k, 2], x1r.at[k, 2], up),
            send(s.at[slot, :, dg, :, hi], yb.at[at, 1], x1s.at[k, 3], x1r.at[k, 3], up),
        ]

    def x2_copies(k):
        (s, _, _, _, _, xb, ya, *_), at, slot, half = buffers(k)
        lo, hi = pl.ds(0, half), pl.ds(half, half)
        return [
            send(s.at[slot, :, yn, :, lo], ya.at[at], x2s.at[k, 0], x2r.at[k, 0], up),
            send(s.at[slot, :, xn, :, hi], xb.at[at], x2s.at[k, 1], x2r.at[k, 1], right),
        ]

    def z_copies(k):
        (s, *_, zb, _), at, slot, _ = buffers(k)
        base = work[k][2] or 0
        return [
            send(
                s.at[slot, (zto[j] - base) % kinds[work[k][0]][0], g], zb.at[at, j],
                z_s.at[k, j], z_r.at[k, j], zpeer[j],
            )
            for j in range(3)
        ]

    def out_at(k, q, part=None):
        name, cut = work[k][4:6]
        if part is not None:
            cut = halves(cut)[part]
        return ref[name].at[q, cut[0], cut[1]]

    def ag_copies(k):
        (*_, fin), at, _, _ = buffers(k)
        return [
            send(fin.at[at], out_at(k, g), ags.at[k, 0], agr.at[k, 0], right),
            send(fin.at[at], out_at(k, g), ags.at[k, 1], agr.at[k, 1], up),
        ]

    def keep_copy(k):
        (*_, fin), at, _, _ = buffers(k)
        return pltpu.make_async_copy(fin.at[at], out_at(k, g), ks.at[k])

    def fwd_copies(k, of_x, of_y):
        return [
            send(out_at(k, of_x, 0), out_at(k, of_x, 0), ags.at[k, 2], agr.at[k, 2], up),
            send(out_at(k, of_y, 1), out_at(k, of_y, 1), ags.at[k, 3], agr.at[k, 3], right),
        ]

    def add_half(k, q, first, other):
        (s, *_), _, slot, half = buffers(k)
        part = pl.ds(0 if first else half, half)

        @pl.loop(0, kinds[work[k][0]][0])
        def _(i):
            s[slot, i, q, :, part] = (s[slot, i, q, :, part].astype(f32) + other[i].astype(f32)).astype(low)

    def load(k):
        kind, at = work[k][:2]
        slots = kinds[kind][4]
        if at >= slots:
            before = [j for j in range(steps) if work[j][:2] == (kind, at - slots)][0]
            left(from_slot[before])
            from_slot[before].clear()
        for copy in own_copies(k):
            copy.start()

    def pair(k):
        (s, _, tmp, *_), _, slot, _ = buffers(k)
        count = kinds[work[k][0]][0]
        got(c_copies(k))
        for i in range(2):
            recv_load(k, i).start()
        for copy in own_copies(k):
            copy.wait()
        for i in range(count):
            recv_load(k, i).wait()

            @pl.loop(0, 4)
            def _(q):
                s[slot, i, q] = (s[slot, i, q].astype(f32) + tmp[i % 2, q].astype(f32)).astype(low)

            if i + 2 < count:
                recv_load(k, i + 2).start()
        go(x1_copies(k), from_slot[k])

    def first_half(k):
        (_, _, _, xa, yb, *_), at, _, _ = buffers(k)
        got(x1_copies(k))
        add_half(k, yn, True, xa.at[at, 1])
        add_half(k, xn, False, yb.at[at, 1])
        go(x2_copies(k), from_slot[k])
        add_half(k, g, True, xa.at[at, 0])
        add_half(k, g, False, yb.at[at, 0])

    def second_half(k):
        (_, _, _, _, _, xb, ya, *_), at, _, _ = buffers(k)
        got(x2_copies(k))
        add_half(k, g, True, ya.at[at])
        add_half(k, g, False, xb.at[at])
        go(z_copies(k), from_slot[k], [mine(k, t) for t in zto])

    def finish(k):
        def act():
            (s, *_, zb, fin), at, slot, _ = buffers(k)
            got(z_copies(k))
            base = work[k][2] or 0
            total = s[slot, (z - base) % kinds[work[k][0]][0], g].astype(f32)
            for j in range(3):
                total = total + zb[at, j].astype(f32)
            fin[at] = total.astype(low)
            keep_copy(k).start()
            square = fin[at].astype(f32)
            square = square * square
            for i in range(square.shape[1] // ss.shape[1]):
                ss[...] += jnp.sum(
                    square[:, i * ss.shape[1] : (i + 1) * ss.shape[1]], 0, keepdims=True
                )

        guarded(mine(k), act)
        go(ag_copies(k), None, [mine(k)] * 2)

    def collect(k):
        guarded(mine(k), lambda: got(ag_copies(k)))
        go(fwd_copies(k, xn, yn), None, [mine(k)] * 2)

    def close(k):
        guarded(mine(k), lambda: got(fwd_copies(k, dg, dg)))

    stages = [load, pair, first_half, second_half, finish, collect, close]

    def share_rounds(value, sem_s, sem_r, store):
        def copy(i, slot, peer):
            return send(value.at[slot], value.at[4 + i], sem_s.at[i], sem_r.at[i], peer)

        def round_pair(i, peer, following):
            got([copy(i, i, peer)])
            value[i + 1] = value[i] + value[4 + i]
            go(following())

        def last():
            return [copy(3 + j, 3, zpeer[j]) for j in range(3)]

        def end():
            got(last())
            total = None
            for at in range(4):
                term = jnp.where(z == at, value[3], jnp.zeros_like(value[3]))
                for j in range(3):
                    term = term + jnp.where((z + 3 - j) % 4 == at, value[7 + j], jnp.zeros_like(value[3]))
                total = term if total is None else total + term
            store[...] = total

        return [
            lambda: go([copy(0, 0, sib)]),
            lambda: round_pair(0, sib, lambda: [copy(1, 1, right)]),
            lambda: round_pair(1, right, lambda: [copy(2, 2, up)]),
            lambda: round_pair(2, up, last),
            end,
        ]

    tokens, width = dx.shape
    ee = width // heads
    groups = width // LANES
    runs = tokens // RUN
    gains = ref["gains"]

    moving = {}

    def move(name, src, dst):
        copy = pltpu.make_async_copy(src, dst, dma.at[lanes_of.index(name)])
        copy.start()
        moving[name] = copy

    def done(*names):
        for name in names:
            if name in moving:
                moving.pop(name).wait()

    lanes_of = (
        "a", "gp", "rows", "cols", "x", "dz", "de", "o", "qkv", "pix", "out_r", "out_c", "out_e",
    )

    def tile(i):
        return pl.ds(i * width, width)

    def gain(i):
        return gains[i : i + 1, :]

    def back(grads, at):
        hat, scaled = unit_rows(xin[...])
        gsum[at : at + 1, :] = jnp.sum(grads * hat, 0, keepdims=True)
        gsum[at + 1 : at + 2, :] = jnp.sum(grads, 0, keepdims=True)
        return unit_back(grads, hat, scaled, gain(at))

    def normed(at):
        hat, _ = unit_rows(xin[...])
        h[...] = (hat * gain(at) + gain(at + 1)).astype(low)

    def column_grads(block, source):
        done("out_c")
        for d in range(8):
            value = dot_tn(h[:, d * 128 : (d + 1) * 128], source()).astype(low)
            out_c[d // 2, d % 2] = value.reshape(out_c.shape[2:])
        move("out_c", out_c, ref["g_cols"].at[:, :, :, :, tile(block)])

    def load_hidden(s):
        move("a", ref["a"].at[:, tile(s)], wide.at[:, tile(0)])
        move("gp", ref["gp"].at[:, tile(s)], wide.at[:, tile(1)])
        move("rows", ref["rows"].at[tile(s)], wt)

    def load_columns(block):
        move("cols", ref["cols"].at[:, tile(block)], wu)

    narrow = ref["dz"].shape[1]

    def first_loads():
        move("x", ref["x2"], xin)
        move("dz", ref["dz"], wide.at[:, pl.ds(2 * width, narrow)])
        move("de", ref["dec_rows"].at[pl.ds(2 * width, width)], wt.at[:, pl.ds(0, narrow)])
        move("a", ref["a"].at[:, tile(0)], wide.at[:, tile(0)])
        move("gp", ref["gp"].at[:, tile(0)], wide.at[:, tile(1)])
        load_columns(4)

    def head_piece(_):
        done("x", "dz", "de")
        dz = wide[:, 2 * width : 2 * width + narrow]
        normed(4)
        for d in range(8):
            out_e[0, d // 4, d % 4] = dot_tn(h[:, d * 128 : (d + 1) * 128], dz).astype(low)
        move("out_e", out_e, ref["g_de"])
        dx[...] = back(dot_nt(dz, wt[:, :narrow]), 4)
        move("rows", ref["rows"].at[tile(0)], wt)
        move("x", ref["x1"], xin)
        dy[...] = dx[...].astype(low)
        done("x")
        normed(2)
        acc[...] = jnp.zeros_like(acc)

    def hidden_piece(s):
        done("a", "gp", "rows", "out_r")
        wide[:, 2 * width :] = (dot_nt(dy[...], wt[...]) * wide[:, width : 2 * width].astype(f32)).astype(low)
        for q in range(4):
            out_r[q] = dot_tn(wide[:, q * 256 : (q + 1) * 256], dy[...]).astype(low)
        move("out_r", out_r, ref["g_down"].at[s // 2, s % 2])
        if s < 3:
            load_hidden(s + 1)
        column_grads(4 + s, lambda: wide[:, 2 * width :])
        done("cols")
        acc[...] += dot_nt(wide[:, 2 * width :], wu[...])
        load_columns(5 + s if s < 3 else 3)
        if s == 3:
            move("o", ref["o"], h)
            move("qkv", ref["qkv"], wide)

    def middle_piece(_):
        dx[...] += back(acc[...], 2)
        dy[...] = dx[...].astype(low)
        move("x", ref["x"], xin)
        done("o")
        column_grads(3, lambda: dy[...])
        done("cols")
        h[...] = dot_nt(dy[...], wu[...]).astype(low)
        load_columns(0)
        done("qkv")

    def attention_loads(n):
        slot = n % 2
        return [
            pltpu.make_async_copy(ref[name].at[n], buf.at[slot], att_sem.at[slot, i])
            for i, (name, buf) in enumerate((("p", p_t), ("inv", inv_t), ("oo", oo_t)))
        ]

    def attention_piece(part):
        count = runs * groups // 4
        first = part * count
        for copy in attention_loads(first):
            copy.start()

        for n in range(first, first + count):
            for copy in attention_loads(n):
                copy.wait()
            if n + 1 < first + count:
                for copy in attention_loads(n + 1):
                    copy.start()
            attend_back(
                n, n % 2, groups, RUN, width, ee, ee ** (-0.5), wide, s_s.at[n % 2], ds_s.at[n % 2], p_t, inv_t,
                oo_t, h, wide,
            )

    def input_piece(t):
        if t == 0:
            done("x")
            normed(0)
            acc[...] = jnp.zeros_like(acc)
        column_grads(t, lambda: wide[:, t * width : (t + 1) * width])
        done("cols")
        acc[...] += dot_nt(wide[:, t * width : (t + 1) * width], wu[...])
        if t < 2:
            load_columns(t + 1)
        else:
            move("pix", ref["pix"], h)

    def first_piece(_):
        dx[...] += back(acc[...], 0)
        dy[...] = dx[...].astype(low)
        sm[0] = ref["small"][...]
        sm[0, 0:6, :] = gsum[0:6, :]

    def embed_piece(b):
        done("pix", "out_r")
        for q in range(4):
            part = h[:, q * 256 : (q + 1) * 256]
            part = jnp.where(ref["band"][...] == b, part, jnp.zeros_like(part))
            out_r[q] = dot_tn(part, dy[...]).astype(low)
        move("out_r", out_r, ref["g_emb"].at[b // 2, b % 2])

    action = {
        "head": head_piece, "hidden": hidden_piece, "middle": middle_piece, "attention": attention_piece,
        "input": input_piece, "first": first_piece, "embed": embed_piece,
    }

    ss[...] = jnp.zeros_like(ss)
    gsum[...] = jnp.zeros_like(gsum)
    small_rounds = share_rounds(sm, sms, smr, ref["small_out"])
    square_rounds = share_rounds(ssx, sss, ssr, ref["ss_out"])
    ends = [w[6] + 6 for w in work]
    last = max(ends)
    squared = max(w[6] + 4 for w in work)
    compute_end = max(t for t, _, _ in pieces)
    for t in range(last + 1):
        done("out_r", "out_c", "out_e")
        for i in (1, 6, 5, 4, 3, 2, 0):
            for k in range(steps):
                if work[k][6] + i == t:
                    stages[i](k)
        if t == 0:
            first_loads()
        for k in range(steps):
            if work[k][7] == t:
                go(c_copies(k))
        for at, name, argument in pieces:
            if at == t:
                action[name](argument)
        if compute_end < t <= compute_end + 5:
            small_rounds[t - compute_end - 1]()
        if t == squared:
            ssx[0] = jnp.broadcast_to(jnp.sum(ss[...], keepdims=True).reshape(1, 1), ssx.shape[1:])
            square_rounds[0]()
        if squared < t < last:
            square_rounds[t - squared]()
        if t == last:
            for following in square_rounds[last - squared :]:
                following()
    for k in range(steps):
        left(from_slot[k])
    left(sent)
    for k in range(steps):
        guarded(mine(k), keep_copy(k).wait)


def back_reduce_call(dz, pix, band, saved, rows, cols, dec_rows, gains, dcols, ddown, dhead, small, heads):
    x, qkv, p, inv, oo, x1, a, gp, x2, o = saved
    tokens, width = x.shape
    low, f32 = jnp.bfloat16, jnp.float32
    narrow = dec_rows.shape[1]
    ins = dict(
        dz=dz, pix=pix, band=band, x=x, x1=x1, x2=x2, qkv=qkv, p=p, inv=inv, oo=oo, o=o, a=a, gp=gp,
        rows=rows, cols=cols, dec_rows=dec_rows, gains=gains, small=small,
        d_cols=dcols.reshape(4, 2, 4, 16, dcols.shape[1]),
        d_down=ddown.reshape(2, 2, 4, 128, narrow),
        d_head=dhead.reshape(1, 2, 4, 128, narrow),
    )
    outs = dict(
        erows=((4, 256, width), low), ecols=((4, 32, cols.shape[1]), low),
        dcols=((4, 16, dcols.shape[1]), low), drows=((4, 128, narrow), low),
        small_out=(small.shape, f32), ss_out=((8, 128), f32),
        g_down=((2, 2, 4, 256, width), low), g_emb=((2, 2, 4, 256, width), low),
        g_cols=((4, 2, 4, 32, cols.shape[1]), low), g_de=((1, 2, 4, 128, narrow), low),
    )
    kinds = ((4, 32, 1024, 16, 6), (4, 16, 2048, 2, 2), (4, 64, 512, 2, 2))

    def column_chunk(at, block):
        cut = (slice(0, 32), slice(block * 1024, (block + 1) * 1024))
        return (0, at, None, (("g_cols", 0, 4, cut),), "ecols", cut)

    def row_chunk(at, i):
        cut = (slice(i * 32, (i + 1) * 32), slice(0, width))
        return (0, at, None, (("g_down", 0, 2, cut), ("g_emb", 2, 2, cut)), "erows", cut)

    chunks = []
    for i in range(2):
        cut = (slice(0, 16), slice(i * 2048, (i + 1) * 2048))
        chunks.append((1, i, None, (("d_cols", 0, 4, cut),), "dcols", cut))
    for i in range(2):
        cut = (slice(i * 64, (i + 1) * 64), slice(0, narrow))
        sources = (("d_down", 0, 2, cut), ("g_de", 2, 1, cut), ("d_head", 3, 1, cut))
        chunks.append((2, i, None, sources, "drows", cut))
    chunks += [column_chunk(i, 4 + i) for i in range(4)]
    chunks += [column_chunk(4 + i, block) for i, block in enumerate((3, 0, 1, 2))]
    chunks += [row_chunk(8 + i, i) for i in range(8)]
    starts = (0, 1, 2, 3, 4, 5, 6, 7, 8, 10, 11, 12) + tuple(range(13, 21))
    begins = (0, 0, 2, 2, 3, 4, 5, 6, 7, 10, 10, 11) + (13,) + tuple(range(13, 20))
    work = tuple(chunk + (starts[i], begins[i]) for i, chunk in enumerate(chunks))
    pieces = [(1, "head", 0)] + [(2 + s, "hidden", s) for s in range(4)] + [(6, "middle", 0)]
    pieces += [(7 + i // 2, "attention", i) for i in range(4)]
    pieces += [(9, "input", 0), (9, "input", 1), (10, "input", 2), (10, "first", 0)]
    pieces += [(11 + i // 2, "embed", i) for i in range(4)]
    steps = len(work)
    hbm = pl.BlockSpec(memory_space=pl.ANY)
    vm = pl.BlockSpec(memory_space=pltpu.VMEM)
    vmem, sems = pltpu.VMEM, pltpu.SemaphoreType.DMA
    scratch, landing = [], {}
    for i, (nz, r, col, count, slots) in enumerate(kinds):
        landing[f"land{i}"] = ((count, nz, 4, r, col), low)
        half = col // 2
        scratch += [
            vmem((slots, nz, 4, r, col), low),
            None,
            vmem((2, 4, r, col), low),
            vmem((count, 2, nz, r, half), low),
            vmem((count, 2, nz, r, half), low),
            vmem((count, nz, r, half), low),
            vmem((count, nz, r, half), low),
            vmem((count, 3, r, col), low),
            vmem((count, r, col), low),
        ]
    outs.update(landing)
    in_names, out_names = tuple(ins), tuple(outs)

    def kernel(*refs):
        n = len(in_names) + len(out_names)
        ref = dict(zip(in_names + out_names, refs))
        kept = list(refs[n:])
        for i in range(len(kinds)):
            kept.insert(9 * i + 1, ref[f"land{i}"])
        back_reduce_kernel(heads, kinds, work, pieces, in_names, out_names, *refs[:n], *kept)

    result = pl.pallas_call(
        kernel,
        out_shape=tuple(jax.ShapeDtypeStruct(*outs[name]) for name in out_names),
        in_specs=[vm if name in ("band", "gains", "small") else hbm for name in in_names],
        out_specs=tuple(vm if name in ("small_out", "ss_out") else hbm for name in out_names),
        scratch_shapes=[s for s in scratch if s is not None]
        + [
            vmem((10,) + small.shape, f32),
            vmem((1, 512), f32),
            vmem((10, 8, 128), f32),
            vmem((tokens, width), f32),
            vmem((tokens, width), f32),
            vmem((tokens, width), f32),
            vmem((tokens, width), low),
            vmem((tokens, width), low),
            vmem((tokens, 3 * width), low),
            vmem((width, width), low),
            vmem((width, width), low),
            vmem((4, 256, width), low),
            vmem((4, 2, 4, 32, width), low),
            vmem((1, 2, 4, 128, narrow), low),
            vmem((2,) + p.shape[1:], low),
            vmem((2,) + inv.shape[1:], f32),
            vmem((2,) + oo.shape[1:], f32),
            vmem((2, p.shape[2], RUN), f32),
            vmem((2, RUN, p.shape[2]), low),
            vmem((8, width), f32),
            sems((steps, 3)), sems((steps, 3)), sems((steps, 4)), sems((steps, 3)),
            sems((steps, 4)), sems((steps, 4)),
            sems((steps, 2)), sems((steps, 2)),
            sems((steps, 3)), sems((steps, 3)),
            sems((steps, 4)), sems((steps, 4)),
            sems((steps,)), sems((6,)), sems((6,)), sems((6,)), sems((6,)), sems((13,)), sems((2, 3)),
        ],
        compiler_params=pltpu.CompilerParams(
            collective_id=1, has_side_effects=True, vmem_limit_bytes=63 * 1024 * 1024
        ),
    )(*ins.values())
    got = dict(zip(out_names, result))
    shards = [got[name].reshape(-1, got[name].shape[-1]) for name in ("ecols", "erows", "dcols", "drows")]
    return shards, got["small_out"], got["ss_out"]


def adam_step(master, moment, square, grad, factor, fix_one, fix_two, decay, rate):
    clipped = grad * factor
    moment_new = beta_first * moment + (1.0 - beta_first) * clipped
    square_new = beta_second * square + (1.0 - beta_second) * clipped * clipped
    direction = moment_new / fix_one / (jnp.sqrt(square_new / fix_two) + adam_eps) + decay * master
    return (clipped, square_new, master - rate * direction)


def adam_kernel(count_e, count_d, *refs):
    scal_ref, small_ref, ss_ref = refs[:3]
    ins, outs = refs[3:25], refs[25:]
    small = small_ref[...]
    width = small.shape[1]
    flat = lax.broadcasted_iota(jnp.int32, small.shape, 0) * width + lax.broadcasted_iota(
        jnp.int32, small.shape, 1
    )
    gains = jnp.where(flat < count_e + count_d, small, 0.0)
    norm = jnp.sqrt(ss_ref[0:1, 0:1] + jnp.sum(gains * gains, keepdims=True).reshape(1, 1))
    factor = clip_level / jnp.maximum(norm, clip_level)
    masked, fix_one, fix_two = scal_ref[0, 0], scal_ref[0, 1], scal_ref[0, 2]

    def update(grad, master, moment, square, decay, rate):
        return adam_step(master, moment, square, grad, factor, fix_one, fix_two, decay, rate)

    for i in range(4):
        grad, master, moment, square = ins[4 * i : 4 * i + 4]
        got = update(
            grad[...].astype(jnp.float32), master[...], moment[...], square[...], weight_decay, learn_rate
        )
        for target, value in zip(outs[3 * i : 3 * i + 3], got):
            target[...] = value

    @pl.when(pl.program_id(0) == 0)
    def _():
        at = 0
        for i in range(2):
            master, moment, square = ins[16 + 3 * i : 19 + 3 * i]
            rows, columns = master.shape
            for r in range(rows):
                row, lane = at // width, at % width
                grad = small[row : row + 1, lane : lane + columns]
                one = slice(r, r + 1)
                got = update(grad, master[one, :], moment[one, :], square[one, :], 0.0, gain_rate)
                for target, value in zip(outs[12 + 3 * i : 15 + 3 * i], got):
                    target[one, :] = value
                at += columns
        outs[18][...] = small[at // width : at // width + 1, at % width : at % width + 1] / masked
        outs[19][...] = norm


def adam_call(scal, small, squares, matrices, gains):
    steps = 4

    def block(array):
        rows, columns = array.shape
        if rows // steps % 16 == 0:
            return pl.BlockSpec((rows // steps, columns), lambda s: (s, 0))
        return pl.BlockSpec((rows, columns // steps), lambda s: (0, s))

    def whole(array):
        return pl.BlockSpec(array.shape, lambda s: (0, 0))

    struct = jax.ShapeDtypeStruct
    f32 = jnp.float32
    ins, in_specs, outs, out_specs = [], [], [], []
    for group in matrices:
        ins += group
        in_specs += [block(array) for array in group]
        outs += [struct(group[1].shape, f32)] * 3
        out_specs += [block(group[1])] * 3
    for group in gains:
        ins += group
        in_specs += [whole(array) for array in group]
        outs += [struct(group[0].shape, f32)] * 3
        out_specs += [whole(group[0])] * 3
    outs += [struct((1, 1), f32)] * 2
    out_specs += [pl.BlockSpec((1, 1), lambda s: (0, 0))] * 2
    out = pl.pallas_call(
        functools.partial(adam_kernel, gains[0][0].size, gains[1][0].size),
        grid=(steps,),
        in_specs=[pl.BlockSpec(memory_space=pltpu.SMEM), whole(small), whole(squares)] + in_specs,
        out_specs=tuple(out_specs),
        out_shape=tuple(outs),
        compiler_params=pltpu.CompilerParams(
            dimension_semantics=("arbitrary",), vmem_limit_bytes=56 * 1024 * 1024
        ),
    )(scal, small, squares, *ins)
    return tuple(out[:18]) + (out[18][0, 0], out[19][0, 0])


def body(
    pixels,
    keep_index,
    band_group,
    gsd_index,
    gsd_table,
    group_items,
    step_count,
    enc_cols,
    enc_rows,
    dec_cols,
    dec_rows,
    enc_gains,
    dec_gains,
    moment_ecols,
    moment_erows,
    moment_dcols,
    moment_drows,
    moment_egains,
    moment_dgains,
    square_ecols,
    square_erows,
    square_dcols,
    square_drows,
    square_egains,
    square_dgains,
):
    n_grp = lax.axis_size("grp")
    grp_at = lax.axis_index("grp")

    def gather_rows(master):
        rows = master.shape[0]
        if rows % (16 * n_grp):
            return lax.all_gather(to_low(master), "dp", axis=0, tiled=True)
        part = rows // n_grp
        mine = lax.dynamic_slice_in_dim(master, grp_at * part, part, 0)
        return lax.all_gather(to_low(mine), ("dp", "grp"), axis=0, tiled=True)

    direct = (n_grp, lax.axis_size("dp")) == (4, 8)
    own_count = jnp.sum(group_items.astype(jnp.float32))
    if direct:
        (whole_rows, whole_cols), total_count = gather_call(
            [enc_rows, enc_cols], own_count, (4, 4), 2, 0
        )
    else:
        total_count = lax.psum(own_count, "grp")
        whole_rows, whole_cols = gather_rows(enc_rows), gather_rows(enc_cols)
    masked = total_count * (L - K)
    count_steps = step_count[0].astype(jnp.float32)
    fix_one = 1.0 - beta_first**count_steps
    fix_two = 1.0 - beta_second**count_steps
    keep_rows = keep_index[0]
    batch = keep_rows.shape[0]
    keep_column = keep_rows[..., None]
    band_row = band_group[0][:, None, :]
    gsd_row = gsd_index[0][:, None, :]
    if direct:
        shards, dec_embed = (dec_cols, dec_rows), None
    else:
        dec_copy, dec_whole = gather_rows(dec_cols), gather_rows(dec_rows)
        shards, dec_embed = (), dec_whole[DFF : DFF + D]
    latent, kept_pixels, kept_bands, saved, gathered = encoder_call(
        pixels[0],
        keep_column,
        band_row,
        gsd_row,
        gsd_table[0],
        whole_rows,
        whole_cols,
        dec_embed,
        enc_gains,
        HEADS,
        shards,
    )
    if direct:
        dec_copy, dec_whole = gathered
    latent = latent.reshape(batch, K, -1)
    first_item = lax.axis_index("dp") * batch
    valid = (first_item + jnp.arange(batch, dtype=jnp.int32) < group_items[0]).astype(jnp.float32)
    scal = jnp.stack([valid / PIX, valid * (2.0 / PIX) / masked])
    grad_latent, grad_dcols, grad_ddown, grad_head, dec_sums, loss_local = decoder_call(
        scal,
        latent,
        keep_column,
        gsd_row,
        gsd_table[0],
        pixels[0],
        dec_copy,
        dec_whole,
        dec_gains,
        DHEADS,
    )
    loss_local = loss_local[0, 0]
    grad_latent = grad_latent.reshape(batch * K, -1)
    grad_dgains = dec_sums[:7]

    def reduce_rows(pieces, axis):
        whole = jnp.concatenate([to_low(piece) for piece in pieces], axis)
        return lax.psum_scatter(whole, "dp", scatter_dimension=0, tiled=True)

    if direct:
        count_e, count_d = enc_gains.size, grad_dgains.size
        flat = jnp.concatenate([grad_dgains.reshape(-1), loss_local[None]])
        small = jnp.pad(flat, (count_e, 16 * D - count_e - flat.shape[0])).reshape(16, D)
        shards, small, squares = back_reduce_call(
            grad_latent,
            kept_pixels,
            kept_bands,
            saved,
            whole_rows,
            whole_cols,
            dec_whole,
            enc_gains,
            grad_dcols,
            grad_ddown,
            grad_head,
            small,
            HEADS,
        )
        matrices = (
            [shards[0], enc_cols, moment_ecols, square_ecols],
            [shards[1], enc_rows, moment_erows, square_erows],
            [shards[2], dec_cols, moment_dcols, square_dcols],
            [shards[3], dec_rows, moment_drows, square_drows],
        )
        gains = ([enc_gains, moment_egains, square_egains], [dec_gains, moment_dgains, square_dgains])
        return adam_call(
            jnp.stack([masked, fix_one, fix_two]).reshape(1, 3), small, squares, matrices, gains
        )
    else:
        grad_erows, grad_ecols, grad_dembed, enc_sums = encoder_back_call(
            grad_latent,
            kept_pixels,
            kept_bands,
            saved,
            whole_rows,
            whole_cols,
            dec_embed,
            enc_gains,
            HEADS,
        )
        grad_egains = enc_sums[:6]
        drows = (grad_ddown, grad_dembed, grad_head)
        enc_sum, dec_sum, loss_sum = lax.psum((grad_egains, grad_dgains, loss_local), ("grp", "dp"))
        shards = tuple(
            lax.psum(reduce_rows(pieces, 0), "grp").astype(jnp.float32)
            for pieces in ((grad_ecols,), (grad_erows,), (grad_dcols,), drows)
        )
        shard_squares = lax.psum(sum((jnp.sum(piece * piece) for piece in shards)), "dp")
    loss = loss_sum / masked
    grad_norm = jnp.sqrt(shard_squares + jnp.sum(enc_sum * enc_sum) + jnp.sum(dec_sum * dec_sum))
    factor = clip_level / jnp.maximum(grad_norm, clip_level)
    clipped_ecols, squares_ecols, updated_ecols = adam_step(
        enc_cols,
        moment_ecols,
        square_ecols,
        shards[0],
        factor,
        fix_one,
        fix_two,
        weight_decay,
        learn_rate,
    )
    clipped_erows, squares_erows, updated_erows = adam_step(
        enc_rows,
        moment_erows,
        square_erows,
        shards[1],
        factor,
        fix_one,
        fix_two,
        weight_decay,
        learn_rate,
    )
    clipped_dcols, squares_dcols, updated_dcols = adam_step(
        dec_cols,
        moment_dcols,
        square_dcols,
        shards[2],
        factor,
        fix_one,
        fix_two,
        weight_decay,
        learn_rate,
    )
    clipped_drows, squares_drows, updated_drows = adam_step(
        dec_rows,
        moment_drows,
        square_drows,
        shards[3],
        factor,
        fix_one,
        fix_two,
        weight_decay,
        learn_rate,
    )
    clipped_egains, squares_egains, updated_egains = adam_step(
        enc_gains, moment_egains, square_egains, enc_sum, factor, fix_one, fix_two, 0.0, gain_rate
    )
    clipped_dgains, squares_dgains, updated_dgains = adam_step(
        dec_gains, moment_dgains, square_dgains, dec_sum, factor, fix_one, fix_two, 0.0, gain_rate
    )
    return (
        clipped_ecols,
        squares_ecols,
        updated_ecols,
        clipped_erows,
        squares_erows,
        updated_erows,
        clipped_dcols,
        squares_dcols,
        updated_dcols,
        clipped_drows,
        squares_drows,
        updated_drows,
        clipped_egains,
        squares_egains,
        updated_egains,
        clipped_dgains,
        squares_dgains,
        updated_dgains,
        loss,
        grad_norm,
    )


def solution(mesh):
    return jax.shard_map(
        body,
        mesh=mesh,
        in_specs=(
            P("grp", "dp", None, None),
            P("grp", "dp", None),
            P("grp", "dp", None),
            P("grp", "dp", None),
            P("grp", None, None),
            P("grp"),
            P(),
            P("dp", None),
            P("dp", None),
            P("dp", None),
            P("dp", None),
            P(),
            P(),
            P("dp", None),
            P("dp", None),
            P("dp", None),
            P("dp", None),
            P(),
            P(),
            P("dp", None),
            P("dp", None),
            P("dp", None),
            P("dp", None),
            P(),
            P(),
        ),
        out_specs=(
            P("dp", None),
            P("dp", None),
            P("dp", None),
            P("dp", None),
            P("dp", None),
            P("dp", None),
            P("dp", None),
            P("dp", None),
            P("dp", None),
            P("dp", None),
            P("dp", None),
            P("dp", None),
            P(),
            P(),
            P(),
            P(),
            P(),
            P(),
            P(),
            P(),
        ),
        check_vma=False,
    )
```
